32 devices in a mesh: shard: 4 (over x, core), ctx: 4 (over z), tp: 2 (over y).
Axes of the slice: x: 2, y: 2, z: 4, core: 2. Of those that a mesh axis runs over, the one named last changes fastest.
Arguments:
- tokens: bfloat16 [10240, 1024], P(('shard', 'ctx')), may hold values from -6 to 6
- cotangent: bfloat16 [10240, 1024], P(('shard', 'ctx')), may hold values from -6 to 6
- seg_ids: int32 [10240], P(('shard', 'ctx')), may hold values from 0 to 51, as said below
- positions: int32 [10240], P(('shard', 'ctx')), may hold values from 0 to 1279, as said below
- parents: int32 [52], replicated, may hold values from 0 to 51, as said below
- w_qkv: bfloat16 [3, 1024, 1024], P(None, ('shard', 'ctx'), 'tp'), may hold values from -0.1875 to 0.1875
- b_qv: float32 [2, 1024], P(None, 'tp'), may hold values from -4 to 4
- w_out: bfloat16 [1024, 1024], P('tp', ('shard', 'ctx')), may hold values from -0.5 to 0.5
- b_out: float32 [1024], replicated, may hold values from -4 to 4
- w_up: bfloat16 [1024, 4096], P(('shard', 'ctx'), 'tp'), may hold values from -0.1875 to 0.1875
- b_up: float32 [4096], P('tp'), may hold values from -4 to 4
- w_down: bfloat16 [4096, 1024], P('tp', ('shard', 'ctx')), may hold values from -0.09375 to 0.09375
- b_down: float32 [1024], replicated, may hold values from -4 to 4
- ln_gain: float32 [2, 1024], replicated, may hold values from 0.5 to 1.5
- ln_bias: float32 [2, 1024], replicated, may hold values from -3 to 3
Outputs:
- result: bfloat16 [10240, 1024], P(('shard', 'ctx'))
- grad_tokens: float32 [10240, 1024], P(('shard', 'ctx'))
- grad_w_qkv: float32 [3, 1024, 1024], P(None, ('shard', 'ctx'), 'tp')
- grad_b_qv: float32 [2, 1024], P(None, 'tp')
- grad_w_out: float32 [1024, 1024], P('tp', ('shard', 'ctx'))
- grad_b_out: float32 [1024], replicated
- grad_w_up: float32 [1024, 4096], P(('shard', 'ctx'), 'tp')
- grad_b_up: float32 [4096], P('tp')
- grad_w_down: float32 [4096, 1024], P('tp', ('shard', 'ctx'))
- grad_b_down: float32 [1024], replicated
- grad_ln_gain: float32 [2, 1024], replicated
- grad_ln_bias: float32 [2, 1024], replicated
The draws below stay inside these ranges and needn't reach their ends.
Inputs may be any that keep to these rules, and one draw needn't show every extreme that they name: `seg_ids`: each aligned run of 2560 tokens is one tree of 13 segments: a trunk of 1024 tokens first, then 4 branches and 8 leaves of 128 tokens each, each segment's tokens adjacent and after its parent's; every segment number labels exactly one segment. Positions count from 0 at the trunk's start along the path; a segment's tokens have consecutive positions following its parent's last. `parents`: A trunk is its own parent; a branch's parent is its trunk, a leaf's parent a branch of its tree, each branch parent of two leaves.
All inputs are finite; a program needn't handle non-finite values.
Results may differ from the reference program's by a relative error of at most 0.015.
Values may be sent and summed in bfloat16 or wider, within the bound.
A program may use at most 192 MiB of HBM per device.

```python
import jax
import jax.numpy as jnp
from jax import lax

D = 1024
HEADS = 16
HD = 64
FF = 4096
TRUNK = 1024
BRANCH = 128
KEY_BLOCK = 512
TREE_LEN = 2560
TOKENS = 10240
SEGS = 52


LINKS = (0, 0, 0, 0, 0, 1, 1, 2, 2, 3, 3, 4, 4)


def tree_tables(key):
    tree_count = TOKENS // TREE_LEN
    base = jax.random.fold_in(key, 4242)
    label_key, order_key = jax.random.split(base, 2)
    labels = jax.random.permutation(label_key, SEGS).astype(jnp.int32).reshape(tree_count, 13)
    links_up = jnp.array(LINKS, dtype=jnp.int32)
    local_ids = jnp.arange(13, dtype=jnp.int32)
    random_part = jax.random.randint(order_key, (tree_count, 13), 0, 1000).astype(jnp.int32)
    level_one = jnp.where(local_ids[None, :] == 0, 0, 1 + random_part)
    ranking = jnp.where(local_ids[None, :] >= 5, level_one[:, links_up] + 1 + random_part, level_one)
    order = jnp.argsort(ranking * 16 + local_ids[None, :], axis=1).astype(jnp.int32)
    parent_labels = labels[:, links_up]
    parent_table = jnp.zeros((SEGS,), jnp.int32).at[labels.reshape(-1)].set(parent_labels.reshape(-1))
    index = jnp.arange(TREE_LEN, dtype=jnp.int32)
    slot = jnp.where(index < TRUNK, 0, 1 + (index - TRUNK) // BRANCH)
    inner = jnp.where(index < TRUNK, index, (index - TRUNK) % BRANCH)
    local_at = order[:, slot]
    seg_table = jnp.take_along_axis(labels, local_at, axis=1)
    start = jnp.where(local_at == 0, 0, jnp.where(local_at < 5, TRUNK, TRUNK + BRANCH))
    pos_table = start + inner[None, :]
    return (seg_table.reshape(-1).astype(jnp.int32), pos_table.reshape(-1).astype(jnp.int32), parent_table)


def draw_seg_ids(key, part):
    return tree_tables(key)[0]


def draw_positions(key, part):
    return tree_tables(key)[1]


def draw_parents(key, part):
    return tree_tables(key)[2]


def block_scale(rng, dims, cuts, smallest, high):
    loudness, own = 1.0, jax.random.fold_in(rng, 6)
    for axis_at, shards_of in cuts:
        draws = jnp.exp(jax.random.uniform(jax.random.fold_in(own, axis_at), (shards_of,), jnp.float32, smallest / len(cuts), high / len(cuts)))
        loudness = loudness * jnp.repeat(draws, dims[axis_at] // shards_of).reshape([-1 if axis == axis_at else 1 for axis in range(len(dims))])
    return loudness


def bell_draw(own_key, extent, scale, bound, pieces=(), kind=jnp.bfloat16):
    values = jax.random.normal(own_key, extent, jnp.float32) * scale
    if len(pieces) > 0:
        values = block_scale(own_key, extent, pieces, -0.22, 0.18) * values
    return jnp.clip(values, min=-bound, max=bound).astype(kind)


def setup_inputs(seed: int = 0) -> dict:
    key_list = jax.random.split(jax.random.key(seed), 16)
    tokens = bell_draw(key_list[0], (TOKENS, D), 1.0, 6.0, ((0, 16),))
    cotangent = bell_draw(key_list[1], (TOKENS, D), 1.0, 6.0, ((0, 16),))
    seg_ids = draw_seg_ids(jax.random.fold_in(key_list[15], 71), 0)
    positions = draw_positions(jax.random.fold_in(key_list[15], 71), 0)
    parents = draw_parents(jax.random.fold_in(key_list[15], 71), 0)
    w_qkv = bell_draw(key_list[5], (3, D, D), D ** -0.5, 0.1875, ((1, 16), (2, 2)))
    b_qv = bell_draw(key_list[6], (2, D), 0.3, 4.0, ((1, 2),), jnp.float32)
    w_out = bell_draw(key_list[7], (D, D), (D // 8) ** -0.5, 0.5, ((0, 2), (1, 16)))
    b_out = bell_draw(key_list[8], (D,), 0.3, 4.0, (), jnp.float32)
    w_up = bell_draw(key_list[9], (D, FF), D ** -0.5, 0.1875, ((0, 16), (1, 2)))
    b_up = bell_draw(key_list[10], (FF,), 0.3, 4.0, ((0, 2),), jnp.float32)
    w_down = bell_draw(key_list[11], (FF, D), FF ** -0.5, 0.09375, ((0, 2), (1, 16)))
    b_down = bell_draw(key_list[12], (D,), 0.3, 4.0, (), jnp.float32)
    ln_gain = jnp.clip(1.0 + 0.1 * jax.random.normal(key_list[13], (2, D), jnp.float32), 0.5, 1.5)
    ln_bias = bell_draw(key_list[14], (2, D), 0.2, 3.0, (), jnp.float32)
    return dict(tokens=tokens, cotangent=cotangent, seg_ids=seg_ids, positions=positions, parents=parents, w_qkv=w_qkv, b_qv=b_qv, w_out=w_out, b_out=b_out, w_up=w_up, b_up=b_up, w_down=w_down, b_down=b_down, ln_gain=ln_gain, ln_bias=ln_bias)


EPS = 1e-05
NEG = -1e+30
HIGH = lax.Precision.HIGHEST

@jax.custom_vjp
def low(v):
    return lax.optimization_barrier(v.astype(jnp.bfloat16)).astype(jnp.float32)

@jax.custom_vjp
def low_back(v):
    return v

def low_keep(v):
    return (low(v), None)

def low_pass(kept, grad):
    return (grad,)

def back_keep(v):
    return (v, None)

def back_low(kept, grad):
    return (low(grad),)
low.defvjp(low_keep, low_pass)
low_back.defvjp(back_keep, back_low)

def norm_layer(inputs_in, gain_row, shift_row):
    centre = inputs_in - lax.optimization_barrier(jnp.mean(inputs_in, axis=-1, keepdims=True))
    inverse = lax.rsqrt(lax.optimization_barrier(jnp.mean(centre * centre, axis=-1, keepdims=True)) + EPS)
    return centre * inverse * gain_row + shift_row

def tree_attention(queries, keys_in, values_in, seg_tree, pos_tree, parents):
    first_up = parents[seg_tree]
    second_up = parents[first_up]
    slopes = 2.0 ** (-8.0 * (jnp.arange(HEADS, dtype=jnp.float32) + 1.0) / HEADS)
    block_count = TREE_LEN // KEY_BLOCK

    def one_block(block_parts):
        query_part, seg_part, first_part, second_part, pos_part = block_parts
        raw_scores = jnp.einsum('qhd,khd->hqk', query_part, keys_in, precision=HIGH) * HD ** (-0.5)
        distance = (pos_part[:, None] - pos_tree[None, :]).astype(jnp.float32)
        scores = low_back(raw_scores - slopes[:, None, None] * distance[None])
        related = (seg_tree[None, :] == seg_part[:, None]) | (seg_tree[None, :] == first_part[:, None]) | (seg_tree[None, :] == second_part[:, None])
        allowed = (related & (pos_tree[None, :] <= pos_part[:, None]))[None]
        row_max = lax.optimization_barrier(jnp.max(jnp.where(allowed, scores, NEG), axis=-1, keepdims=True))
        exp_terms = jnp.exp(jnp.where(allowed, scores - row_max, NEG))
        prob_low = low(exp_terms / lax.optimization_barrier(jnp.sum(exp_terms, axis=-1, keepdims=True)))
        return jnp.einsum('hqk,khd->qhd', prob_low, values_in, precision=HIGH)

    def in_blocks(array_in):
        return array_in.reshape((block_count, KEY_BLOCK) + array_in.shape[1:])
    blocks_out = lax.map(jax.checkpoint(one_block), (in_blocks(queries), in_blocks(seg_tree), in_blocks(first_up), in_blocks(second_up), in_blocks(pos_tree)))
    return blocks_out.reshape(TREE_LEN, HEADS, HD)

def layer(tokens_f, w_qkv, b_qv, w_out, b_out, w_up, b_up, w_down, b_down, ln_gain, ln_bias, seg_ids, positions, parents):
    act_one = low(norm_layer(tokens_f, ln_gain[0], ln_bias[0]))
    queries = low(low_back(jnp.dot(act_one, w_qkv[0], precision=HIGH) + b_qv[0]))
    keys_all = low(low_back(jnp.dot(act_one, w_qkv[1], precision=HIGH)))
    values_all = low(low_back(jnp.dot(act_one, w_qkv[2], precision=HIGH) + b_qv[1]))
    tree_count = TOKENS // TREE_LEN
    head_shape = (tree_count, TREE_LEN, HEADS, HD)
    tag_shape = (tree_count, TREE_LEN)

    def per_tree(tree_parts):
        return tree_attention(tree_parts[0], tree_parts[1], tree_parts[2], tree_parts[3], tree_parts[4], parents)
    attended = lax.map(per_tree, (queries.reshape(head_shape), keys_all.reshape(head_shape), values_all.reshape(head_shape), seg_ids.reshape(tag_shape), positions.reshape(tag_shape)))
    attended_low = low(low_back(attended.reshape(TOKENS, D)))
    middle = tokens_f + low_back(jnp.dot(attended_low, w_out, precision=HIGH) + b_out)
    act_two = low(norm_layer(middle, ln_gain[1], ln_bias[1]))
    upper_in = low_back(jnp.dot(act_two, w_up, precision=HIGH) + b_up)
    hidden = low(jax.nn.gelu(upper_in, approximate=True))
    return middle + low_back(jnp.dot(hidden, w_down, precision=HIGH) + b_down)

def reference(tokens, cotangent, seg_ids, positions, parents, w_qkv, b_qv, w_out, b_out, w_up, b_up, w_down, b_down, ln_gain, ln_bias):

    def forward(*params_in):
        return layer(*params_in, seg_ids, positions, parents)
    floats = tuple((param.astype(jnp.float32) for param in (tokens, w_qkv, b_qv, w_out, b_out, w_up, b_up, w_down, b_down, ln_gain, ln_bias)))
    output, pull = jax.vjp(forward, *floats)
    grads = pull(cotangent.astype(jnp.float32))
    return (output.astype(jnp.bfloat16), grads[0], grads[1], grads[2], grads[3], grads[4], grads[5], grads[6], grads[7], grads[8], grads[9], grads[10])
```

```python
from functools import partial

import jax
import jax.numpy as jnp
from jax import lax
from jax.experimental import pallas as pl
from jax.experimental.pallas import tpu as pltpu
from jax.sharding import PartitionSpec as P

HEADS = 16
HD = 64
KEY_BLOCK = 512
TRUNK = 1024
BRANCH = 128
SLOTS = 12
TREE = TRUNK + SLOTS * BRANCH
PAIR = 2 * HD

EPS = 1e-05
NEG = -1e30
LOG2E = 1.4426950408889634
MESH = pl.DeviceIdType.MESH
BF = jnp.bfloat16
F32 = jnp.float32
ROWS_WAVE = 4


def nt(left, right):
    return lax.dot_general(left, right, (((1,), (1,)), ((), ())), preferred_element_type=F32)


def nn(left, right):
    return lax.dot_general(left, right, (((1,), (0,)), ((), ())), preferred_element_type=F32)


def rcopy(src, dst, send, recv, device):
    return pltpu.make_async_remote_copy(
        src_ref=src, dst_ref=dst, send_sem=send, recv_sem=recv, device_id=device, device_id_type=MESH
    )


def greet(devices):
    barrier = pltpu.get_barrier_semaphore()
    for device in devices:
        pl.semaphore_signal(barrier, inc=1, device_id=device, device_id_type=MESH)
    pl.semaphore_wait(barrier, len(devices))


def norm_rows(values, gain_row, shift_row):
    centre = values - jnp.mean(values, axis=-1, keepdims=True)
    inverse = lax.rsqrt(jnp.mean(centre * centre, axis=-1, keepdims=True) + EPS)
    normed = centre * inverse
    return normed * gain_row + shift_row, normed, inverse


def norm_rows_back(grad_in, normed, inverse, gain_row):
    scaled = grad_in * gain_row
    mean_grad = jnp.mean(scaled, axis=-1, keepdims=True)
    mean_cross = jnp.mean(scaled * normed, axis=-1, keepdims=True)
    return inverse * (scaled - mean_grad - normed * mean_cross)


def head_masks():
    lane = lax.broadcasted_iota(jnp.int32, (1, PAIR), 1)
    first = (lane < HD).astype(F32).astype(BF)
    second = (lane >= HD).astype(F32).astype(BF)
    return first, second


def stack_heads(rows):
    first, second = head_masks()
    return jnp.concatenate([rows * first, rows * second], axis=0)


def unstack_turned(turned, rows):
    return jnp.concatenate([turned[:HD, :rows], turned[HD:, rows:]], axis=0).T


def key_features(high, low, flag, rows):
    lane = lax.broadcasted_iota(jnp.int32, (rows, 128), 1)
    feats = jnp.where(lane < 3, high, jnp.where(lane < 6, low, jnp.where(lane == 6, flag, 0.0)))
    return feats.astype(BF)


def query_features(slope_ref, rows):
    return jnp.concatenate(
        [
            jnp.broadcast_to(slope_ref[0:1, :], (rows, 128)),
            jnp.broadcast_to(slope_ref[1:2, :], (rows, 128)),
        ],
        axis=0,
    ).astype(BF)


def fill_trunk_keys(key_ref, keys_aug):
    keys_aug[:, 0:PAIR] = key_ref[0:TRUNK, :]
    pos = lax.broadcasted_iota(jnp.int32, (TRUNK, 128), 0)
    low = pos & 255
    keys_aug[:, PAIR:] = key_features((pos - low).astype(F32), low.astype(F32), 0.0, TRUNK)


def fill_labels(info_all, blocks, labels, parents):
    labels[...] = jnp.full(labels.shape, -1.0, F32)
    parents[...] = jnp.full(parents.shape, -2.0, F32)
    for slot in range(SLOTS):
        block = TRUNK // BRANCH + slot
        owner, inner = block // blocks, block % blocks
        labels[slot : slot + 1, :] = info_all[owner, inner : inner + 1, :]
        parents[slot : slot + 1, :] = info_all[owner, 8 + inner : 9 + inner, :]


def parent_pick(slot, labels, parents, key_ref, value_ref):
    mine = parents[pl.ds(slot, 1), :]
    leaf = jnp.zeros((1, 128), F32)
    key_sum = jnp.zeros((BRANCH, PAIR), BF)
    value_sum = jnp.zeros((BRANCH, PAIR), BF)
    for other in range(SLOTS):
        same = (mine == labels[other : other + 1, :]).astype(F32)
        leaf = leaf + same
        same_low = same.astype(BF)
        at = TRUNK + other * BRANCH
        key_sum = key_sum + same_low * key_ref[at : at + BRANCH, :]
        value_sum = value_sum + same_low * value_ref[at : at + BRANCH, :]
    return leaf, key_sum, value_sum


def segment_key_features(leaf):
    row = lax.broadcasted_iota(jnp.int32, (BRANCH, 128), 0).astype(F32)
    own = key_features(float(TRUNK), row + leaf * float(BRANCH), 0.0, BRANCH)
    above = key_features(float(TRUNK), row, (leaf - 1.0) * 1e30, BRANCH)
    return own, above


def causal(rows):
    key = lax.broadcasted_iota(jnp.int32, (rows, rows), 0)
    query = lax.broadcasted_iota(jnp.int32, (rows, rows), 1)
    once = key <= query
    return jnp.concatenate([once, once], axis=1)


def tree_kernel(
    dims,
    tok,
    wq,
    info,
    bias_qv,
    slopes,
    gain,
    shift,
    act_turned,
    query,
    key,
    value,
    out_heads,
    lse,
    info_all,
    att,
    tree,
    wcat,
    keys_aug,
    values_turned,
    labels,
    parents,
    info_send,
    info_recv,
    wz_send,
    wz_recv,
    ws_send,
    ws_recv,
    z_send,
    z_recv,
    y_send,
    y_recv,
    a_send,
    a_recv,
    local_sem,
):
    ns, nz, rows = dims
    s, z, y = lax.axis_index("shard"), lax.axis_index("ctx"), lax.axis_index("tp")
    half = rows // 2
    sub = half // 2
    greet(
        [{"ctx": lax.rem(z + d, nz)} for d in range(1, nz)]
        + [{"shard": lax.rem(s + d, ns)} for d in range(1, ns)]
        + [{"tp": 1 - y}]
    )
    start = pltpu.make_async_copy(tok, tree.at[pl.ds(z * rows, rows), :], local_sem)
    start.start()

    depth = wq.shape[0]
    wide = 3 * PAIR
    my_rows = pl.ds((s * nz + z) * depth, depth)

    def info_copy(d):
        return rcopy(
            info, info_all.at[z], info_send.at[d - 1], info_recv.at[d - 1], {"ctx": lax.rem(z + d, nz)}
        )

    def wz_copy(d):
        to = lax.rem(z + d, nz)
        return rcopy(
            wq.at[:, pl.ds(pl.multiple_of(to * wide, 128), wide)],
            wcat.at[my_rows, :],
            wz_send.at[d - 1],
            wz_recv.at[d - 1],
            {"ctx": to},
        )

    shard_rows = pl.ds(s * (nz * depth), nz * depth)

    def ws_copy(d):
        return rcopy(
            wcat.at[shard_rows, :],
            wcat.at[shard_rows, :],
            ws_send.at[d - 1],
            ws_recv.at[d - 1],
            {"shard": lax.rem(s + d, ns)},
        )

    for d in range(1, nz):
        wz_copy(d).start()
    for d in range(1, nz):
        info_copy(d).start()
    wcat[my_rows, :] = wq[:, pl.ds(pl.multiple_of(z * wide, 128), wide)]
    info_all[z] = info[...]
    start.wait()

    def piece(block, second, part):
        at = block * rows + jnp.where(second, 1 - y, y) * half + part * sub
        return tree.at[pl.ds(pl.multiple_of(at, 32), sub), :]

    def z_copy(direction, k, part):
        block = z - k if direction == 0 else z + k
        to = z + 1 if direction == 0 else z - 1
        ref = piece(block, False, part)
        return rcopy(ref, ref, z_send.at[direction, k, part], z_recv.at[direction, k, part], {"ctx": to})

    def z_arrival(direction, k, part):
        block = z - k if direction == 0 else z + k
        ref = piece(block, False, part)
        return rcopy(
            ref, ref, z_send.at[direction, k - 1, part], z_recv.at[direction, k - 1, part], {"ctx": z}
        )

    def y_copy(direction, k, part):
        block = z - k if direction == 0 else z + k
        ref = piece(block, False, part)
        return rcopy(
            ref, ref, y_send.at[direction, k - 1, part], y_recv.at[direction, k - 1, part], {"tp": 1 - y}
        )

    def y_arrival(direction, k, part):
        block = z - k if direction == 0 else z + k
        ref = piece(block, True, part)
        return rcopy(
            ref, ref, y_send.at[direction, k - 1, part], y_recv.at[direction, k - 1, part], {"tp": 1 - y}
        )

    def place(direction, k):
        block = z - k if direction == 0 else z + k
        nxt = z + 1 if direction == 0 else z - 1
        here = (block >= 0) & (block < nz)
        onward = here & (nxt >= 0) & (nxt < nz)
        return block, here, onward

    def forward(k, first):
        for part in range(2):
            for direction in range(2):
                _, here, onward = place(direction, k)
                if not first:

                    @pl.when(here)
                    def _():
                        z_arrival(direction, k, part).wait_recv()

                @pl.when(onward & (k < nz - 1))
                def _():
                    z_copy(direction, k, part).start()

                if not first:

                    @pl.when(here)
                    def _():
                        y_copy(direction, k, part).start()

    forward(0, True)
    for d in range(1, nz):
        wz_copy(d).wait_recv()
    for d in range(1, ns):
        ws_copy(d).start()

    bias_at = pl.ds(pl.multiple_of(z * PAIR, 128), PAIR)
    bias_q = bias_qv[0:1, bias_at]
    bias_v = bias_qv[1:2, bias_at]

    def project(block):
        def tile(t, carry):
            at = pl.multiple_of(block * rows + t * 128, 128)
            here = pl.ds(at, 128)
            act = norm_rows(tree[here, :].astype(F32), gain[0:1, :], shift[0:1, :])[0].astype(BF)
            act_turned[:, here] = act.T
            both = nn(act, wcat[...])
            query[here, :] = ((both[:, :PAIR] + bias_q).astype(BF).astype(F32) * HD ** (-0.5)).astype(BF)
            key[here, :] = both[:, PAIR : 2 * PAIR].astype(BF)
            value[here, :] = (both[:, 2 * PAIR :] + bias_v).astype(BF)
            return carry

        lax.fori_loop(0, rows // 128, tile, 0)

    for d in range(1, ns):
        ws_copy(d).wait_recv()

    def wave(k, carry):
        @pl.when(k > 0)
        def _():
            forward(k, False)
            for part in range(2):
                for direction in range(2):
                    _, here, _ = place(direction, k)

                    @pl.when(here)
                    def _():
                        y_arrival(direction, k, part).wait_recv()

        def side(direction, inner):
            block = z + (2 * direction - 1) * k

            @pl.when((block >= 0) & (block < nz) & ((k > 0) | (direction == 0)))
            def _():
                project(block)

            return inner

        return lax.fori_loop(0, 2, side, carry)

    lax.fori_loop(0, nz, wave, 0)

    for d in range(1, nz):
        info_copy(d).wait_recv()

    fill_labels(info_all, rows // BRANCH, labels, parents)
    fill_trunk_keys(key, keys_aug)
    values_turned[...] = value[0:TRUNK, :].T

    def att_copy(to):
        return rcopy(
            out_heads.at[pl.ds(to * rows, rows), :],
            att.at[:, pl.ds(pl.multiple_of(z * PAIR, 128), PAIR)],
            a_send.at[to],
            a_recv.at[z],
            {"ctx": to},
        )

    def send_out(to):
        @pl.when(z != to)
        def _():
            att_copy(to).start()

        @pl.when(z == to)
        def _():
            att[:, pl.ds(pl.multiple_of(z * PAIR, 128), PAIR)] = out_heads[to * rows : (to + 1) * rows, :]

    tile_mask = causal(BRANCH)
    owners = [((owner + 1) * rows - TRUNK) // BRANCH - 1 for owner in range(nz)]

    def segment(slot, carry):
        here = pl.ds(pl.multiple_of(TRUNK + slot * BRANCH, 128), BRANCH)
        asked = jnp.concatenate(
            [stack_heads(query[here, :]), query_features(slopes, BRANCH)], axis=1
        )
        leaf, key_up, value_up = parent_pick(slot, labels, parents, key, value)
        own_feats, up_feats = segment_key_features(leaf)
        trunk_part = nt(keys_aug[...], asked) * LOG2E
        own_part = nt(jnp.concatenate([key[here, :], own_feats], axis=1), asked) * LOG2E
        own_part = jnp.where(tile_mask, own_part, NEG)
        up_part = nt(jnp.concatenate([key_up, up_feats], axis=1), asked) * LOG2E
        top = jnp.maximum(
            jnp.max(trunk_part, axis=0, keepdims=True),
            jnp.maximum(
                jnp.max(own_part, axis=0, keepdims=True), jnp.max(up_part, axis=0, keepdims=True)
            ),
        )
        trunk_part = jnp.exp2(trunk_part - top)
        own_part = jnp.exp2(own_part - top)
        up_part = jnp.exp2(up_part - top)
        total = (
            jnp.sum(trunk_part, axis=0, keepdims=True)
            + jnp.sum(own_part, axis=0, keepdims=True)
            + jnp.sum(up_part, axis=0, keepdims=True)
        )
        turned = nn(values_turned[...], trunk_part.astype(BF))
        turned = turned + nn(value[here, :].T, own_part.astype(BF))
        turned = turned + nn(value_up.T, up_part.astype(BF))
        turned = turned / total
        out_heads[here, :] = unstack_turned(turned, BRANCH).astype(BF)
        lse[pl.ds(4 + slot, 1), 0 : 2 * BRANCH] = top + jnp.log2(total)
        for owner in range(nz):
            if owners[owner] >= 0 and owner * rows >= TRUNK:

                @pl.when(slot == owners[owner])
                def _():
                    send_out(owner)

        return carry

    lax.fori_loop(0, SLOTS, segment, 0)

    wave_rows = TRUNK // 4
    wave_mask = causal(wave_rows)
    sent = 0
    for tile in range(4):
        lo, hi = tile * wave_rows, (tile + 1) * wave_rows
        asked = jnp.concatenate(
            [stack_heads(query[lo:hi, :]), query_features(slopes, wave_rows)], axis=1
        )
        edge = jnp.where(wave_mask, nt(keys_aug[lo:hi, :], asked) * LOG2E, NEG)
        top = jnp.max(edge, axis=0, keepdims=True)
        if tile:
            body = nt(keys_aug[0:lo, :], asked) * LOG2E
            top = jnp.maximum(top, jnp.max(body, axis=0, keepdims=True))
            body = jnp.exp2(body - top)
        edge = jnp.exp2(edge - top)
        total = jnp.sum(edge, axis=0, keepdims=True)
        turned = nn(values_turned[:, lo:hi], edge.astype(BF))
        if tile:
            total = total + jnp.sum(body, axis=0, keepdims=True)
            turned = turned + nn(values_turned[:, 0:lo], body.astype(BF))
        turned = turned / total
        out_heads[lo:hi, :] = unstack_turned(turned, wave_rows).astype(BF)
        lse[tile : tile + 1, :] = top + jnp.log2(total)
        while sent < nz and sent * rows < TRUNK and (sent + 1) * rows <= (hi if hi < TRUNK else TREE):
            send_out(sent)
            sent += 1

    for owner in range(nz):

        @pl.when(z != owner)
        def _():
            rcopy(
                out_heads.at[0:rows, :],
                att.at[:, owner * PAIR : (owner + 1) * PAIR],
                a_send.at[owner],
                a_recv.at[owner],
                {"ctx": owner},
            ).wait_recv()

    for owner in range(nz):

        @pl.when(z != owner)
        def _():
            att_copy(owner).wait_send()

    for d in range(1, nz):
        info_copy(d).wait_send()
        wz_copy(d).wait_send()
    for d in range(1, ns):
        ws_copy(d).wait_send()

    def drain(k, carry):
        for part in range(2):
            for direction in range(2):
                _, here, onward = place(direction, k)

                @pl.when(onward & (k < nz - 1))
                def _():
                    z_copy(direction, k, part).wait_send()

                @pl.when(here & (k > 0))
                def _():
                    y_copy(direction, k, part).wait_send()

        return carry

    lax.fori_loop(0, nz, drain, 0)


def vmem():
    return pl.BlockSpec(memory_space=pltpu.VMEM)


def shape(dims, kind):
    return jax.ShapeDtypeStruct(dims, kind)


def dma(*dims):
    return pltpu.SemaphoreType.DMA(dims)


def run_tree(dims, tok, wq, info, bias_qv, slopes, gain, shift):
    ns, nz, rows = dims
    width = tok.shape[1]
    return pl.pallas_call(
        partial(tree_kernel, dims),
        name="tree_forward",
        out_shape=(
            shape((width, TREE), BF),
            shape((TREE, PAIR), BF),
            shape((TREE, PAIR), BF),
            shape((TREE, PAIR), BF),
            shape((TREE, PAIR), BF),
            shape((16, 512), F32),
            shape((nz, 16, 128), F32),
            shape((rows, nz * PAIR), BF),
        ),
        in_specs=[pl.BlockSpec(memory_space=pl.ANY)] + [vmem()] * 6,
        out_specs=[vmem()] * 8,
        scratch_shapes=[
            pltpu.VMEM((TREE, width), BF),
            pltpu.VMEM((width, 3 * PAIR), BF),
            pltpu.VMEM((TRUNK, 2 * PAIR), BF),
            pltpu.VMEM((PAIR, TRUNK), BF),
            pltpu.VMEM((16, 128), F32),
            pltpu.VMEM((16, 128), F32),
            dma(nz - 1),
            dma(nz - 1),
            dma(nz - 1),
            dma(nz - 1),
            dma(ns - 1),
            dma(ns - 1),
            dma(2, nz, 2),
            dma(2, nz, 2),
            dma(2, nz, 2),
            dma(2, nz, 2),
            dma(nz),
            dma(nz),
            pltpu.SemaphoreType.DMA,
        ],
        compiler_params=pltpu.CompilerParams(
            collective_id=0, has_side_effects=True, vmem_limit_bytes=48 << 20
        ),
        cost_estimate=pl.CostEstimate(flops=40_000_000_000, bytes_accessed=20_000_000, transcendentals=0),
    )(tok, wq, info, bias_qv, slopes, gain, shift)


UP, OUT, DOWN = "up", "out", "down"
BLOCK = 512
CURVE = 0.044715
ROOT = 0.7978845608028654


def feed_kernel(
    dims,
    tok,
    cot,
    att,
    wa,
    wd,
    b_out,
    b_up,
    b_down,
    gain,
    shift,
    gsum,
    ga_all,
    down_part,
    resid,
    gmid,
    sums,
    act,
    hidden,
    gup,
    gbranch,
    mid,
    o_send,
    o_recv,
    g_send,
    g_recv,
    ga_send,
    bup_acc,
    os_sem,
    or_sem,
    gs_sem,
    gr_sem,
    as_sem,
    ar_sem,
):
    ns, nz, rows = dims
    z, y = lax.axis_index("ctx"), lax.axis_index("tp")
    chunk = rows // ROWS_WAVE
    width = tok.shape[1]
    units = b_up.shape[1]
    inner = att.shape[1]
    greet([{"tp": 1 - y}] + [{"ctx": lax.rem(z + d, nz)} for d in range(1, nz)])
    other = {"tp": 1 - y}

    def at(i):
        return pl.ds(pl.multiple_of(i * chunk, 32), chunk)

    def o_copy(i):
        return rcopy(o_send.at[at(i), :], o_recv.at[at(i), :], os_sem.at[i], or_sem.at[i], other)

    def g_copy(i):
        return rcopy(g_send.at[at(i), :], g_recv.at[at(i), :], gs_sem.at[i], gr_sem.at[i], other)

    def a_copy(i, d):
        to = lax.rem(z + d, nz)
        return rcopy(
            ga_send.at[at(i), pl.ds(pl.multiple_of(to * PAIR, 128), PAIR)],
            ga_all.at[pl.ds(pl.multiple_of(z * rows + i * chunk, 32), chunk), :],
            as_sem.at[d - 1, i],
            ar_sem.at[d - 1, i],
            {"ctx": to},
        )

    sums[...] = jnp.zeros(sums.shape, F32)
    bup_acc[...] = jnp.zeros(bup_acc.shape, F32)

    def stage_a(i, carry):
        o_send[at(i), :] = nt(att[at(i), :], wa[:, units : units + inner]).astype(BF)
        o_copy(i).start()
        return carry

    lax.fori_loop(0, ROWS_WAVE, stage_a, 0)

    def stage_b(i, carry):
        o_copy(i).wait_recv()
        here = at(i)
        branch = o_send[here, :].astype(F32) + o_recv[here, :].astype(F32) + b_out[...]
        middle = tok[here, :].astype(F32) + branch
        mid[here, :] = middle
        resid[here, :] = middle + b_down[...]
        act[here, :] = norm_rows(middle, gain[1:2, :], shift[1:2, :])[0].astype(BF)

        def columns(c, inner_carry):
            cols = pl.ds(pl.multiple_of(c * BLOCK, 128), BLOCK)
            upper = nn(act[here, :], wa[:, cols]) + b_up[:, cols]
            slope = nn(cot[here, :], wd[:, cols])
            square = upper * upper
            turn = jnp.tanh(ROOT * (upper + CURVE * (square * upper)))
            hidden[here, cols] = (0.5 * upper * (1.0 + turn)).astype(BF)
            steep = 0.5 * (1.0 + turn) + (0.5 * ROOT) * upper * (1.0 - turn * turn) * (
                1.0 + (3.0 * CURVE) * square
            )
            low = (slope * steep).astype(BF)
            gup[here, cols] = low
            bup_acc[:, cols] += jnp.sum(low.astype(F32), axis=0, keepdims=True)
            return inner_carry

        lax.fori_loop(0, units // BLOCK, columns, 0)
        g_send[here, :] = nt(gup[here, :], wa[:, 0:units]).astype(BF)
        g_copy(i).start()
        down_part[here, :] = nt(hidden[here, :], wd[:, 0:units]).astype(BF)
        return carry

    lax.fori_loop(0, ROWS_WAVE, stage_b, 0)

    def weight_one(d, carry):
        cols = pl.ds(pl.multiple_of(d * 128, 128), 128)
        gsum[cols, units + inner : 2 * units + inner] = nn(cot[:, cols].T, hidden[...]).astype(BF)
        gsum[cols, 0:units] = nn(act[:, cols].T, gup[...]).astype(BF)
        return carry

    lax.fori_loop(0, width // 128, weight_one, 0)

    def stage_c(i, carry):
        g_copy(i).wait_recv()
        here = at(i)
        grad = g_send[here, :].astype(F32) + g_recv[here, :].astype(F32)
        _, normed, inverse = norm_rows(mid[here, :], gain[1:2, :], shift[1:2, :])
        given = cot[here, :].astype(F32)
        grad_middle = given + norm_rows_back(grad, normed, inverse, gain[1:2, :])
        gmid[here, :] = grad_middle
        low = grad_middle.astype(BF)
        gbranch[here, :] = low
        sums[2:3, :] += jnp.sum(low.astype(F32), axis=0, keepdims=True)
        sums[3:4, :] += jnp.sum(given, axis=0, keepdims=True)
        sums[4:5, :] += jnp.sum(grad * normed, axis=0, keepdims=True)
        sums[5:6, :] += jnp.sum(grad, axis=0, keepdims=True)
        ga_send[here, :] = nn(low, wa[:, units : units + inner]).astype(BF)
        for d in range(1, nz):
            a_copy(i, d).start()
        ga_all[pl.ds(pl.multiple_of(z * rows + i * chunk, 32), chunk), :] = ga_send[
            here, pl.ds(pl.multiple_of(z * PAIR, 128), PAIR)
        ]
        return carry

    lax.fori_loop(0, ROWS_WAVE, stage_c, 0)

    def weight_two(d, carry):
        cols = pl.ds(pl.multiple_of(d * 128, 128), 128)
        gsum[cols, units : units + inner] = nn(gbranch[:, cols].T, att[...]).astype(BF)
        return carry

    lax.fori_loop(0, width // 128, weight_two, 0)
    for part in range(units // width):
        sums[part : part + 1, :] = bup_acc[:, part * width : (part + 1) * width]

    def finish(i, carry):
        o_copy(i).wait_send()
        g_copy(i).wait_send()
        for d in range(1, nz):
            a_copy(i, d).wait_send()
            a_copy(i, d).wait_recv()
        return carry

    lax.fori_loop(0, ROWS_WAVE, finish, 0)


def run_feed(dims, tok, cot, att, wa, wd, b_out, b_up, b_down, gain, shift):
    ns, nz, rows = dims
    width, units, inner = tok.shape[1], b_up.shape[1], att.shape[1]
    return pl.pallas_call(
        partial(feed_kernel, dims),
        name="feed_both",
        out_shape=(
            shape((width, 2 * units + inner), BF),
            shape((TREE, PAIR), BF),
            shape((rows, width), BF),
            shape((rows, width), F32),
            shape((rows, width), F32),
            shape((8, width), F32),
        ),
        in_specs=[vmem()] * 10,
        out_specs=[vmem()] * 6,
        scratch_shapes=[
            pltpu.VMEM((rows, width), BF),
            pltpu.VMEM((rows, units), BF),
            pltpu.VMEM((rows, units), BF),
            pltpu.VMEM((rows, width), BF),
            pltpu.VMEM((rows, width), F32),
            pltpu.VMEM((rows, width), BF),
            pltpu.VMEM((rows, width), BF),
            pltpu.VMEM((rows, width), BF),
            pltpu.VMEM((rows, width), BF),
            pltpu.VMEM((rows, inner), BF),
            pltpu.VMEM((1, units), F32),
            dma(ROWS_WAVE),
            dma(ROWS_WAVE),
            dma(ROWS_WAVE),
            dma(ROWS_WAVE),
            dma(nz - 1, ROWS_WAVE),
            dma(nz - 1, ROWS_WAVE),
        ],
        compiler_params=pltpu.CompilerParams(
            collective_id=1, has_side_effects=True, vmem_limit_bytes=60 << 20
        ),
        cost_estimate=pl.CostEstimate(flops=40_000_000_000, bytes_accessed=20_000_000, transcendentals=0),
    )(tok, cot, att, wa, wd, b_out, b_up, b_down, gain, shift)


def back_kernel(
    dims,
    query,
    key,
    value,
    out_heads,
    lse,
    info_all,
    ga_all,
    act_turned,
    wd,
    down_part,
    resid,
    gmid,
    tok,
    slopes,
    gain,
    shift,
    early,
    result,
    gtok,
    gwqkv,
    early_sum,
    late_sum,
    dqkv,
    dk_trunk,
    dv_trunk,
    dk_seg,
    dv_seg,
    dk_up,
    dv_up,
    keys_aug,
    keys_turned,
    labels,
    parents,
    dq_all,
    n_send,
    n_recv,
    down_recv,
    wg_send,
    wg_recv,
    early_recv,
    late,
    late_recv,
    d_sem,
    e_send,
    e_recv,
    l_send,
    l_recv,
    w_send,
    w_recv,
    p_send,
    p_recv,
    ns_sem,
    nr_sem,
):
    ns, nz, rows = dims
    s, z, y = lax.axis_index("shard"), lax.axis_index("ctx"), lax.axis_index("tp")
    count = ns * nz
    me = s * nz + z
    chunk = rows // ROWS_WAVE
    width = tok.shape[1]
    depth = width // count
    wide = 3 * PAIR
    units = wd.shape[1] - nz * wide
    other = {"tp": 1 - y}

    def peer(d):
        index = lax.rem(me + d, count)
        return index, {"shard": index // nz, "ctx": lax.rem(index, nz)}

    greet([other] + [peer(d)[1] for d in range(1, count)])

    def down_copy():
        return rcopy(down_part, down_recv, d_sem.at[0], d_sem.at[1], other)

    def early_copy(d):
        return rcopy(early, early_recv.at[me], e_send.at[d - 1], e_recv.at[d - 1], peer(d)[1])

    def late_copy(d):
        return rcopy(late, late_recv.at[me], l_send.at[d - 1], l_recv.at[d - 1], peer(d)[1])

    def wg_copy(d):
        index, device = peer(d)
        return rcopy(
            wg_send.at[pl.ds(pl.multiple_of(index * depth, depth), depth), :],
            wg_recv.at[me],
            w_send.at[d - 1],
            w_recv.at[d - 1],
            device,
        )

    def over_peers(act):
        def one(d, carry):
            act(d)
            return carry

        lax.fori_loop(1, count, one, 0)

    down_copy().start()
    over_peers(lambda d: early_copy(d).start())
    early_recv[me] = early[...]

    fill_labels(info_all, rows // BRANCH, labels, parents)
    fill_trunk_keys(key, keys_aug)
    keys_turned[...] = key[0:TRUNK, :].T
    dk_trunk[...] = jnp.zeros(dk_trunk.shape, F32)
    dv_trunk[...] = jnp.zeros(dv_trunk.shape, F32)
    tile_mask = causal(BRANCH)

    def row_products(here, count_rows):
        turned = (ga_all[here, :].astype(F32) * out_heads[here, :].astype(F32)).T
        return jnp.concatenate(
            [
                jnp.sum(turned[:HD, :], axis=0, keepdims=True),
                jnp.sum(turned[HD:, :], axis=0, keepdims=True),
            ],
            axis=1,
        )

    def part_back(key_aug, value_rows, asked, given, level, drow, mask):
        logits = nt(key_aug, asked) * LOG2E - level
        if mask is not None:
            logits = jnp.where(mask, logits, NEG)
        probs = jnp.exp2(logits)
        grads = (probs * (nt(value_rows, given) - drow)).astype(BF)
        return probs.astype(BF), grads

    def segment(slot, carry):
        here = pl.ds(pl.multiple_of(TRUNK + slot * BRANCH, 128), BRANCH)
        seg = pl.ds(pl.multiple_of(slot * BRANCH, 128), BRANCH)
        stacked = stack_heads(query[here, :])
        asked = jnp.concatenate([stacked, query_features(slopes, BRANCH)], axis=1)
        given = stack_heads(ga_all[here, :])
        leaf, key_up, value_up = parent_pick(slot, labels, parents, key, value)
        own_feats, up_feats = segment_key_features(leaf)
        level = lse[pl.ds(4 + slot, 1), 0 : 2 * BRANCH]
        drow = row_products(here, BRANCH)
        probs, grads = part_back(keys_aug[...], value[0:TRUNK, :], asked, given, level, drow, None)
        dv_trunk[...] += nn(probs, given)
        dk_trunk[...] += nn(grads, stacked)
        turned = nn(keys_turned[...], grads)
        key_own = key[here, :]
        probs, grads = part_back(
            jnp.concatenate([key_own, own_feats], axis=1), value[here, :], asked, given, level, drow, tile_mask
        )
        dv_seg[seg, :] = nn(probs, given)
        dk_seg[seg, :] = nn(grads, stacked)
        turned = turned + nn(key_own.T, grads)
        probs, grads = part_back(
            jnp.concatenate([key_up, up_feats], axis=1), value_up, asked, given, level, drow, None
        )
        dv_up[seg, :] = nn(probs, given)
        dk_up[seg, :] = nn(grads, stacked)
        turned = turned + nn(key_up.T, grads)
        dqkv[here, 0:PAIR] = (unstack_turned(turned, BRANCH) * HD ** (-0.5)).astype(BF)
        return carry

    lax.fori_loop(0, SLOTS, segment, 0)

    def gather_up(slot, carry):
        here = pl.ds(pl.multiple_of(TRUNK + slot * BRANCH, 128), BRANCH)
        seg = pl.ds(pl.multiple_of(slot * BRANCH, 128), BRANCH)
        mine = labels[pl.ds(slot, 1), :]
        dk, dv = dk_seg[seg, :], dv_seg[seg, :]
        for below in range(SLOTS):
            same = (parents[below : below + 1, :] == mine).astype(F32)
            at = below * BRANCH
            dk = dk + same * dk_up[at : at + BRANCH, :]
            dv = dv + same * dv_up[at : at + BRANCH, :]
        dqkv[here, PAIR : 2 * PAIR] = dk.astype(BF)
        dqkv[here, 2 * PAIR :] = dv.astype(BF)
        return carry

    lax.fori_loop(0, SLOTS, gather_up, 0)

    def piece_copy(to):
        return rcopy(
            dqkv.at[pl.ds(to * rows, rows), :],
            dq_all.at[:, pl.ds(pl.multiple_of(z * wide, 128), wide)],
            p_send.at[to],
            p_recv.at[z],
            {"ctx": to},
        )

    def send_piece(to):
        @pl.when(z != to)
        def _():
            piece_copy(to).start()

        @pl.when(z == to)
        def _():
            dq_all[:, pl.ds(pl.multiple_of(z * wide, 128), wide)] = dqkv[to * rows : (to + 1) * rows, :]

    for to in range(nz):
        if to * rows >= TRUNK:
            send_piece(to)

    wave_rows = TRUNK // 4
    wave_mask = causal(wave_rows)
    for tile in range(4):
        lo, hi = tile * wave_rows, (tile + 1) * wave_rows
        stacked = stack_heads(query[lo:hi, :])
        asked = jnp.concatenate([stacked, query_features(slopes, wave_rows)], axis=1)
        given = stack_heads(ga_all[lo:hi, :])
        level = lse[tile : tile + 1, :]
        drow = row_products(pl.ds(lo, wave_rows), wave_rows)
        probs, grads = part_back(
            keys_aug[lo:hi, :], value[lo:hi, :], asked, given, level, drow, wave_mask
        )
        dv_trunk[lo:hi, :] += nn(probs, given)
        dk_trunk[lo:hi, :] += nn(grads, stacked)
        turned = nn(keys_turned[:, lo:hi], grads)
        if tile:
            probs, grads = part_back(
                keys_aug[0:lo, :], value[0:lo, :], asked, given, level, drow, None
            )
            dv_trunk[0:lo, :] += nn(probs, given)
            dk_trunk[0:lo, :] += nn(grads, stacked)
            turned = turned + nn(keys_turned[:, 0:lo], grads)
        dqkv[lo:hi, 0:PAIR] = (unstack_turned(turned, wave_rows) * HD ** (-0.5)).astype(BF)
    dqkv[0:TRUNK, PAIR : 2 * PAIR] = dk_trunk[...].astype(BF)
    dqkv[0:TRUNK, 2 * PAIR :] = dv_trunk[...].astype(BF)
    for to in range(nz):
        if to * rows < TRUNK:
            send_piece(to)

    def weight(block, carry):
        here = pl.ds(pl.multiple_of(block * 128, 128), 128)
        wg_send[here, :] = nn(act_turned[here, :], dqkv[...]).astype(BF)
        return carry

    lax.fori_loop(0, width // 128, weight, 0)
    over_peers(lambda d: wg_copy(d).start())
    wg_recv[me] = wg_send[pl.ds(pl.multiple_of(me * depth, depth), depth), :]

    late[...] = jnp.zeros(late.shape, F32)
    late[2:3, pl.ds(pl.multiple_of(z * PAIR, 128), PAIR)] = jnp.sum(
        dqkv[:, 0:PAIR].astype(F32), axis=0, keepdims=True
    )
    late[2:3, pl.ds(pl.multiple_of((nz + z) * PAIR, 128), PAIR)] = jnp.sum(
        dqkv[:, 2 * PAIR :].astype(F32), axis=0, keepdims=True
    )

    for owner in range(nz):

        @pl.when(z != owner)
        def _():
            rcopy(
                dqkv.at[0:rows, :],
                dq_all.at[:, owner * wide : (owner + 1) * wide],
                p_send.at[owner],
                p_recv.at[owner],
                {"ctx": owner},
            ).wait_recv()

    def at(i):
        return pl.ds(pl.multiple_of(i * chunk, 32), chunk)

    def n_copy(i):
        return rcopy(n_send.at[at(i), :], n_recv.at[at(i), :], ns_sem.at[i], nr_sem.at[i], other)

    def first(i, carry):
        n_send[at(i), :] = nt(dq_all[at(i), :], wd[:, units:]).astype(BF)
        n_copy(i).start()
        return carry

    lax.fori_loop(0, ROWS_WAVE, first, 0)

    down_copy().wait_recv()

    def output(i, carry):
        here = at(i)
        result[here, :] = (
            resid[here, :] + (down_part[here, :].astype(F32) + down_recv[here, :].astype(F32))
        ).astype(BF)
        return carry

    lax.fori_loop(0, ROWS_WAVE, output, 0)
    over_peers(lambda d: early_copy(d).wait_recv())
    total = early_recv[0]
    for index in range(1, count):
        total = total + early_recv[index]
    early_sum[...] = total

    def second(i, carry):
        n_copy(i).wait_recv()
        here = at(i)
        grad = n_send[here, :].astype(F32) + n_recv[here, :].astype(F32)
        _, normed, inverse = norm_rows(tok[here, :].astype(F32), gain[0:1, :], shift[0:1, :])
        gtok[here, :] = gmid[here, :] + norm_rows_back(grad, normed, inverse, gain[0:1, :])
        late[0:1, :] += jnp.sum(grad * normed, axis=0, keepdims=True)
        late[1:2, :] += jnp.sum(grad, axis=0, keepdims=True)
        return carry

    lax.fori_loop(0, ROWS_WAVE, second, 0)
    over_peers(lambda d: late_copy(d).start())
    late_recv[me] = late[...]

    over_peers(lambda d: wg_copy(d).wait_recv())
    for owner in range(nz):
        block = wg_recv[owner].astype(F32)
        for source in range(1, ns):
            block = block + wg_recv[source * nz + owner].astype(F32)
        for part in range(3):
            gwqkv[part, :, owner * PAIR : (owner + 1) * PAIR] = block[:, part * PAIR : (part + 1) * PAIR]

    over_peers(lambda d: late_copy(d).wait_recv())
    total = late_recv[0]
    for index in range(1, count):
        total = total + late_recv[index]
    late_sum[...] = total

    down_copy().wait_send()
    over_peers(lambda d: early_copy(d).wait_send())
    over_peers(lambda d: late_copy(d).wait_send())
    over_peers(lambda d: wg_copy(d).wait_send())

    def finish(i, carry):
        n_copy(i).wait_send()
        return carry

    lax.fori_loop(0, ROWS_WAVE, finish, 0)
    for owner in range(nz):

        @pl.when(z != owner)
        def _():
            piece_copy(owner).wait_send()


def run_back(dims, *inputs):
    ns, nz, rows = dims
    width = inputs[12].shape[1]
    count = ns * nz
    depth = width // count
    wide = 3 * PAIR
    return pl.pallas_call(
        partial(back_kernel, dims),
        name="tree_backward",
        out_shape=(
            shape((rows, width), BF),
            shape((rows, width), F32),
            shape((3, depth, nz * PAIR), F32),
            shape((8, width), F32),
            shape((8, width), F32),
        ),
        in_specs=[vmem()] * 17,
        out_specs=[vmem()] * 5,
        scratch_shapes=[
            pltpu.VMEM((TREE, wide), BF),
            pltpu.VMEM((TRUNK, PAIR), F32),
            pltpu.VMEM((TRUNK, PAIR), F32),
            pltpu.VMEM((TREE - TRUNK, PAIR), F32),
            pltpu.VMEM((TREE - TRUNK, PAIR), F32),
            pltpu.VMEM((TREE - TRUNK, PAIR), F32),
            pltpu.VMEM((TREE - TRUNK, PAIR), F32),
            pltpu.VMEM((TRUNK, 2 * PAIR), BF),
            pltpu.VMEM((PAIR, TRUNK), BF),
            pltpu.VMEM((16, 128), F32),
            pltpu.VMEM((16, 128), F32),
            pltpu.VMEM((rows, nz * wide), BF),
            pltpu.VMEM((rows, width), BF),
            pltpu.VMEM((rows, width), BF),
            pltpu.VMEM((rows, width), BF),
            pltpu.VMEM((width, wide), BF),
            pltpu.VMEM((count, depth, wide), BF),
            pltpu.VMEM((count, 8, width), F32),
            pltpu.VMEM((8, width), F32),
            pltpu.VMEM((count, 8, width), F32),
            dma(2),
            dma(count - 1),
            dma(count - 1),
            dma(count - 1),
            dma(count - 1),
            dma(count - 1),
            dma(count - 1),
            dma(nz),
            dma(nz),
            dma(ROWS_WAVE),
            dma(ROWS_WAVE),
        ],
        compiler_params=pltpu.CompilerParams(
            collective_id=2, has_side_effects=True, vmem_limit_bytes=60 << 20
        ),
        cost_estimate=pl.CostEstimate(flops=40_000_000_000, bytes_accessed=20_000_000, transcendentals=0),
    )(*inputs)


def fast_device(
    tokens, cotangent, seg_ids, positions, parents, w_qkv, b_qv, w_out, b_out, w_up, b_up, w_down, b_down, ln_gain, ln_bias
):
    rows = tokens.shape[0]
    ns, nz, ntp = lax.axis_size("shard"), lax.axis_size("ctx"), lax.axis_size("tp")
    dims = (ns, nz, rows)
    depth = w_qkv.shape[1]
    wq = w_qkv.reshape(3, depth, nz, PAIR).transpose(1, 2, 0, 3).reshape(depth, nz * 3 * PAIR)
    both = ("shard", "ctx")
    wa = lax.all_gather(jnp.concatenate([w_up, w_out.T], axis=1), both, axis=0, tiled=True)
    wd = lax.all_gather(jnp.concatenate([w_down.T, wq], axis=1), both, axis=0, tiled=True)

    labels = seg_ids.reshape(rows // BRANCH, BRANCH)[:, 0]
    match = labels[:, None] == jnp.arange(parents.shape[0], dtype=jnp.int32)[None, :]
    above = jnp.sum(jnp.where(match, parents[None, :], 0), axis=1)
    fill = 8 - rows // BRANCH
    lines = jnp.concatenate([jnp.pad(labels, (0, fill)), jnp.pad(above, (0, fill))]).astype(F32)
    info = jnp.broadcast_to(lines[:, None], (16, 128))
    per = HEADS // ntp
    index = lax.axis_index("tp") * per + lax.axis_index("ctx") * 2 + jnp.arange(2)
    slope = 2.0 ** (-8.0 * (index.astype(F32) + 1.0) / HEADS)
    one = lax.reduce_precision(slope, 8, 7)
    two = lax.reduce_precision(slope - one, 8, 7)
    three = lax.reduce_precision(slope - one - two, 8, 7)
    table = jnp.stack([one, two, three, one, two, three, jnp.ones_like(one)], axis=1)
    slopes = jnp.pad(table, ((0, 0), (0, 121)))

    act_turned, query, key, value, out_heads, lse, info_all, att = run_tree(
        dims, tokens, wq, info, b_qv, slopes, ln_gain, ln_bias
    )
    gsum, ga_all, down_part, resid, gmid, sums = run_feed(
        dims, tokens, cotangent, att, wa, wd, b_out[None, :], b_up[None, :], b_down[None, :], ln_gain, ln_bias
    )
    grads = lax.psum_scatter(gsum, both, scatter_dimension=0, tiled=True)
    result, grad_tokens, grad_w_qkv, early, late = run_back(
        dims, query, key, value, out_heads, lse, info_all, ga_all, act_turned, wd, down_part, resid, gmid,
        tokens, slopes, ln_gain, ln_bias, sums,
    )
    units, inner = b_up.shape[0], w_out.shape[0]
    grads = grads.astype(F32)
    width = tokens.shape[1]
    return (
        result,
        grad_tokens,
        grad_w_qkv,
        late[2].reshape(2, nz * PAIR),
        grads[:, units : units + inner].T,
        early[2],
        grads[:, 0:units],
        early[0:2].reshape(units),
        grads[:, units + inner :].T,
        early[3],
        jnp.stack([late[0], early[4]]),
        jnp.stack([late[1], early[5]]),
    )


def norm_forward(inputs_in, gain_row, shift_row):
    centre = inputs_in - jnp.mean(inputs_in, axis=-1, keepdims=True)
    inverse = lax.rsqrt(jnp.mean(centre * centre, axis=-1, keepdims=True) + EPS)
    normed = centre * inverse
    return (normed * gain_row + shift_row, normed, inverse)


def norm_backward(grad_in, normed, inverse, gain_row):
    scaled = grad_in * gain_row
    mean_grad = jnp.mean(scaled, axis=-1, keepdims=True)
    mean_cross = jnp.mean(scaled * normed, axis=-1, keepdims=True)
    return inverse * (scaled - mean_grad - normed * mean_cross)


def ancestry(seg_vals, parents):
    first_up = jnp.take(parents, seg_vals)
    return (first_up, jnp.take(parents, first_up))


def block_scores(query_heads, key_heads, query_tags, key_tags, slopes):
    q_seg, q_first, q_second, q_pos = query_tags
    k_seg, k_pos = key_tags
    raw_scores = jnp.einsum(
        "qhd,khd->hqk", query_heads, key_heads, preferred_element_type=jnp.float32
    ) * HD ** (-0.5)
    distance = (q_pos[:, None] - k_pos[None, :]).astype(jnp.float32)
    scores = raw_scores - slopes[:, None, None] * distance[None]
    related = (
        (k_seg[None, :] == q_seg[:, None])
        | (k_seg[None, :] == q_first[:, None])
        | (k_seg[None, :] == q_second[:, None])
    )
    allowed = related & (k_pos[None, :] <= q_pos[:, None])
    return (scores, allowed[None])


def probabilities(scores, allowed, row_max, row_sum):
    shifted = jnp.where(allowed, scores - row_max[:, :, None], NEG)
    return jnp.exp(shifted) / row_sum[:, :, None]


def per_device(
    tokens,
    cotangent,
    seg_ids,
    positions,
    parents,
    w_qkv,
    b_qv,
    w_out,
    b_out,
    w_up,
    b_up,
    w_down,
    b_down,
    ln_gain,
    ln_bias,
):
    num_rows = tokens.shape[0]
    head_count = HEADS // lax.axis_size("tp")
    head_width = head_count * HD
    head_index = (lax.axis_index("tp") * head_count + jnp.arange(head_count)).astype(jnp.float32)
    slopes = 2.0 ** (-8.0 * (head_index + 1.0) / HEADS)
    scale = HD ** (-0.5)
    full_qkv, full_out = (
        lax.all_gather(w_qkv, ("shard", "ctx"), axis=1, tiled=True),
        lax.all_gather(w_out, ("shard", "ctx"), axis=1, tiled=True),
    )
    group_seg, group_pos = (
        lax.all_gather(seg_ids, "ctx", axis=0, tiled=True),
        lax.all_gather(positions, "ctx", axis=0, tiled=True),
    )
    own_first, own_second = ancestry(seg_ids, parents)
    own_tags = (seg_ids, own_first, own_second, positions)
    inputs = tokens.astype(jnp.float32)
    norm_one, normed_one, inverse_one = norm_forward(inputs, ln_gain[0], ln_bias[0])
    act_one = norm_one.astype(jnp.bfloat16)
    projected = jnp.einsum("td,cde->cte", act_one, full_qkv, preferred_element_type=jnp.float32)
    qkv_bias = jnp.stack([b_qv[0], jnp.zeros((head_width,), jnp.float32), b_qv[1]])
    qkv_low = (projected + qkv_bias[:, None, :]).astype(jnp.bfloat16)
    query_flat, key_flat, value_flat = (qkv_low[0], qkv_low[1], qkv_low[2])
    group_keys, group_values = (
        lax.all_gather(key_flat, "ctx", axis=0, tiled=True),
        lax.all_gather(value_flat, "ctx", axis=0, tiled=True),
    )
    group_rows = group_keys.shape[0]
    block_count = group_rows // KEY_BLOCK
    key_blocks = group_keys.reshape(block_count, KEY_BLOCK, head_count, HD)
    value_blocks = group_values.reshape(block_count, KEY_BLOCK, head_count, HD)
    seg_blocks = group_seg.reshape(block_count, KEY_BLOCK)
    pos_blocks = group_pos.reshape(block_count, KEY_BLOCK)
    query_heads = query_flat.reshape(num_rows, head_count, HD)

    def stats_step(carry_in, block_parts):
        row_max, row_sum = carry_in
        key_part, seg_part, pos_part = block_parts
        scores, allowed = block_scores(
            query_heads, key_part, own_tags, (seg_part, pos_part), slopes
        )
        new_max = jnp.maximum(row_max, jnp.max(jnp.where(allowed, scores, NEG), axis=-1))
        shifted = jnp.where(allowed, scores - new_max[:, :, None], NEG)
        row_sum = row_sum * jnp.exp(row_max - new_max) + jnp.sum(jnp.exp(shifted), axis=-1)
        return ((new_max, row_sum), None)

    start_stats = (
        jnp.full((head_count, num_rows), NEG, jnp.float32),
        jnp.zeros((head_count, num_rows), jnp.float32),
    )
    (row_max, row_sum), _ = lax.scan(stats_step, start_stats, (key_blocks, seg_blocks, pos_blocks))

    def output_step(out_accum, block_parts):
        key_part, value_part, seg_part, pos_part = block_parts
        scores, allowed = block_scores(
            query_heads, key_part, own_tags, (seg_part, pos_part), slopes
        )
        prob_low = probabilities(scores, allowed, row_max, row_sum).astype(jnp.bfloat16)
        return (
            out_accum
            + jnp.einsum("hqk,khd->qhd", prob_low, value_part, preferred_element_type=jnp.float32),
            None,
        )

    attended, _ = lax.scan(
        output_step,
        jnp.zeros((num_rows, head_count, HD), jnp.float32),
        (key_blocks, value_blocks, seg_blocks, pos_blocks),
    )
    attended_low = attended.reshape(num_rows, head_width).astype(jnp.bfloat16)
    branch_one = (
        lax.psum(
            jnp.dot(attended_low, full_out, preferred_element_type=jnp.float32).astype(
                jnp.bfloat16
            ),
            "tp",
        ).astype(jnp.float32)
        + b_out
    )
    middle = inputs + branch_one
    full_up, full_down = (
        lax.all_gather(w_up, ("shard", "ctx"), axis=0, tiled=True),
        lax.all_gather(w_down, ("shard", "ctx"), axis=1, tiled=True),
    )
    norm_two, normed_two, inverse_two = norm_forward(middle, ln_gain[1], ln_bias[1])
    act_two = norm_two.astype(jnp.bfloat16)
    upper_in = jnp.dot(act_two, full_up, preferred_element_type=jnp.float32) + b_up
    gelu_vals, gelu_pull = jax.vjp(partial(jax.nn.gelu, approximate=True), upper_in)
    hidden = gelu_vals.astype(jnp.bfloat16)
    branch_two = (
        lax.psum(
            jnp.dot(hidden, full_down, preferred_element_type=jnp.float32).astype(jnp.bfloat16),
            "tp",
        ).astype(jnp.float32)
        + b_down
    )
    result = (middle + branch_two).astype(jnp.bfloat16)
    grad_out = cotangent.astype(jnp.float32)
    grad_hidden = jnp.einsum("td,fd->tf", cotangent, full_down, preferred_element_type=jnp.float32)
    grad_upper = gelu_pull(grad_hidden)[0].astype(jnp.bfloat16)
    down_term = jnp.einsum("tf,td->fd", hidden, cotangent, preferred_element_type=jnp.float32)
    up_term = jnp.einsum("td,tf->df", act_two, grad_upper, preferred_element_type=jnp.float32)
    grad_w_up, grad_w_down = (
        lax.psum_scatter(up_term, ("shard", "ctx"), scatter_dimension=0, tiled=True),
        lax.psum_scatter(down_term, ("shard", "ctx"), scatter_dimension=1, tiled=True),
    )
    grad_norm_two = lax.psum(
        jnp.einsum("tf,df->td", grad_upper, full_up, preferred_element_type=jnp.float32).astype(
            jnp.bfloat16
        ),
        "tp",
    ).astype(jnp.float32)
    grad_middle = grad_out + norm_backward(grad_norm_two, normed_two, inverse_two, ln_gain[1])
    grad_branch = grad_middle.astype(jnp.bfloat16)
    out_term = jnp.einsum(
        "te,td->ed", attended_low, grad_branch, preferred_element_type=jnp.float32
    )
    grad_att = jnp.einsum(
        "td,ed->te", grad_branch, full_out, preferred_element_type=jnp.float32
    ).astype(jnp.bfloat16)
    grad_heads = grad_att.reshape(num_rows, head_count, HD)
    row_terms = jnp.einsum("qhd,qhd->hq", grad_heads.astype(jnp.float32), attended)

    def joint_step(grad_accum, block_parts):
        key_part, value_part, seg_part, pos_part = block_parts
        scores, allowed = block_scores(
            query_heads, key_part, own_tags, (seg_part, pos_part), slopes
        )
        prob_vals = probabilities(scores, allowed, row_max, row_sum)
        grad_probs = jnp.einsum(
            "qhd,khd->hqk", grad_heads, value_part, preferred_element_type=jnp.float32
        )
        grad_scores = (prob_vals * (grad_probs - row_terms[:, :, None])).astype(jnp.bfloat16)
        grad_accum = (
            grad_accum
            + jnp.einsum("hqk,khd->qhd", grad_scores, key_part, preferred_element_type=jnp.float32)
            * scale
        )
        key_part_grad = (
            jnp.einsum("hqk,qhd->khd", grad_scores, query_heads, preferred_element_type=jnp.float32)
            * scale
        )
        value_part_grad = jnp.einsum(
            "hqk,qhd->khd",
            prob_vals.astype(jnp.bfloat16),
            grad_heads,
            preferred_element_type=jnp.float32,
        )
        return (
            grad_accum,
            (
                key_part_grad.reshape(KEY_BLOCK, head_width),
                value_part_grad.reshape(KEY_BLOCK, head_width),
            ),
        )

    grad_query_sum, (key_terms, value_terms) = lax.scan(
        joint_step,
        jnp.zeros((num_rows, head_count, HD), jnp.float32),
        (key_blocks, value_blocks, seg_blocks, pos_blocks),
    )
    key_grad_sum, value_grad_sum = (
        lax.psum_scatter(
            key_terms.reshape(group_rows, head_width).astype(jnp.bfloat16),
            "ctx",
            scatter_dimension=0,
            tiled=True,
        ).astype(jnp.float32),
        lax.psum_scatter(
            value_terms.reshape(group_rows, head_width).astype(jnp.bfloat16),
            "ctx",
            scatter_dimension=0,
            tiled=True,
        ).astype(jnp.float32),
    )
    grad_query_low = grad_query_sum.reshape(num_rows, head_width).astype(jnp.bfloat16)
    grad_key_low = key_grad_sum.astype(jnp.bfloat16)
    grad_value_low = value_grad_sum.astype(jnp.bfloat16)
    grad_qkv = jnp.stack([grad_query_low, grad_key_low, grad_value_low])
    grad_norm_one = lax.psum(
        jnp.einsum("cte,cde->td", grad_qkv, full_qkv, preferred_element_type=jnp.float32).astype(
            jnp.bfloat16
        ),
        "tp",
    ).astype(jnp.float32)
    grad_tokens = grad_middle + norm_backward(grad_norm_one, normed_one, inverse_one, ln_gain[0])
    qkv_term = jnp.einsum("td,cte->cde", act_one, grad_qkv, preferred_element_type=jnp.float32)
    grad_w_qkv, grad_w_out = (
        lax.psum_scatter(qkv_term, ("shard", "ctx"), scatter_dimension=1, tiled=True),
        lax.psum_scatter(out_term, ("shard", "ctx"), scatter_dimension=1, tiled=True),
    )
    bias_qv_part = jnp.stack(
        [
            jnp.sum(grad_query_low.astype(jnp.float32), axis=0),
            jnp.sum(grad_value_low.astype(jnp.float32), axis=0),
        ]
    )
    out_bias_part = jnp.sum(grad_branch.astype(jnp.float32), axis=0)
    up_bias_part = jnp.sum(grad_upper.astype(jnp.float32), axis=0)
    down_bias_part = jnp.sum(grad_out, axis=0)
    gain_part = jnp.stack(
        [jnp.sum(grad_norm_one * normed_one, axis=0), jnp.sum(grad_norm_two * normed_two, axis=0)]
    )
    shift_part = jnp.stack([jnp.sum(grad_norm_one, axis=0), jnp.sum(grad_norm_two, axis=0)])
    grad_b_qv, grad_b_out, grad_b_up, grad_b_down, grad_gain, grad_shift = lax.psum(
        (bias_qv_part, out_bias_part, up_bias_part, down_bias_part, gain_part, shift_part),
        ("shard", "ctx"),
    )
    return (
        result,
        grad_tokens,
        grad_w_qkv,
        grad_b_qv,
        grad_w_out,
        grad_b_out,
        grad_w_up,
        grad_b_up,
        grad_w_down,
        grad_b_down,
        grad_gain,
        grad_shift,
    )


def solution(mesh):
    placed = (
        P(("shard", "ctx"), None),
        P(("shard", "ctx"), None),
        P(("shard", "ctx")),
        P(("shard", "ctx")),
        P(),
        P(None, ("shard", "ctx"), "tp"),
        P(None, "tp"),
        P("tp", ("shard", "ctx")),
        P(),
        P(("shard", "ctx"), "tp"),
        P("tp"),
        P("tp", ("shard", "ctx")),
        P(),
        P(),
        P(),
    )
    sizes = dict(mesh.shape)
    paired = sizes["tp"] * sizes["ctx"] * 2 == HEADS and sizes["tp"] == 2 and sizes["shard"] == 4
    return jax.shard_map(
        fast_device if paired else per_device,
        mesh=mesh,
        in_specs=placed,
        out_specs=(
            P(("shard", "ctx"), None),
            P(("shard", "ctx"), None),
            P(None, ("shard", "ctx"), "tp"),
            P(None, "tp"),
            P("tp", ("shard", "ctx")),
            P(),
            P(("shard", "ctx"), "tp"),
            P("tp"),
            P("tp", ("shard", "ctx")),
            P(),
            P(),
            P(),
        ),
        check_vma=False,
    )
```

```python
from functools import partial

import jax
import jax.numpy as jnp
from jax import lax
from jax.experimental import pallas as pl
from jax.experimental.pallas import tpu as pltpu
from jax.sharding import PartitionSpec as P

HEADS = 16
HD = 64
KEY_BLOCK = 512
TRUNK = 1024
BRANCH = 128
SLOTS = 12
TREE = TRUNK + SLOTS * BRANCH
PAIR = 2 * HD

EPS = 1e-05
NEG = -1e30
LOG2E = 1.4426950408889634
MESH = pl.DeviceIdType.MESH
BF = jnp.bfloat16
F32 = jnp.float32
ROWS_WAVE = 4
SPREAD_AT = ((1, 3), (2,), ())


def nt(left, right):
    return lax.dot_general(left, right, (((1,), (1,)), ((), ())), preferred_element_type=F32)


def nn(left, right):
    return lax.dot_general(left, right, (((1,), (0,)), ((), ())), preferred_element_type=F32)


def rcopy(src, dst, send, recv, device):
    return pltpu.make_async_remote_copy(
        src_ref=src, dst_ref=dst, send_sem=send, recv_sem=recv, device_id=device, device_id_type=MESH
    )


def greet(devices):
    barrier = pltpu.get_barrier_semaphore()
    for device in devices:
        pl.semaphore_signal(barrier, inc=1, device_id=device, device_id_type=MESH)
    pl.semaphore_wait(barrier, len(devices))


def norm_rows(values, gain_row, shift_row):
    centre = values - jnp.mean(values, axis=-1, keepdims=True)
    inverse = lax.rsqrt(jnp.mean(centre * centre, axis=-1, keepdims=True) + EPS)
    normed = centre * inverse
    return normed * gain_row + shift_row, normed, inverse


def norm_rows_back(grad_in, normed, inverse, gain_row):
    scaled = grad_in * gain_row
    mean_grad = jnp.mean(scaled, axis=-1, keepdims=True)
    mean_cross = jnp.mean(scaled * normed, axis=-1, keepdims=True)
    return inverse * (scaled - mean_grad - normed * mean_cross)


def head_masks():
    lane = lax.broadcasted_iota(jnp.int32, (1, PAIR), 1)
    first = (lane < HD).astype(F32).astype(BF)
    second = (lane >= HD).astype(F32).astype(BF)
    return first, second


def stack_heads(rows):
    first, second = head_masks()
    return jnp.concatenate([rows * first, rows * second], axis=0)


def unstack_turned(turned, rows):
    return jnp.concatenate([turned[:HD, :rows], turned[HD:, rows:]], axis=0).T


def key_features(high, low, flag, rows):
    lane = lax.broadcasted_iota(jnp.int32, (rows, 128), 1)
    feats = jnp.where(lane < 3, high, jnp.where(lane < 6, low, jnp.where(lane == 6, flag, 0.0)))
    return feats.astype(BF)


def query_features(slope_ref, rows):
    return jnp.concatenate(
        [
            jnp.broadcast_to(slope_ref[0:1, :], (rows, 128)),
            jnp.broadcast_to(slope_ref[1:2, :], (rows, 128)),
        ],
        axis=0,
    ).astype(BF)


def fill_trunk_keys(key_ref, keys_aug):
    keys_aug[:, 0:PAIR] = key_ref[0:TRUNK, :]
    pos = lax.broadcasted_iota(jnp.int32, (TRUNK, 128), 0)
    low = pos & 255
    keys_aug[:, PAIR:] = key_features((pos - low).astype(F32), low.astype(F32), 0.0, TRUNK)


def fill_labels(info_all, blocks, labels, parents):
    labels[...] = jnp.full(labels.shape, -1.0, F32)
    parents[...] = jnp.full(parents.shape, -2.0, F32)
    for slot in range(SLOTS):
        block = TRUNK // BRANCH + slot
        owner, inner = block // blocks, block % blocks
        labels[slot : slot + 1, :] = info_all[owner, inner : inner + 1, :]
        parents[slot : slot + 1, :] = info_all[owner, 8 + inner : 9 + inner, :]


def parent_pick(slot, labels, parents, key_ref, value_ref):
    mine = parents[pl.ds(slot, 1), :]
    leaf = jnp.zeros((1, 128), F32)
    key_sum = jnp.zeros((BRANCH, PAIR), BF)
    value_sum = jnp.zeros((BRANCH, PAIR), BF)
    for other in range(SLOTS):
        same = (mine == labels[other : other + 1, :]).astype(F32)
        leaf = leaf + same
        same_low = same.astype(BF)
        at = TRUNK + other * BRANCH
        key_sum = key_sum + same_low * key_ref[at : at + BRANCH, :]
        value_sum = value_sum + same_low * value_ref[at : at + BRANCH, :]
    return leaf, key_sum, value_sum


def segment_key_features(leaf):
    row = lax.broadcasted_iota(jnp.int32, (BRANCH, 128), 0).astype(F32)
    own = key_features(float(TRUNK), row + leaf * float(BRANCH), 0.0, BRANCH)
    above = key_features(float(TRUNK), row, (leaf - 1.0) * 1e30, BRANCH)
    return own, above


def causal(rows):
    key = lax.broadcasted_iota(jnp.int32, (rows, rows), 0)
    query = lax.broadcasted_iota(jnp.int32, (rows, rows), 1)
    once = key <= query
    return jnp.concatenate([once, once], axis=1)


class Spread:
    def __init__(self, full, dims, depth, sems):
        self.full, self.depth = full, depth
        self.ns, self.nz, _ = dims
        self.s, self.z = lax.axis_index("shard"), lax.axis_index("ctx")
        self.zs, self.zr, self.xs, self.xr, self.cs, self.cr = sems

    def rows(self, shard, place):
        at = pl.multiple_of((shard * self.nz + place) * self.depth, self.depth)
        return self.full.at[pl.ds(at, self.depth), :]

    def flip(self, bits):
        low = lax.rem(self.s, 2)
        high = lax.div(self.s, 2)
        if bits & 1:
            low = 1 - low
        if bits & 2:
            high = 1 - high
        return 2 * high + low

    def z_copy(self, d):
        ref = self.rows(self.s, self.z)
        return rcopy(ref, ref, self.zs.at[d - 1], self.zr.at[d - 1], {"ctx": lax.rem(self.z + d, self.nz)})

    def source(self, d):
        return lax.rem(self.z + self.nz - d, self.nz)

    def x_copy(self, d):
        ref = self.rows(self.s, self.source(d))
        return rcopy(ref, ref, self.xs.at[d], self.xr.at[d], {"shard": self.flip(2)})

    def c_copy(self, far, d):
        ref = self.rows(self.flip(2) if far else self.s, self.source(d))
        return rcopy(ref, ref, self.cs.at[far, d], self.cr.at[far, d], {"shard": self.flip(1)})

    def z_start(self, d):
        self.z_copy(d).start()

    def own(self):
        self.x_copy(0).start()
        self.c_copy(0, 0).start()

    def z_done(self, d):
        ref = self.rows(self.s, self.source(d))
        rcopy(ref, ref, self.zs.at[d - 1], self.zr.at[d - 1], {"ctx": self.z}).wait_recv()
        self.x_copy(d).start()
        self.c_copy(0, d).start()

    def x_done(self, d):
        ref = self.rows(self.flip(2), self.source(d))
        rcopy(ref, ref, self.xs.at[d], self.xr.at[d], {"shard": self.flip(2)}).wait_recv()
        self.c_copy(1, d).start()

    def c_done(self, far, d):
        ref = self.rows(self.flip(3) if far else self.flip(1), self.source(d))
        rcopy(ref, ref, self.cs.at[far, d], self.cr.at[far, d], {"shard": self.flip(1)}).wait_recv()

    def finish(self):
        for d in range(self.nz):
            self.c_done(0, d)
            self.c_done(1, d)
        for d in range(self.nz):
            if d:
                self.z_copy(d).wait_send()
            self.x_copy(d).wait_send()
            self.c_copy(0, d).wait_send()
            self.c_copy(1, d).wait_send()


def spread_sems(nz):
    return [dma(nz - 1), dma(nz - 1), dma(nz), dma(nz), dma(2, nz), dma(2, nz)]


def vmem():
    return pl.BlockSpec(memory_space=pltpu.VMEM)


def shape(dims, kind):
    return jax.ShapeDtypeStruct(dims, kind)


def dma(*dims):
    return pltpu.SemaphoreType.DMA(dims)


def tree_kernel(
    dims,
    tok,
    w_up,
    w_out,
    w_down,
    wq3,
    info,
    bias_qv,
    slopes,
    gain,
    shift,
    wfull,
    wq,
    act_turned,
    query,
    key,
    value,
    out_heads,
    lse,
    info_all,
    att,
    tree,
    wcat,
    keys_aug,
    values_turned,
    labels,
    parents,
    info_send,
    info_recv,
    wz_send,
    wz_recv,
    ws_send,
    ws_recv,
    z_send,
    z_recv,
    y_send,
    y_recv,
    a_send,
    a_recv,
    local_sem,
    *spread,
):
    ns, nz, rows = dims
    s, z, y = lax.axis_index("shard"), lax.axis_index("ctx"), lax.axis_index("tp")
    half = rows // 2
    sub = half // 2
    depth = wq.shape[0]
    wide = 3 * PAIR
    my_rows = pl.ds(pl.multiple_of((s * nz + z) * depth, depth), depth)
    units, inner = w_up.shape[1], w_out.shape[1]
    starts = [
        pltpu.make_async_copy(tok, tree.at[pl.ds(pl.multiple_of(z * rows, 128), rows), :], local_sem.at[0]),
        pltpu.make_async_copy(w_up, wfull.at[my_rows, 0:units], local_sem.at[1]),
        pltpu.make_async_copy(w_out, wfull.at[my_rows, units : units + inner], local_sem.at[2]),
        pltpu.make_async_copy(w_down, wfull.at[my_rows, units + inner :], local_sem.at[3]),
    ]
    for one in starts:
        one.start()
    for to in range(nz):
        for part in range(3):
            wq[:, to * wide + part * PAIR : to * wide + (part + 1) * PAIR] = wq3[
                part, :, to * PAIR : (to + 1) * PAIR
            ]
    greet(
        [{"ctx": lax.rem(z + d, nz)} for d in range(1, nz)]
        + [{"shard": lax.rem(s + d, ns)} for d in range(1, ns)]
        + [{"tp": 1 - y}]
    )
    weights = Spread(wfull, dims, depth, spread)

    def info_copy(d):
        return rcopy(
            info, info_all.at[z], info_send.at[d - 1], info_recv.at[d - 1], {"ctx": lax.rem(z + d, nz)}
        )

    def wz_copy(d):
        to = lax.rem(z + d, nz)
        return rcopy(
            wq.at[:, pl.ds(pl.multiple_of(to * wide, 128), wide)],
            wcat.at[my_rows, :],
            wz_send.at[d - 1],
            wz_recv.at[d - 1],
            {"ctx": to},
        )

    shard_rows = pl.ds(s * (nz * depth), nz * depth)

    def ws_copy(d):
        return rcopy(
            wcat.at[shard_rows, :],
            wcat.at[shard_rows, :],
            ws_send.at[d - 1],
            ws_recv.at[d - 1],
            {"shard": lax.rem(s + d, ns)},
        )

    for d in range(1, nz):
        wz_copy(d).start()
    for d in range(1, nz):
        info_copy(d).start()
    wcat[my_rows, :] = wq[:, pl.ds(pl.multiple_of(z * wide, 128), wide)]
    info_all[z] = info[...]
    for one in starts:
        one.wait()

    def piece(block, second, part):
        at = block * rows + jnp.where(second, 1 - y, y) * half + part * sub
        return tree.at[pl.ds(pl.multiple_of(at, 32), sub), :]

    def z_copy(direction, k, part):
        block = z - k if direction == 0 else z + k
        to = z + 1 if direction == 0 else z - 1
        ref = piece(block, False, part)
        return rcopy(ref, ref, z_send.at[direction, k, part], z_recv.at[direction, k, part], {"ctx": to})

    def z_arrival(direction, k, part):
        block = z - k if direction == 0 else z + k
        ref = piece(block, False, part)
        return rcopy(
            ref, ref, z_send.at[direction, k - 1, part], z_recv.at[direction, k - 1, part], {"ctx": z}
        )

    def y_copy(direction, k, part):
        block = z - k if direction == 0 else z + k
        ref = piece(block, False, part)
        return rcopy(
            ref, ref, y_send.at[direction, k - 1, part], y_recv.at[direction, k - 1, part], {"tp": 1 - y}
        )

    def y_arrival(direction, k, part):
        block = z - k if direction == 0 else z + k
        ref = piece(block, True, part)
        return rcopy(
            ref, ref, y_send.at[direction, k - 1, part], y_recv.at[direction, k - 1, part], {"tp": 1 - y}
        )

    def place(direction, k):
        block = z - k if direction == 0 else z + k
        nxt = z + 1 if direction == 0 else z - 1
        here = (block >= 0) & (block < nz)
        onward = here & (nxt >= 0) & (nxt < nz)
        return block, here, onward

    def forward(k, first):
        for part in range(2):
            for direction in range(2):
                _, here, onward = place(direction, k)
                if not first:

                    @pl.when(here)
                    def _():
                        z_arrival(direction, k, part).wait_recv()

                @pl.when(onward & (k < nz - 1))
                def _():
                    z_copy(direction, k, part).start()

                if not first:

                    @pl.when(here)
                    def _():
                        y_copy(direction, k, part).start()

    forward(0, True)
    weights.own()
    for d in range(1, nz):
        wz_copy(d).wait_recv()
    for d in range(1, ns):
        ws_copy(d).start()

    bias_at = pl.ds(pl.multiple_of(z * PAIR, 128), PAIR)
    bias_q = bias_qv[0:1, bias_at]
    bias_v = bias_qv[1:2, bias_at]

    def project(k):
        def side(direction, inner_carry):
            block = z + (2 * direction - 1) * k

            @pl.when((block >= 0) & (block < nz) & ((k > 0) | (direction == 0)))
            def _():
                def tile(t, carry):
                    here = pl.ds(pl.multiple_of(block * rows + t * 128, 128), 128)
                    act = norm_rows(tree[here, :].astype(F32), gain[0:1, :], shift[0:1, :])[0].astype(BF)
                    act_turned[:, here] = act.T
                    both = nn(act, wcat[...])
                    query[here, :] = (
                        (both[:, :PAIR] + bias_q).astype(BF).astype(F32) * HD ** (-0.5)
                    ).astype(BF)
                    key[here, :] = both[:, PAIR : 2 * PAIR].astype(BF)
                    value[here, :] = (both[:, 2 * PAIR :] + bias_v).astype(BF)
                    return carry

                lax.fori_loop(0, rows // 128, tile, 0)

            return inner_carry

        lax.fori_loop(0, 2, side, 0)

    def shared(k):
        for part in range(2):
            for direction in range(2):
                _, here, _ = place(direction, k)

                @pl.when(here)
                def _():
                    y_arrival(direction, k, part).wait_recv()

    forward(1, False)
    for d in SPREAD_AT[0]:
        weights.z_start(d)
    for d in range(1, ns):
        ws_copy(d).wait_recv()
    project(0)

    def wave(k, carry):
        forward(k, False)

        @pl.when(k == 2)
        def _():
            for d in SPREAD_AT[1]:
                weights.z_start(d)

        @pl.when(k == 3)
        def _():
            for d in SPREAD_AT[2]:
                weights.z_start(d)

        shared(k - 1)
        project(k - 1)
        return carry

    lax.fori_loop(2, nz, wave, 0)
    for d in SPREAD_AT[0]:
        weights.z_done(d)
    shared(nz - 1)
    project(nz - 1)

    for d in range(1, nz):
        info_copy(d).wait_recv()

    fill_labels(info_all, rows // BRANCH, labels, parents)
    fill_trunk_keys(key, keys_aug)
    values_turned[...] = value[0:TRUNK, :].T

    def att_copy(to):
        return rcopy(
            out_heads.at[pl.ds(to * rows, rows), :],
            att.at[:, pl.ds(pl.multiple_of(z * PAIR, 128), PAIR)],
            a_send.at[to],
            a_recv.at[z],
            {"ctx": to},
        )

    def send_out(to):
        @pl.when(z != to)
        def _():
            att_copy(to).start()

        @pl.when(z == to)
        def _():
            att[:, pl.ds(pl.multiple_of(z * PAIR, 128), PAIR)] = out_heads[to * rows : (to + 1) * rows, :]

    tile_mask = causal(BRANCH)
    owners = [((owner + 1) * rows - TRUNK) // BRANCH - 1 for owner in range(nz)]

    def segment(slot, carry):
        here = pl.ds(pl.multiple_of(TRUNK + slot * BRANCH, 128), BRANCH)
        asked = jnp.concatenate(
            [stack_heads(query[here, :]), query_features(slopes, BRANCH)], axis=1
        )
        leaf, key_up, value_up = parent_pick(slot, labels, parents, key, value)
        own_feats, up_feats = segment_key_features(leaf)
        trunk_part = nt(keys_aug[...], asked) * LOG2E
        own_part = nt(jnp.concatenate([key[here, :], own_feats], axis=1), asked) * LOG2E
        own_part = jnp.where(tile_mask, own_part, NEG)
        up_part = nt(jnp.concatenate([key_up, up_feats], axis=1), asked) * LOG2E
        top = jnp.maximum(
            jnp.max(trunk_part, axis=0, keepdims=True),
            jnp.maximum(
                jnp.max(own_part, axis=0, keepdims=True), jnp.max(up_part, axis=0, keepdims=True)
            ),
        )
        trunk_part = jnp.exp2(trunk_part - top)
        own_part = jnp.exp2(own_part - top)
        up_part = jnp.exp2(up_part - top)
        total = (
            jnp.sum(trunk_part, axis=0, keepdims=True)
            + jnp.sum(own_part, axis=0, keepdims=True)
            + jnp.sum(up_part, axis=0, keepdims=True)
        )
        turned = nn(values_turned[...], trunk_part.astype(BF))
        turned = turned + nn(value[here, :].T, own_part.astype(BF))
        turned = turned + nn(value_up.T, up_part.astype(BF))
        turned = turned / total
        out_heads[here, :] = unstack_turned(turned, BRANCH).astype(BF)
        lse[pl.ds(4 + slot, 1), 0 : 2 * BRANCH] = top + jnp.log2(total)
        for owner in range(nz):
            if owners[owner] >= 0 and owner * rows >= TRUNK:

                @pl.when(slot == owners[owner])
                def _():
                    send_out(owner)

        return carry

    lax.fori_loop(0, SLOTS, segment, 0)

    wave_rows = TRUNK // 4
    wave_mask = causal(wave_rows)
    sent = 0
    for tile in range(4):
        lo, hi = tile * wave_rows, (tile + 1) * wave_rows
        asked = jnp.concatenate(
            [stack_heads(query[lo:hi, :]), query_features(slopes, wave_rows)], axis=1
        )
        edge = jnp.where(wave_mask, nt(keys_aug[lo:hi, :], asked) * LOG2E, NEG)
        top = jnp.max(edge, axis=0, keepdims=True)
        if tile:
            body = nt(keys_aug[0:lo, :], asked) * LOG2E
            top = jnp.maximum(top, jnp.max(body, axis=0, keepdims=True))
            body = jnp.exp2(body - top)
        edge = jnp.exp2(edge - top)
        total = jnp.sum(edge, axis=0, keepdims=True)
        turned = nn(values_turned[:, lo:hi], edge.astype(BF))
        if tile:
            total = total + jnp.sum(body, axis=0, keepdims=True)
            turned = turned + nn(values_turned[:, 0:lo], body.astype(BF))
        turned = turned / total
        out_heads[lo:hi, :] = unstack_turned(turned, wave_rows).astype(BF)
        lse[tile : tile + 1, :] = top + jnp.log2(total)
        while sent < nz and sent * rows < TRUNK and (sent + 1) * rows <= (hi if hi < TRUNK else TREE):
            send_out(sent)
            sent += 1

    for d in SPREAD_AT[1] + SPREAD_AT[2]:
        weights.z_done(d)
    for d in (0,) + SPREAD_AT[0] + SPREAD_AT[1] + SPREAD_AT[2]:
        weights.x_done(d)

    for owner in range(nz):

        @pl.when(z != owner)
        def _():
            rcopy(
                out_heads.at[0:rows, :],
                att.at[:, owner * PAIR : (owner + 1) * PAIR],
                a_send.at[owner],
                a_recv.at[owner],
                {"ctx": owner},
            ).wait_recv()

    for owner in range(nz):

        @pl.when(z != owner)
        def _():
            att_copy(owner).wait_send()

    weights.finish()
    for d in range(1, nz):
        info_copy(d).wait_send()
        wz_copy(d).wait_send()
    for d in range(1, ns):
        ws_copy(d).wait_send()

    def drain(k, carry):
        for part in range(2):
            for direction in range(2):
                _, here, onward = place(direction, k)

                @pl.when(onward & (k < nz - 1))
                def _():
                    z_copy(direction, k, part).wait_send()

                @pl.when(here & (k > 0))
                def _():
                    y_copy(direction, k, part).wait_send()

        return carry

    lax.fori_loop(0, nz, drain, 0)


def run_tree(dims, tok, w_up, w_out, w_down, wq3, info, bias_qv, slopes, gain, shift):
    ns, nz, rows = dims
    width = tok.shape[1]
    depth = wq3.shape[1]
    total = w_up.shape[1] + w_out.shape[1] + w_down.shape[1]
    return pl.pallas_call(
        partial(tree_kernel, dims),
        name="tree_forward",
        out_shape=(
            shape((width, total), BF),
            shape((depth, nz * 3 * PAIR), BF),
            shape((width, TREE), BF),
            shape((TREE, PAIR), BF),
            shape((TREE, PAIR), BF),
            shape((TREE, PAIR), BF),
            shape((TREE, PAIR), BF),
            shape((16, 512), F32),
            shape((nz, 16, 128), F32),
            shape((rows, nz * PAIR), BF),
        ),
        in_specs=[pl.BlockSpec(memory_space=pl.ANY)] * 4 + [vmem()] * 6,
        out_specs=[vmem()] * 10,
        scratch_shapes=[
            pltpu.VMEM((TREE, width), BF),
            pltpu.VMEM((width, 3 * PAIR), BF),
            pltpu.VMEM((TRUNK, 2 * PAIR), BF),
            pltpu.VMEM((PAIR, TRUNK), BF),
            pltpu.VMEM((16, 128), F32),
            pltpu.VMEM((16, 128), F32),
            dma(nz - 1),
            dma(nz - 1),
            dma(nz - 1),
            dma(nz - 1),
            dma(ns - 1),
            dma(ns - 1),
            dma(2, nz, 2),
            dma(2, nz, 2),
            dma(2, nz, 2),
            dma(2, nz, 2),
            dma(nz),
            dma(nz),
            dma(4),
            *spread_sems(nz),
        ],
        compiler_params=pltpu.CompilerParams(
            collective_id=0, has_side_effects=True, vmem_limit_bytes=48 << 20
        ),
        cost_estimate=pl.CostEstimate(flops=40_000_000_000, bytes_accessed=20_000_000, transcendentals=0),
    )(tok, w_up, w_out, w_down, wq3, info, bias_qv, slopes, gain, shift)


UP, OUT, DOWN = "up", "out", "down"
BLOCK = 512
CURVE = 0.044715
ROOT = 0.7978845608028654


def feed_kernel(
    dims,
    tok,
    cot,
    att,
    wa,
    wq,
    b_out,
    b_up,
    b_down,
    gain,
    shift,
    wqkv,
    gsum,
    ga_all,
    down_part,
    resid,
    gmid,
    sums,
    act,
    hidden,
    gup,
    gbranch,
    mid,
    o_send,
    o_recv,
    g_send,
    g_recv,
    ga_send,
    bup_acc,
    os_sem,
    or_sem,
    gs_sem,
    gr_sem,
    as_sem,
    ar_sem,
    *spread,
):
    ns, nz, rows = dims
    s, z, y = lax.axis_index("shard"), lax.axis_index("ctx"), lax.axis_index("tp")
    chunk = rows // ROWS_WAVE
    width = tok.shape[1]
    units = b_up.shape[1]
    inner = att.shape[1]
    wd = wa.at[:, units + inner :]
    weights = Spread(wqkv, dims, wq.shape[0], spread)
    greet(
        [{"tp": 1 - y}]
        + [{"ctx": lax.rem(z + d, nz)} for d in range(1, nz)]
        + [{"shard": weights.flip(bits)} for bits in (1, 2)]
    )
    other = {"tp": 1 - y}
    wqkv[pl.ds(pl.multiple_of((s * nz + z) * wq.shape[0], wq.shape[0]), wq.shape[0]), :] = wq[...]

    def at(i):
        return pl.ds(pl.multiple_of(i * chunk, 32), chunk)

    def o_copy(i):
        return rcopy(o_send.at[at(i), :], o_recv.at[at(i), :], os_sem.at[i], or_sem.at[i], other)

    def g_copy(i):
        return rcopy(g_send.at[at(i), :], g_recv.at[at(i), :], gs_sem.at[i], gr_sem.at[i], other)

    def a_copy(i, d):
        to = lax.rem(z + d, nz)
        return rcopy(
            ga_send.at[at(i), pl.ds(pl.multiple_of(to * PAIR, 128), PAIR)],
            ga_all.at[pl.ds(pl.multiple_of(z * rows + i * chunk, 32), chunk), :],
            as_sem.at[d - 1, i],
            ar_sem.at[d - 1, i],
            {"ctx": to},
        )

    sums[...] = jnp.zeros(sums.shape, F32)
    bup_acc[...] = jnp.zeros(bup_acc.shape, F32)

    def stage_a(i, carry):
        o_send[at(i), :] = nt(att[at(i), :], wa[:, units : units + inner]).astype(BF)
        o_copy(i).start()
        return carry

    lax.fori_loop(0, ROWS_WAVE, stage_a, 0)
    weights.own()
    for d in range(1, nz):
        weights.z_start(d)

    def stage_b(i, carry):
        o_copy(i).wait_recv()
        here = at(i)
        branch = o_send[here, :].astype(F32) + o_recv[here, :].astype(F32) + b_out[...]
        middle = tok[here, :].astype(F32) + branch
        mid[here, :] = middle
        resid[here, :] = middle + b_down[...]
        act[here, :] = norm_rows(middle, gain[1:2, :], shift[1:2, :])[0].astype(BF)

        def columns(c, inner_carry):
            cols = pl.ds(pl.multiple_of(c * BLOCK, 128), BLOCK)
            upper = nn(act[here, :], wa[:, cols]) + b_up[:, cols]
            slope = nn(cot[here, :], wd[:, cols])
            square = upper * upper
            turn = jnp.tanh(ROOT * (upper + CURVE * (square * upper)))
            hidden[here, cols] = (0.5 * upper * (1.0 + turn)).astype(BF)
            steep = 0.5 * (1.0 + turn) + (0.5 * ROOT) * upper * (1.0 - turn * turn) * (
                1.0 + (3.0 * CURVE) * square
            )
            low = (slope * steep).astype(BF)
            gup[here, cols] = low
            bup_acc[:, cols] += jnp.sum(low.astype(F32), axis=0, keepdims=True)
            return inner_carry

        lax.fori_loop(0, units // BLOCK, columns, 0)
        g_send[here, :] = nt(gup[here, :], wa[:, 0:units]).astype(BF)
        g_copy(i).start()
        down_part[here, :] = nt(hidden[here, :], wd[:, 0:units]).astype(BF)
        return carry

    lax.fori_loop(0, ROWS_WAVE, stage_b, 0)

    def weight_one(d, carry):
        cols = pl.ds(pl.multiple_of(d * 128, 128), 128)
        gsum[cols, units + inner : 2 * units + inner] = nn(cot[:, cols].T, hidden[...]).astype(BF)
        gsum[cols, 0:units] = nn(act[:, cols].T, gup[...]).astype(BF)
        return carry

    for d in range(1, nz):
        weights.z_done(d)
    lax.fori_loop(0, width // 128, weight_one, 0)
    for d in range(nz):
        weights.x_done(d)

    def stage_c(i, carry):
        g_copy(i).wait_recv()
        here = at(i)
        grad = g_send[here, :].astype(F32) + g_recv[here, :].astype(F32)
        _, normed, inverse = norm_rows(mid[here, :], gain[1:2, :], shift[1:2, :])
        given = cot[here, :].astype(F32)
        grad_middle = given + norm_rows_back(grad, normed, inverse, gain[1:2, :])
        gmid[here, :] = grad_middle
        low = grad_middle.astype(BF)
        gbranch[here, :] = low
        sums[2:3, :] += jnp.sum(low.astype(F32), axis=0, keepdims=True)
        sums[3:4, :] += jnp.sum(given, axis=0, keepdims=True)
        sums[4:5, :] += jnp.sum(grad * normed, axis=0, keepdims=True)
        sums[5:6, :] += jnp.sum(grad, axis=0, keepdims=True)
        ga_send[here, :] = nn(low, wa[:, units : units + inner]).astype(BF)
        for d in range(1, nz):
            a_copy(i, d).start()
        ga_all[pl.ds(pl.multiple_of(z * rows + i * chunk, 32), chunk), :] = ga_send[
            here, pl.ds(pl.multiple_of(z * PAIR, 128), PAIR)
        ]
        return carry

    lax.fori_loop(0, ROWS_WAVE, stage_c, 0)

    def weight_two(d, carry):
        cols = pl.ds(pl.multiple_of(d * 128, 128), 128)
        gsum[cols, units : units + inner] = nn(gbranch[:, cols].T, att[...]).astype(BF)
        return carry

    lax.fori_loop(0, width // 128, weight_two, 0)
    for part in range(units // width):
        sums[part : part + 1, :] = bup_acc[:, part * width : (part + 1) * width]

    weights.finish()

    def finish(i, carry):
        o_copy(i).wait_send()
        g_copy(i).wait_send()
        for d in range(1, nz):
            a_copy(i, d).wait_send()
            a_copy(i, d).wait_recv()
        return carry

    lax.fori_loop(0, ROWS_WAVE, finish, 0)


def run_feed(dims, tok, cot, att, wa, wq, b_out, b_up, b_down, gain, shift):
    ns, nz, rows = dims
    width, units, inner = tok.shape[1], b_up.shape[1], att.shape[1]
    return pl.pallas_call(
        partial(feed_kernel, dims),
        name="feed_both",
        out_shape=(
            shape((width, wq.shape[1]), BF),
            shape((width, 2 * units + inner), BF),
            shape((TREE, PAIR), BF),
            shape((rows, width), BF),
            shape((rows, width), F32),
            shape((rows, width), F32),
            shape((8, width), F32),
        ),
        in_specs=[vmem()] * 10,
        out_specs=[vmem()] * 7,
        scratch_shapes=[
            pltpu.VMEM((rows, width), BF),
            pltpu.VMEM((rows, units), BF),
            pltpu.VMEM((rows, units), BF),
            pltpu.VMEM((rows, width), BF),
            pltpu.VMEM((rows, width), F32),
            pltpu.VMEM((rows, width), BF),
            pltpu.VMEM((rows, width), BF),
            pltpu.VMEM((rows, width), BF),
            pltpu.VMEM((rows, width), BF),
            pltpu.VMEM((rows, inner), BF),
            pltpu.VMEM((1, units), F32),
            dma(ROWS_WAVE),
            dma(ROWS_WAVE),
            dma(ROWS_WAVE),
            dma(ROWS_WAVE),
            dma(nz - 1, ROWS_WAVE),
            dma(nz - 1, ROWS_WAVE),
            *spread_sems(nz),
        ],
        compiler_params=pltpu.CompilerParams(
            collective_id=1, has_side_effects=True, vmem_limit_bytes=60 << 20
        ),
        cost_estimate=pl.CostEstimate(flops=40_000_000_000, bytes_accessed=20_000_000, transcendentals=0),
    )(tok, cot, att, wa, wq, b_out, b_up, b_down, gain, shift)


def back_kernel(
    dims,
    query,
    key,
    value,
    out_heads,
    lse,
    info_all,
    ga_all,
    act_turned,
    wqkv,
    down_part,
    resid,
    gmid,
    tok,
    slopes,
    gain,
    shift,
    early,
    result,
    gtok,
    gwqkv,
    early_sum,
    late_sum,
    dqkv,
    dk_trunk,
    dv_trunk,
    dk_seg,
    dv_seg,
    dk_up,
    dv_up,
    keys_aug,
    keys_turned,
    labels,
    parents,
    dq_all,
    n_send,
    n_recv,
    down_recv,
    wg_send,
    wg_recv,
    early_recv,
    late,
    late_recv,
    d_sem,
    e_send,
    e_recv,
    l_send,
    l_recv,
    w_send,
    w_recv,
    p_send,
    p_recv,
    ns_sem,
    nr_sem,
):
    ns, nz, rows = dims
    s, z, y = lax.axis_index("shard"), lax.axis_index("ctx"), lax.axis_index("tp")
    count = ns * nz
    me = s * nz + z
    chunk = rows // ROWS_WAVE
    width = tok.shape[1]
    depth = width // count
    wide = 3 * PAIR
    other = {"tp": 1 - y}

    def peer(d):
        index = lax.rem(me + d, count)
        return index, {"shard": index // nz, "ctx": lax.rem(index, nz)}

    greet([other] + [peer(d)[1] for d in range(1, count)])

    def down_copy():
        return rcopy(down_part, down_recv, d_sem.at[0], d_sem.at[1], other)

    def early_copy(d):
        return rcopy(early, early_recv.at[me], e_send.at[d - 1], e_recv.at[d - 1], peer(d)[1])

    def late_copy(d):
        return rcopy(late, late_recv.at[me], l_send.at[d - 1], l_recv.at[d - 1], peer(d)[1])

    def wg_copy(d):
        index, device = peer(d)
        return rcopy(
            wg_send.at[pl.ds(pl.multiple_of(index * depth, depth), depth), :],
            wg_recv.at[me],
            w_send.at[d - 1],
            w_recv.at[d - 1],
            device,
        )

    def over_peers(act):
        def one(d, carry):
            act(d)
            return carry

        lax.fori_loop(1, count, one, 0)

    down_copy().start()
    over_peers(lambda d: early_copy(d).start())
    early_recv[me] = early[...]

    fill_labels(info_all, rows // BRANCH, labels, parents)
    fill_trunk_keys(key, keys_aug)
    keys_turned[...] = key[0:TRUNK, :].T
    dk_trunk[...] = jnp.zeros(dk_trunk.shape, F32)
    dv_trunk[...] = jnp.zeros(dv_trunk.shape, F32)
    tile_mask = causal(BRANCH)

    def row_products(here, count_rows):
        turned = (ga_all[here, :].astype(F32) * out_heads[here, :].astype(F32)).T
        return jnp.concatenate(
            [
                jnp.sum(turned[:HD, :], axis=0, keepdims=True),
                jnp.sum(turned[HD:, :], axis=0, keepdims=True),
            ],
            axis=1,
        )

    def part_back(key_aug, value_rows, asked, given, level, drow, mask):
        logits = nt(key_aug, asked) * LOG2E - level
        if mask is not None:
            logits = jnp.where(mask, logits, NEG)
        probs = jnp.exp2(logits)
        grads = (probs * (nt(value_rows, given) - drow)).astype(BF)
        return probs.astype(BF), grads

    def segment(slot, carry):
        here = pl.ds(pl.multiple_of(TRUNK + slot * BRANCH, 128), BRANCH)
        seg = pl.ds(pl.multiple_of(slot * BRANCH, 128), BRANCH)
        stacked = stack_heads(query[here, :])
        asked = jnp.concatenate([stacked, query_features(slopes, BRANCH)], axis=1)
        given = stack_heads(ga_all[here, :])
        leaf, key_up, value_up = parent_pick(slot, labels, parents, key, value)
        own_feats, up_feats = segment_key_features(leaf)
        level = lse[pl.ds(4 + slot, 1), 0 : 2 * BRANCH]
        drow = row_products(here, BRANCH)
        probs, grads = part_back(keys_aug[...], value[0:TRUNK, :], asked, given, level, drow, None)
        dv_trunk[...] += nn(probs, given)
        dk_trunk[...] += nn(grads, stacked)
        turned = nn(keys_turned[...], grads)
        key_own = key[here, :]
        probs, grads = part_back(
            jnp.concatenate([key_own, own_feats], axis=1), value[here, :], asked, given, level, drow, tile_mask
        )
        dv_seg[seg, :] = nn(probs, given)
        dk_seg[seg, :] = nn(grads, stacked)
        turned = turned + nn(key_own.T, grads)
        probs, grads = part_back(
            jnp.concatenate([key_up, up_feats], axis=1), value_up, asked, given, level, drow, None
        )
        dv_up[seg, :] = nn(probs, given)
        dk_up[seg, :] = nn(grads, stacked)
        turned = turned + nn(key_up.T, grads)
        dqkv[here, 0:PAIR] = (unstack_turned(turned, BRANCH) * HD ** (-0.5)).astype(BF)
        return carry

    lax.fori_loop(0, SLOTS, segment, 0)

    def gather_up(slot, carry):
        here = pl.ds(pl.multiple_of(TRUNK + slot * BRANCH, 128), BRANCH)
        seg = pl.ds(pl.multiple_of(slot * BRANCH, 128), BRANCH)
        mine = labels[pl.ds(slot, 1), :]
        dk, dv = dk_seg[seg, :], dv_seg[seg, :]
        for below in range(SLOTS):
            same = (parents[below : below + 1, :] == mine).astype(F32)
            at = below * BRANCH
            dk = dk + same * dk_up[at : at + BRANCH, :]
            dv = dv + same * dv_up[at : at + BRANCH, :]
        dqkv[here, PAIR : 2 * PAIR] = dk.astype(BF)
        dqkv[here, 2 * PAIR :] = dv.astype(BF)
        return carry

    lax.fori_loop(0, SLOTS, gather_up, 0)

    def piece_copy(to):
        return rcopy(
            dqkv.at[pl.ds(to * rows, rows), :],
            dq_all.at[:, pl.ds(pl.multiple_of(z * wide, 128), wide)],
            p_send.at[to],
            p_recv.at[z],
            {"ctx": to},
        )

    def send_piece(to):
        @pl.when(z != to)
        def _():
            piece_copy(to).start()

        @pl.when(z == to)
        def _():
            dq_all[:, pl.ds(pl.multiple_of(z * wide, 128), wide)] = dqkv[to * rows : (to + 1) * rows, :]

    for to in range(nz):
        if to * rows >= TRUNK:
            send_piece(to)

    wave_rows = TRUNK // 4
    wave_mask = causal(wave_rows)
    for tile in range(4):
        lo, hi = tile * wave_rows, (tile + 1) * wave_rows
        stacked = stack_heads(query[lo:hi, :])
        asked = jnp.concatenate([stacked, query_features(slopes, wave_rows)], axis=1)
        given = stack_heads(ga_all[lo:hi, :])
        level = lse[tile : tile + 1, :]
        drow = row_products(pl.ds(lo, wave_rows), wave_rows)
        probs, grads = part_back(
            keys_aug[lo:hi, :], value[lo:hi, :], asked, given, level, drow, wave_mask
        )
        dv_trunk[lo:hi, :] += nn(probs, given)
        dk_trunk[lo:hi, :] += nn(grads, stacked)
        turned = nn(keys_turned[:, lo:hi], grads)
        if tile:
            probs, grads = part_back(
                keys_aug[0:lo, :], value[0:lo, :], asked, given, level, drow, None
            )
            dv_trunk[0:lo, :] += nn(probs, given)
            dk_trunk[0:lo, :] += nn(grads, stacked)
            turned = turned + nn(keys_turned[:, 0:lo], grads)
        dqkv[lo:hi, 0:PAIR] = (unstack_turned(turned, wave_rows) * HD ** (-0.5)).astype(BF)
    dqkv[0:TRUNK, PAIR : 2 * PAIR] = dk_trunk[...].astype(BF)
    dqkv[0:TRUNK, 2 * PAIR :] = dv_trunk[...].astype(BF)
    for to in range(nz):
        if to * rows < TRUNK:
            send_piece(to)

    def weight(block, carry):
        here = pl.ds(pl.multiple_of(block * 128, 128), 128)
        wg_send[here, :] = nn(act_turned[here, :], dqkv[...]).astype(BF)
        return carry

    lax.fori_loop(0, width // 128, weight, 0)
    over_peers(lambda d: wg_copy(d).start())
    wg_recv[me] = wg_send[pl.ds(pl.multiple_of(me * depth, depth), depth), :]

    late[...] = jnp.zeros(late.shape, F32)
    late[2:3, pl.ds(pl.multiple_of(z * PAIR, 128), PAIR)] = jnp.sum(
        dqkv[:, 0:PAIR].astype(F32), axis=0, keepdims=True
    )
    late[2:3, pl.ds(pl.multiple_of((nz + z) * PAIR, 128), PAIR)] = jnp.sum(
        dqkv[:, 2 * PAIR :].astype(F32), axis=0, keepdims=True
    )

    for owner in range(nz):

        @pl.when(z != owner)
        def _():
            rcopy(
                dqkv.at[0:rows, :],
                dq_all.at[:, owner * wide : (owner + 1) * wide],
                p_send.at[owner],
                p_recv.at[owner],
                {"ctx": owner},
            ).wait_recv()

    def at(i):
        return pl.ds(pl.multiple_of(i * chunk, 32), chunk)

    def n_copy(i):
        return rcopy(n_send.at[at(i), :], n_recv.at[at(i), :], ns_sem.at[i], nr_sem.at[i], other)

    def first(i, carry):
        n_send[at(i), :] = nt(dq_all[at(i), :], wqkv[...]).astype(BF)
        n_copy(i).start()
        return carry

    lax.fori_loop(0, ROWS_WAVE, first, 0)

    down_copy().wait_recv()

    def output(i, carry):
        here = at(i)
        result[here, :] = (
            resid[here, :] + (down_part[here, :].astype(F32) + down_recv[here, :].astype(F32))
        ).astype(BF)
        return carry

    lax.fori_loop(0, ROWS_WAVE, output, 0)
    over_peers(lambda d: early_copy(d).wait_recv())
    total = early_recv[0]
    for index in range(1, count):
        total = total + early_recv[index]
    early_sum[...] = total

    def second(i, carry):
        n_copy(i).wait_recv()
        here = at(i)
        grad = n_send[here, :].astype(F32) + n_recv[here, :].astype(F32)
        _, normed, inverse = norm_rows(tok[here, :].astype(F32), gain[0:1, :], shift[0:1, :])
        gtok[here, :] = gmid[here, :] + norm_rows_back(grad, normed, inverse, gain[0:1, :])
        late[0:1, :] += jnp.sum(grad * normed, axis=0, keepdims=True)
        late[1:2, :] += jnp.sum(grad, axis=0, keepdims=True)
        return carry

    lax.fori_loop(0, ROWS_WAVE, second, 0)
    over_peers(lambda d: late_copy(d).start())
    late_recv[me] = late[...]

    over_peers(lambda d: wg_copy(d).wait_recv())
    for owner in range(nz):
        block = wg_recv[owner].astype(F32)
        for source in range(1, ns):
            block = block + wg_recv[source * nz + owner].astype(F32)
        for part in range(3):
            gwqkv[part, :, owner * PAIR : (owner + 1) * PAIR] = block[:, part * PAIR : (part + 1) * PAIR]

    over_peers(lambda d: late_copy(d).wait_recv())
    total = late_recv[0]
    for index in range(1, count):
        total = total + late_recv[index]
    late_sum[...] = total

    down_copy().wait_send()
    over_peers(lambda d: early_copy(d).wait_send())
    over_peers(lambda d: late_copy(d).wait_send())
    over_peers(lambda d: wg_copy(d).wait_send())

    def finish(i, carry):
        n_copy(i).wait_send()
        return carry

    lax.fori_loop(0, ROWS_WAVE, finish, 0)
    for owner in range(nz):

        @pl.when(z != owner)
        def _():
            piece_copy(owner).wait_send()


def run_back(dims, *inputs):
    ns, nz, rows = dims
    width = inputs[12].shape[1]
    count = ns * nz
    depth = width // count
    wide = 3 * PAIR
    return pl.pallas_call(
        partial(back_kernel, dims),
        name="tree_backward",
        out_shape=(
            shape((rows, width), BF),
            shape((rows, width), F32),
            shape((3, depth, nz * PAIR), F32),
            shape((8, width), F32),
            shape((8, width), F32),
        ),
        in_specs=[vmem()] * 17,
        out_specs=[vmem()] * 5,
        scratch_shapes=[
            pltpu.VMEM((TREE, wide), BF),
            pltpu.VMEM((TRUNK, PAIR), F32),
            pltpu.VMEM((TRUNK, PAIR), F32),
            pltpu.VMEM((TREE - TRUNK, PAIR), F32),
            pltpu.VMEM((TREE - TRUNK, PAIR), F32),
            pltpu.VMEM((TREE - TRUNK, PAIR), F32),
            pltpu.VMEM((TREE - TRUNK, PAIR), F32),
            pltpu.VMEM((TRUNK, 2 * PAIR), BF),
            pltpu.VMEM((PAIR, TRUNK), BF),
            pltpu.VMEM((16, 128), F32),
            pltpu.VMEM((16, 128), F32),
            pltpu.VMEM((rows, nz * wide), BF),
            pltpu.VMEM((rows, width), BF),
            pltpu.VMEM((rows, width), BF),
            pltpu.VMEM((rows, width), BF),
            pltpu.VMEM((width, wide), BF),
            pltpu.VMEM((count, depth, wide), BF),
            pltpu.VMEM((count, 8, width), F32),
            pltpu.VMEM((8, width), F32),
            pltpu.VMEM((count, 8, width), F32),
            dma(2),
            dma(count - 1),
            dma(count - 1),
            dma(count - 1),
            dma(count - 1),
            dma(count - 1),
            dma(count - 1),
            dma(nz),
            dma(nz),
            dma(ROWS_WAVE),
            dma(ROWS_WAVE),
        ],
        compiler_params=pltpu.CompilerParams(
            collective_id=2, has_side_effects=True, vmem_limit_bytes=60 << 20
        ),
        cost_estimate=pl.CostEstimate(flops=40_000_000_000, bytes_accessed=20_000_000, transcendentals=0),
    )(*inputs)


def fast_device(
    tokens, cotangent, seg_ids, positions, parents, w_qkv, b_qv, w_out, b_out, w_up, b_up, w_down, b_down, ln_gain, ln_bias
):
    rows = tokens.shape[0]
    ns, nz, ntp = lax.axis_size("shard"), lax.axis_size("ctx"), lax.axis_size("tp")
    dims = (ns, nz, rows)
    both = ("shard", "ctx")

    labels = seg_ids.reshape(rows // BRANCH, BRANCH)[:, 0]
    match = labels[:, None] == jnp.arange(parents.shape[0], dtype=jnp.int32)[None, :]
    above = jnp.sum(jnp.where(match, parents[None, :], 0), axis=1)
    fill = 8 - rows // BRANCH
    lines = jnp.concatenate([jnp.pad(labels, (0, fill)), jnp.pad(above, (0, fill))]).astype(F32)
    info = jnp.broadcast_to(lines[:, None], (16, 128))
    per = HEADS // ntp
    index = lax.axis_index("tp") * per + lax.axis_index("ctx") * 2 + jnp.arange(2)
    slope = 2.0 ** (-8.0 * (index.astype(F32) + 1.0) / HEADS)
    one = lax.reduce_precision(slope, 8, 7)
    two = lax.reduce_precision(slope - one, 8, 7)
    three = lax.reduce_precision(slope - one - two, 8, 7)
    table = jnp.stack([one, two, three, one, two, three, jnp.ones_like(one)], axis=1)
    slopes = jnp.pad(table, ((0, 0), (0, 121)))

    wfull, wq, act_turned, query, key, value, out_heads, lse, info_all, att = run_tree(
        dims, tokens, w_up, w_out.T, w_down.T, w_qkv, info, b_qv, slopes, ln_gain, ln_bias
    )
    wqkv, gsum, ga_all, down_part, resid, gmid, sums = run_feed(
        dims, tokens, cotangent, att, wfull, wq, b_out[None, :], b_up[None, :], b_down[None, :], ln_gain, ln_bias
    )
    grads = lax.psum_scatter(gsum, both, scatter_dimension=0, tiled=True)
    result, grad_tokens, grad_w_qkv, early, late = run_back(
        dims, query, key, value, out_heads, lse, info_all, ga_all, act_turned, wqkv, down_part, resid, gmid,
        tokens, slopes, ln_gain, ln_bias, sums,
    )
    units, inner = b_up.shape[0], w_out.shape[0]
    grads = grads.astype(F32)
    width = tokens.shape[1]
    return (
        result,
        grad_tokens,
        grad_w_qkv,
        late[2].reshape(2, nz * PAIR),
        grads[:, units : units + inner].T,
        early[2],
        grads[:, 0:units],
        early[0:2].reshape(units),
        grads[:, units + inner :].T,
        early[3],
        jnp.stack([late[0], early[4]]),
        jnp.stack([late[1], early[5]]),
    )


def norm_forward(inputs_in, gain_row, shift_row):
    centre = inputs_in - jnp.mean(inputs_in, axis=-1, keepdims=True)
    inverse = lax.rsqrt(jnp.mean(centre * centre, axis=-1, keepdims=True) + EPS)
    normed = centre * inverse
    return (normed * gain_row + shift_row, normed, inverse)


def norm_backward(grad_in, normed, inverse, gain_row):
    scaled = grad_in * gain_row
    mean_grad = jnp.mean(scaled, axis=-1, keepdims=True)
    mean_cross = jnp.mean(scaled * normed, axis=-1, keepdims=True)
    return inverse * (scaled - mean_grad - normed * mean_cross)


def ancestry(seg_vals, parents):
    first_up = jnp.take(parents, seg_vals)
    return (first_up, jnp.take(parents, first_up))


def block_scores(query_heads, key_heads, query_tags, key_tags, slopes):
    q_seg, q_first, q_second, q_pos = query_tags
    k_seg, k_pos = key_tags
    raw_scores = jnp.einsum(
        "qhd,khd->hqk", query_heads, key_heads, preferred_element_type=jnp.float32
    ) * HD ** (-0.5)
    distance = (q_pos[:, None] - k_pos[None, :]).astype(jnp.float32)
    scores = raw_scores - slopes[:, None, None] * distance[None]
    related = (
        (k_seg[None, :] == q_seg[:, None])
        | (k_seg[None, :] == q_first[:, None])
        | (k_seg[None, :] == q_second[:, None])
    )
    allowed = related & (k_pos[None, :] <= q_pos[:, None])
    return (scores, allowed[None])


def probabilities(scores, allowed, row_max, row_sum):
    shifted = jnp.where(allowed, scores - row_max[:, :, None], NEG)
    return jnp.exp(shifted) / row_sum[:, :, None]


def per_device(
    tokens,
    cotangent,
    seg_ids,
    positions,
    parents,
    w_qkv,
    b_qv,
    w_out,
    b_out,
    w_up,
    b_up,
    w_down,
    b_down,
    ln_gain,
    ln_bias,
):
    num_rows = tokens.shape[0]
    head_count = HEADS // lax.axis_size("tp")
    head_width = head_count * HD
    head_index = (lax.axis_index("tp") * head_count + jnp.arange(head_count)).astype(jnp.float32)
    slopes = 2.0 ** (-8.0 * (head_index + 1.0) / HEADS)
    scale = HD ** (-0.5)
    full_qkv, full_out = (
        lax.all_gather(w_qkv, ("shard", "ctx"), axis=1, tiled=True),
        lax.all_gather(w_out, ("shard", "ctx"), axis=1, tiled=True),
    )
    group_seg, group_pos = (
        lax.all_gather(seg_ids, "ctx", axis=0, tiled=True),
        lax.all_gather(positions, "ctx", axis=0, tiled=True),
    )
    own_first, own_second = ancestry(seg_ids, parents)
    own_tags = (seg_ids, own_first, own_second, positions)
    inputs = tokens.astype(jnp.float32)
    norm_one, normed_one, inverse_one = norm_forward(inputs, ln_gain[0], ln_bias[0])
    act_one = norm_one.astype(jnp.bfloat16)
    projected = jnp.einsum("td,cde->cte", act_one, full_qkv, preferred_element_type=jnp.float32)
    qkv_bias = jnp.stack([b_qv[0], jnp.zeros((head_width,), jnp.float32), b_qv[1]])
    qkv_low = (projected + qkv_bias[:, None, :]).astype(jnp.bfloat16)
    query_flat, key_flat, value_flat = (qkv_low[0], qkv_low[1], qkv_low[2])
    group_keys, group_values = (
        lax.all_gather(key_flat, "ctx", axis=0, tiled=True),
        lax.all_gather(value_flat, "ctx", axis=0, tiled=True),
    )
    group_rows = group_keys.shape[0]
    block_count = group_rows // KEY_BLOCK
    key_blocks = group_keys.reshape(block_count, KEY_BLOCK, head_count, HD)
    value_blocks = group_values.reshape(block_count, KEY_BLOCK, head_count, HD)
    seg_blocks = group_seg.reshape(block_count, KEY_BLOCK)
    pos_blocks = group_pos.reshape(block_count, KEY_BLOCK)
    query_heads = query_flat.reshape(num_rows, head_count, HD)

    def stats_step(carry_in, block_parts):
        row_max, row_sum = carry_in
        key_part, seg_part, pos_part = block_parts
        scores, allowed = block_scores(
            query_heads, key_part, own_tags, (seg_part, pos_part), slopes
        )
        new_max = jnp.maximum(row_max, jnp.max(jnp.where(allowed, scores, NEG), axis=-1))
        shifted = jnp.where(allowed, scores - new_max[:, :, None], NEG)
        row_sum = row_sum * jnp.exp(row_max - new_max) + jnp.sum(jnp.exp(shifted), axis=-1)
        return ((new_max, row_sum), None)

    start_stats = (
        jnp.full((head_count, num_rows), NEG, jnp.float32),
        jnp.zeros((head_count, num_rows), jnp.float32),
    )
    (row_max, row_sum), _ = lax.scan(stats_step, start_stats, (key_blocks, seg_blocks, pos_blocks))

    def output_step(out_accum, block_parts):
        key_part, value_part, seg_part, pos_part = block_parts
        scores, allowed = block_scores(
            query_heads, key_part, own_tags, (seg_part, pos_part), slopes
        )
        prob_low = probabilities(scores, allowed, row_max, row_sum).astype(jnp.bfloat16)
        return (
            out_accum
            + jnp.einsum("hqk,khd->qhd", prob_low, value_part, preferred_element_type=jnp.float32),
            None,
        )

    attended, _ = lax.scan(
        output_step,
        jnp.zeros((num_rows, head_count, HD), jnp.float32),
        (key_blocks, value_blocks, seg_blocks, pos_blocks),
    )
    attended_low = attended.reshape(num_rows, head_width).astype(jnp.bfloat16)
    branch_one = (
        lax.psum(
            jnp.dot(attended_low, full_out, preferred_element_type=jnp.float32).astype(
                jnp.bfloat16
            ),
            "tp",
        ).astype(jnp.float32)
        + b_out
    )
    middle = inputs + branch_one
    full_up, full_down = (
        lax.all_gather(w_up, ("shard", "ctx"), axis=0, tiled=True),
        lax.all_gather(w_down, ("shard", "ctx"), axis=1, tiled=True),
    )
    norm_two, normed_two, inverse_two = norm_forward(middle, ln_gain[1], ln_bias[1])
    act_two = norm_two.astype(jnp.bfloat16)
    upper_in = jnp.dot(act_two, full_up, preferred_element_type=jnp.float32) + b_up
    gelu_vals, gelu_pull = jax.vjp(partial(jax.nn.gelu, approximate=True), upper_in)
    hidden = gelu_vals.astype(jnp.bfloat16)
    branch_two = (
        lax.psum(
            jnp.dot(hidden, full_down, preferred_element_type=jnp.float32).astype(jnp.bfloat16),
            "tp",
        ).astype(jnp.float32)
        + b_down
    )
    result = (middle + branch_two).astype(jnp.bfloat16)
    grad_out = cotangent.astype(jnp.float32)
    grad_hidden = jnp.einsum("td,fd->tf", cotangent, full_down, preferred_element_type=jnp.float32)
    grad_upper = gelu_pull(grad_hidden)[0].astype(jnp.bfloat16)
    down_term = jnp.einsum("tf,td->fd", hidden, cotangent, preferred_element_type=jnp.float32)
    up_term = jnp.einsum("td,tf->df", act_two, grad_upper, preferred_element_type=jnp.float32)
    grad_w_up, grad_w_down = (
        lax.psum_scatter(up_term, ("shard", "ctx"), scatter_dimension=0, tiled=True),
        lax.psum_scatter(down_term, ("shard", "ctx"), scatter_dimension=1, tiled=True),
    )
    grad_norm_two = lax.psum(
        jnp.einsum("tf,df->td", grad_upper, full_up, preferred_element_type=jnp.float32).astype(
            jnp.bfloat16
        ),
        "tp",
    ).astype(jnp.float32)
    grad_middle = grad_out + norm_backward(grad_norm_two, normed_two, inverse_two, ln_gain[1])
    grad_branch = grad_middle.astype(jnp.bfloat16)
    out_term = jnp.einsum(
        "te,td->ed", attended_low, grad_branch, preferred_element_type=jnp.float32
    )
    grad_att = jnp.einsum(
        "td,ed->te", grad_branch, full_out, preferred_element_type=jnp.float32
    ).astype(jnp.bfloat16)
    grad_heads = grad_att.reshape(num_rows, head_count, HD)
    row_terms = jnp.einsum("qhd,qhd->hq", grad_heads.astype(jnp.float32), attended)

    def joint_step(grad_accum, block_parts):
        key_part, value_part, seg_part, pos_part = block_parts
        scores, allowed = block_scores(
            query_heads, key_part, own_tags, (seg_part, pos_part), slopes
        )
        prob_vals = probabilities(scores, allowed, row_max, row_sum)
        grad_probs = jnp.einsum(
            "qhd,khd->hqk", grad_heads, value_part, preferred_element_type=jnp.float32
        )
        grad_scores = (prob_vals * (grad_probs - row_terms[:, :, None])).astype(jnp.bfloat16)
        grad_accum = (
            grad_accum
            + jnp.einsum("hqk,khd->qhd", grad_scores, key_part, preferred_element_type=jnp.float32)
            * scale
        )
        key_part_grad = (
            jnp.einsum("hqk,qhd->khd", grad_scores, query_heads, preferred_element_type=jnp.float32)
            * scale
        )
        value_part_grad = jnp.einsum(
            "hqk,qhd->khd",
            prob_vals.astype(jnp.bfloat16),
            grad_heads,
            preferred_element_type=jnp.float32,
        )
        return (
            grad_accum,
            (
                key_part_grad.reshape(KEY_BLOCK, head_width),
                value_part_grad.reshape(KEY_BLOCK, head_width),
            ),
        )

    grad_query_sum, (key_terms, value_terms) = lax.scan(
        joint_step,
        jnp.zeros((num_rows, head_count, HD), jnp.float32),
        (key_blocks, value_blocks, seg_blocks, pos_blocks),
    )
    key_grad_sum, value_grad_sum = (
        lax.psum_scatter(
            key_terms.reshape(group_rows, head_width).astype(jnp.bfloat16),
            "ctx",
            scatter_dimension=0,
            tiled=True,
        ).astype(jnp.float32),
        lax.psum_scatter(
            value_terms.reshape(group_rows, head_width).astype(jnp.bfloat16),
            "ctx",
            scatter_dimension=0,
            tiled=True,
        ).astype(jnp.float32),
    )
    grad_query_low = grad_query_sum.reshape(num_rows, head_width).astype(jnp.bfloat16)
    grad_key_low = key_grad_sum.astype(jnp.bfloat16)
    grad_value_low = value_grad_sum.astype(jnp.bfloat16)
    grad_qkv = jnp.stack([grad_query_low, grad_key_low, grad_value_low])
    grad_norm_one = lax.psum(
        jnp.einsum("cte,cde->td", grad_qkv, full_qkv, preferred_element_type=jnp.float32).astype(
            jnp.bfloat16
        ),
        "tp",
    ).astype(jnp.float32)
    grad_tokens = grad_middle + norm_backward(grad_norm_one, normed_one, inverse_one, ln_gain[0])
    qkv_term = jnp.einsum("td,cte->cde", act_one, grad_qkv, preferred_element_type=jnp.float32)
    grad_w_qkv, grad_w_out = (
        lax.psum_scatter(qkv_term, ("shard", "ctx"), scatter_dimension=1, tiled=True),
        lax.psum_scatter(out_term, ("shard", "ctx"), scatter_dimension=1, tiled=True),
    )
    bias_qv_part = jnp.stack(
        [
            jnp.sum(grad_query_low.astype(jnp.float32), axis=0),
            jnp.sum(grad_value_low.astype(jnp.float32), axis=0),
        ]
    )
    out_bias_part = jnp.sum(grad_branch.astype(jnp.float32), axis=0)
    up_bias_part = jnp.sum(grad_upper.astype(jnp.float32), axis=0)
    down_bias_part = jnp.sum(grad_out, axis=0)
    gain_part = jnp.stack(
        [jnp.sum(grad_norm_one * normed_one, axis=0), jnp.sum(grad_norm_two * normed_two, axis=0)]
    )
    shift_part = jnp.stack([jnp.sum(grad_norm_one, axis=0), jnp.sum(grad_norm_two, axis=0)])
    grad_b_qv, grad_b_out, grad_b_up, grad_b_down, grad_gain, grad_shift = lax.psum(
        (bias_qv_part, out_bias_part, up_bias_part, down_bias_part, gain_part, shift_part),
        ("shard", "ctx"),
    )
    return (
        result,
        grad_tokens,
        grad_w_qkv,
        grad_b_qv,
        grad_w_out,
        grad_b_out,
        grad_w_up,
        grad_b_up,
        grad_w_down,
        grad_b_down,
        grad_gain,
        grad_shift,
    )


def solution(mesh):
    placed = (
        P(("shard", "ctx"), None),
        P(("shard", "ctx"), None),
        P(("shard", "ctx")),
        P(("shard", "ctx")),
        P(),
        P(None, ("shard", "ctx"), "tp"),
        P(None, "tp"),
        P("tp", ("shard", "ctx")),
        P(),
        P(("shard", "ctx"), "tp"),
        P("tp"),
        P("tp", ("shard", "ctx")),
        P(),
        P(),
        P(),
    )
    sizes = dict(mesh.shape)
    paired = sizes["tp"] * sizes["ctx"] * 2 == HEADS and sizes["tp"] == 2 and sizes["shard"] == 4
    return jax.shard_map(
        fast_device if paired else per_device,
        mesh=mesh,
        in_specs=placed,
        out_specs=(
            P(("shard", "ctx"), None),
            P(("shard", "ctx"), None),
            P(None, ("shard", "ctx"), "tp"),
            P(None, "tp"),
            P("tp", ("shard", "ctx")),
            P(),
            P(("shard", "ctx"), "tp"),
            P("tp"),
            P("tp", ("shard", "ctx")),
            P(),
            P(),
            P(),
        ),
        check_vma=False,
    )
```

```python
from functools import partial

import jax
import jax.numpy as jnp
from jax import lax
from jax.experimental import pallas as pl
from jax.experimental.pallas import tpu as pltpu
from jax.sharding import PartitionSpec as P

HEADS = 16
HD = 64
KEY_BLOCK = 512
TRUNK = 1024
BRANCH = 128
SLOTS = 12
TREE = TRUNK + SLOTS * BRANCH
PAIR = 2 * HD

EPS = 1e-05
NEG = -1e30
LOG2E = 1.4426950408889634
MESH = pl.DeviceIdType.MESH
BF = jnp.bfloat16
F32 = jnp.float32
ROWS_WAVE = 4
SPREAD_AT = ((1, 3), (2,), ())


def nt(left, right):
    return lax.dot_general(left, right, (((1,), (1,)), ((), ())), preferred_element_type=F32)


def nn(left, right):
    return lax.dot_general(left, right, (((1,), (0,)), ((), ())), preferred_element_type=F32)


def rcopy(src, dst, send, recv, device):
    return pltpu.make_async_remote_copy(
        src_ref=src, dst_ref=dst, send_sem=send, recv_sem=recv, device_id=device, device_id_type=MESH
    )


def greet(devices):
    barrier = pltpu.get_barrier_semaphore()
    for device in devices:
        pl.semaphore_signal(barrier, inc=1, device_id=device, device_id_type=MESH)
    pl.semaphore_wait(barrier, len(devices))


def norm_rows(values, gain_row, shift_row):
    centre = values - jnp.mean(values, axis=-1, keepdims=True)
    inverse = lax.rsqrt(jnp.mean(centre * centre, axis=-1, keepdims=True) + EPS)
    normed = centre * inverse
    return normed * gain_row + shift_row, normed, inverse


def norm_rows_back(grad_in, normed, inverse, gain_row):
    scaled = grad_in * gain_row
    mean_grad = jnp.mean(scaled, axis=-1, keepdims=True)
    mean_cross = jnp.mean(scaled * normed, axis=-1, keepdims=True)
    return inverse * (scaled - mean_grad - normed * mean_cross)


def head_masks():
    lane = lax.broadcasted_iota(jnp.int32, (1, PAIR), 1)
    first = (lane < HD).astype(F32).astype(BF)
    second = (lane >= HD).astype(F32).astype(BF)
    return first, second


def stack_heads(rows):
    first, second = head_masks()
    return jnp.concatenate([rows * first, rows * second], axis=0)


def unstack_turned(turned, rows):
    return jnp.concatenate([turned[:HD, :rows], turned[HD:, rows:]], axis=0).T


def key_features(high, low, flag, rows):
    lane = lax.broadcasted_iota(jnp.int32, (rows, 128), 1)
    feats = jnp.where(lane < 3, high, jnp.where(lane < 6, low, jnp.where(lane == 6, flag, 0.0)))
    return feats.astype(BF)


def query_features(slope_ref, rows):
    return jnp.concatenate(
        [
            jnp.broadcast_to(slope_ref[0:1, :], (rows, 128)),
            jnp.broadcast_to(slope_ref[1:2, :], (rows, 128)),
        ],
        axis=0,
    ).astype(BF)


def fill_trunk_keys(key_ref, keys_aug):
    keys_aug[:, 0:PAIR] = key_ref[0:TRUNK, :]
    pos = lax.broadcasted_iota(jnp.int32, (TRUNK, 128), 0)
    low = pos & 255
    keys_aug[:, PAIR:] = key_features((pos - low).astype(F32), low.astype(F32), 0.0, TRUNK)


def fill_labels(info_all, blocks, labels, parents):
    labels[...] = jnp.full(labels.shape, -1.0, F32)
    parents[...] = jnp.full(parents.shape, -2.0, F32)
    for slot in range(SLOTS):
        block = TRUNK // BRANCH + slot
        owner, inner = block // blocks, block % blocks
        labels[slot : slot + 1, :] = info_all[owner, inner : inner + 1, :]
        parents[slot : slot + 1, :] = info_all[owner, 8 + inner : 9 + inner, :]


def parent_pick(slot, labels, parents, key_ref, value_ref):
    mine = parents[pl.ds(slot, 1), :]
    leaf = jnp.zeros((1, 128), F32)
    key_sum = jnp.zeros((BRANCH, PAIR), BF)
    value_sum = jnp.zeros((BRANCH, PAIR), BF)
    for other in range(SLOTS):
        same = (mine == labels[other : other + 1, :]).astype(F32)
        leaf = leaf + same
        same_low = same.astype(BF)
        at = TRUNK + other * BRANCH
        key_sum = key_sum + same_low * key_ref[at : at + BRANCH, :]
        value_sum = value_sum + same_low * value_ref[at : at + BRANCH, :]
    return leaf, key_sum, value_sum


def segment_key_features(leaf):
    row = lax.broadcasted_iota(jnp.int32, (BRANCH, 128), 0).astype(F32)
    own = key_features(float(TRUNK), row + leaf * float(BRANCH), 0.0, BRANCH)
    above = key_features(float(TRUNK), row, (leaf - 1.0) * 1e30, BRANCH)
    return own, above


def causal(rows):
    key = lax.broadcasted_iota(jnp.int32, (rows, rows), 0)
    query = lax.broadcasted_iota(jnp.int32, (rows, rows), 1)
    once = key <= query
    return jnp.concatenate([once, once], axis=1)


class Spread:
    def __init__(self, full, dims, depth, cols, sems):
        self.full, self.depth, self.cols = full, depth, cols
        self.ns, self.nz, _ = dims
        self.s, self.z = lax.axis_index("shard"), lax.axis_index("ctx")
        self.zs, self.zr, self.xs, self.xr, self.cs, self.cr = sems

    def rows(self, shard, place):
        at = pl.multiple_of((shard * self.nz + place) * self.depth, self.depth)
        return self.full.at[pl.ds(at, self.depth), self.cols]

    def flip(self, bits):
        low = lax.rem(self.s, 2)
        high = lax.div(self.s, 2)
        if bits & 1:
            low = 1 - low
        if bits & 2:
            high = 1 - high
        return 2 * high + low

    def z_copy(self, d):
        ref = self.rows(self.s, self.z)
        return rcopy(ref, ref, self.zs.at[d - 1], self.zr.at[d - 1], {"ctx": lax.rem(self.z + d, self.nz)})

    def source(self, d):
        return lax.rem(self.z + self.nz - d, self.nz)

    def x_copy(self, d):
        ref = self.rows(self.s, self.source(d))
        return rcopy(ref, ref, self.xs.at[d], self.xr.at[d], {"shard": self.flip(2)})

    def c_copy(self, far, d):
        ref = self.rows(self.flip(2) if far else self.s, self.source(d))
        return rcopy(ref, ref, self.cs.at[far, d], self.cr.at[far, d], {"shard": self.flip(1)})

    def z_start(self, d):
        self.z_copy(d).start()

    def own(self):
        self.x_copy(0).start()
        self.c_copy(0, 0).start()

    def z_done(self, d):
        ref = self.rows(self.s, self.source(d))
        rcopy(ref, ref, self.zs.at[d - 1], self.zr.at[d - 1], {"ctx": self.z}).wait_recv()
        self.x_copy(d).start()
        self.c_copy(0, d).start()

    def x_done(self, d):
        ref = self.rows(self.flip(2), self.source(d))
        rcopy(ref, ref, self.xs.at[d], self.xr.at[d], {"shard": self.flip(2)}).wait_recv()
        self.c_copy(1, d).start()

    def c_done(self, far, d):
        ref = self.rows(self.flip(3) if far else self.flip(1), self.source(d))
        rcopy(ref, ref, self.cs.at[far, d], self.cr.at[far, d], {"shard": self.flip(1)}).wait_recv()

    def all_here(self):
        for d in range(self.nz):
            self.c_done(0, d)
            self.c_done(1, d)

    def finish(self):
        for d in range(self.nz):
            if d:
                self.z_copy(d).wait_send()
            self.x_copy(d).wait_send()
            self.c_copy(0, d).wait_send()
            self.c_copy(1, d).wait_send()


def spread_sems(nz):
    return [dma(nz - 1), dma(nz - 1), dma(nz), dma(nz), dma(2, nz), dma(2, nz)]


def vmem():
    return pl.BlockSpec(memory_space=pltpu.VMEM)


def shape(dims, kind):
    return jax.ShapeDtypeStruct(dims, kind)


def dma(*dims):
    return pltpu.SemaphoreType.DMA(dims)


def tree_kernel(
    dims,
    tok,
    w_up,
    w_out,
    w_down,
    wq3,
    info,
    bias_qv,
    slopes,
    gain,
    shift,
    wfull,
    wq,
    act_turned,
    query,
    key,
    value,
    out_heads,
    lse,
    info_all,
    att,
    tree,
    wcat,
    keys_aug,
    values_turned,
    labels,
    parents,
    info_send,
    info_recv,
    wz_send,
    wz_recv,
    ws_send,
    ws_recv,
    z_send,
    z_recv,
    y_send,
    y_recv,
    a_send,
    a_recv,
    local_sem,
    b_send,
    b_recv,
    t_send,
    t_recv,
    *spread,
):
    ns, nz, rows = dims
    s, z, y = lax.axis_index("shard"), lax.axis_index("ctx"), lax.axis_index("tp")
    half = rows // 2
    sub = half // 2
    depth = wq.shape[0]
    wide = 3 * PAIR
    my_rows = pl.ds(pl.multiple_of((s * nz + z) * depth, depth), depth)
    units, inner = w_up.shape[1], w_out.shape[1]
    own_cols = pl.multiple_of(2 * units + y * inner, 128)
    starts = [
        pltpu.make_async_copy(tok, tree.at[pl.ds(pl.multiple_of(z * rows, 128), rows), :], local_sem.at[0]),
        pltpu.make_async_copy(w_up, wfull.at[my_rows, 0:units], local_sem.at[1]),
        pltpu.make_async_copy(w_down, wfull.at[my_rows, units : 2 * units], local_sem.at[2]),
        pltpu.make_async_copy(w_out, wfull.at[my_rows, pl.ds(own_cols, inner)], local_sem.at[3]),
    ]
    for one in starts:
        one.start()
    for to in range(nz):
        for part in range(3):
            wq[:, to * wide + part * PAIR : to * wide + (part + 1) * PAIR] = wq3[
                part, :, to * PAIR : (to + 1) * PAIR
            ]
    greet(
        [{"ctx": lax.rem(z + d, nz)} for d in range(1, nz)]
        + [{"shard": lax.rem(s + d, ns)} for d in range(1, ns)]
        + [{"tp": 1 - y}]
    )
    weights = Spread(wfull, dims, depth, slice(0, 2 * units), spread[:6])
    outer = Spread(wfull, dims, depth, pl.ds(own_cols, inner), spread[6:])

    def info_copy(d):
        return rcopy(
            info, info_all.at[z], info_send.at[d - 1], info_recv.at[d - 1], {"ctx": lax.rem(z + d, nz)}
        )

    def wz_copy(d):
        to = lax.rem(z + d, nz)
        return rcopy(
            wq.at[:, pl.ds(pl.multiple_of(to * wide, 128), wide)],
            wcat.at[my_rows, :],
            wz_send.at[d - 1],
            wz_recv.at[d - 1],
            {"ctx": to},
        )

    shard_rows = pl.ds(s * (nz * depth), nz * depth)

    def ws_copy(d):
        return rcopy(
            wcat.at[shard_rows, :],
            wcat.at[shard_rows, :],
            ws_send.at[d - 1],
            ws_recv.at[d - 1],
            {"shard": lax.rem(s + d, ns)},
        )

    for d in range(1, nz):
        wz_copy(d).start()
    for d in range(1, nz):
        info_copy(d).start()
    wcat[my_rows, :] = wq[:, pl.ds(pl.multiple_of(z * wide, 128), wide)]
    info_all[z] = info[...]
    for one in starts:
        one.wait()

    def piece(block, second, part):
        at = block * rows + jnp.where(second, 1 - y, y) * half + part * sub
        return tree.at[pl.ds(pl.multiple_of(at, 32), sub), :]

    def z_copy(direction, k, part):
        block = z - k if direction == 0 else z + k
        to = z + 1 if direction == 0 else z - 1
        ref = piece(block, False, part)
        return rcopy(ref, ref, z_send.at[direction, k, part], z_recv.at[direction, k, part], {"ctx": to})

    def z_arrival(direction, k, part):
        block = z - k if direction == 0 else z + k
        ref = piece(block, False, part)
        return rcopy(
            ref, ref, z_send.at[direction, k - 1, part], z_recv.at[direction, k - 1, part], {"ctx": z}
        )

    def y_copy(direction, k, part):
        block = z - k if direction == 0 else z + k
        ref = piece(block, False, part)
        return rcopy(
            ref, ref, y_send.at[direction, k - 1, part], y_recv.at[direction, k - 1, part], {"tp": 1 - y}
        )

    def y_arrival(direction, k, part):
        block = z - k if direction == 0 else z + k
        ref = piece(block, True, part)
        return rcopy(
            ref, ref, y_send.at[direction, k - 1, part], y_recv.at[direction, k - 1, part], {"tp": 1 - y}
        )

    def place(direction, k):
        block = z - k if direction == 0 else z + k
        nxt = z + 1 if direction == 0 else z - 1
        here = (block >= 0) & (block < nz)
        onward = here & (nxt >= 0) & (nxt < nz)
        return block, here, onward

    def forward(k, first):
        for part in range(2):
            for direction in range(2):
                _, here, onward = place(direction, k)
                if not first:

                    @pl.when(here)
                    def _():
                        z_arrival(direction, k, part).wait_recv()

                @pl.when(onward & (k < nz - 1))
                def _():
                    z_copy(direction, k, part).start()

                if not first:

                    @pl.when(here)
                    def _():
                        y_copy(direction, k, part).start()

    forward(0, True)
    weights.own()
    outer.own()
    for d in range(1, nz):
        wz_copy(d).wait_recv()
    for d in range(1, ns):
        ws_copy(d).start()

    bias_at = pl.ds(pl.multiple_of(z * PAIR, 128), PAIR)
    bias_q = bias_qv[0:1, bias_at]
    bias_v = bias_qv[1:2, bias_at]

    def project(k):
        def side(direction, inner_carry):
            block = z + (2 * direction - 1) * k

            @pl.when((block >= 0) & (block < nz) & ((k > 0) | (direction == 0)))
            def _():
                def tile(t, carry):
                    here = pl.ds(pl.multiple_of(block * rows + t * 128, 128), 128)
                    act = norm_rows(tree[here, :].astype(F32), gain[0:1, :], shift[0:1, :])[0].astype(BF)
                    act_turned[:, here] = act.T
                    both = nn(act, wcat[...])
                    query[here, :] = (
                        (both[:, :PAIR] + bias_q).astype(BF).astype(F32) * HD ** (-0.5)
                    ).astype(BF)
                    key[here, :] = both[:, PAIR : 2 * PAIR].astype(BF)
                    value[here, :] = (both[:, 2 * PAIR :] + bias_v).astype(BF)
                    return carry

                lax.fori_loop(0, rows // 128, tile, 0)

            return inner_carry

        lax.fori_loop(0, 2, side, 0)

    def shared(k):
        for part in range(2):
            for direction in range(2):
                _, here, _ = place(direction, k)

                @pl.when(here)
                def _():
                    y_arrival(direction, k, part).wait_recv()

    forward(1, False)
    for d in range(1, nz):
        outer.z_start(d)
    for d in SPREAD_AT[0]:
        weights.z_start(d)
    for d in range(1, ns):
        ws_copy(d).wait_recv()
    project(0)

    def wave(k, carry):
        forward(k, False)

        @pl.when(k == 2)
        def _():
            for d in SPREAD_AT[1]:
                weights.z_start(d)

        @pl.when(k == 3)
        def _():
            for d in SPREAD_AT[2]:
                weights.z_start(d)

        shared(k - 1)
        project(k - 1)
        return carry

    lax.fori_loop(2, nz, wave, 0)
    for d in range(1, nz):
        outer.z_done(d)
    for d in SPREAD_AT[0]:
        weights.z_done(d)
    for d in range(nz):
        outer.x_done(d)
    shared(nz - 1)
    project(nz - 1)

    for d in range(1, nz):
        info_copy(d).wait_recv()

    fill_labels(info_all, rows // BRANCH, labels, parents)
    fill_trunk_keys(key, keys_aug)
    values_turned[...] = value[0:TRUNK, :].T

    def att_cols(half_at, owner):
        return pl.ds(pl.multiple_of(half_at * inner + owner * PAIR, 128), PAIR)

    def att_copy(to):
        return rcopy(
            out_heads.at[pl.ds(to * rows, rows), :],
            att.at[:, att_cols(y, z)],
            a_send.at[to],
            a_recv.at[z],
            {"ctx": to},
        )

    def pass_on(owner):
        return rcopy(
            att.at[:, att_cols(y, owner)],
            att.at[:, att_cols(y, owner)],
            b_send.at[owner],
            b_recv.at[owner],
            {"tp": 1 - y},
        )

    half_rows = pl.ds(pl.multiple_of(lax.rem(s, 2) * (ns * nz * depth // 2), 128), ns * nz * depth // 2)
    far_rows = pl.ds(pl.multiple_of((1 - lax.rem(s, 2)) * (ns * nz * depth // 2), 128), ns * nz * depth // 2)
    far_cols = pl.ds(pl.multiple_of(2 * units + (1 - y) * inner, 128), inner)

    def plane_copy():
        ref = wfull.at[half_rows, pl.ds(own_cols, inner)]
        return rcopy(ref, ref, t_send.at[0], t_recv.at[0], {"tp": 1 - y})

    def plane_arrival():
        ref = wfull.at[half_rows, far_cols]
        return rcopy(ref, ref, t_send.at[0], t_recv.at[0], {"tp": 1 - y})

    def core_copy():
        ref = wfull.at[half_rows, far_cols]
        return rcopy(ref, ref, t_send.at[1], t_recv.at[1], {"shard": outer.flip(1)})

    def core_arrival():
        ref = wfull.at[far_rows, far_cols]
        return rcopy(ref, ref, t_send.at[1], t_recv.at[1], {"shard": outer.flip(1)})

    outer.all_here()
    plane_copy().start()

    def send_out(to):
        @pl.when(z != to)
        def _():
            att_copy(to).start()

        @pl.when(z == to)
        def _():
            att[:, att_cols(y, z)] = out_heads[to * rows : (to + 1) * rows, :]
            pass_on(z).start()

    tile_mask = causal(BRANCH)
    owners = [((owner + 1) * rows - TRUNK) // BRANCH - 1 for owner in range(nz)]

    def segment(slot, carry):
        here = pl.ds(pl.multiple_of(TRUNK + slot * BRANCH, 128), BRANCH)
        asked = jnp.concatenate(
            [stack_heads(query[here, :]), query_features(slopes, BRANCH)], axis=1
        )
        leaf, key_up, value_up = parent_pick(slot, labels, parents, key, value)
        own_feats, up_feats = segment_key_features(leaf)
        trunk_part = nt(keys_aug[...], asked) * LOG2E
        own_part = nt(jnp.concatenate([key[here, :], own_feats], axis=1), asked) * LOG2E
        own_part = jnp.where(tile_mask, own_part, NEG)
        up_part = nt(jnp.concatenate([key_up, up_feats], axis=1), asked) * LOG2E
        top = jnp.maximum(
            jnp.max(trunk_part, axis=0, keepdims=True),
            jnp.maximum(
                jnp.max(own_part, axis=0, keepdims=True), jnp.max(up_part, axis=0, keepdims=True)
            ),
        )
        trunk_part = jnp.exp2(trunk_part - top)
        own_part = jnp.exp2(own_part - top)
        up_part = jnp.exp2(up_part - top)
        total = (
            jnp.sum(trunk_part, axis=0, keepdims=True)
            + jnp.sum(own_part, axis=0, keepdims=True)
            + jnp.sum(up_part, axis=0, keepdims=True)
        )
        turned = nn(values_turned[...], trunk_part.astype(BF))
        turned = turned + nn(value[here, :].T, own_part.astype(BF))
        turned = turned + nn(value_up.T, up_part.astype(BF))
        turned = turned / total
        out_heads[here, :] = unstack_turned(turned, BRANCH).astype(BF)
        lse[pl.ds(4 + slot, 1), 0 : 2 * BRANCH] = top + jnp.log2(total)
        for owner in range(nz):
            if owners[owner] >= 0 and owner * rows >= TRUNK:

                @pl.when(slot == owners[owner])
                def _():
                    send_out(owner)

        return carry

    lax.fori_loop(0, SLOTS, segment, 0)

    wave_rows = TRUNK // 4
    wave_mask = causal(wave_rows)
    sent = 0
    for tile in range(4):
        lo, hi = tile * wave_rows, (tile + 1) * wave_rows
        asked = jnp.concatenate(
            [stack_heads(query[lo:hi, :]), query_features(slopes, wave_rows)], axis=1
        )
        edge = jnp.where(wave_mask, nt(keys_aug[lo:hi, :], asked) * LOG2E, NEG)
        top = jnp.max(edge, axis=0, keepdims=True)
        if tile:
            body = nt(keys_aug[0:lo, :], asked) * LOG2E
            top = jnp.maximum(top, jnp.max(body, axis=0, keepdims=True))
            body = jnp.exp2(body - top)
        edge = jnp.exp2(edge - top)
        total = jnp.sum(edge, axis=0, keepdims=True)
        turned = nn(values_turned[:, lo:hi], edge.astype(BF))
        if tile:
            total = total + jnp.sum(body, axis=0, keepdims=True)
            turned = turned + nn(values_turned[:, 0:lo], body.astype(BF))
        turned = turned / total
        out_heads[lo:hi, :] = unstack_turned(turned, wave_rows).astype(BF)
        lse[tile : tile + 1, :] = top + jnp.log2(total)
        while sent < nz and sent * rows < TRUNK and (sent + 1) * rows <= (hi if hi < TRUNK else TREE):
            send_out(sent)
            sent += 1

    for d in SPREAD_AT[1] + SPREAD_AT[2]:
        weights.z_done(d)
    plane_arrival().wait_recv()
    core_copy().start()
    for owner in range(nz):

        @pl.when(z != owner)
        def _():
            rcopy(
                out_heads.at[0:rows, :],
                att.at[:, att_cols(y, owner)],
                a_send.at[owner],
                a_recv.at[owner],
                {"ctx": owner},
            ).wait_recv()
            pass_on(owner).start()

    for d in (0,) + SPREAD_AT[0] + SPREAD_AT[1] + SPREAD_AT[2]:
        weights.x_done(d)
    for owner in range(nz):
        ref = att.at[:, att_cols(1 - y, owner)]
        rcopy(ref, ref, b_send.at[owner], b_recv.at[owner], {"tp": 1 - y}).wait_recv()
    core_arrival().wait_recv()
    weights.all_here()
    plane_copy().wait_send()
    core_copy().wait_send()
    for owner in range(nz):
        pass_on(owner).wait_send()

    for owner in range(nz):

        @pl.when(z != owner)
        def _():
            att_copy(owner).wait_send()

    weights.finish()
    outer.finish()
    for d in range(1, nz):
        info_copy(d).wait_send()
        wz_copy(d).wait_send()
    for d in range(1, ns):
        ws_copy(d).wait_send()

    def drain(k, carry):
        for part in range(2):
            for direction in range(2):
                _, here, onward = place(direction, k)

                @pl.when(onward & (k < nz - 1))
                def _():
                    z_copy(direction, k, part).wait_send()

                @pl.when(here & (k > 0))
                def _():
                    y_copy(direction, k, part).wait_send()

        return carry

    lax.fori_loop(0, nz, drain, 0)


def run_tree(dims, tok, w_up, w_out, w_down, wq3, info, bias_qv, slopes, gain, shift):
    ns, nz, rows = dims
    width = tok.shape[1]
    depth = wq3.shape[1]
    total = w_up.shape[1] + 2 * w_out.shape[1] + w_down.shape[1]
    return pl.pallas_call(
        partial(tree_kernel, dims),
        name="tree_forward",
        out_shape=(
            shape((width, total), BF),
            shape((depth, nz * 3 * PAIR), BF),
            shape((width, TREE), BF),
            shape((TREE, PAIR), BF),
            shape((TREE, PAIR), BF),
            shape((TREE, PAIR), BF),
            shape((TREE, PAIR), BF),
            shape((16, 512), F32),
            shape((nz, 16, 128), F32),
            shape((rows, 2 * nz * PAIR), BF),
        ),
        in_specs=[pl.BlockSpec(memory_space=pl.ANY)] * 4 + [vmem()] * 6,
        out_specs=[vmem()] * 10,
        scratch_shapes=[
            pltpu.VMEM((TREE, width), BF),
            pltpu.VMEM((width, 3 * PAIR), BF),
            pltpu.VMEM((TRUNK, 2 * PAIR), BF),
            pltpu.VMEM((PAIR, TRUNK), BF),
            pltpu.VMEM((16, 128), F32),
            pltpu.VMEM((16, 128), F32),
            dma(nz - 1),
            dma(nz - 1),
            dma(nz - 1),
            dma(nz - 1),
            dma(ns - 1),
            dma(ns - 1),
            dma(2, nz, 2),
            dma(2, nz, 2),
            dma(2, nz, 2),
            dma(2, nz, 2),
            dma(nz),
            dma(nz),
            dma(4),
            dma(nz),
            dma(nz),
            dma(2),
            dma(2),
            *spread_sems(nz),
            *spread_sems(nz),
        ],
        compiler_params=pltpu.CompilerParams(
            collective_id=0, has_side_effects=True, vmem_limit_bytes=48 << 20
        ),
        cost_estimate=pl.CostEstimate(flops=40_000_000_000, bytes_accessed=20_000_000, transcendentals=0),
    )(tok, w_up, w_out, w_down, wq3, info, bias_qv, slopes, gain, shift)


BLOCK = 512
CURVE = 0.044715
ROOT = 0.7978845608028654


def feed_kernel(
    dims,
    tok,
    cot,
    att,
    wa,
    wq,
    b_out,
    b_up,
    gain,
    shift,
    wqkv,
    near,
    far,
    ga_all,
    down_part,
    mid,
    gmid,
    sums,
    gsum,
    core_in,
    act,
    hidden,
    gup,
    gbranch,
    g_send,
    g_recv,
    ga_send,
    bup_acc,
    gs_sem,
    gr_sem,
    as_sem,
    ar_sem,
    cs_sem,
    cr_sem,
    *spread,
):
    ns, nz, rows = dims
    s, z, y = lax.axis_index("shard"), lax.axis_index("ctx"), lax.axis_index("tp")
    chunk = rows // ROWS_WAVE
    width = tok.shape[1]
    units = b_up.shape[1]
    inner = att.shape[1] // 2
    wd = wa.at[:, units : 2 * units]
    wo = wa.at[:, 2 * units :]
    own_heads = pl.ds(pl.multiple_of(y * inner, 128), inner)
    depth = wq.shape[0]
    weights = Spread(wqkv, dims, depth, slice(None), spread)
    greet(
        [{"tp": 1 - y}]
        + [{"ctx": lax.rem(z + d, nz)} for d in range(1, nz)]
        + [{"shard": weights.flip(bits)} for bits in (1, 2)]
    )
    other = {"tp": 1 - y}
    wqkv[pl.ds(pl.multiple_of((s * nz + z) * depth, depth), depth), :] = wq[...]

    def at(i):
        return pl.ds(pl.multiple_of(i * chunk, 32), chunk)

    def g_copy(i):
        return rcopy(g_send.at[at(i), :], g_recv.at[at(i), :], gs_sem.at[i], gr_sem.at[i], other)

    def a_copy(i, d):
        to = lax.rem(z + d, nz)
        return rcopy(
            ga_send.at[at(i), pl.ds(pl.multiple_of(to * PAIR, 128), PAIR)],
            ga_all.at[pl.ds(pl.multiple_of(z * rows + i * chunk, 32), chunk), :],
            as_sem.at[d - 1, i],
            ar_sem.at[d - 1, i],
            {"ctx": to},
        )

    span = nz * depth
    parts = ((0, 2 * units), (2 * units, 2 * units + inner))

    def group(bits):
        return pl.ds(pl.multiple_of(weights.flip(bits) * span, 128), span)

    def c_copy(part, index):
        lo, hi = parts[part]
        return rcopy(
            gsum.at[group((1, 3)[index]), lo:hi],
            core_in.at[index, :, lo:hi],
            cs_sem.at[part, index],
            cr_sem.at[part, index],
            {"shard": weights.flip(1)},
        )

    sums[...] = jnp.zeros(sums.shape, F32)
    bup_acc[...] = jnp.zeros(bup_acc.shape, F32)
    weights.own()
    for d in range(1, nz):
        weights.z_start(d)

    def stage_b(i, carry):
        here = at(i)
        branch = nt(att[here, :], wo[...]) + b_out[...]
        middle = tok[here, :].astype(F32) + branch
        mid[here, :] = middle
        act[here, :] = norm_rows(middle, gain[1:2, :], shift[1:2, :])[0].astype(BF)

        def columns(c, inner_carry):
            cols = pl.ds(pl.multiple_of(c * BLOCK, 128), BLOCK)
            upper = nn(act[here, :], wa[:, cols]) + b_up[:, cols]
            slope = nn(cot[here, :], wd[:, cols])
            square = upper * upper
            turn = jnp.tanh(ROOT * (upper + CURVE * (square * upper)))
            hidden[here, cols] = (0.5 * upper * (1.0 + turn)).astype(BF)
            steep = 0.5 * (1.0 + turn) + (0.5 * ROOT) * upper * (1.0 - turn * turn) * (
                1.0 + (3.0 * CURVE) * square
            )
            low = (slope * steep).astype(BF)
            gup[here, cols] = low
            bup_acc[:, cols] += jnp.sum(low.astype(F32), axis=0, keepdims=True)
            return inner_carry

        lax.fori_loop(0, units // BLOCK, columns, 0)
        g_send[here, :] = nt(gup[here, :], wa[:, 0:units]).astype(BF)
        g_copy(i).start()
        return carry

    lax.fori_loop(0, ROWS_WAVE, stage_b, 0)
    for d in range(1, nz):
        weights.z_done(d)

    def weight_one(d, carry):
        cols = pl.ds(pl.multiple_of(d * 128, 128), 128)
        gsum[cols, 0:units] = nn(act[:, cols].T, gup[...]).astype(BF)
        gsum[cols, units : 2 * units] = nn(cot[:, cols].T, hidden[...]).astype(BF)
        return carry

    lax.fori_loop(0, width // 128, weight_one, 0)
    for index in range(2):
        c_copy(0, index).start()
    for d in range(nz):
        weights.x_done(d)

    def stage_c(i, carry):
        g_copy(i).wait_recv()
        here = at(i)
        grad = g_send[here, :].astype(F32) + g_recv[here, :].astype(F32)
        _, normed, inverse = norm_rows(mid[here, :], gain[1:2, :], shift[1:2, :])
        given = cot[here, :].astype(F32)
        grad_middle = given + norm_rows_back(grad, normed, inverse, gain[1:2, :])
        gmid[here, :] = grad_middle
        low = grad_middle.astype(BF)
        gbranch[here, :] = low
        sums[2:3, :] += jnp.sum(low.astype(F32), axis=0, keepdims=True)
        sums[3:4, :] += jnp.sum(given, axis=0, keepdims=True)
        sums[4:5, :] += jnp.sum(grad * normed, axis=0, keepdims=True)
        sums[5:6, :] += jnp.sum(grad, axis=0, keepdims=True)
        ga_send[here, :] = nn(low, wo[:, own_heads]).astype(BF)
        for d in range(1, nz):
            a_copy(i, d).start()
        ga_all[pl.ds(pl.multiple_of(z * rows + i * chunk, 32), chunk), :] = ga_send[
            here, pl.ds(pl.multiple_of(z * PAIR, 128), PAIR)
        ]
        return carry

    lax.fori_loop(0, ROWS_WAVE, stage_c, 0)

    def weight_two(d, carry):
        cols = pl.ds(pl.multiple_of(d * 128, 128), 128)
        gsum[cols, 2 * units : 2 * units + inner] = nn(gbranch[:, cols].T, att[:, own_heads]).astype(BF)
        return carry

    lax.fori_loop(0, width // 128, weight_two, 0)
    for index in range(2):
        c_copy(1, index).start()

    def down(i, carry):
        down_part[at(i), :] = nt(hidden[at(i), :], wd[...]).astype(BF)
        return carry

    lax.fori_loop(0, ROWS_WAVE, down, 0)
    for part in range(units // width):
        sums[part : part + 1, :] = bup_acc[:, part * width : (part + 1) * width]

    def join(part):
        lo, hi = parts[part]
        for index in range(2):
            c_copy(part, index).wait_recv()

        def one(r, carry):
            here = pl.ds(pl.multiple_of(r * 32, 32), 32)
            for index, target in ((0, near), (1, far)):
                mine = pl.ds(pl.multiple_of(weights.flip((0, 2)[index]) * span + r * 32, 32), 32)
                target[here, lo:hi] = (
                    gsum[mine, lo:hi].astype(F32) + core_in[index, here, lo:hi].astype(F32)
                ).astype(BF)
            return carry

        lax.fori_loop(0, span // 32, one, 0)

    join(0)
    join(1)
    weights.all_here()
    weights.finish()
    for part in range(2):
        for index in range(2):
            c_copy(part, index).wait_send()

    def finish(i, carry):
        g_copy(i).wait_send()
        for d in range(1, nz):
            a_copy(i, d).wait_send()
            a_copy(i, d).wait_recv()
        return carry

    lax.fori_loop(0, ROWS_WAVE, finish, 0)


def run_feed(dims, tok, cot, att, wa, wq, b_out, b_up, gain, shift):
    ns, nz, rows = dims
    width, units, inner = tok.shape[1], b_up.shape[1], att.shape[1] // 2
    span = nz * wq.shape[0]
    total = 2 * units + inner
    return pl.pallas_call(
        partial(feed_kernel, dims),
        name="feed_both",
        out_shape=(
            shape((width, wq.shape[1]), BF),
            shape((span, total), BF),
            shape((span, total), BF),
            shape((TREE, PAIR), BF),
            shape((rows, width), BF),
            shape((rows, width), F32),
            shape((rows, width), F32),
            shape((8, width), F32),
        ),
        in_specs=[vmem()] * 9,
        out_specs=[vmem()] * 8,
        scratch_shapes=[
            pltpu.VMEM((width, total), BF),
            pltpu.VMEM((2, span, total), BF),
            pltpu.VMEM((rows, width), BF),
            pltpu.VMEM((rows, units), BF),
            pltpu.VMEM((rows, units), BF),
            pltpu.VMEM((rows, width), BF),
            pltpu.VMEM((rows, width), BF),
            pltpu.VMEM((rows, width), BF),
            pltpu.VMEM((rows, inner), BF),
            pltpu.VMEM((1, units), F32),
            dma(ROWS_WAVE),
            dma(ROWS_WAVE),
            dma(nz - 1, ROWS_WAVE),
            dma(nz - 1, ROWS_WAVE),
            dma(2, 2),
            dma(2, 2),
            *spread_sems(nz),
        ],
        compiler_params=pltpu.CompilerParams(
            collective_id=1, has_side_effects=True, vmem_limit_bytes=62 << 20
        ),
        cost_estimate=pl.CostEstimate(flops=40_000_000_000, bytes_accessed=20_000_000, transcendentals=0),
    )(tok, cot, att, wa, wq, b_out, b_up, gain, shift)


class Halve:
    def __init__(self, near, far, cols, dims, depth, bufs, sems):
        self.near, self.far, self.cols, self.depth = near, far, cols, depth
        self.nz = dims[1]
        self.s, self.z = lax.axis_index("shard"), lax.axis_index("ctx")
        self.x_in, self.a_in, self.b_out, self.b_in = bufs
        self.xs, self.xr, self.as_, self.ar, self.bs, self.br = sems

    def place(self, bits):
        low, high = lax.rem(self.z, 2), lax.div(self.z, 2)
        low = 1 - low if bits & 1 else low
        high = 1 - high if bits & 2 else high
        return 2 * high + low

    def block(self, bits):
        return pl.ds(pl.multiple_of(self.place(bits) * self.depth, self.depth), self.depth)

    def x_copy(self):
        low, high = lax.rem(self.s, 2), lax.div(self.s, 2)
        return rcopy(
            self.far.at[:, self.cols],
            self.x_in.at[:, self.cols],
            self.xs,
            self.xr,
            {"shard": 2 * (1 - high) + low},
        )

    def a_copy(self, index):
        return rcopy(
            self.near.at[self.block((1, 3)[index]), self.cols],
            self.a_in.at[index, :, self.cols],
            self.as_.at[index],
            self.ar.at[index],
            {"ctx": self.place(1)},
        )

    def b_copy(self):
        return rcopy(
            self.b_out.at[:, self.cols], self.b_in.at[:, self.cols], self.bs, self.br, {"ctx": self.place(2)}
        )

    def step_x(self):
        self.x_copy().wait_recv()

        def one(r, carry):
            here = pl.ds(pl.multiple_of(r * 32, 32), 32)
            self.near[here, self.cols] = (
                self.near[here, self.cols].astype(F32) + self.x_in[here, self.cols].astype(F32)
            ).astype(BF)
            return carry

        lax.fori_loop(0, self.near.shape[0] // 32, one, 0)
        self.a_copy(0).start()
        self.a_copy(1).start()

    def step_a(self):
        self.a_copy(0).wait_recv()
        self.a_copy(1).wait_recv()
        self.b_out[:, self.cols] = (
            self.near[self.block(2), self.cols].astype(F32) + self.a_in[1, :, self.cols].astype(F32)
        ).astype(BF)
        self.b_copy().start()

    def step_b(self):
        self.b_copy().wait_recv()
        return (
            self.near[self.block(0), self.cols].astype(F32)
            + self.a_in[0, :, self.cols].astype(F32)
            + self.b_in[:, self.cols].astype(F32)
        )

    def finish(self):
        self.x_copy().wait_send()
        self.a_copy(0).wait_send()
        self.a_copy(1).wait_send()
        self.b_copy().wait_send()


PIECES = 4


def back_kernel(
    dims,
    query,
    key,
    value,
    out_heads,
    lse,
    info_all,
    ga_all,
    act_turned,
    wqkv,
    near_in,
    far,
    down_part,
    mid,
    b_down,
    gmid,
    tok,
    slopes,
    gain,
    shift,
    early,
    result,
    gtok,
    gup,
    gdown,
    gout,
    gwqkv,
    early_sum,
    late_sum,
    near,
    x_in,
    a_in,
    b_out,
    b_in,
    q_near,
    q_far,
    q_core,
    qx_in,
    q_all,
    dqkv,
    dk_trunk,
    dv_trunk,
    dk_seg,
    dv_seg,
    dk_up,
    dv_up,
    keys_aug,
    keys_turned,
    labels,
    parents,
    dq_all,
    n_send,
    n_recv,
    down_recv,
    wg_send,
    early_mine,
    early_recv,
    late,
    late_recv,
    d_sem,
    e_send,
    e_recv,
    f_send,
    f_recv,
    l_send,
    l_recv,
    p_send,
    p_recv,
    ns_sem,
    nr_sem,
    xs_sem,
    xr_sem,
    as_sem,
    ar_sem,
    bs_sem,
    br_sem,
    qc_send,
    qc_recv,
    qx_sem,
    qz_send,
    qz_recv,
    n_local,
):
    ns, nz, rows = dims
    s, z, y = lax.axis_index("shard"), lax.axis_index("ctx"), lax.axis_index("tp")
    count = ns * nz
    me = s * nz + z
    chunk = rows // ROWS_WAVE
    width = tok.shape[1]
    depth = width // count
    span = nz * depth
    wide = 3 * PAIR
    other = {"tp": 1 - y}
    total_cols = near.shape[1]
    step_cols = total_cols // PIECES
    units = gup.shape[1]

    load = pltpu.make_async_copy(near_in, near, n_local)
    load.start()

    def peer(d):
        index = lax.rem(me + d, count)
        return index, {"shard": lax.div(index, nz), "ctx": lax.rem(index, nz)}

    greet([other] + [peer(d)[1] for d in range(1, count)])

    halves = [
        Halve(
            near,
            far,
            slice(i * step_cols, (i + 1) * step_cols),
            dims,
            depth,
            (x_in, a_in, b_out, b_in),
            (xs_sem.at[i], xr_sem.at[i], as_sem.at[i], ar_sem.at[i], bs_sem.at[i], br_sem.at[i]),
        )
        for i in range(PIECES)
    ]
    def shard_flip(bits):
        low, high = lax.rem(s, 2), lax.div(s, 2)
        low = 1 - low if bits & 1 else low
        high = 1 - high if bits & 2 else high
        return 2 * high + low

    def q_copy(index):
        return rcopy(
            wg_send.at[pl.ds(pl.multiple_of(shard_flip((1, 3)[index]) * span, 128), span), :],
            q_core.at[index],
            qc_send.at[index],
            qc_recv.at[index],
            {"shard": shard_flip(1)},
        )

    def qx_copy():
        return rcopy(q_far, qx_in, qx_sem.at[0], qx_sem.at[1], {"shard": shard_flip(2)})

    def qz_copy(d):
        to = lax.rem(z + d, nz)
        return rcopy(
            q_near.at[pl.ds(pl.multiple_of(to * depth, depth), depth), :],
            q_all.at[z],
            qz_send.at[d - 1],
            qz_recv.at[d - 1],
            {"ctx": to},
        )

    def q_spread():
        qx_copy().wait_recv()
        q_near[...] = (q_near[...].astype(F32) + qx_in[...].astype(F32)).astype(BF)
        for d in range(1, nz):
            qz_copy(d).start()
        q_all[z] = q_near[pl.ds(pl.multiple_of(z * depth, depth), depth), :]

    def down_copy():
        return rcopy(down_part, down_recv, d_sem.at[0], d_sem.at[1], other)

    owners = width // 128

    def owner_cols(index):
        return pl.ds(pl.multiple_of(index * 128, 128), 128)

    def early_copy(d):
        index, device = peer(d)
        return index, rcopy(
            early_mine.at[:, owner_cols(lax.rem(index, owners))],
            early_recv.at[me],
            e_send.at[d - 1],
            e_recv.at[d - 1],
            device,
        )

    def spread_copy(d):
        cols = owner_cols(lax.rem(me, owners))
        return rcopy(
            early_sum.at[:, cols], early_sum.at[:, cols], f_send.at[d - 1], f_recv.at[d - 1], peer(d)[1]
        )

    def spread_arrival(d):
        index = lax.rem(me + count - d, count)
        cols = owner_cols(lax.rem(index, owners))
        return index, rcopy(
            early_sum.at[:, cols], early_sum.at[:, cols], f_send.at[d - 1], f_recv.at[d - 1], other
        )

    def late_copy(d):
        return rcopy(late, late_recv.at[me], l_send.at[d - 1], l_recv.at[d - 1], peer(d)[1])

    def over_peers(act):
        def one(d, carry):
            act(d)
            return carry

        lax.fori_loop(1, count, one, 0)

    for half in halves:
        half.x_copy().start()
    down_copy().start()

    fill_labels(info_all, rows // BRANCH, labels, parents)
    fill_trunk_keys(key, keys_aug)
    keys_turned[...] = key[0:TRUNK, :].T
    dk_trunk[...] = jnp.zeros(dk_trunk.shape, F32)
    dv_trunk[...] = jnp.zeros(dv_trunk.shape, F32)
    tile_mask = causal(BRANCH)

    def row_products(here, count_rows):
        turned = (ga_all[here, :].astype(F32) * out_heads[here, :].astype(F32)).T
        return jnp.concatenate(
            [
                jnp.sum(turned[:HD, :], axis=0, keepdims=True),
                jnp.sum(turned[HD:, :], axis=0, keepdims=True),
            ],
            axis=1,
        )

    def part_back(key_aug, value_rows, asked, given, level, drow, mask):
        logits = nt(key_aug, asked) * LOG2E - level
        if mask is not None:
            logits = jnp.where(mask, logits, NEG)
        probs = jnp.exp2(logits)
        grads = (probs * (nt(value_rows, given) - drow)).astype(BF)
        return probs.astype(BF), grads

    def segment(slot, carry):
        here = pl.ds(pl.multiple_of(TRUNK + slot * BRANCH, 128), BRANCH)
        seg = pl.ds(pl.multiple_of(slot * BRANCH, 128), BRANCH)
        stacked = stack_heads(query[here, :])
        asked = jnp.concatenate([stacked, query_features(slopes, BRANCH)], axis=1)
        given = stack_heads(ga_all[here, :])
        leaf, key_up, value_up = parent_pick(slot, labels, parents, key, value)
        own_feats, up_feats = segment_key_features(leaf)
        level = lse[pl.ds(4 + slot, 1), 0 : 2 * BRANCH]
        drow = row_products(here, BRANCH)
        probs, grads = part_back(keys_aug[...], value[0:TRUNK, :], asked, given, level, drow, None)
        dv_trunk[...] += nn(probs, given)
        dk_trunk[...] += nn(grads, stacked)
        turned = nn(keys_turned[...], grads)
        key_own = key[here, :]
        probs, grads = part_back(
            jnp.concatenate([key_own, own_feats], axis=1), value[here, :], asked, given, level, drow, tile_mask
        )
        dv_seg[seg, :] = nn(probs, given)
        dk_seg[seg, :] = nn(grads, stacked)
        turned = turned + nn(key_own.T, grads)
        probs, grads = part_back(
            jnp.concatenate([key_up, up_feats], axis=1), value_up, asked, given, level, drow, None
        )
        dv_up[seg, :] = nn(probs, given)
        dk_up[seg, :] = nn(grads, stacked)
        turned = turned + nn(key_up.T, grads)
        dqkv[here, 0:PAIR] = (unstack_turned(turned, BRANCH) * HD ** (-0.5)).astype(BF)
        return carry

    lax.fori_loop(0, SLOTS, segment, 0)

    def gather_up(slot, carry):
        here = pl.ds(pl.multiple_of(TRUNK + slot * BRANCH, 128), BRANCH)
        seg = pl.ds(pl.multiple_of(slot * BRANCH, 128), BRANCH)
        mine = labels[pl.ds(slot, 1), :]
        dk, dv = dk_seg[seg, :], dv_seg[seg, :]
        for below in range(SLOTS):
            same = (parents[below : below + 1, :] == mine).astype(F32)
            at = below * BRANCH
            dk = dk + same * dk_up[at : at + BRANCH, :]
            dv = dv + same * dv_up[at : at + BRANCH, :]
        dqkv[here, PAIR : 2 * PAIR] = dk.astype(BF)
        dqkv[here, 2 * PAIR :] = dv.astype(BF)
        return carry

    lax.fori_loop(0, SLOTS, gather_up, 0)

    def piece_copy(to, i):
        return rcopy(
            dqkv.at[to * rows + i * chunk : to * rows + (i + 1) * chunk, :],
            dq_all.at[i * chunk : (i + 1) * chunk, pl.ds(pl.multiple_of(z * wide, 128), wide)],
            p_send.at[to, i],
            p_recv.at[z, i],
            {"ctx": to},
        )

    def send_pieces(targets):
        for i in range(ROWS_WAVE):
            for to in targets:

                @pl.when(z != to)
                def _():
                    piece_copy(to, i).start()

        for to in targets:

            @pl.when(z == to)
            def _():
                dq_all[:, pl.ds(pl.multiple_of(z * wide, 128), wide)] = dqkv[to * rows : (to + 1) * rows, :]

    send_pieces([to for to in range(nz) if to * rows >= TRUNK])

    wave_rows = TRUNK // 4
    wave_mask = causal(wave_rows)
    for tile in range(4):
        lo, hi = tile * wave_rows, (tile + 1) * wave_rows
        stacked = stack_heads(query[lo:hi, :])
        asked = jnp.concatenate([stacked, query_features(slopes, wave_rows)], axis=1)
        given = stack_heads(ga_all[lo:hi, :])
        level = lse[tile : tile + 1, :]
        drow = row_products(pl.ds(lo, wave_rows), wave_rows)
        probs, grads = part_back(
            keys_aug[lo:hi, :], value[lo:hi, :], asked, given, level, drow, wave_mask
        )
        dv_trunk[lo:hi, :] += nn(probs, given)
        dk_trunk[lo:hi, :] += nn(grads, stacked)
        turned = nn(keys_turned[:, lo:hi], grads)
        if tile:
            probs, grads = part_back(
                keys_aug[0:lo, :], value[0:lo, :], asked, given, level, drow, None
            )
            dv_trunk[0:lo, :] += nn(probs, given)
            dk_trunk[0:lo, :] += nn(grads, stacked)
            turned = turned + nn(keys_turned[:, 0:lo], grads)
        dqkv[lo:hi, 0:PAIR] = (unstack_turned(turned, wave_rows) * HD ** (-0.5)).astype(BF)
    dqkv[0:TRUNK, PAIR : 2 * PAIR] = dk_trunk[...].astype(BF)
    dqkv[0:TRUNK, 2 * PAIR :] = dv_trunk[...].astype(BF)
    send_pieces([to for to in range(nz) if to * rows < TRUNK])

    def weight(block, carry):
        here = pl.ds(pl.multiple_of(block * 128, 128), 128)
        wg_send[here, :] = nn(act_turned[here, :], dqkv[...]).astype(BF)
        return carry

    lax.fori_loop(0, width // 128, weight, 0)
    q_copy(0).start()
    q_copy(1).start()

    early_mine[...] = early[...]
    early_mine[6:7, pl.ds(pl.multiple_of(z * PAIR, 128), PAIR)] = jnp.sum(
        dqkv[:, 0:PAIR].astype(F32), axis=0, keepdims=True
    )
    early_mine[6:7, pl.ds(pl.multiple_of((nz + z) * PAIR, 128), PAIR)] = jnp.sum(
        dqkv[:, 2 * PAIR :].astype(F32), axis=0, keepdims=True
    )

    def early_send(d):
        index, copy = early_copy(d)

        @pl.when(index < owners)
        def _():
            copy.start()

    over_peers(early_send)
    early_recv[me] = early_mine[:, owner_cols(lax.rem(me, owners))]
    load.wait()

    def at(i):
        return pl.ds(pl.multiple_of(i * chunk, 32), chunk)

    def n_copy(i):
        return rcopy(n_send.at[at(i), :], n_recv.at[at(i), :], ns_sem.at[i], nr_sem.at[i], other)

    def core_join():
        for index in range(2):
            q_copy(index).wait_recv()
            mine = pl.ds(pl.multiple_of(shard_flip((0, 2)[index]) * span, 128), span)
            (q_near, q_far)[index][...] = (wg_send[mine, :].astype(F32) + q_core[index].astype(F32)).astype(BF)
        qx_copy().start()

    def first(i):
        for owner in range(nz):

            @pl.when(z != owner)
            def _():
                rcopy(
                    dqkv.at[0:chunk, :],
                    dq_all.at[i * chunk : (i + 1) * chunk, owner * wide : (owner + 1) * wide],
                    p_send.at[owner, i],
                    p_recv.at[owner, i],
                    {"ctx": owner},
                ).wait_recv()

        n_send[at(i), :] = nt(dq_all[at(i), :], wqkv[...]).astype(BF)
        n_copy(i).start()

    def second(i, carry):
        n_copy(i).wait_recv()
        here = at(i)
        grad = n_send[here, :].astype(F32) + n_recv[here, :].astype(F32)
        _, normed, inverse = norm_rows(tok[here, :].astype(F32), gain[0:1, :], shift[0:1, :])
        gtok[here, :] = gmid[here, :] + norm_rows_back(grad, normed, inverse, gain[0:1, :])
        late[0:1, :] += jnp.sum(grad * normed, axis=0, keepdims=True)
        late[1:2, :] += jnp.sum(grad, axis=0, keepdims=True)
        return carry

    def output(i, carry):
        here = at(i)
        result[here, :] = (
            mid[here, :] + b_down[...] + (down_part[here, :].astype(F32) + down_recv[here, :].astype(F32))
        ).astype(BF)
        return carry

    late[...] = jnp.zeros(late.shape, F32)
    halves[0].step_x()
    core_join()
    first(0)
    halves[1].step_x()
    first(1)
    q_spread()

    @pl.when(me < owners)
    def _():
        over_peers(lambda d: early_copy(d)[1].wait_recv())
        total = early_recv[0]
        for index in range(1, count):
            total = total + early_recv[index]
        early_sum[:, owner_cols(lax.rem(me, owners))] = total
        over_peers(lambda d: spread_copy(d).start())

    halves[2].step_x()
    first(2)
    halves[0].step_a()
    halves[3].step_x()
    first(3)
    down_copy().wait_recv()
    lax.fori_loop(0, ROWS_WAVE, output, 0)
    halves[1].step_a()
    lax.fori_loop(0, ROWS_WAVE, second, 0)
    over_peers(lambda d: late_copy(d).start())
    late_recv[me] = late[...]
    halves[2].step_a()
    halves[3].step_a()

    for d in range(1, nz):
        qz_copy(d).wait_recv()
    for owner in range(nz):
        for part in range(3):
            gwqkv[part, :, owner * PAIR : (owner + 1) * PAIR] = q_all[
                owner, :, part * PAIR : (part + 1) * PAIR
            ].astype(F32)
    bounds = (0, units, 2 * units, total_cols)
    for i, half in enumerate(halves):
        block = half.step_b()
        lo, hi = i * step_cols, (i + 1) * step_cols
        for target, start_at, end_at in (
            (gup, bounds[0], bounds[1]),
            (gdown, bounds[1], bounds[2]),
            (gout, bounds[2], bounds[3]),
        ):
            a, b = max(lo, start_at), min(hi, end_at)
            if a < b:
                target[:, a - start_at : b - start_at] = block[:, a - lo : b - lo]

    def early_wait(d):
        index, copy = spread_arrival(d)

        @pl.when(index < owners)
        def _():
            copy.wait_recv()

    over_peers(early_wait)
    over_peers(lambda d: late_copy(d).wait_recv())
    total = late_recv[0]
    for index in range(1, count):
        total = total + late_recv[index]
    late_sum[...] = total

    down_copy().wait_send()
    for half in halves:
        half.finish()
    qx_copy().wait_send()
    for d in range(1, nz):
        qz_copy(d).wait_send()
    q_copy(0).wait_send()
    q_copy(1).wait_send()

    def early_drain(d):
        index, copy = early_copy(d)

        @pl.when(index < owners)
        def _():
            copy.wait_send()

    over_peers(early_drain)

    @pl.when(me < owners)
    def _():
        over_peers(lambda d: spread_copy(d).wait_send())

    over_peers(lambda d: late_copy(d).wait_send())

    def finish(i, carry):
        n_copy(i).wait_send()
        return carry

    lax.fori_loop(0, ROWS_WAVE, finish, 0)
    for owner in range(nz):

        @pl.when(z != owner)
        def _():
            for i in range(ROWS_WAVE):
                piece_copy(owner, i).wait_send()


def run_back(dims, units, *inputs):
    ns, nz, rows = dims
    width = inputs[15].shape[1]
    span, total = inputs[9].shape
    count = ns * nz
    depth = width // count
    wide = 3 * PAIR
    anywhere = pl.BlockSpec(memory_space=pl.ANY)
    return pl.pallas_call(
        partial(back_kernel, dims),
        name="tree_backward",
        out_shape=(
            shape((rows, width), BF),
            shape((rows, width), F32),
            shape((depth, units), F32),
            shape((depth, units), F32),
            shape((depth, total - 2 * units), F32),
            shape((3, depth, nz * PAIR), F32),
            shape((8, width), F32),
            shape((2, width), F32),
        ),
        in_specs=[vmem()] * 9 + [anywhere] * 2 + [vmem()] * 9,
        out_specs=[vmem()] * 8,
        scratch_shapes=[
            pltpu.VMEM((span, total), BF),
            pltpu.VMEM((span, total), BF),
            pltpu.VMEM((2, depth, total), BF),
            pltpu.VMEM((depth, total), BF),
            pltpu.VMEM((depth, total), BF),
            pltpu.VMEM((span, wide), BF),
            pltpu.VMEM((span, wide), BF),
            pltpu.VMEM((2, span, wide), BF),
            pltpu.VMEM((span, wide), BF),
            pltpu.VMEM((nz, depth, wide), BF),
            pltpu.VMEM((TREE, wide), BF),
            pltpu.VMEM((TRUNK, PAIR), F32),
            pltpu.VMEM((TRUNK, PAIR), F32),
            pltpu.VMEM((TREE - TRUNK, PAIR), F32),
            pltpu.VMEM((TREE - TRUNK, PAIR), F32),
            pltpu.VMEM((TREE - TRUNK, PAIR), F32),
            pltpu.VMEM((TREE - TRUNK, PAIR), F32),
            pltpu.VMEM((TRUNK, 2 * PAIR), BF),
            pltpu.VMEM((PAIR, TRUNK), BF),
            pltpu.VMEM((16, 128), F32),
            pltpu.VMEM((16, 128), F32),
            pltpu.VMEM((rows, nz * wide), BF),
            pltpu.VMEM((rows, width), BF),
            pltpu.VMEM((rows, width), BF),
            pltpu.VMEM((rows, width), BF),
            pltpu.VMEM((width, wide), BF),
            pltpu.VMEM((8, width), F32),
            pltpu.VMEM((count, 8, 128), F32),
            pltpu.VMEM((2, width), F32),
            pltpu.VMEM((count, 2, width), F32),
            dma(2),
            dma(count - 1),
            dma(count - 1),
            dma(count - 1),
            dma(count - 1),
            dma(count - 1),
            dma(count - 1),
            dma(nz, ROWS_WAVE),
            dma(nz, ROWS_WAVE),
            dma(ROWS_WAVE),
            dma(ROWS_WAVE),
            dma(PIECES),
            dma(PIECES),
            dma(PIECES, 2),
            dma(PIECES, 2),
            dma(PIECES),
            dma(PIECES),
            dma(2),
            dma(2),
            dma(2),
            dma(nz - 1),
            dma(nz - 1),
            pltpu.SemaphoreType.DMA,
        ],
        compiler_params=pltpu.CompilerParams(
            collective_id=2, has_side_effects=True, vmem_limit_bytes=60 << 20
        ),
        cost_estimate=pl.CostEstimate(flops=40_000_000_000, bytes_accessed=20_000_000, transcendentals=0),
    )(*inputs)


def fast_device(
    tokens, cotangent, seg_ids, positions, parents, w_qkv, b_qv, w_out, b_out, w_up, b_up, w_down, b_down, ln_gain, ln_bias
):
    rows = tokens.shape[0]
    ns, nz, ntp = lax.axis_size("shard"), lax.axis_size("ctx"), lax.axis_size("tp")
    dims = (ns, nz, rows)

    labels = seg_ids.reshape(rows // BRANCH, BRANCH)[:, 0]
    match = labels[:, None] == jnp.arange(parents.shape[0], dtype=jnp.int32)[None, :]
    above = jnp.sum(jnp.where(match, parents[None, :], 0), axis=1)
    fill = 8 - rows // BRANCH
    lines = jnp.concatenate([jnp.pad(labels, (0, fill)), jnp.pad(above, (0, fill))]).astype(F32)
    info = jnp.broadcast_to(lines[:, None], (16, 128))
    per = HEADS // ntp
    index = lax.axis_index("tp") * per + lax.axis_index("ctx") * 2 + jnp.arange(2)
    slope = 2.0 ** (-8.0 * (index.astype(F32) + 1.0) / HEADS)
    one = lax.reduce_precision(slope, 8, 7)
    two = lax.reduce_precision(slope - one, 8, 7)
    three = lax.reduce_precision(slope - one - two, 8, 7)
    table = jnp.stack([one, two, three, one, two, three, jnp.ones_like(one)], axis=1)
    slopes = jnp.pad(table, ((0, 0), (0, 121)))

    wfull, wq, act_turned, query, key, value, out_heads, lse, info_all, att = run_tree(
        dims, tokens, w_up, w_out.T, w_down.T, w_qkv, info, b_qv, slopes, ln_gain, ln_bias
    )
    units, inner = b_up.shape[0], w_out.shape[0]
    wqkv, near, far, ga_all, down_part, mid, gmid, sums = run_feed(
        dims, tokens, cotangent, att, wfull, wq, b_out[None, :], b_up[None, :], ln_gain, ln_bias
    )
    result, grad_tokens, gup, gdown, gout, grad_w_qkv, early, late = run_back(
        dims, units, query, key, value, out_heads, lse, info_all, ga_all, act_turned, wqkv, near, far, down_part,
        mid, b_down[None, :], gmid, tokens, slopes, ln_gain, ln_bias, sums,
    )
    return (
        result,
        grad_tokens,
        grad_w_qkv,
        early[6].reshape(2, nz * PAIR),
        gout.T,
        early[2],
        gup,
        early[0:2].reshape(units),
        gdown.T,
        early[3],
        jnp.stack([late[0], early[4]]),
        jnp.stack([late[1], early[5]]),
    )


def norm_forward(inputs_in, gain_row, shift_row):
    centre = inputs_in - jnp.mean(inputs_in, axis=-1, keepdims=True)
    inverse = lax.rsqrt(jnp.mean(centre * centre, axis=-1, keepdims=True) + EPS)
    normed = centre * inverse
    return (normed * gain_row + shift_row, normed, inverse)


def norm_backward(grad_in, normed, inverse, gain_row):
    scaled = grad_in * gain_row
    mean_grad = jnp.mean(scaled, axis=-1, keepdims=True)
    mean_cross = jnp.mean(scaled * normed, axis=-1, keepdims=True)
    return inverse * (scaled - mean_grad - normed * mean_cross)


def ancestry(seg_vals, parents):
    first_up = jnp.take(parents, seg_vals)
    return (first_up, jnp.take(parents, first_up))


def block_scores(query_heads, key_heads, query_tags, key_tags, slopes):
    q_seg, q_first, q_second, q_pos = query_tags
    k_seg, k_pos = key_tags
    raw_scores = jnp.einsum(
        "qhd,khd->hqk", query_heads, key_heads, preferred_element_type=jnp.float32
    ) * HD ** (-0.5)
    distance = (q_pos[:, None] - k_pos[None, :]).astype(jnp.float32)
    scores = raw_scores - slopes[:, None, None] * distance[None]
    related = (
        (k_seg[None, :] == q_seg[:, None])
        | (k_seg[None, :] == q_first[:, None])
        | (k_seg[None, :] == q_second[:, None])
    )
    allowed = related & (k_pos[None, :] <= q_pos[:, None])
    return (scores, allowed[None])


def probabilities(scores, allowed, row_max, row_sum):
    shifted = jnp.where(allowed, scores - row_max[:, :, None], NEG)
    return jnp.exp(shifted) / row_sum[:, :, None]


def per_device(
    tokens,
    cotangent,
    seg_ids,
    positions,
    parents,
    w_qkv,
    b_qv,
    w_out,
    b_out,
    w_up,
    b_up,
    w_down,
    b_down,
    ln_gain,
    ln_bias,
):
    num_rows = tokens.shape[0]
    head_count = HEADS // lax.axis_size("tp")
    head_width = head_count * HD
    head_index = (lax.axis_index("tp") * head_count + jnp.arange(head_count)).astype(jnp.float32)
    slopes = 2.0 ** (-8.0 * (head_index + 1.0) / HEADS)
    scale = HD ** (-0.5)
    full_qkv, full_out = (
        lax.all_gather(w_qkv, ("shard", "ctx"), axis=1, tiled=True),
        lax.all_gather(w_out, ("shard", "ctx"), axis=1, tiled=True),
    )
    group_seg, group_pos = (
        lax.all_gather(seg_ids, "ctx", axis=0, tiled=True),
        lax.all_gather(positions, "ctx", axis=0, tiled=True),
    )
    own_first, own_second = ancestry(seg_ids, parents)
    own_tags = (seg_ids, own_first, own_second, positions)
    inputs = tokens.astype(jnp.float32)
    norm_one, normed_one, inverse_one = norm_forward(inputs, ln_gain[0], ln_bias[0])
    act_one = norm_one.astype(jnp.bfloat16)
    projected = jnp.einsum("td,cde->cte", act_one, full_qkv, preferred_element_type=jnp.float32)
    qkv_bias = jnp.stack([b_qv[0], jnp.zeros((head_width,), jnp.float32), b_qv[1]])
    qkv_low = (projected + qkv_bias[:, None, :]).astype(jnp.bfloat16)
    query_flat, key_flat, value_flat = (qkv_low[0], qkv_low[1], qkv_low[2])
    group_keys, group_values = (
        lax.all_gather(key_flat, "ctx", axis=0, tiled=True),
        lax.all_gather(value_flat, "ctx", axis=0, tiled=True),
    )
    group_rows = group_keys.shape[0]
    block_count = group_rows // KEY_BLOCK
    key_blocks = group_keys.reshape(block_count, KEY_BLOCK, head_count, HD)
    value_blocks = group_values.reshape(block_count, KEY_BLOCK, head_count, HD)
    seg_blocks = group_seg.reshape(block_count, KEY_BLOCK)
    pos_blocks = group_pos.reshape(block_count, KEY_BLOCK)
    query_heads = query_flat.reshape(num_rows, head_count, HD)

    def stats_step(carry_in, block_parts):
        row_max, row_sum = carry_in
        key_part, seg_part, pos_part = block_parts
        scores, allowed = block_scores(
            query_heads, key_part, own_tags, (seg_part, pos_part), slopes
        )
        new_max = jnp.maximum(row_max, jnp.max(jnp.where(allowed, scores, NEG), axis=-1))
        shifted = jnp.where(allowed, scores - new_max[:, :, None], NEG)
        row_sum = row_sum * jnp.exp(row_max - new_max) + jnp.sum(jnp.exp(shifted), axis=-1)
        return ((new_max, row_sum), None)

    start_stats = (
        jnp.full((head_count, num_rows), NEG, jnp.float32),
        jnp.zeros((head_count, num_rows), jnp.float32),
    )
    (row_max, row_sum), _ = lax.scan(stats_step, start_stats, (key_blocks, seg_blocks, pos_blocks))

    def output_step(out_accum, block_parts):
        key_part, value_part, seg_part, pos_part = block_parts
        scores, allowed = block_scores(
            query_heads, key_part, own_tags, (seg_part, pos_part), slopes
        )
        prob_low = probabilities(scores, allowed, row_max, row_sum).astype(jnp.bfloat16)
        return (
            out_accum
            + jnp.einsum("hqk,khd->qhd", prob_low, value_part, preferred_element_type=jnp.float32),
            None,
        )

    attended, _ = lax.scan(
        output_step,
        jnp.zeros((num_rows, head_count, HD), jnp.float32),
        (key_blocks, value_blocks, seg_blocks, pos_blocks),
    )
    attended_low = attended.reshape(num_rows, head_width).astype(jnp.bfloat16)
    branch_one = (
        lax.psum(
            jnp.dot(attended_low, full_out, preferred_element_type=jnp.float32).astype(
                jnp.bfloat16
            ),
            "tp",
        ).astype(jnp.float32)
        + b_out
    )
    middle = inputs + branch_one
    full_up, full_down = (
        lax.all_gather(w_up, ("shard", "ctx"), axis=0, tiled=True),
        lax.all_gather(w_down, ("shard", "ctx"), axis=1, tiled=True),
    )
    norm_two, normed_two, inverse_two = norm_forward(middle, ln_gain[1], ln_bias[1])
    act_two = norm_two.astype(jnp.bfloat16)
    upper_in = jnp.dot(act_two, full_up, preferred_element_type=jnp.float32) + b_up
    gelu_vals, gelu_pull = jax.vjp(partial(jax.nn.gelu, approximate=True), upper_in)
    hidden = gelu_vals.astype(jnp.bfloat16)
    branch_two = (
        lax.psum(
            jnp.dot(hidden, full_down, preferred_element_type=jnp.float32).astype(jnp.bfloat16),
            "tp",
        ).astype(jnp.float32)
        + b_down
    )
    result = (middle + branch_two).astype(jnp.bfloat16)
    grad_out = cotangent.astype(jnp.float32)
    grad_hidden = jnp.einsum("td,fd->tf", cotangent, full_down, preferred_element_type=jnp.float32)
    grad_upper = gelu_pull(grad_hidden)[0].astype(jnp.bfloat16)
    down_term = jnp.einsum("tf,td->fd", hidden, cotangent, preferred_element_type=jnp.float32)
    up_term = jnp.einsum("td,tf->df", act_two, grad_upper, preferred_element_type=jnp.float32)
    grad_w_up, grad_w_down = (
        lax.psum_scatter(up_term, ("shard", "ctx"), scatter_dimension=0, tiled=True),
        lax.psum_scatter(down_term, ("shard", "ctx"), scatter_dimension=1, tiled=True),
    )
    grad_norm_two = lax.psum(
        jnp.einsum("tf,df->td", grad_upper, full_up, preferred_element_type=jnp.float32).astype(
            jnp.bfloat16
        ),
        "tp",
    ).astype(jnp.float32)
    grad_middle = grad_out + norm_backward(grad_norm_two, normed_two, inverse_two, ln_gain[1])
    grad_branch = grad_middle.astype(jnp.bfloat16)
    out_term = jnp.einsum(
        "te,td->ed", attended_low, grad_branch, preferred_element_type=jnp.float32
    )
    grad_att = jnp.einsum(
        "td,ed->te", grad_branch, full_out, preferred_element_type=jnp.float32
    ).astype(jnp.bfloat16)
    grad_heads = grad_att.reshape(num_rows, head_count, HD)
    row_terms = jnp.einsum("qhd,qhd->hq", grad_heads.astype(jnp.float32), attended)

    def joint_step(grad_accum, block_parts):
        key_part, value_part, seg_part, pos_part = block_parts
        scores, allowed = block_scores(
            query_heads, key_part, own_tags, (seg_part, pos_part), slopes
        )
        prob_vals = probabilities(scores, allowed, row_max, row_sum)
        grad_probs = jnp.einsum(
            "qhd,khd->hqk", grad_heads, value_part, preferred_element_type=jnp.float32
        )
        grad_scores = (prob_vals * (grad_probs - row_terms[:, :, None])).astype(jnp.bfloat16)
        grad_accum = (
            grad_accum
            + jnp.einsum("hqk,khd->qhd", grad_scores, key_part, preferred_element_type=jnp.float32)
            * scale
        )
        key_part_grad = (
            jnp.einsum("hqk,qhd->khd", grad_scores, query_heads, preferred_element_type=jnp.float32)
            * scale
        )
        value_part_grad = jnp.einsum(
            "hqk,qhd->khd",
            prob_vals.astype(jnp.bfloat16),
            grad_heads,
            preferred_element_type=jnp.float32,
        )
        return (
            grad_accum,
            (
                key_part_grad.reshape(KEY_BLOCK, head_width),
                value_part_grad.reshape(KEY_BLOCK, head_width),
            ),
        )

    grad_query_sum, (key_terms, value_terms) = lax.scan(
        joint_step,
        jnp.zeros((num_rows, head_count, HD), jnp.float32),
        (key_blocks, value_blocks, seg_blocks, pos_blocks),
    )
    key_grad_sum, value_grad_sum = (
        lax.psum_scatter(
            key_terms.reshape(group_rows, head_width).astype(jnp.bfloat16),
            "ctx",
            scatter_dimension=0,
            tiled=True,
        ).astype(jnp.float32),
        lax.psum_scatter(
            value_terms.reshape(group_rows, head_width).astype(jnp.bfloat16),
            "ctx",
            scatter_dimension=0,
            tiled=True,
        ).astype(jnp.float32),
    )
    grad_query_low = grad_query_sum.reshape(num_rows, head_width).astype(jnp.bfloat16)
    grad_key_low = key_grad_sum.astype(jnp.bfloat16)
    grad_value_low = value_grad_sum.astype(jnp.bfloat16)
    grad_qkv = jnp.stack([grad_query_low, grad_key_low, grad_value_low])
    grad_norm_one = lax.psum(
        jnp.einsum("cte,cde->td", grad_qkv, full_qkv, preferred_element_type=jnp.float32).astype(
            jnp.bfloat16
        ),
        "tp",
    ).astype(jnp.float32)
    grad_tokens = grad_middle + norm_backward(grad_norm_one, normed_one, inverse_one, ln_gain[0])
    qkv_term = jnp.einsum("td,cte->cde", act_one, grad_qkv, preferred_element_type=jnp.float32)
    grad_w_qkv, grad_w_out = (
        lax.psum_scatter(qkv_term, ("shard", "ctx"), scatter_dimension=1, tiled=True),
        lax.psum_scatter(out_term, ("shard", "ctx"), scatter_dimension=1, tiled=True),
    )
    bias_qv_part = jnp.stack(
        [
            jnp.sum(grad_query_low.astype(jnp.float32), axis=0),
            jnp.sum(grad_value_low.astype(jnp.float32), axis=0),
        ]
    )
    out_bias_part = jnp.sum(grad_branch.astype(jnp.float32), axis=0)
    up_bias_part = jnp.sum(grad_upper.astype(jnp.float32), axis=0)
    down_bias_part = jnp.sum(grad_out, axis=0)
    gain_part = jnp.stack(
        [jnp.sum(grad_norm_one * normed_one, axis=0), jnp.sum(grad_norm_two * normed_two, axis=0)]
    )
    shift_part = jnp.stack([jnp.sum(grad_norm_one, axis=0), jnp.sum(grad_norm_two, axis=0)])
    grad_b_qv, grad_b_out, grad_b_up, grad_b_down, grad_gain, grad_shift = lax.psum(
        (bias_qv_part, out_bias_part, up_bias_part, down_bias_part, gain_part, shift_part),
        ("shard", "ctx"),
    )
    return (
        result,
        grad_tokens,
        grad_w_qkv,
        grad_b_qv,
        grad_w_out,
        grad_b_out,
        grad_w_up,
        grad_b_up,
        grad_w_down,
        grad_b_down,
        grad_gain,
        grad_shift,
    )


def solution(mesh):
    placed = (
        P(("shard", "ctx"), None),
        P(("shard", "ctx"), None),
        P(("shard", "ctx")),
        P(("shard", "ctx")),
        P(),
        P(None, ("shard", "ctx"), "tp"),
        P(None, "tp"),
        P("tp", ("shard", "ctx")),
        P(),
        P(("shard", "ctx"), "tp"),
        P("tp"),
        P("tp", ("shard", "ctx")),
        P(),
        P(),
        P(),
    )
    sizes = dict(mesh.shape)
    paired = sizes["tp"] * sizes["ctx"] * 2 == HEADS and sizes["tp"] == 2 and sizes["shard"] == 4
    return jax.shard_map(
        fast_device if paired else per_device,
        mesh=mesh,
        in_specs=placed,
        out_specs=(
            P(("shard", "ctx"), None),
            P(("shard", "ctx"), None),
            P(None, ("shard", "ctx"), "tp"),
            P(None, "tp"),
            P("tp", ("shard", "ctx")),
            P(),
            P(("shard", "ctx"), "tp"),
            P("tp"),
            P("tp", ("shard", "ctx")),
            P(),
            P(),
            P(),
        ),
        check_vma=False,
    )
```

```python
from functools import partial

import jax
import jax.numpy as jnp
from jax import lax
from jax.experimental import pallas as pl
from jax.experimental.pallas import tpu as pltpu
from jax.sharding import PartitionSpec as P

HEADS = 16
HD = 64
KEY_BLOCK = 512
TRUNK = 1024
BRANCH = 128
SLOTS = 12
TREE = TRUNK + SLOTS * BRANCH
PAIR = 2 * HD

EPS = 1e-05
NEG = -1e30
LOG2E = 1.4426950408889634
MESH = pl.DeviceIdType.MESH
BF = jnp.bfloat16
F32 = jnp.float32
ROWS_WAVE = 4
FRONT_LIMIT = 62 << 20
BLOCK = 512
CURVE = 0.044715
ROOT = 0.7978845608028654
SUBS = 2


def nt(left, right):
    return lax.dot_general(left, right, (((1,), (1,)), ((), ())), preferred_element_type=F32)


def nn(left, right):
    return lax.dot_general(left, right, (((1,), (0,)), ((), ())), preferred_element_type=F32)


def rcopy(src, dst, send, recv, device):
    return pltpu.make_async_remote_copy(
        src_ref=src, dst_ref=dst, send_sem=send, recv_sem=recv, device_id=device, device_id_type=MESH
    )


def greet(devices):
    barrier = pltpu.get_barrier_semaphore()
    for device in devices:
        pl.semaphore_signal(barrier, inc=1, device_id=device, device_id_type=MESH)
    pl.semaphore_wait(barrier, len(devices))


def norm_rows(values, gain_row, shift_row):
    centre = values - jnp.mean(values, axis=-1, keepdims=True)
    inverse = lax.rsqrt(jnp.mean(centre * centre, axis=-1, keepdims=True) + EPS)
    normed = centre * inverse
    return normed * gain_row + shift_row, normed, inverse


def norm_rows_back(grad_in, normed, inverse, gain_row):
    scaled = grad_in * gain_row
    mean_grad = jnp.mean(scaled, axis=-1, keepdims=True)
    mean_cross = jnp.mean(scaled * normed, axis=-1, keepdims=True)
    return inverse * (scaled - mean_grad - normed * mean_cross)


def head_masks():
    lane = lax.broadcasted_iota(jnp.int32, (1, PAIR), 1)
    first = (lane < HD).astype(F32).astype(BF)
    second = (lane >= HD).astype(F32).astype(BF)
    return first, second


def stack_heads(rows):
    first, second = head_masks()
    return jnp.concatenate([rows * first, rows * second], axis=0)


def unstack_turned(turned, rows):
    return jnp.concatenate([turned[:HD, :rows], turned[HD:, rows:]], axis=0).T


def key_features(high, low, flag, rows):
    lane = lax.broadcasted_iota(jnp.int32, (rows, 128), 1)
    feats = jnp.where(lane < 3, high, jnp.where(lane < 6, low, jnp.where(lane == 6, flag, 0.0)))
    return feats.astype(BF)


def query_features(slope_ref, rows):
    return jnp.concatenate(
        [
            jnp.broadcast_to(slope_ref[0:1, :], (rows, 128)),
            jnp.broadcast_to(slope_ref[1:2, :], (rows, 128)),
        ],
        axis=0,
    ).astype(BF)


def fill_trunk_keys(key_ref, keys_aug):
    keys_aug[:, 0:PAIR] = key_ref[0:TRUNK, :]
    pos = lax.broadcasted_iota(jnp.int32, (TRUNK, 128), 0)
    low = pos & 255
    keys_aug[:, PAIR:] = key_features((pos - low).astype(F32), low.astype(F32), 0.0, TRUNK)


def fill_labels(info_all, blocks, labels, parents):
    labels[...] = jnp.full(labels.shape, -1.0, F32)
    parents[...] = jnp.full(parents.shape, -2.0, F32)
    for slot in range(SLOTS):
        block = TRUNK // BRANCH + slot
        owner, inner = block // blocks, block % blocks
        labels[slot : slot + 1, :] = info_all[owner, inner : inner + 1, :]
        parents[slot : slot + 1, :] = info_all[owner, 8 + inner : 9 + inner, :]


def parent_pick(slot, labels, parents, key_ref, value_ref):
    mine = parents[pl.ds(slot, 1), :]
    leaf = jnp.zeros((1, 128), F32)
    key_sum = jnp.zeros((BRANCH, PAIR), BF)
    value_sum = jnp.zeros((BRANCH, PAIR), BF)
    for other in range(SLOTS):
        same = (mine == labels[other : other + 1, :]).astype(F32)
        leaf = leaf + same
        same_low = same.astype(BF)
        at = TRUNK + other * BRANCH
        key_sum = key_sum + same_low * key_ref[at : at + BRANCH, :]
        value_sum = value_sum + same_low * value_ref[at : at + BRANCH, :]
    return leaf, key_sum, value_sum


def segment_key_features(leaf):
    row = lax.broadcasted_iota(jnp.int32, (BRANCH, 128), 0).astype(F32)
    own = key_features(float(TRUNK), row + leaf * float(BRANCH), 0.0, BRANCH)
    above = key_features(float(TRUNK), row, (leaf - 1.0) * 1e30, BRANCH)
    return own, above


def causal(rows):
    key = lax.broadcasted_iota(jnp.int32, (rows, rows), 0)
    query = lax.broadcasted_iota(jnp.int32, (rows, rows), 1)
    once = key <= query
    return jnp.concatenate([once, once], axis=1)


class Spread:
    def __init__(self, full, dims, depth, cols, sems):
        self.full, self.depth, self.cols = full, depth, cols
        self.ns, self.nz, _ = dims
        self.s, self.z = lax.axis_index("shard"), lax.axis_index("ctx")
        self.zs, self.zr, self.xs, self.xr, self.cs, self.cr = sems

    def rows(self, shard, place):
        at = pl.multiple_of((shard * self.nz + place) * self.depth, self.depth)
        return self.full.at[pl.ds(at, self.depth), self.cols]

    def flip(self, bits):
        low = lax.rem(self.s, 2)
        high = lax.div(self.s, 2)
        if bits & 1:
            low = 1 - low
        if bits & 2:
            high = 1 - high
        return 2 * high + low

    def source(self, d):
        return lax.rem(self.z + self.nz - d, self.nz)

    def z_copy(self, d):
        ref = self.rows(self.s, self.z)
        return rcopy(ref, ref, self.zs.at[d - 1], self.zr.at[d - 1], {"ctx": lax.rem(self.z + d, self.nz)})

    def x_copy(self, d):
        ref = self.rows(self.s, self.source(d))
        return rcopy(ref, ref, self.xs.at[d], self.xr.at[d], {"shard": self.flip(2)})

    def c_copy(self, far, d):
        ref = self.rows(self.flip(2) if far else self.s, self.source(d))
        return rcopy(ref, ref, self.cs.at[far, d], self.cr.at[far, d], {"shard": self.flip(1)})

    def z_start(self):
        for d in (1, 3, 2):
            self.z_copy(d).start()

    def own(self):
        self.x_copy(0).start()
        self.c_copy(0, 0).start()

    def z_done(self, d):
        ref = self.rows(self.s, self.source(d))
        rcopy(ref, ref, self.zs.at[d - 1], self.zr.at[d - 1], {"ctx": self.z}).wait_recv()
        self.x_copy(d).start()
        self.c_copy(0, d).start()

    def x_done(self, d):
        ref = self.rows(self.flip(2), self.source(d))
        rcopy(ref, ref, self.xs.at[d], self.xr.at[d], {"shard": self.flip(2)}).wait_recv()
        self.c_copy(1, d).start()

    def c_done(self, far, d):
        ref = self.rows(self.flip(3) if far else self.flip(1), self.source(d))
        rcopy(ref, ref, self.cs.at[far, d], self.cr.at[far, d], {"shard": self.flip(1)}).wait_recv()

    def all_here(self):
        for d in range(self.nz):
            self.c_done(0, d)
            self.c_done(1, d)

    def finish(self):
        for d in range(self.nz):
            if d:
                self.z_copy(d).wait_send()
            self.x_copy(d).wait_send()
            self.c_copy(0, d).wait_send()
            self.c_copy(1, d).wait_send()


def spread_sems(nz):
    return [dma(nz - 1), dma(nz - 1), dma(nz), dma(nz), dma(2, nz), dma(2, nz)]


def vmem():
    return pl.BlockSpec(memory_space=pltpu.VMEM)


def shape(dims, kind):
    return jax.ShapeDtypeStruct(dims, kind)


def dma(*dims):
    return pltpu.SemaphoreType.DMA(dims)


def front_kernel(
    dims,
    tok,
    w_up,
    w_out,
    w_down,
    cot_in,
    wq3,
    info,
    bias_qv,
    slopes,
    gain,
    shift,
    b_out,
    b_up,
    act_turned,
    query,
    key,
    value,
    out_heads,
    lse,
    info_all,
    wqkv,
    core_in,
    ga_all,
    down_part,
    mid,
    gmid,
    sums,
    wfull,
    wq,
    att,
    tree,
    wcat,
    keys_aug,
    values_turned,
    labels,
    parents,
    cot,
    far,
    act,
    gbranch,
    g_send,
    g_recv,
    ga_send,
    bup_acc,
    info_send,
    info_recv,
    wz_send,
    wz_recv,
    ws_send,
    ws_recv,
    z_send,
    z_recv,
    y_send,
    y_recv,
    a_send,
    a_recv,
    local_sem,
    b_send,
    b_recv,
    t_send,
    t_recv,
    gs_sem,
    gr_sem,
    as_sem,
    ar_sem,
    cs_sem,
    cr_sem,
    *spread,
):
    ns, nz, rows = dims
    s, z, y = lax.axis_index("shard"), lax.axis_index("ctx"), lax.axis_index("tp")
    half = rows // 2
    sub = half // SUBS
    depth = wq.shape[0]
    wide = 3 * PAIR
    my_rows = pl.ds(pl.multiple_of((s * nz + z) * depth, depth), depth)
    units, inner = w_up.shape[1], w_out.shape[1]
    own_cols = pl.multiple_of(2 * units + y * inner, 128)
    starts = [
        pltpu.make_async_copy(tok, tree.at[pl.ds(pl.multiple_of(z * rows, 128), rows), :], local_sem.at[0]),
        pltpu.make_async_copy(w_up, wfull.at[my_rows, 0:units], local_sem.at[1]),
        pltpu.make_async_copy(w_down, wfull.at[my_rows, units : 2 * units], local_sem.at[2]),
        pltpu.make_async_copy(w_out, wfull.at[my_rows, pl.ds(own_cols, inner)], local_sem.at[3]),
    ]
    given_load = pltpu.make_async_copy(cot_in, cot, local_sem.at[4])
    given_load.start()
    for one in starts:
        one.start()
    for to in range(nz):
        for part in range(3):
            wq[:, to * wide + part * PAIR : to * wide + (part + 1) * PAIR] = wq3[
                part, :, to * PAIR : (to + 1) * PAIR
            ]
    greet(
        [{"ctx": lax.rem(z + d, nz)} for d in range(1, nz)]
        + [{"shard": lax.rem(s + d, ns)} for d in range(1, ns)]
        + [{"tp": 1 - y}]
    )
    ups = Spread(wfull, dims, depth, slice(0, units), spread[:6])
    downs = Spread(wfull, dims, depth, slice(units, 2 * units), spread[6:12])
    weights = Spread(wqkv, dims, depth, slice(None), spread[18:])
    outer = Spread(wfull, dims, depth, pl.ds(own_cols, inner), spread[12:18])

    def info_copy(d):
        return rcopy(
            info, info_all.at[z], info_send.at[d - 1], info_recv.at[d - 1], {"ctx": lax.rem(z + d, nz)}
        )

    def wz_copy(d):
        to = lax.rem(z + d, nz)
        return rcopy(
            wq.at[:, pl.ds(pl.multiple_of(to * wide, 128), wide)],
            wcat.at[my_rows, :],
            wz_send.at[d - 1],
            wz_recv.at[d - 1],
            {"ctx": to},
        )

    shard_rows = pl.ds(s * (nz * depth), nz * depth)

    def ws_copy(d):
        return rcopy(
            wcat.at[shard_rows, :],
            wcat.at[shard_rows, :],
            ws_send.at[d - 1],
            ws_recv.at[d - 1],
            {"shard": lax.rem(s + d, ns)},
        )

    wqkv[my_rows, :] = wq[...]
    for d in range(1, nz):
        wz_copy(d).start()
    for d in range(1, nz):
        info_copy(d).start()
    wcat[my_rows, :] = wq[:, pl.ds(pl.multiple_of(z * wide, 128), wide)]
    info_all[z] = info[...]
    for one in starts:
        one.wait()

    def piece(block, second, part):
        at = block * rows + jnp.where(second, 1 - y, y) * half + part * sub
        return tree.at[pl.ds(pl.multiple_of(at, 32), sub), :]

    def z_copy(direction, k, part):
        block = z - k if direction == 0 else z + k
        to = z + 1 if direction == 0 else z - 1
        ref = piece(block, False, part)
        return rcopy(ref, ref, z_send.at[direction, k, part], z_recv.at[direction, k, part], {"ctx": to})

    def z_arrival(direction, k, part):
        block = z - k if direction == 0 else z + k
        ref = piece(block, False, part)
        return rcopy(
            ref, ref, z_send.at[direction, k - 1, part], z_recv.at[direction, k - 1, part], {"ctx": z}
        )

    def y_copy(direction, k, part):
        block = z - k if direction == 0 else z + k
        ref = piece(block, False, part)
        return rcopy(
            ref, ref, y_send.at[direction, k - 1, part], y_recv.at[direction, k - 1, part], {"tp": 1 - y}
        )

    def y_arrival(direction, k, part):
        block = z - k if direction == 0 else z + k
        ref = piece(block, True, part)
        return rcopy(
            ref, ref, y_send.at[direction, k - 1, part], y_recv.at[direction, k - 1, part], {"tp": 1 - y}
        )

    def place(direction, k):
        block = z - k if direction == 0 else z + k
        nxt = z + 1 if direction == 0 else z - 1
        here = (block >= 0) & (block < nz)
        onward = here & (nxt >= 0) & (nxt < nz)
        return block, here, onward

    def forward(k, first):
        for part in range(SUBS):
            for direction in range(2):
                _, here, onward = place(direction, k)
                if not first:

                    @pl.when(here)
                    def _():
                        z_arrival(direction, k, part).wait_recv()

                @pl.when(onward & (k < nz - 1))
                def _():
                    z_copy(direction, k, part).start()

                if not first:

                    @pl.when(here)
                    def _():
                        y_copy(direction, k, part).start()

    forward(0, True)
    outer.own()
    ups.own()
    downs.own()
    for d in range(1, nz):
        wz_copy(d).wait_recv()
    for d in range(1, ns):
        ws_copy(d).start()

    bias_at = pl.ds(pl.multiple_of(z * PAIR, 128), PAIR)
    bias_q = bias_qv[0:1, bias_at]
    bias_v = bias_qv[1:2, bias_at]

    def project(k):
        def side(direction, inner_carry):
            block = z + (2 * direction - 1) * k

            @pl.when((block >= 0) & (block < nz) & ((k > 0) | (direction == 0)))
            def _():
                def tile(t, carry):
                    here = pl.ds(pl.multiple_of(block * rows + t * 128, 128), 128)
                    act = norm_rows(tree[here, :].astype(F32), gain[0:1, :], shift[0:1, :])[0].astype(BF)
                    act_turned[:, here] = act.T
                    both = nn(act, wcat[...])
                    query[here, :] = (
                        (both[:, :PAIR] + bias_q).astype(BF).astype(F32) * HD ** (-0.5)
                    ).astype(BF)
                    key[here, :] = both[:, PAIR : 2 * PAIR].astype(BF)
                    value[here, :] = (both[:, 2 * PAIR :] + bias_v).astype(BF)
                    return carry

                lax.fori_loop(0, rows // 128, tile, 0)

            return inner_carry

        lax.fori_loop(0, 2, side, 0)

    def shared(k):
        for part in range(SUBS):
            for direction in range(2):
                _, here, _ = place(direction, k)

                @pl.when(here)
                def _():
                    y_arrival(direction, k, part).wait_recv()

    forward(1, False)
    for d in range(1, ns):
        ws_copy(d).wait_recv()
    project(0)

    def wave(k, carry):
        forward(k, False)

        @pl.when(k == nz - 2)
        def _():
            outer.z_start()
            ups.z_start()

        shared(k - 1)
        project(k - 1)
        return carry

    lax.fori_loop(2, nz, wave, 0)
    for d in (1, 3, 2):
        outer.z_done(d)
    shared(nz - 1)
    project(nz - 1)
    for d in (0, 1, 3, 2):
        outer.x_done(d)

    for d in range(1, nz):
        info_copy(d).wait_recv()

    fill_labels(info_all, rows // BRANCH, labels, parents)
    fill_trunk_keys(key, keys_aug)
    values_turned[...] = value[0:TRUNK, :].T

    def att_cols(half_at, owner):
        return pl.ds(pl.multiple_of(half_at * inner + owner * PAIR, 128), PAIR)

    def att_copy(to):
        return rcopy(
            out_heads.at[pl.ds(to * rows, rows), :],
            att.at[:, att_cols(y, z)],
            a_send.at[to],
            a_recv.at[z],
            {"ctx": to},
        )

    def pass_on(owner):
        return rcopy(
            att.at[:, att_cols(y, owner)],
            att.at[:, att_cols(y, owner)],
            b_send.at[owner],
            b_recv.at[owner],
            {"tp": 1 - y},
        )

    half_rows = pl.ds(pl.multiple_of(lax.rem(s, 2) * (ns * nz * depth // 2), 128), ns * nz * depth // 2)
    far_rows = pl.ds(pl.multiple_of((1 - lax.rem(s, 2)) * (ns * nz * depth // 2), 128), ns * nz * depth // 2)
    far_cols = pl.ds(pl.multiple_of(2 * units + (1 - y) * inner, 128), inner)

    def plane_copy():
        ref = wfull.at[half_rows, pl.ds(own_cols, inner)]
        return rcopy(ref, ref, t_send.at[0], t_recv.at[0], {"tp": 1 - y})

    def plane_arrival():
        ref = wfull.at[half_rows, far_cols]
        return rcopy(ref, ref, t_send.at[0], t_recv.at[0], {"tp": 1 - y})

    def core_copy():
        ref = wfull.at[half_rows, far_cols]
        return rcopy(ref, ref, t_send.at[1], t_recv.at[1], {"shard": outer.flip(1)})

    def core_arrival():
        ref = wfull.at[far_rows, far_cols]
        return rcopy(ref, ref, t_send.at[1], t_recv.at[1], {"shard": outer.flip(1)})

    outer.all_here()
    plane_copy().start()

    def send_out(to):
        @pl.when(z != to)
        def _():
            att_copy(to).start()

        @pl.when(z == to)
        def _():
            att[:, att_cols(y, z)] = out_heads[to * rows : (to + 1) * rows, :]
            pass_on(z).start()

    tile_mask = causal(BRANCH)

    def segment(slot, carry):
        here = pl.ds(pl.multiple_of(TRUNK + slot * BRANCH, 128), BRANCH)
        asked = jnp.concatenate(
            [stack_heads(query[here, :]), query_features(slopes, BRANCH)], axis=1
        )
        leaf, key_up, value_up = parent_pick(slot, labels, parents, key, value)
        own_feats, up_feats = segment_key_features(leaf)
        trunk_part = nt(keys_aug[...], asked) * LOG2E
        own_part = nt(jnp.concatenate([key[here, :], own_feats], axis=1), asked) * LOG2E
        own_part = jnp.where(tile_mask, own_part, NEG)
        up_part = nt(jnp.concatenate([key_up, up_feats], axis=1), asked) * LOG2E
        top = jnp.maximum(
            jnp.max(trunk_part, axis=0, keepdims=True),
            jnp.maximum(
                jnp.max(own_part, axis=0, keepdims=True), jnp.max(up_part, axis=0, keepdims=True)
            ),
        )
        trunk_part = jnp.exp2(trunk_part - top)
        own_part = jnp.exp2(own_part - top)
        up_part = jnp.exp2(up_part - top)
        total = (
            jnp.sum(trunk_part, axis=0, keepdims=True)
            + jnp.sum(own_part, axis=0, keepdims=True)
            + jnp.sum(up_part, axis=0, keepdims=True)
        )
        turned = nn(values_turned[...], trunk_part.astype(BF))
        turned = turned + nn(value[here, :].T, own_part.astype(BF))
        turned = turned + nn(value_up.T, up_part.astype(BF))
        turned = turned / total
        out_heads[here, :] = unstack_turned(turned, BRANCH).astype(BF)
        lse[pl.ds(4 + slot, 1), 0 : 2 * BRANCH] = top + jnp.log2(total)
        return carry

    wave_rows = TRUNK // 4
    wave_mask = causal(wave_rows)

    def trunk_tile(tile):
        lo, hi = tile * wave_rows, (tile + 1) * wave_rows
        asked = jnp.concatenate(
            [stack_heads(query[lo:hi, :]), query_features(slopes, wave_rows)], axis=1
        )
        edge = jnp.where(wave_mask, nt(keys_aug[lo:hi, :], asked) * LOG2E, NEG)
        top = jnp.max(edge, axis=0, keepdims=True)
        if tile:
            body = nt(keys_aug[0:lo, :], asked) * LOG2E
            top = jnp.maximum(top, jnp.max(body, axis=0, keepdims=True))
            body = jnp.exp2(body - top)
        edge = jnp.exp2(edge - top)
        total = jnp.sum(edge, axis=0, keepdims=True)
        turned = nn(values_turned[:, lo:hi], edge.astype(BF))
        if tile:
            total = total + jnp.sum(body, axis=0, keepdims=True)
            turned = turned + nn(values_turned[:, 0:lo], body.astype(BF))
        turned = turned / total
        out_heads[lo:hi, :] = unstack_turned(turned, wave_rows).astype(BF)
        lse[tile : tile + 1, :] = top + jnp.log2(total)

    def segments(lo, hi):
        lax.fori_loop((lo - TRUNK) // BRANCH, (hi - TRUNK) // BRANCH, segment, 0)

    segments(2 * rows, 3 * rows)
    send_out(2)
    for tile in range(3):
        trunk_tile(tile)
    send_out(0)
    ups.z_done(1)
    ups.z_done(3)
    segments(3 * rows, 4 * rows)
    send_out(3)
    trunk_tile(3)
    segments(TRUNK, 2 * rows)
    send_out(1)
    downs.z_start()
    ups.z_done(2)
    plane_arrival().wait_recv()
    core_copy().start()
    for owner in range(nz):

        @pl.when(z != owner)
        def _():
            rcopy(
                out_heads.at[0:rows, :],
                att.at[:, att_cols(y, owner)],
                a_send.at[owner],
                a_recv.at[owner],
                {"ctx": owner},
            ).wait_recv()
            pass_on(owner).start()

    mid[...] = tree[pl.ds(pl.multiple_of(z * rows, 128), rows), :].astype(F32) + b_out[...]
    for d in (0, 1, 3, 2):
        ups.x_done(d)
    for d in (1, 3):
        downs.z_done(d)
    given_load.wait()
    for owner in range(nz):
        ref = att.at[:, att_cols(1 - y, owner)]
        rcopy(ref, ref, b_send.at[owner], b_recv.at[owner], {"tp": 1 - y}).wait_recv()
    core_arrival().wait_recv()
    ups.all_here()
    other = {"tp": 1 - y}
    chunk = rows // ROWS_WAVE
    width = act.shape[1]
    halves = units // width
    own_heads = pl.ds(pl.multiple_of(y * inner, 128), inner)
    own_wide = pl.ds(own_cols, inner)
    sums[...] = jnp.zeros(sums.shape, F32)
    bup_acc[...] = jnp.zeros(bup_acc.shape, F32)

    def at(i):
        return pl.ds(pl.multiple_of(i * chunk, 32), chunk)

    def g_copy(i):
        return rcopy(g_send.at[at(i), :], g_recv.at[at(i), :], gs_sem.at[i], gr_sem.at[i], other)

    def a_copy(i, d):
        to = lax.rem(z + d, nz)
        return rcopy(
            ga_send.at[at(i), pl.ds(pl.multiple_of(to * PAIR, 128), PAIR)],
            ga_all.at[pl.ds(pl.multiple_of(z * rows + i * chunk, 32), chunk), :],
            as_sem.at[d - 1, i],
            ar_sem.at[d - 1, i],
            {"ctx": to},
        )

    span = nz * depth
    parts = ((0, 2 * units), (2 * units, 2 * units + inner))

    def c_copy(part, index):
        lo, hi = parts[part]
        return rcopy(
            far.at[index, :, lo:hi],
            core_in.at[index, :, lo:hi],
            cs_sem.at[part, index],
            cr_sem.at[part, index],
            {"shard": weights.flip(1)},
        )

    sums[...] = jnp.zeros(sums.shape, F32)
    bup_acc[...] = jnp.zeros(bup_acc.shape, F32)
    per = width // BLOCK

    def spot(first, i, c):
        row = (first + lax.div(c, per)) * rows + i * chunk
        col = lax.rem(c, per) * BLOCK
        return pl.ds(pl.multiple_of(row, 32), chunk), pl.ds(pl.multiple_of(col, 128), BLOCK)

    def stage_one(i, carry):
        here = at(i)
        middle = mid[here, :] + nt(att[here, :], wfull[:, 2 * units :])
        mid[here, :] = middle
        act[here, :] = norm_rows(middle, gain[1:2, :], shift[1:2, :])[0].astype(BF)

        def columns(c, inner_carry):
            cols = pl.ds(pl.multiple_of(c * BLOCK, 128), BLOCK)
            upper = nn(act[here, :], wfull[:, cols]) + b_up[:, cols]
            square = upper * upper
            turn = jnp.tanh(ROOT * (upper + CURVE * (square * upper)))
            tree[spot(0, i, c)] = (0.5 * upper * (1.0 + turn)).astype(BF)
            steep = 0.5 * (1.0 + turn) + (0.5 * ROOT) * upper * (1.0 - turn * turn) * (
                1.0 + (3.0 * CURVE) * square
            )
            tree[spot(halves, i, c)] = steep.astype(BF)
            return inner_carry

        lax.fori_loop(0, units // BLOCK, columns, 0)
        return carry

    def stage_two(i, carry):
        here = at(i)

        def columns(c, inner_carry):
            cols = pl.ds(pl.multiple_of(c * BLOCK, 128), BLOCK)
            down_cols = pl.ds(pl.multiple_of(units + c * BLOCK, 128), BLOCK)
            slope = nn(cot[here, :], wfull[:, down_cols])
            low = (slope * tree[spot(halves, i, c)].astype(F32)).astype(BF)
            tree[spot(halves, i, c)] = low
            bup_acc[:, cols] += jnp.sum(low.astype(F32), axis=0, keepdims=True)
            return inner_carry

        lax.fori_loop(0, units // BLOCK, columns, 0)
        total = jnp.zeros((chunk, width), F32)
        for part in range(halves):
            total = total + nt(
                tree[spot(halves + part, i, 0)[0], :], wfull[:, part * width : (part + 1) * width]
            )
        g_send[here, :] = total.astype(BF)
        g_copy(i).start()
        return carry

    def drain(k, carry):
        for part in range(SUBS):
            for direction in range(2):
                _, here, onward = place(direction, k)

                @pl.when(onward & (k < nz - 1))
                def _():
                    z_copy(direction, k, part).wait_send()

                @pl.when(here & (k > 0))
                def _():
                    y_copy(direction, k, part).wait_send()

        return carry

    lax.fori_loop(0, nz, drain, 0)
    lax.fori_loop(0, 2, stage_one, 0)
    downs.z_done(2)
    weights.own()
    weights.z_start()
    for d in (0, 1, 3, 2):
        downs.x_done(d)
    lax.fori_loop(2, ROWS_WAVE, stage_one, 0)
    downs.all_here()
    lax.fori_loop(0, ROWS_WAVE, stage_two, 0)
    for d in (1, 3, 2):
        weights.z_done(d)

    def group_cols(index, block):
        return pl.ds(pl.multiple_of(weights.flip(index) * span + block * 128, 128), 128)

    def products(cols):
        turned_act, turned_cot = act[:, cols].T, cot[:, cols].T
        for part in range(halves):
            lo = part * width
            yield lo, nn(turned_act, tree[(halves + part) * rows : (halves + part + 1) * rows, :])
            yield units + lo, nn(turned_cot, tree[part * rows : (part + 1) * rows, :])

    def each_block(act_on):
        for index in range(2):

            def one(block, carry):
                act_on(index, block)
                return carry

            lax.fori_loop(0, span // 128, one, 0)

    def far_one(index, block):
        target = pl.ds(pl.multiple_of(block * 128, 128), 128)
        for lo, value_block in products(group_cols((1, 3)[index], block)):
            far[index, target, lo : lo + width] = value_block.astype(BF)

    def near_one(index, block):
        target = pl.ds(pl.multiple_of(block * 128, 128), 128)
        for lo, value_block in products(group_cols((0, 2)[index], block)):
            here = slice(lo, lo + width)
            core_in[index, target, here] = (core_in[index, target, here].astype(F32) + value_block).astype(BF)

    def out_product(cols):
        return nn(gbranch[:, cols].T, att[:, own_heads])

    def far_two(index, block):
        target = pl.ds(pl.multiple_of(block * 128, 128), 128)
        far[index, target, 2 * units :] = out_product(group_cols((1, 3)[index], block)).astype(BF)

    def near_two(index, block):
        target = pl.ds(pl.multiple_of(block * 128, 128), 128)
        here = slice(2 * units, 2 * units + inner)
        core_in[index, target, here] = (
            core_in[index, target, here].astype(F32) + out_product(group_cols((0, 2)[index], block))
        ).astype(BF)

    def stage_c(i, carry):
        g_copy(i).wait_recv()
        here = at(i)
        grad = g_send[here, :].astype(F32) + g_recv[here, :].astype(F32)
        _, normed, inverse = norm_rows(mid[here, :], gain[1:2, :], shift[1:2, :])
        given = cot[here, :].astype(F32)
        grad_middle = given + norm_rows_back(grad, normed, inverse, gain[1:2, :])
        gmid[here, :] = grad_middle
        low = grad_middle.astype(BF)
        gbranch[here, :] = low
        sums[2:3, :] += jnp.sum(low.astype(F32), axis=0, keepdims=True)
        sums[3:4, :] += jnp.sum(given, axis=0, keepdims=True)
        sums[4:5, :] += jnp.sum(grad * normed, axis=0, keepdims=True)
        sums[5:6, :] += jnp.sum(grad, axis=0, keepdims=True)
        ga_send[here, :] = nn(low, wfull[:, own_wide]).astype(BF)
        for d in range(1, nz):
            a_copy(i, d).start()
        ga_all[pl.ds(pl.multiple_of(z * rows + i * chunk, 32), chunk), :] = ga_send[
            here, pl.ds(pl.multiple_of(z * PAIR, 128), PAIR)
        ]
        return carry

    lax.fori_loop(0, 2, stage_c, 0)
    each_block(far_one)
    for index in range(2):
        c_copy(0, index).start()
    for d in (0, 1, 3, 2):
        weights.x_done(d)
    lax.fori_loop(2, ROWS_WAVE, stage_c, 0)
    each_block(far_two)
    for index in range(2):
        c_copy(1, index).start()

    def down(i, carry):
        total = jnp.zeros((chunk, width), F32)
        for part in range(halves):
            total = total + nt(
                tree[spot(part, i, 0)[0], :], wfull[:, units + part * width : units + (part + 1) * width]
            )
        down_part[at(i), :] = total.astype(BF)
        return carry

    lax.fori_loop(0, ROWS_WAVE, down, 0)
    for index in range(2):
        c_copy(0, index).wait_recv()
    each_block(near_one)
    for index in range(2):
        c_copy(1, index).wait_recv()
    each_block(near_two)
    for part in range(halves):
        sums[part : part + 1, :] = bup_acc[:, part * width : (part + 1) * width]
    weights.all_here()
    weights.finish()
    for part in range(2):
        for index in range(2):
            c_copy(part, index).wait_send()

    def finish(i, carry):
        g_copy(i).wait_send()
        for d in range(1, nz):
            a_copy(i, d).wait_send()
            a_copy(i, d).wait_recv()
        return carry

    lax.fori_loop(0, ROWS_WAVE, finish, 0)
    plane_copy().wait_send()
    core_copy().wait_send()
    for owner in range(nz):
        pass_on(owner).wait_send()

    for owner in range(nz):

        @pl.when(z != owner)
        def _():
            att_copy(owner).wait_send()

    ups.finish()
    downs.finish()
    outer.finish()
    for d in range(1, nz):
        info_copy(d).wait_send()
        wz_copy(d).wait_send()
    for d in range(1, ns):
        ws_copy(d).wait_send()


def run_front(
    dims, tok, w_up, w_out, w_down, cot, wq3, info, bias_qv, slopes, gain, shift, b_out, b_up
):
    ns, nz, rows = dims
    width, units, inner, depth = tok.shape[1], w_up.shape[1], w_out.shape[1], wq3.shape[1]
    span, total, wide = nz * depth, 2 * units + inner, 3 * PAIR
    return pl.pallas_call(
        partial(front_kernel, dims),
        name="front",
        out_shape=(
            shape((width, TREE), BF),
            shape((TREE, PAIR), BF),
            shape((TREE, PAIR), BF),
            shape((TREE, PAIR), BF),
            shape((TREE, PAIR), BF),
            shape((16, 512), F32),
            shape((nz, 16, 128), F32),
            shape((width, nz * wide), BF),
            shape((2, span, total), BF),
            shape((TREE, PAIR), BF),
            shape((rows, width), BF),
            shape((rows, width), F32),
            shape((rows, width), F32),
            shape((8, width), F32),
        ),
        in_specs=[pl.BlockSpec(memory_space=pl.ANY)] * 5 + [vmem()] * 8,
        out_specs=[vmem()] * 14,
        scratch_shapes=[
            pltpu.VMEM((width, 2 * units + 2 * inner), BF),
            pltpu.VMEM((depth, nz * wide), BF),
            pltpu.VMEM((rows, 2 * inner), BF),
            pltpu.VMEM((TREE, width), BF),
            pltpu.VMEM((width, wide), BF),
            pltpu.VMEM((TRUNK, 2 * PAIR), BF),
            pltpu.VMEM((PAIR, TRUNK), BF),
            pltpu.VMEM((16, 128), F32),
            pltpu.VMEM((16, 128), F32),
            pltpu.VMEM((rows, width), BF),
            pltpu.VMEM((2, span, total), BF),
            pltpu.VMEM((rows, width), BF),
            pltpu.VMEM((rows, width), BF),
            pltpu.VMEM((rows, width), BF),
            pltpu.VMEM((rows, width), BF),
            pltpu.VMEM((rows, inner), BF),
            pltpu.VMEM((1, units), F32),
            dma(nz - 1),
            dma(nz - 1),
            dma(nz - 1),
            dma(nz - 1),
            dma(ns - 1),
            dma(ns - 1),
            dma(2, nz, SUBS),
            dma(2, nz, SUBS),
            dma(2, nz, SUBS),
            dma(2, nz, SUBS),
            dma(nz),
            dma(nz),
            dma(5),
            dma(nz),
            dma(nz),
            dma(2),
            dma(2),
            dma(ROWS_WAVE),
            dma(ROWS_WAVE),
            dma(nz - 1, ROWS_WAVE),
            dma(nz - 1, ROWS_WAVE),
            dma(2, 2),
            dma(2, 2),
            *spread_sems(nz),
            *spread_sems(nz),
            *spread_sems(nz),
            *spread_sems(nz),
        ],
        compiler_params=pltpu.CompilerParams(
            collective_id=0, has_side_effects=True, vmem_limit_bytes=FRONT_LIMIT
        ),
        cost_estimate=pl.CostEstimate(flops=40_000_000_000, bytes_accessed=20_000_000, transcendentals=0),
    )(tok, w_up, w_out, w_down, cot, wq3, info, bias_qv, slopes, gain, shift, b_out, b_up)


class Halve:
    def __init__(self, near, far, cols, dims, depth, bufs, sems):
        self.near, self.far, self.cols, self.depth = near, far, cols, depth
        self.nz = dims[1]
        self.s, self.z = lax.axis_index("shard"), lax.axis_index("ctx")
        self.x_in, self.a_in, self.b_out, self.b_in = bufs
        self.xs, self.xr, self.as_, self.ar, self.bs, self.br = sems

    def place(self, bits):
        low, high = lax.rem(self.z, 2), lax.div(self.z, 2)
        low = 1 - low if bits & 1 else low
        high = 1 - high if bits & 2 else high
        return 2 * high + low

    def block(self, bits):
        return pl.ds(pl.multiple_of(self.place(bits) * self.depth, self.depth), self.depth)

    def x_copy(self):
        low, high = lax.rem(self.s, 2), lax.div(self.s, 2)
        return rcopy(
            self.far.at[:, self.cols],
            self.x_in.at[:, self.cols],
            self.xs,
            self.xr,
            {"shard": 2 * (1 - high) + low},
        )

    def a_copy(self, index):
        return rcopy(
            self.near.at[self.block((1, 3)[index]), self.cols],
            self.a_in.at[index, :, self.cols],
            self.as_.at[index],
            self.ar.at[index],
            {"ctx": self.place(1)},
        )

    def b_copy(self):
        return rcopy(
            self.b_out.at[:, self.cols], self.b_in.at[:, self.cols], self.bs, self.br, {"ctx": self.place(2)}
        )

    def step_x(self):
        self.x_copy().wait_recv()

        def one(r, carry):
            here = pl.ds(pl.multiple_of(r * 32, 32), 32)
            self.near[here, self.cols] = (
                self.near[here, self.cols].astype(F32) + self.x_in[here, self.cols].astype(F32)
            ).astype(BF)
            return carry

        lax.fori_loop(0, self.near.shape[0] // 32, one, 0)
        self.a_copy(0).start()
        self.a_copy(1).start()

    def step_a(self):
        self.a_copy(0).wait_recv()
        self.a_copy(1).wait_recv()
        self.b_out[:, self.cols] = (
            self.near[self.block(2), self.cols].astype(F32) + self.a_in[1, :, self.cols].astype(F32)
        ).astype(BF)
        self.b_copy().start()

    def step_b(self):
        self.b_copy().wait_recv()
        return (
            self.near[self.block(0), self.cols].astype(F32)
            + self.a_in[0, :, self.cols].astype(F32)
            + self.b_in[:, self.cols].astype(F32)
        )

    def finish(self):
        self.x_copy().wait_send()
        self.a_copy(0).wait_send()
        self.a_copy(1).wait_send()
        self.b_copy().wait_send()


PIECES = 4


def back_kernel(
    dims,
    query,
    key,
    value,
    out_heads,
    lse,
    info_all,
    ga_all,
    act_turned,
    wqkv,
    partial_in,
    down_part,
    mid,
    b_down,
    gmid,
    tok,
    slopes,
    gain,
    shift,
    early,
    result,
    gtok,
    gup,
    gdown,
    gout,
    gwqkv,
    early_sum,
    late_sum,
    near,
    x_in,
    a_in,
    b_out,
    b_in,
    q_near,
    q_far,
    q_core,
    qx_in,
    q_all,
    dqkv,
    dk_trunk,
    dv_trunk,
    dk_seg,
    dv_seg,
    dk_up,
    dv_up,
    keys_aug,
    keys_turned,
    labels,
    parents,
    dq_all,
    n_send,
    n_recv,
    down_recv,
    wg_send,
    early_mine,
    early_recv,
    late,
    late_recv,
    d_sem,
    e_send,
    e_recv,
    f_send,
    f_recv,
    l_send,
    l_recv,
    p_send,
    p_recv,
    r_send,
    r_recv,
    ns_sem,
    nr_sem,
    xs_sem,
    xr_sem,
    as_sem,
    ar_sem,
    bs_sem,
    br_sem,
    qc_send,
    qc_recv,
    qx_sem,
    qz_send,
    qz_recv,
    n_local,
):
    ns, nz, rows = dims
    s, z, y = lax.axis_index("shard"), lax.axis_index("ctx"), lax.axis_index("tp")
    count = ns * nz
    me = s * nz + z
    chunk = rows // ROWS_WAVE
    width = tok.shape[1]
    depth = width // count
    span = nz * depth
    wide = 3 * PAIR
    other = {"tp": 1 - y}
    total_cols = near.shape[1]
    step_cols = total_cols // PIECES
    units = gup.shape[1]

    far = partial_in.at[1]
    load = pltpu.make_async_copy(partial_in.at[0], near, n_local)
    load.start()

    def peer(d):
        index = lax.rem(me + d, count)
        return index, {"shard": lax.div(index, nz), "ctx": lax.rem(index, nz)}

    greet([other] + [peer(d)[1] for d in range(1, count)])

    halves = [
        Halve(
            near,
            far,
            slice(i * step_cols, (i + 1) * step_cols),
            dims,
            depth,
            (x_in, a_in, b_out, b_in),
            (xs_sem.at[i], xr_sem.at[i], as_sem.at[i], ar_sem.at[i], bs_sem.at[i], br_sem.at[i]),
        )
        for i in range(PIECES)
    ]
    def shard_flip(bits):
        low, high = lax.rem(s, 2), lax.div(s, 2)
        low = 1 - low if bits & 1 else low
        high = 1 - high if bits & 2 else high
        return 2 * high + low

    def q_copy(index):
        return rcopy(
            wg_send.at[pl.ds(pl.multiple_of(shard_flip((1, 3)[index]) * span, 128), span), :],
            q_core.at[index],
            qc_send.at[index],
            qc_recv.at[index],
            {"shard": shard_flip(1)},
        )

    def qx_copy():
        return rcopy(q_far, qx_in, qx_sem.at[0], qx_sem.at[1], {"shard": shard_flip(2)})

    def qz_copy(d):
        to = lax.rem(z + d, nz)
        return rcopy(
            q_near.at[pl.ds(pl.multiple_of(to * depth, depth), depth), :],
            q_all.at[z],
            qz_send.at[d - 1],
            qz_recv.at[d - 1],
            {"ctx": to},
        )

    def q_spread():
        qx_copy().wait_recv()
        q_near[...] = (q_near[...].astype(F32) + qx_in[...].astype(F32)).astype(BF)
        for d in range(1, nz):
            qz_copy(d).start()
        q_all[z] = q_near[pl.ds(pl.multiple_of(z * depth, depth), depth), :]

    def down_copy():
        return rcopy(down_part, down_recv, d_sem.at[0], d_sem.at[1], other)

    owners = width // 128

    def owner_cols(index):
        return pl.ds(pl.multiple_of(index * 128, 128), 128)

    def early_copy(d):
        index, device = peer(d)
        return index, rcopy(
            early_mine.at[:, owner_cols(lax.rem(index, owners))],
            early_recv.at[me],
            e_send.at[d - 1],
            e_recv.at[d - 1],
            device,
        )

    def spread_copy(d):
        cols = owner_cols(lax.rem(me, owners))
        return rcopy(
            early_sum.at[:, cols], early_sum.at[:, cols], f_send.at[d - 1], f_recv.at[d - 1], peer(d)[1]
        )

    def spread_arrival(d):
        index = lax.rem(me + count - d, count)
        cols = owner_cols(lax.rem(index, owners))
        return index, rcopy(
            early_sum.at[:, cols], early_sum.at[:, cols], f_send.at[d - 1], f_recv.at[d - 1], other
        )

    def late_copy(d):
        return rcopy(late, late_recv.at[me], l_send.at[d - 1], l_recv.at[d - 1], peer(d)[1])

    def over_peers(act):
        def one(d, carry):
            act(d)
            return carry

        lax.fori_loop(1, count, one, 0)

    for half in halves:
        half.x_copy().start()
    down_copy().start()

    fill_labels(info_all, rows // BRANCH, labels, parents)
    fill_trunk_keys(key, keys_aug)
    keys_turned[...] = key[0:TRUNK, :].T
    dk_trunk[...] = jnp.zeros(dk_trunk.shape, F32)
    dv_trunk[...] = jnp.zeros(dv_trunk.shape, F32)
    tile_mask = causal(BRANCH)

    def row_products(here, count_rows):
        turned = (ga_all[here, :].astype(F32) * out_heads[here, :].astype(F32)).T
        return jnp.concatenate(
            [
                jnp.sum(turned[:HD, :], axis=0, keepdims=True),
                jnp.sum(turned[HD:, :], axis=0, keepdims=True),
            ],
            axis=1,
        )

    def part_back(key_aug, value_rows, asked, given, level, drow, mask):
        logits = nt(key_aug, asked) * LOG2E - level
        if mask is not None:
            logits = jnp.where(mask, logits, NEG)
        probs = jnp.exp2(logits)
        grads = (probs * (nt(value_rows, given) - drow)).astype(BF)
        return probs.astype(BF), grads

    def segment(slot, carry):
        here = pl.ds(pl.multiple_of(TRUNK + slot * BRANCH, 128), BRANCH)
        seg = pl.ds(pl.multiple_of(slot * BRANCH, 128), BRANCH)
        stacked = stack_heads(query[here, :])
        asked = jnp.concatenate([stacked, query_features(slopes, BRANCH)], axis=1)
        given = stack_heads(ga_all[here, :])
        leaf, key_up, value_up = parent_pick(slot, labels, parents, key, value)
        own_feats, up_feats = segment_key_features(leaf)
        level = lse[pl.ds(4 + slot, 1), 0 : 2 * BRANCH]
        drow = row_products(here, BRANCH)
        probs, grads = part_back(keys_aug[...], value[0:TRUNK, :], asked, given, level, drow, None)
        dv_trunk[...] += nn(probs, given)
        dk_trunk[...] += nn(grads, stacked)
        turned = nn(keys_turned[...], grads)
        key_own = key[here, :]
        probs, grads = part_back(
            jnp.concatenate([key_own, own_feats], axis=1), value[here, :], asked, given, level, drow, tile_mask
        )
        dv_seg[seg, :] = nn(probs, given)
        dk_seg[seg, :] = nn(grads, stacked)
        turned = turned + nn(key_own.T, grads)
        probs, grads = part_back(
            jnp.concatenate([key_up, up_feats], axis=1), value_up, asked, given, level, drow, None
        )
        dv_up[seg, :] = nn(probs, given)
        dk_up[seg, :] = nn(grads, stacked)
        turned = turned + nn(key_up.T, grads)
        dqkv[here, 0:PAIR] = (unstack_turned(turned, BRANCH) * HD ** (-0.5)).astype(BF)
        return carry

    def dq_copy(to):
        return rcopy(
            dqkv.at[to * rows : (to + 1) * rows, 0:PAIR],
            dq_all.at[:, pl.ds(pl.multiple_of(z * wide, 128), PAIR)],
            r_send.at[to],
            r_recv.at[z],
            {"ctx": to},
        )

    def send_dq(to):
        @pl.when(z != to)
        def _():
            dq_copy(to).start()

    def piece_copy(to, i):
        return rcopy(
            dqkv.at[to * rows + i * chunk : to * rows + (i + 1) * chunk, PAIR:],
            dq_all.at[i * chunk : (i + 1) * chunk, pl.ds(pl.multiple_of(z * wide + PAIR, 128), 2 * PAIR)],
            p_send.at[to, i],
            p_recv.at[z, i],
            {"ctx": to},
        )

    wave_rows = TRUNK // 4
    wave_mask = causal(wave_rows)
    for tile in range(4):
        lo, hi = tile * wave_rows, (tile + 1) * wave_rows
        stacked = stack_heads(query[lo:hi, :])
        asked = jnp.concatenate([stacked, query_features(slopes, wave_rows)], axis=1)
        given = stack_heads(ga_all[lo:hi, :])
        level = lse[tile : tile + 1, :]
        drow = row_products(pl.ds(lo, wave_rows), wave_rows)
        probs, grads = part_back(
            keys_aug[lo:hi, :], value[lo:hi, :], asked, given, level, drow, wave_mask
        )
        dv_trunk[lo:hi, :] += nn(probs, given)
        dk_trunk[lo:hi, :] += nn(grads, stacked)
        turned = nn(keys_turned[:, lo:hi], grads)
        if tile:
            probs, grads = part_back(
                keys_aug[0:lo, :], value[0:lo, :], asked, given, level, drow, None
            )
            dv_trunk[0:lo, :] += nn(probs, given)
            dk_trunk[0:lo, :] += nn(grads, stacked)
            turned = turned + nn(keys_turned[:, 0:lo], grads)
        dqkv[lo:hi, 0:PAIR] = (unstack_turned(turned, wave_rows) * HD ** (-0.5)).astype(BF)
    send_dq(0)

    def segments(lo, hi):
        lax.fori_loop((lo - TRUNK) // BRANCH, (hi - TRUNK) // BRANCH, segment, 0)

    segments(2 * rows, 3 * rows)
    send_dq(2)
    segments(TRUNK, 2 * rows)
    send_dq(1)
    segments(3 * rows, 4 * rows)
    send_dq(3)

    def gather_up(slot, carry):
        here = pl.ds(pl.multiple_of(TRUNK + slot * BRANCH, 128), BRANCH)
        seg = pl.ds(pl.multiple_of(slot * BRANCH, 128), BRANCH)
        mine = labels[pl.ds(slot, 1), :]
        dk, dv = dk_seg[seg, :], dv_seg[seg, :]
        for below in range(SLOTS):
            same = (parents[below : below + 1, :] == mine).astype(F32)
            at = below * BRANCH
            dk = dk + same * dk_up[at : at + BRANCH, :]
            dv = dv + same * dv_up[at : at + BRANCH, :]
        dqkv[here, PAIR : 2 * PAIR] = dk.astype(BF)
        dqkv[here, 2 * PAIR :] = dv.astype(BF)
        return carry

    lax.fori_loop(0, SLOTS, gather_up, 0)
    dqkv[0:TRUNK, PAIR : 2 * PAIR] = dk_trunk[...].astype(BF)
    dqkv[0:TRUNK, 2 * PAIR :] = dv_trunk[...].astype(BF)
    for i in range(ROWS_WAVE):
        for to in range(nz):

            @pl.when(z != to)
            def _():
                piece_copy(to, i).start()

    for to in range(nz):

        @pl.when(z == to)
        def _():
            dq_all[:, pl.ds(pl.multiple_of(z * wide, 128), wide)] = dqkv[to * rows : (to + 1) * rows, :]

    def weight(block, carry):
        here = pl.ds(pl.multiple_of(block * 128, 128), 128)
        wg_send[here, :] = nn(act_turned[here, :], dqkv[...]).astype(BF)
        return carry

    lax.fori_loop(0, width // 128, weight, 0)
    q_copy(0).start()
    q_copy(1).start()

    early_mine[...] = early[...]
    early_mine[6:7, pl.ds(pl.multiple_of(z * PAIR, 128), PAIR)] = jnp.sum(
        dqkv[:, 0:PAIR].astype(F32), axis=0, keepdims=True
    )
    early_mine[6:7, pl.ds(pl.multiple_of((nz + z) * PAIR, 128), PAIR)] = jnp.sum(
        dqkv[:, 2 * PAIR :].astype(F32), axis=0, keepdims=True
    )

    def early_send(d):
        index, copy = early_copy(d)

        @pl.when(index < owners)
        def _():
            copy.start()

    over_peers(early_send)
    early_recv[me] = early_mine[:, owner_cols(lax.rem(me, owners))]
    load.wait()

    def at(i):
        return pl.ds(pl.multiple_of(i * chunk, 32), chunk)

    def n_copy(i):
        return rcopy(n_send.at[at(i), :], n_recv.at[at(i), :], ns_sem.at[i], nr_sem.at[i], other)

    def core_join():
        for index in range(2):
            q_copy(index).wait_recv()
            mine = pl.ds(pl.multiple_of(shard_flip((0, 2)[index]) * span, 128), span)
            (q_near, q_far)[index][...] = (wg_send[mine, :].astype(F32) + q_core[index].astype(F32)).astype(BF)
        qx_copy().start()

    def first(i):
        for owner in range(nz):

            @pl.when(z != owner)
            def _():
                if i == 0:
                    rcopy(
                        dqkv.at[0:rows, 0:PAIR],
                        dq_all.at[:, owner * wide : owner * wide + PAIR],
                        r_send.at[owner],
                        r_recv.at[owner],
                        {"ctx": owner},
                    ).wait_recv()
                rcopy(
                    dqkv.at[0:chunk, PAIR:],
                    dq_all.at[i * chunk : (i + 1) * chunk, owner * wide + PAIR : (owner + 1) * wide],
                    p_send.at[owner, i],
                    p_recv.at[owner, i],
                    {"ctx": owner},
                ).wait_recv()

        n_send[at(i), :] = nt(dq_all[at(i), :], wqkv[...]).astype(BF)
        n_copy(i).start()

    def second(i, carry):
        n_copy(i).wait_recv()
        here = at(i)
        grad = n_send[here, :].astype(F32) + n_recv[here, :].astype(F32)
        _, normed, inverse = norm_rows(tok[here, :].astype(F32), gain[0:1, :], shift[0:1, :])
        gtok[here, :] = gmid[here, :] + norm_rows_back(grad, normed, inverse, gain[0:1, :])
        late[0:1, :] += jnp.sum(grad * normed, axis=0, keepdims=True)
        late[1:2, :] += jnp.sum(grad, axis=0, keepdims=True)
        return carry

    def output(i, carry):
        here = at(i)
        result[here, :] = (
            mid[here, :] + b_down[...] + (down_part[here, :].astype(F32) + down_recv[here, :].astype(F32))
        ).astype(BF)
        return carry

    late[...] = jnp.zeros(late.shape, F32)
    core_join()
    halves[0].step_x()
    halves[1].step_x()
    first(0)
    first(1)
    halves[2].step_x()
    first(2)
    halves[3].step_x()
    first(3)
    down_copy().wait_recv()
    lax.fori_loop(0, ROWS_WAVE, output, 0)

    @pl.when(me < owners)
    def _():
        over_peers(lambda d: early_copy(d)[1].wait_recv())
        total = early_recv[0]
        for index in range(1, count):
            total = total + early_recv[index]
        early_sum[:, owner_cols(lax.rem(me, owners))] = total
        over_peers(lambda d: spread_copy(d).start())

    q_spread()
    halves[0].step_a()
    lax.fori_loop(0, 2, second, 0)
    halves[1].step_a()
    lax.fori_loop(2, ROWS_WAVE, second, 0)
    over_peers(lambda d: late_copy(d).start())
    late_recv[me] = late[...]
    halves[2].step_a()
    halves[3].step_a()

    for d in range(1, nz):
        qz_copy(d).wait_recv()
    for owner in range(nz):
        for part in range(3):
            gwqkv[part, :, owner * PAIR : (owner + 1) * PAIR] = q_all[
                owner, :, part * PAIR : (part + 1) * PAIR
            ].astype(F32)
    bounds = (0, units, 2 * units, total_cols)
    for i, half in enumerate(halves):
        block = half.step_b()
        lo, hi = i * step_cols, (i + 1) * step_cols
        for target, start_at, end_at in (
            (gup, bounds[0], bounds[1]),
            (gdown, bounds[1], bounds[2]),
            (gout, bounds[2], bounds[3]),
        ):
            a, b = max(lo, start_at), min(hi, end_at)
            if a < b:
                target[:, a - start_at : b - start_at] = block[:, a - lo : b - lo]

    def early_wait(d):
        index, copy = spread_arrival(d)

        @pl.when(index < owners)
        def _():
            copy.wait_recv()

    over_peers(early_wait)
    over_peers(lambda d: late_copy(d).wait_recv())
    total = late_recv[0]
    for index in range(1, count):
        total = total + late_recv[index]
    late_sum[...] = total

    down_copy().wait_send()
    for half in halves:
        half.finish()
    qx_copy().wait_send()
    for d in range(1, nz):
        qz_copy(d).wait_send()
    q_copy(0).wait_send()
    q_copy(1).wait_send()

    def early_drain(d):
        index, copy = early_copy(d)

        @pl.when(index < owners)
        def _():
            copy.wait_send()

    over_peers(early_drain)

    @pl.when(me < owners)
    def _():
        over_peers(lambda d: spread_copy(d).wait_send())

    over_peers(lambda d: late_copy(d).wait_send())

    def finish(i, carry):
        n_copy(i).wait_send()
        return carry

    lax.fori_loop(0, ROWS_WAVE, finish, 0)
    for owner in range(nz):

        @pl.when(z != owner)
        def _():
            dq_copy(owner).wait_send()
            for i in range(ROWS_WAVE):
                piece_copy(owner, i).wait_send()


def run_back(dims, units, *inputs):
    ns, nz, rows = dims
    width = inputs[14].shape[1]
    _, span, total = inputs[9].shape
    count = ns * nz
    depth = width // count
    wide = 3 * PAIR
    anywhere = pl.BlockSpec(memory_space=pl.ANY)
    return pl.pallas_call(
        partial(back_kernel, dims),
        name="tree_backward",
        out_shape=(
            shape((rows, width), BF),
            shape((rows, width), F32),
            shape((depth, units), F32),
            shape((depth, units), F32),
            shape((depth, total - 2 * units), F32),
            shape((3, depth, nz * PAIR), F32),
            shape((8, width), F32),
            shape((2, width), F32),
        ),
        in_specs=[vmem()] * 9 + [anywhere] + [vmem()] * 9,
        out_specs=[vmem()] * 8,
        scratch_shapes=[
            pltpu.VMEM((span, total), BF),
            pltpu.VMEM((span, total), BF),
            pltpu.VMEM((2, depth, total), BF),
            pltpu.VMEM((depth, total), BF),
            pltpu.VMEM((depth, total), BF),
            pltpu.VMEM((span, wide), BF),
            pltpu.VMEM((span, wide), BF),
            pltpu.VMEM((2, span, wide), BF),
            pltpu.VMEM((span, wide), BF),
            pltpu.VMEM((nz, depth, wide), BF),
            pltpu.VMEM((TREE, wide), BF),
            pltpu.VMEM((TRUNK, PAIR), F32),
            pltpu.VMEM((TRUNK, PAIR), F32),
            pltpu.VMEM((TREE - TRUNK, PAIR), F32),
            pltpu.VMEM((TREE - TRUNK, PAIR), F32),
            pltpu.VMEM((TREE - TRUNK, PAIR), F32),
            pltpu.VMEM((TREE - TRUNK, PAIR), F32),
            pltpu.VMEM((TRUNK, 2 * PAIR), BF),
            pltpu.VMEM((PAIR, TRUNK), BF),
            pltpu.VMEM((16, 128), F32),
            pltpu.VMEM((16, 128), F32),
            pltpu.VMEM((rows, nz * wide), BF),
            pltpu.VMEM((rows, width), BF),
            pltpu.VMEM((rows, width), BF),
            pltpu.VMEM((rows, width), BF),
            pltpu.VMEM((width, wide), BF),
            pltpu.VMEM((8, width), F32),
            pltpu.VMEM((count, 8, 128), F32),
            pltpu.VMEM((2, width), F32),
            pltpu.VMEM((count, 2, width), F32),
            dma(2),
            dma(count - 1),
            dma(count - 1),
            dma(count - 1),
            dma(count - 1),
            dma(count - 1),
            dma(count - 1),
            dma(nz, ROWS_WAVE),
            dma(nz, ROWS_WAVE),
            dma(nz),
            dma(nz),
            dma(ROWS_WAVE),
            dma(ROWS_WAVE),
            dma(PIECES),
            dma(PIECES),
            dma(PIECES, 2),
            dma(PIECES, 2),
            dma(PIECES),
            dma(PIECES),
            dma(2),
            dma(2),
            dma(2),
            dma(nz - 1),
            dma(nz - 1),
            pltpu.SemaphoreType.DMA,
        ],
        compiler_params=pltpu.CompilerParams(
            collective_id=2, has_side_effects=True, vmem_limit_bytes=60 << 20
        ),
        cost_estimate=pl.CostEstimate(flops=40_000_000_000, bytes_accessed=20_000_000, transcendentals=0),
    )(*inputs)


def fast_device(
    tokens, cotangent, seg_ids, positions, parents, w_qkv, b_qv, w_out, b_out, w_up, b_up, w_down, b_down, ln_gain, ln_bias
):
    rows = tokens.shape[0]
    ns, nz, ntp = lax.axis_size("shard"), lax.axis_size("ctx"), lax.axis_size("tp")
    dims = (ns, nz, rows)

    labels = seg_ids.reshape(rows // BRANCH, BRANCH)[:, 0]
    match = labels[:, None] == jnp.arange(parents.shape[0], dtype=jnp.int32)[None, :]
    above = jnp.sum(jnp.where(match, parents[None, :], 0), axis=1)
    fill = 8 - rows // BRANCH
    lines = jnp.concatenate([jnp.pad(labels, (0, fill)), jnp.pad(above, (0, fill))]).astype(F32)
    info = jnp.broadcast_to(lines[:, None], (16, 128))
    per = HEADS // ntp
    index = lax.axis_index("tp") * per + lax.axis_index("ctx") * 2 + jnp.arange(2)
    slope = 2.0 ** (-8.0 * (index.astype(F32) + 1.0) / HEADS)
    one = lax.reduce_precision(slope, 8, 7)
    two = lax.reduce_precision(slope - one, 8, 7)
    three = lax.reduce_precision(slope - one - two, 8, 7)
    table = jnp.stack([one, two, three, one, two, three, jnp.ones_like(one)], axis=1)
    slopes = jnp.pad(table, ((0, 0), (0, 121)))

    units = b_up.shape[0]
    (
        act_turned, query, key, value, out_heads, lse, info_all, wqkv, partial_sums, ga_all, down_part, mid, gmid, sums
    ) = run_front(
        dims, tokens, w_up, w_out.T, w_down.T, cotangent, w_qkv, info, b_qv, slopes, ln_gain, ln_bias,
        b_out[None, :], b_up[None, :],
    )
    result, grad_tokens, gup, gdown, gout, grad_w_qkv, early, late = run_back(
        dims, units, query, key, value, out_heads, lse, info_all, ga_all, act_turned, wqkv, partial_sums, down_part,
        mid, b_down[None, :], gmid, tokens, slopes, ln_gain, ln_bias, sums,
    )
    return (
        result,
        grad_tokens,
        grad_w_qkv,
        early[6].reshape(2, nz * PAIR),
        gout.T,
        early[2],
        gup,
        early[0:2].reshape(units),
        gdown.T,
        early[3],
        jnp.stack([late[0], early[4]]),
        jnp.stack([late[1], early[5]]),
    )


def norm_forward(inputs_in, gain_row, shift_row):
    centre = inputs_in - jnp.mean(inputs_in, axis=-1, keepdims=True)
    inverse = lax.rsqrt(jnp.mean(centre * centre, axis=-1, keepdims=True) + EPS)
    normed = centre * inverse
    return (normed * gain_row + shift_row, normed, inverse)


def norm_backward(grad_in, normed, inverse, gain_row):
    scaled = grad_in * gain_row
    mean_grad = jnp.mean(scaled, axis=-1, keepdims=True)
    mean_cross = jnp.mean(scaled * normed, axis=-1, keepdims=True)
    return inverse * (scaled - mean_grad - normed * mean_cross)


def ancestry(seg_vals, parents):
    first_up = jnp.take(parents, seg_vals)
    return (first_up, jnp.take(parents, first_up))


def block_scores(query_heads, key_heads, query_tags, key_tags, slopes):
    q_seg, q_first, q_second, q_pos = query_tags
    k_seg, k_pos = key_tags
    raw_scores = jnp.einsum(
        "qhd,khd->hqk", query_heads, key_heads, preferred_element_type=jnp.float32
    ) * HD ** (-0.5)
    distance = (q_pos[:, None] - k_pos[None, :]).astype(jnp.float32)
    scores = raw_scores - slopes[:, None, None] * distance[None]
    related = (
        (k_seg[None, :] == q_seg[:, None])
        | (k_seg[None, :] == q_first[:, None])
        | (k_seg[None, :] == q_second[:, None])
    )
    allowed = related & (k_pos[None, :] <= q_pos[:, None])
    return (scores, allowed[None])


def probabilities(scores, allowed, row_max, row_sum):
    shifted = jnp.where(allowed, scores - row_max[:, :, None], NEG)
    return jnp.exp(shifted) / row_sum[:, :, None]


def per_device(
    tokens,
    cotangent,
    seg_ids,
    positions,
    parents,
    w_qkv,
    b_qv,
    w_out,
    b_out,
    w_up,
    b_up,
    w_down,
    b_down,
    ln_gain,
    ln_bias,
):
    num_rows = tokens.shape[0]
    head_count = HEADS // lax.axis_size("tp")
    head_width = head_count * HD
    head_index = (lax.axis_index("tp") * head_count + jnp.arange(head_count)).astype(jnp.float32)
    slopes = 2.0 ** (-8.0 * (head_index + 1.0) / HEADS)
    scale = HD ** (-0.5)
    full_qkv, full_out = (
        lax.all_gather(w_qkv, ("shard", "ctx"), axis=1, tiled=True),
        lax.all_gather(w_out, ("shard", "ctx"), axis=1, tiled=True),
    )
    group_seg, group_pos = (
        lax.all_gather(seg_ids, "ctx", axis=0, tiled=True),
        lax.all_gather(positions, "ctx", axis=0, tiled=True),
    )
    own_first, own_second = ancestry(seg_ids, parents)
    own_tags = (seg_ids, own_first, own_second, positions)
    inputs = tokens.astype(jnp.float32)
    norm_one, normed_one, inverse_one = norm_forward(inputs, ln_gain[0], ln_bias[0])
    act_one = norm_one.astype(jnp.bfloat16)
    projected = jnp.einsum("td,cde->cte", act_one, full_qkv, preferred_element_type=jnp.float32)
    qkv_bias = jnp.stack([b_qv[0], jnp.zeros((head_width,), jnp.float32), b_qv[1]])
    qkv_low = (projected + qkv_bias[:, None, :]).astype(jnp.bfloat16)
    query_flat, key_flat, value_flat = (qkv_low[0], qkv_low[1], qkv_low[2])
    group_keys, group_values = (
        lax.all_gather(key_flat, "ctx", axis=0, tiled=True),
        lax.all_gather(value_flat, "ctx", axis=0, tiled=True),
    )
    group_rows = group_keys.shape[0]
    block_count = group_rows // KEY_BLOCK
    key_blocks = group_keys.reshape(block_count, KEY_BLOCK, head_count, HD)
    value_blocks = group_values.reshape(block_count, KEY_BLOCK, head_count, HD)
    seg_blocks = group_seg.reshape(block_count, KEY_BLOCK)
    pos_blocks = group_pos.reshape(block_count, KEY_BLOCK)
    query_heads = query_flat.reshape(num_rows, head_count, HD)

    def stats_step(carry_in, block_parts):
        row_max, row_sum = carry_in
        key_part, seg_part, pos_part = block_parts
        scores, allowed = block_scores(
            query_heads, key_part, own_tags, (seg_part, pos_part), slopes
        )
        new_max = jnp.maximum(row_max, jnp.max(jnp.where(allowed, scores, NEG), axis=-1))
        shifted = jnp.where(allowed, scores - new_max[:, :, None], NEG)
        row_sum = row_sum * jnp.exp(row_max - new_max) + jnp.sum(jnp.exp(shifted), axis=-1)
        return ((new_max, row_sum), None)

    start_stats = (
        jnp.full((head_count, num_rows), NEG, jnp.float32),
        jnp.zeros((head_count, num_rows), jnp.float32),
    )
    (row_max, row_sum), _ = lax.scan(stats_step, start_stats, (key_blocks, seg_blocks, pos_blocks))

    def output_step(out_accum, block_parts):
        key_part, value_part, seg_part, pos_part = block_parts
        scores, allowed = block_scores(
            query_heads, key_part, own_tags, (seg_part, pos_part), slopes
        )
        prob_low = probabilities(scores, allowed, row_max, row_sum).astype(jnp.bfloat16)
        return (
            out_accum
            + jnp.einsum("hqk,khd->qhd", prob_low, value_part, preferred_element_type=jnp.float32),
            None,
        )

    attended, _ = lax.scan(
        output_step,
        jnp.zeros((num_rows, head_count, HD), jnp.float32),
        (key_blocks, value_blocks, seg_blocks, pos_blocks),
    )
    attended_low = attended.reshape(num_rows, head_width).astype(jnp.bfloat16)
    branch_one = (
        lax.psum(
            jnp.dot(attended_low, full_out, preferred_element_type=jnp.float32).astype(
                jnp.bfloat16
            ),
            "tp",
        ).astype(jnp.float32)
        + b_out
    )
    middle = inputs + branch_one
    full_up, full_down = (
        lax.all_gather(w_up, ("shard", "ctx"), axis=0, tiled=True),
        lax.all_gather(w_down, ("shard", "ctx"), axis=1, tiled=True),
    )
    norm_two, normed_two, inverse_two = norm_forward(middle, ln_gain[1], ln_bias[1])
    act_two = norm_two.astype(jnp.bfloat16)
    upper_in = jnp.dot(act_two, full_up, preferred_element_type=jnp.float32) + b_up
    gelu_vals, gelu_pull = jax.vjp(partial(jax.nn.gelu, approximate=True), upper_in)
    hidden = gelu_vals.astype(jnp.bfloat16)
    branch_two = (
        lax.psum(
            jnp.dot(hidden, full_down, preferred_element_type=jnp.float32).astype(jnp.bfloat16),
            "tp",
        ).astype(jnp.float32)
        + b_down
    )
    result = (middle + branch_two).astype(jnp.bfloat16)
    grad_out = cotangent.astype(jnp.float32)
    grad_hidden = jnp.einsum("td,fd->tf", cotangent, full_down, preferred_element_type=jnp.float32)
    grad_upper = gelu_pull(grad_hidden)[0].astype(jnp.bfloat16)
    down_term = jnp.einsum("tf,td->fd", hidden, cotangent, preferred_element_type=jnp.float32)
    up_term = jnp.einsum("td,tf->df", act_two, grad_upper, preferred_element_type=jnp.float32)
    grad_w_up, grad_w_down = (
        lax.psum_scatter(up_term, ("shard", "ctx"), scatter_dimension=0, tiled=True),
        lax.psum_scatter(down_term, ("shard", "ctx"), scatter_dimension=1, tiled=True),
    )
    grad_norm_two = lax.psum(
        jnp.einsum("tf,df->td", grad_upper, full_up, preferred_element_type=jnp.float32).astype(
            jnp.bfloat16
        ),
        "tp",
    ).astype(jnp.float32)
    grad_middle = grad_out + norm_backward(grad_norm_two, normed_two, inverse_two, ln_gain[1])
    grad_branch = grad_middle.astype(jnp.bfloat16)
    out_term = jnp.einsum(
        "te,td->ed", attended_low, grad_branch, preferred_element_type=jnp.float32
    )
    grad_att = jnp.einsum(
        "td,ed->te", grad_branch, full_out, preferred_element_type=jnp.float32
    ).astype(jnp.bfloat16)
    grad_heads = grad_att.reshape(num_rows, head_count, HD)
    row_terms = jnp.einsum("qhd,qhd->hq", grad_heads.astype(jnp.float32), attended)

    def joint_step(grad_accum, block_parts):
        key_part, value_part, seg_part, pos_part = block_parts
        scores, allowed = block_scores(
            query_heads, key_part, own_tags, (seg_part, pos_part), slopes
        )
        prob_vals = probabilities(scores, allowed, row_max, row_sum)
        grad_probs = jnp.einsum(
            "qhd,khd->hqk", grad_heads, value_part, preferred_element_type=jnp.float32
        )
        grad_scores = (prob_vals * (grad_probs - row_terms[:, :, None])).astype(jnp.bfloat16)
        grad_accum = (
            grad_accum
            + jnp.einsum("hqk,khd->qhd", grad_scores, key_part, preferred_element_type=jnp.float32)
            * scale
        )
        key_part_grad = (
            jnp.einsum("hqk,qhd->khd", grad_scores, query_heads, preferred_element_type=jnp.float32)
            * scale
        )
        value_part_grad = jnp.einsum(
            "hqk,qhd->khd",
            prob_vals.astype(jnp.bfloat16),
            grad_heads,
            preferred_element_type=jnp.float32,
        )
        return (
            grad_accum,
            (
                key_part_grad.reshape(KEY_BLOCK, head_width),
                value_part_grad.reshape(KEY_BLOCK, head_width),
            ),
        )

    grad_query_sum, (key_terms, value_terms) = lax.scan(
        joint_step,
        jnp.zeros((num_rows, head_count, HD), jnp.float32),
        (key_blocks, value_blocks, seg_blocks, pos_blocks),
    )
    key_grad_sum, value_grad_sum = (
        lax.psum_scatter(
            key_terms.reshape(group_rows, head_width).astype(jnp.bfloat16),
            "ctx",
            scatter_dimension=0,
            tiled=True,
        ).astype(jnp.float32),
        lax.psum_scatter(
            value_terms.reshape(group_rows, head_width).astype(jnp.bfloat16),
            "ctx",
            scatter_dimension=0,
            tiled=True,
        ).astype(jnp.float32),
    )
    grad_query_low = grad_query_sum.reshape(num_rows, head_width).astype(jnp.bfloat16)
    grad_key_low = key_grad_sum.astype(jnp.bfloat16)
    grad_value_low = value_grad_sum.astype(jnp.bfloat16)
    grad_qkv = jnp.stack([grad_query_low, grad_key_low, grad_value_low])
    grad_norm_one = lax.psum(
        jnp.einsum("cte,cde->td", grad_qkv, full_qkv, preferred_element_type=jnp.float32).astype(
            jnp.bfloat16
        ),
        "tp",
    ).astype(jnp.float32)
    grad_tokens = grad_middle + norm_backward(grad_norm_one, normed_one, inverse_one, ln_gain[0])
    qkv_term = jnp.einsum("td,cte->cde", act_one, grad_qkv, preferred_element_type=jnp.float32)
    grad_w_qkv, grad_w_out = (
        lax.psum_scatter(qkv_term, ("shard", "ctx"), scatter_dimension=1, tiled=True),
        lax.psum_scatter(out_term, ("shard", "ctx"), scatter_dimension=1, tiled=True),
    )
    bias_qv_part = jnp.stack(
        [
            jnp.sum(grad_query_low.astype(jnp.float32), axis=0),
            jnp.sum(grad_value_low.astype(jnp.float32), axis=0),
        ]
    )
    out_bias_part = jnp.sum(grad_branch.astype(jnp.float32), axis=0)
    up_bias_part = jnp.sum(grad_upper.astype(jnp.float32), axis=0)
    down_bias_part = jnp.sum(grad_out, axis=0)
    gain_part = jnp.stack(
        [jnp.sum(grad_norm_one * normed_one, axis=0), jnp.sum(grad_norm_two * normed_two, axis=0)]
    )
    shift_part = jnp.stack([jnp.sum(grad_norm_one, axis=0), jnp.sum(grad_norm_two, axis=0)])
    grad_b_qv, grad_b_out, grad_b_up, grad_b_down, grad_gain, grad_shift = lax.psum(
        (bias_qv_part, out_bias_part, up_bias_part, down_bias_part, gain_part, shift_part),
        ("shard", "ctx"),
    )
    return (
        result,
        grad_tokens,
        grad_w_qkv,
        grad_b_qv,
        grad_w_out,
        grad_b_out,
        grad_w_up,
        grad_b_up,
        grad_w_down,
        grad_b_down,
        grad_gain,
        grad_shift,
    )


def solution(mesh):
    placed = (
        P(("shard", "ctx"), None),
        P(("shard", "ctx"), None),
        P(("shard", "ctx")),
        P(("shard", "ctx")),
        P(),
        P(None, ("shard", "ctx"), "tp"),
        P(None, "tp"),
        P("tp", ("shard", "ctx")),
        P(),
        P(("shard", "ctx"), "tp"),
        P("tp"),
        P("tp", ("shard", "ctx")),
        P(),
        P(),
        P(),
    )
    sizes = dict(mesh.shape)
    paired = sizes["tp"] * sizes["ctx"] * 2 == HEADS and sizes["tp"] == 2 and sizes["shard"] == 4
    return jax.shard_map(
        fast_device if paired else per_device,
        mesh=mesh,
        in_specs=placed,
        out_specs=(
            P(("shard", "ctx"), None),
            P(("shard", "ctx"), None),
            P(None, ("shard", "ctx"), "tp"),
            P(None, "tp"),
            P("tp", ("shard", "ctx")),
            P(),
            P(("shard", "ctx"), "tp"),
            P("tp"),
            P("tp", ("shard", "ctx")),
            P(),
            P(),
            P(),
        ),
        check_vma=False,
    )
```

```python
from functools import partial

import jax
import jax.numpy as jnp
from jax import lax
from jax.experimental import pallas as pl
from jax.experimental.pallas import tpu as pltpu
from jax.sharding import PartitionSpec as P

HEADS = 16
HD = 64
KEY_BLOCK = 512
TRUNK = 1024
BRANCH = 128
SLOTS = 12
TREE = TRUNK + SLOTS * BRANCH
PAIR = 2 * HD

EPS = 1e-05
NEG = -1e30
LOG2E = 1.4426950408889634
MESH = pl.DeviceIdType.MESH
BF = jnp.bfloat16
F32 = jnp.float32
ROWS_WAVE = 4
FRONT_LIMIT = 62 << 20
BLOCK = 512
CURVE = 0.044715
ROOT = 0.7978845608028654
SUBS = 2


def nt(left, right):
    return lax.dot_general(left, right, (((1,), (1,)), ((), ())), preferred_element_type=F32)


def nn(left, right):
    return lax.dot_general(left, right, (((1,), (0,)), ((), ())), preferred_element_type=F32)


def rcopy(src, dst, send, recv, device):
    return pltpu.make_async_remote_copy(
        src_ref=src, dst_ref=dst, send_sem=send, recv_sem=recv, device_id=device, device_id_type=MESH
    )


def greet(devices):
    barrier = pltpu.get_barrier_semaphore()
    for device in devices:
        pl.semaphore_signal(barrier, inc=1, device_id=device, device_id_type=MESH)
    pl.semaphore_wait(barrier, len(devices))


def norm_rows(values, gain_row, shift_row):
    centre = values - jnp.mean(values, axis=-1, keepdims=True)
    inverse = lax.rsqrt(jnp.mean(centre * centre, axis=-1, keepdims=True) + EPS)
    normed = centre * inverse
    return normed * gain_row + shift_row, normed, inverse


def norm_rows_back(grad_in, normed, inverse, gain_row):
    scaled = grad_in * gain_row
    mean_grad = jnp.mean(scaled, axis=-1, keepdims=True)
    mean_cross = jnp.mean(scaled * normed, axis=-1, keepdims=True)
    return inverse * (scaled - mean_grad - normed * mean_cross)


def head_masks():
    lane = lax.broadcasted_iota(jnp.int32, (1, PAIR), 1)
    first = (lane < HD).astype(F32).astype(BF)
    second = (lane >= HD).astype(F32).astype(BF)
    return first, second


def stack_heads(rows):
    first, second = head_masks()
    return jnp.concatenate([rows * first, rows * second], axis=0)


def unstack_turned(turned, rows):
    return jnp.concatenate([turned[:HD, :rows], turned[HD:, rows:]], axis=0).T


def key_features(high, low, flag, rows):
    lane = lax.broadcasted_iota(jnp.int32, (rows, 128), 1)
    feats = jnp.where(lane < 3, high, jnp.where(lane < 6, low, jnp.where(lane == 6, flag, 0.0)))
    return feats.astype(BF)


def query_features(slope_ref, rows):
    return jnp.concatenate(
        [
            jnp.broadcast_to(slope_ref[0:1, :], (rows, 128)),
            jnp.broadcast_to(slope_ref[1:2, :], (rows, 128)),
        ],
        axis=0,
    ).astype(BF)


def fill_trunk_keys(key_ref, keys_aug):
    keys_aug[:, 0:PAIR] = key_ref[0:TRUNK, :]
    pos = lax.broadcasted_iota(jnp.int32, (TRUNK, 128), 0)
    low = pos & 255
    keys_aug[:, PAIR:] = key_features((pos - low).astype(F32), low.astype(F32), 0.0, TRUNK)


def fill_labels(info_all, blocks, labels, parents):
    labels[...] = jnp.full(labels.shape, -1.0, F32)
    parents[...] = jnp.full(parents.shape, -2.0, F32)
    for slot in range(SLOTS):
        block = TRUNK // BRANCH + slot
        owner, inner = block // blocks, block % blocks
        labels[slot : slot + 1, :] = info_all[owner, inner : inner + 1, :]
        parents[slot : slot + 1, :] = info_all[owner, 8 + inner : 9 + inner, :]


def parent_pick(slot, labels, parents, key_ref, value_ref):
    mine = parents[pl.ds(slot, 1), :]
    leaf = jnp.zeros((1, 128), F32)
    key_sum = jnp.zeros((BRANCH, PAIR), BF)
    value_sum = jnp.zeros((BRANCH, PAIR), BF)
    for other in range(SLOTS):
        same = (mine == labels[other : other + 1, :]).astype(F32)
        leaf = leaf + same
        same_low = same.astype(BF)
        at = TRUNK + other * BRANCH
        key_sum = key_sum + same_low * key_ref[at : at + BRANCH, :]
        value_sum = value_sum + same_low * value_ref[at : at + BRANCH, :]
    return leaf, key_sum, value_sum


def segment_key_features(leaf):
    row = lax.broadcasted_iota(jnp.int32, (BRANCH, 128), 0).astype(F32)
    own = key_features(float(TRUNK), row + leaf * float(BRANCH), 0.0, BRANCH)
    above = key_features(float(TRUNK), row, (leaf - 1.0) * 1e30, BRANCH)
    return own, above


def causal(rows):
    key = lax.broadcasted_iota(jnp.int32, (rows, rows), 0)
    query = lax.broadcasted_iota(jnp.int32, (rows, rows), 1)
    once = key <= query
    return jnp.concatenate([once, once], axis=1)


class Spread:
    def __init__(self, full, dims, depth, cols, sems, doubling=True):
        self.doubling = doubling
        self.full, self.depth, self.cols = full, depth, cols
        self.ns, self.nz, _ = dims
        self.s, self.z = lax.axis_index("shard"), lax.axis_index("ctx")
        self.zs, self.zr, self.xs, self.xr, self.cs, self.cr = sems

    def rows(self, shard, place):
        at = pl.multiple_of((shard * self.nz + place) * self.depth, self.depth)
        return self.full.at[pl.ds(at, self.depth), self.cols]

    def flip(self, bits):
        low = lax.rem(self.s, 2)
        high = lax.div(self.s, 2)
        if bits & 1:
            low = 1 - low
        if bits & 2:
            high = 1 - high
        return 2 * high + low

    def source(self, d):
        low, high = lax.rem(self.z, 2), lax.div(self.z, 2)
        low = 1 - low if d & 1 else low
        high = 1 - high if d & 2 else high
        return 2 * high + low

    def z_copy(self, d):
        ref = self.rows(self.s, self.source(2 if self.doubling and d == 3 else 0))
        to = self.source(1 if self.doubling and d == 3 else d)
        return rcopy(ref, ref, self.zs.at[d - 1], self.zr.at[d - 1], {"ctx": to})

    def x_copy(self, d):
        ref = self.rows(self.s, self.source(d))
        return rcopy(ref, ref, self.xs.at[d], self.xr.at[d], {"shard": self.flip(2)})

    def c_copy(self, far, d):
        ref = self.rows(self.flip(2) if far else self.s, self.source(d))
        return rcopy(ref, ref, self.cs.at[far, d], self.cr.at[far, d], {"shard": self.flip(1)})

    def z_start(self):
        self.z_copy(2).start()
        self.z_copy(1).start()
        if not self.doubling:
            self.z_copy(3).start()

    def own(self):
        self.x_copy(0).start()
        self.c_copy(0, 0).start()

    def z_done(self, d):
        ref = self.rows(self.s, self.source(d))
        rcopy(ref, ref, self.zs.at[d - 1], self.zr.at[d - 1], {"ctx": self.source(1)}).wait_recv()
        if self.doubling and d == 2:
            self.z_copy(3).start()
        self.x_copy(d).start()
        self.c_copy(0, d).start()

    def x_done(self, d):
        ref = self.rows(self.flip(2), self.source(d))
        rcopy(ref, ref, self.xs.at[d], self.xr.at[d], {"shard": self.flip(2)}).wait_recv()
        self.c_copy(1, d).start()

    def c_done(self, far, d):
        ref = self.rows(self.flip(3) if far else self.flip(1), self.source(d))
        rcopy(ref, ref, self.cs.at[far, d], self.cr.at[far, d], {"shard": self.flip(1)}).wait_recv()

    def all_here(self):
        for d in range(self.nz):
            self.c_done(0, d)
            self.c_done(1, d)

    def finish(self):
        for d in range(self.nz):
            if d:
                self.z_copy(d).wait_send()
            self.x_copy(d).wait_send()
            self.c_copy(0, d).wait_send()
            self.c_copy(1, d).wait_send()


def spread_sems(nz):
    return [dma(nz - 1), dma(nz - 1), dma(nz), dma(nz), dma(2, nz), dma(2, nz)]


def vmem():
    return pl.BlockSpec(memory_space=pltpu.VMEM)


def shape(dims, kind):
    return jax.ShapeDtypeStruct(dims, kind)


def dma(*dims):
    return pltpu.SemaphoreType.DMA(dims)


def front_kernel(
    dims,
    tok,
    w_up,
    w_out,
    w_down,
    cot_in,
    wq3,
    info,
    bias_qv,
    slopes,
    gain,
    shift,
    b_out,
    b_up,
    act_turned,
    query,
    key,
    value,
    out_heads,
    lse,
    info_all,
    wqkv,
    core_in,
    ga_all,
    down_part,
    mid,
    gmid,
    sums,
    wfull,
    wq,
    att,
    tree,
    wcat,
    keys_aug,
    values_turned,
    labels,
    parents,
    cot,
    far,
    act,
    gbranch,
    g_send,
    g_recv,
    ga_send,
    bup_acc,
    info_send,
    info_recv,
    wz_send,
    wz_recv,
    ws_send,
    ws_recv,
    z_send,
    z_recv,
    y_send,
    y_recv,
    a_send,
    a_recv,
    local_sem,
    b_send,
    b_recv,
    t_send,
    t_recv,
    gs_sem,
    gr_sem,
    as_sem,
    ar_sem,
    cs_sem,
    cr_sem,
    *spread,
):
    ns, nz, rows = dims
    s, z, y = lax.axis_index("shard"), lax.axis_index("ctx"), lax.axis_index("tp")
    half = rows // 2
    sub = half // SUBS
    depth = wq.shape[0]
    wide = 3 * PAIR
    my_rows = pl.ds(pl.multiple_of((s * nz + z) * depth, depth), depth)
    units, inner = w_up.shape[1], w_out.shape[1]
    own_cols = pl.multiple_of(2 * units + y * inner, 128)
    starts = [
        pltpu.make_async_copy(tok, tree.at[pl.ds(pl.multiple_of(z * rows, 128), rows), :], local_sem.at[0]),
        pltpu.make_async_copy(w_up, wfull.at[my_rows, 0:units], local_sem.at[1]),
        pltpu.make_async_copy(w_down, wfull.at[my_rows, units : 2 * units], local_sem.at[2]),
        pltpu.make_async_copy(w_out, wfull.at[my_rows, pl.ds(own_cols, inner)], local_sem.at[3]),
    ]
    given_load = pltpu.make_async_copy(cot_in, cot, local_sem.at[4])
    given_load.start()
    for one in starts:
        one.start()
    for to in range(nz):
        for part in range(3):
            wq[:, to * wide + part * PAIR : to * wide + (part + 1) * PAIR] = wq3[
                part, :, to * PAIR : (to + 1) * PAIR
            ]
    greet(
        [{"ctx": lax.rem(z + d, nz)} for d in range(1, nz)]
        + [{"shard": lax.rem(s + d, ns)} for d in range(1, ns)]
        + [{"tp": 1 - y}]
    )
    ups = Spread(wfull, dims, depth, slice(0, units), spread[:6])
    downs = Spread(wfull, dims, depth, slice(units, 2 * units), spread[6:12])
    weights = Spread(wqkv, dims, depth, slice(None), spread[18:])
    outer = Spread(wfull, dims, depth, pl.ds(own_cols, inner), spread[12:18], False)

    def info_copy(d):
        return rcopy(
            info, info_all.at[z], info_send.at[d - 1], info_recv.at[d - 1], {"ctx": lax.rem(z + d, nz)}
        )

    def wz_copy(d):
        to = lax.rem(z + d, nz)
        return rcopy(
            wq.at[:, pl.ds(pl.multiple_of(to * wide, 128), wide)],
            wcat.at[my_rows, :],
            wz_send.at[d - 1],
            wz_recv.at[d - 1],
            {"ctx": to},
        )

    shard_rows = pl.ds(s * (nz * depth), nz * depth)

    def ws_copy(d):
        return rcopy(
            wcat.at[shard_rows, :],
            wcat.at[shard_rows, :],
            ws_send.at[d - 1],
            ws_recv.at[d - 1],
            {"shard": lax.rem(s + d, ns)},
        )

    wqkv[my_rows, :] = wq[...]
    for d in range(1, nz):
        wz_copy(d).start()
    for d in range(1, nz):
        info_copy(d).start()
    wcat[my_rows, :] = wq[:, pl.ds(pl.multiple_of(z * wide, 128), wide)]
    info_all[z] = info[...]
    for one in starts:
        one.wait()

    def piece(block, second, part):
        at = block * rows + jnp.where(second, 1 - y, y) * half + part * sub
        return tree.at[pl.ds(pl.multiple_of(at, 32), sub), :]

    def z_copy(direction, k, part):
        block = z - k if direction == 0 else z + k
        to = z + 1 if direction == 0 else z - 1
        ref = piece(block, False, part)
        return rcopy(ref, ref, z_send.at[direction, k, part], z_recv.at[direction, k, part], {"ctx": to})

    def z_arrival(direction, k, part):
        block = z - k if direction == 0 else z + k
        ref = piece(block, False, part)
        return rcopy(
            ref, ref, z_send.at[direction, k - 1, part], z_recv.at[direction, k - 1, part], {"ctx": z}
        )

    def y_copy(direction, k, part):
        block = z - k if direction == 0 else z + k
        ref = piece(block, False, part)
        return rcopy(
            ref, ref, y_send.at[direction, k - 1, part], y_recv.at[direction, k - 1, part], {"tp": 1 - y}
        )

    def y_arrival(direction, k, part):
        block = z - k if direction == 0 else z + k
        ref = piece(block, True, part)
        return rcopy(
            ref, ref, y_send.at[direction, k - 1, part], y_recv.at[direction, k - 1, part], {"tp": 1 - y}
        )

    def place(direction, k):
        block = z - k if direction == 0 else z + k
        nxt = z + 1 if direction == 0 else z - 1
        here = (block >= 0) & (block < nz)
        onward = here & (nxt >= 0) & (nxt < nz)
        return block, here, onward

    def forward(k, first):
        for part in range(SUBS):
            for direction in range(2):
                _, here, onward = place(direction, k)
                if not first:

                    @pl.when(here)
                    def _():
                        z_arrival(direction, k, part).wait_recv()

                @pl.when(onward & (k < nz - 1))
                def _():
                    z_copy(direction, k, part).start()

                if not first:

                    @pl.when(here)
                    def _():
                        y_copy(direction, k, part).start()

    forward(0, True)
    outer.own()
    ups.own()
    downs.own()
    for d in range(1, nz):
        wz_copy(d).wait_recv()
    for d in range(1, ns):
        ws_copy(d).start()

    bias_at = pl.ds(pl.multiple_of(z * PAIR, 128), PAIR)
    bias_q = bias_qv[0:1, bias_at]
    bias_v = bias_qv[1:2, bias_at]

    def project(k):
        def side(direction, inner_carry):
            block = z + (2 * direction - 1) * k

            @pl.when((block >= 0) & (block < nz) & ((k > 0) | (direction == 0)))
            def _():
                def tile(t, carry):
                    here = pl.ds(pl.multiple_of(block * rows + t * 128, 128), 128)
                    act = norm_rows(tree[here, :].astype(F32), gain[0:1, :], shift[0:1, :])[0].astype(BF)
                    act_turned[:, here] = act.T
                    both = nn(act, wcat[...])
                    query[here, :] = (
                        (both[:, :PAIR] + bias_q).astype(BF).astype(F32) * HD ** (-0.5)
                    ).astype(BF)
                    key[here, :] = both[:, PAIR : 2 * PAIR].astype(BF)
                    value[here, :] = (both[:, 2 * PAIR :] + bias_v).astype(BF)
                    return carry

                lax.fori_loop(0, rows // 128, tile, 0)

            return inner_carry

        lax.fori_loop(0, 2, side, 0)

    def shared(k):
        for part in range(SUBS):
            for direction in range(2):
                _, here, _ = place(direction, k)

                @pl.when(here)
                def _():
                    y_arrival(direction, k, part).wait_recv()

    forward(1, False)
    for d in range(1, ns):
        ws_copy(d).wait_recv()
    project(0)

    def wave(k, carry):
        forward(k, False)

        @pl.when(k == nz - 2)
        def _():
            outer.z_start()
            ups.z_start()
            downs.z_start()

        shared(k - 1)
        project(k - 1)
        return carry

    lax.fori_loop(2, nz, wave, 0)
    for d in (1, 3, 2):
        outer.z_done(d)
    shared(nz - 1)
    project(nz - 1)
    for d in (0, 1, 3, 2):
        outer.x_done(d)
    ups.z_done(2)
    ups.z_done(1)

    for d in range(1, nz):
        info_copy(d).wait_recv()

    fill_labels(info_all, rows // BRANCH, labels, parents)
    fill_trunk_keys(key, keys_aug)
    values_turned[...] = value[0:TRUNK, :].T

    def att_cols(half_at, owner):
        return pl.ds(pl.multiple_of(half_at * inner + owner * PAIR, 128), PAIR)

    def att_copy(to):
        return rcopy(
            out_heads.at[pl.ds(to * rows, rows), :],
            att.at[:, att_cols(y, z)],
            a_send.at[to],
            a_recv.at[z],
            {"ctx": to},
        )

    def pass_on(owner):
        return rcopy(
            att.at[:, att_cols(y, owner)],
            att.at[:, att_cols(y, owner)],
            b_send.at[owner],
            b_recv.at[owner],
            {"tp": 1 - y},
        )

    half_rows = pl.ds(pl.multiple_of(lax.rem(s, 2) * (ns * nz * depth // 2), 128), ns * nz * depth // 2)
    far_rows = pl.ds(pl.multiple_of((1 - lax.rem(s, 2)) * (ns * nz * depth // 2), 128), ns * nz * depth // 2)
    far_cols = pl.ds(pl.multiple_of(2 * units + (1 - y) * inner, 128), inner)

    def plane_copy():
        ref = wfull.at[half_rows, pl.ds(own_cols, inner)]
        return rcopy(ref, ref, t_send.at[0], t_recv.at[0], {"tp": 1 - y})

    def plane_arrival():
        ref = wfull.at[half_rows, far_cols]
        return rcopy(ref, ref, t_send.at[0], t_recv.at[0], {"tp": 1 - y})

    def core_copy():
        ref = wfull.at[half_rows, far_cols]
        return rcopy(ref, ref, t_send.at[1], t_recv.at[1], {"shard": outer.flip(1)})

    def core_arrival():
        ref = wfull.at[far_rows, far_cols]
        return rcopy(ref, ref, t_send.at[1], t_recv.at[1], {"shard": outer.flip(1)})

    outer.all_here()
    plane_copy().start()

    def send_out(to):
        @pl.when(z != to)
        def _():
            att_copy(to).start()

        @pl.when(z == to)
        def _():
            att[:, att_cols(y, z)] = out_heads[to * rows : (to + 1) * rows, :]
            pass_on(z).start()

    tile_mask = causal(BRANCH)

    def segment(slot, carry):
        here = pl.ds(pl.multiple_of(TRUNK + slot * BRANCH, 128), BRANCH)
        asked = jnp.concatenate(
            [stack_heads(query[here, :]), query_features(slopes, BRANCH)], axis=1
        )
        leaf, key_up, value_up = parent_pick(slot, labels, parents, key, value)
        own_feats, up_feats = segment_key_features(leaf)
        trunk_part = nt(keys_aug[...], asked) * LOG2E
        own_part = nt(jnp.concatenate([key[here, :], own_feats], axis=1), asked) * LOG2E
        own_part = jnp.where(tile_mask, own_part, NEG)
        up_part = nt(jnp.concatenate([key_up, up_feats], axis=1), asked) * LOG2E
        top = jnp.maximum(
            jnp.max(trunk_part, axis=0, keepdims=True),
            jnp.maximum(
                jnp.max(own_part, axis=0, keepdims=True), jnp.max(up_part, axis=0, keepdims=True)
            ),
        )
        trunk_part = jnp.exp2(trunk_part - top)
        own_part = jnp.exp2(own_part - top)
        up_part = jnp.exp2(up_part - top)
        total = (
            jnp.sum(trunk_part, axis=0, keepdims=True)
            + jnp.sum(own_part, axis=0, keepdims=True)
            + jnp.sum(up_part, axis=0, keepdims=True)
        )
        turned = nn(values_turned[...], trunk_part.astype(BF))
        turned = turned + nn(value[here, :].T, own_part.astype(BF))
        turned = turned + nn(value_up.T, up_part.astype(BF))
        turned = turned / total
        out_heads[here, :] = unstack_turned(turned, BRANCH).astype(BF)
        lse[pl.ds(4 + slot, 1), 0 : 2 * BRANCH] = top + jnp.log2(total)
        return carry

    wave_rows = TRUNK // 4
    wave_mask = causal(wave_rows)

    def trunk_tile(tile):
        lo, hi = tile * wave_rows, (tile + 1) * wave_rows
        asked = jnp.concatenate(
            [stack_heads(query[lo:hi, :]), query_features(slopes, wave_rows)], axis=1
        )
        edge = jnp.where(wave_mask, nt(keys_aug[lo:hi, :], asked) * LOG2E, NEG)
        top = jnp.max(edge, axis=0, keepdims=True)
        if tile:
            body = nt(keys_aug[0:lo, :], asked) * LOG2E
            top = jnp.maximum(top, jnp.max(body, axis=0, keepdims=True))
            body = jnp.exp2(body - top)
        edge = jnp.exp2(edge - top)
        total = jnp.sum(edge, axis=0, keepdims=True)
        turned = nn(values_turned[:, lo:hi], edge.astype(BF))
        if tile:
            total = total + jnp.sum(body, axis=0, keepdims=True)
            turned = turned + nn(values_turned[:, 0:lo], body.astype(BF))
        turned = turned / total
        out_heads[lo:hi, :] = unstack_turned(turned, wave_rows).astype(BF)
        lse[tile : tile + 1, :] = top + jnp.log2(total)

    def segments(lo, hi):
        lax.fori_loop((lo - TRUNK) // BRANCH, (hi - TRUNK) // BRANCH, segment, 0)

    segments(2 * rows, 3 * rows)
    send_out(2)
    for tile in range(3):
        trunk_tile(tile)
    send_out(0)
    downs.z_done(2)
    segments(3 * rows, 4 * rows)
    send_out(3)
    trunk_tile(3)
    segments(TRUNK, 2 * rows)
    send_out(1)
    downs.z_done(1)
    ups.z_done(3)
    plane_arrival().wait_recv()
    core_copy().start()
    downs.z_done(3)
    for owner in range(nz):

        @pl.when(z != owner)
        def _():
            rcopy(
                out_heads.at[0:rows, :],
                att.at[:, att_cols(y, owner)],
                a_send.at[owner],
                a_recv.at[owner],
                {"ctx": owner},
            ).wait_recv()
            pass_on(owner).start()

    mid[...] = tree[pl.ds(pl.multiple_of(z * rows, 128), rows), :].astype(F32) + b_out[...]
    for d in (0, 2, 1, 3):
        ups.x_done(d)
    given_load.wait()
    for owner in range(nz):
        ref = att.at[:, att_cols(1 - y, owner)]
        rcopy(ref, ref, b_send.at[owner], b_recv.at[owner], {"tp": 1 - y}).wait_recv()
    core_arrival().wait_recv()
    ups.all_here()
    other = {"tp": 1 - y}
    chunk = rows // ROWS_WAVE
    width = act.shape[1]
    halves = units // width
    own_heads = pl.ds(pl.multiple_of(y * inner, 128), inner)
    own_wide = pl.ds(own_cols, inner)
    sums[...] = jnp.zeros(sums.shape, F32)
    bup_acc[...] = jnp.zeros(bup_acc.shape, F32)

    def at(i):
        return pl.ds(pl.multiple_of(i * chunk, 32), chunk)

    def g_copy(i):
        return rcopy(g_send.at[at(i), :], g_recv.at[at(i), :], gs_sem.at[i], gr_sem.at[i], other)

    def a_copy(i, d):
        to = lax.rem(z + d, nz)
        return rcopy(
            ga_send.at[at(i), pl.ds(pl.multiple_of(to * PAIR, 128), PAIR)],
            ga_all.at[pl.ds(pl.multiple_of(z * rows + i * chunk, 32), chunk), :],
            as_sem.at[d - 1, i],
            ar_sem.at[d - 1, i],
            {"ctx": to},
        )

    span = nz * depth
    parts = ((0, 2 * units), (2 * units, 2 * units + inner))

    def c_copy(part, index):
        lo, hi = parts[part]
        return rcopy(
            far.at[index, :, lo:hi],
            core_in.at[index, :, lo:hi],
            cs_sem.at[part, index],
            cr_sem.at[part, index],
            {"shard": weights.flip(1)},
        )

    sums[...] = jnp.zeros(sums.shape, F32)
    bup_acc[...] = jnp.zeros(bup_acc.shape, F32)
    per = width // BLOCK

    def spot(first, i, c):
        row = (first + lax.div(c, per)) * rows + i * chunk
        col = lax.rem(c, per) * BLOCK
        return pl.ds(pl.multiple_of(row, 32), chunk), pl.ds(pl.multiple_of(col, 128), BLOCK)

    def stage_one(i, carry):
        here = at(i)
        middle = mid[here, :] + nt(att[here, :], wfull[:, 2 * units :])
        mid[here, :] = middle
        act[here, :] = norm_rows(middle, gain[1:2, :], shift[1:2, :])[0].astype(BF)

        def columns(c, inner_carry):
            cols = pl.ds(pl.multiple_of(c * BLOCK, 128), BLOCK)
            upper = nn(act[here, :], wfull[:, cols]) + b_up[:, cols]
            square = upper * upper
            turn = jnp.tanh(ROOT * (upper + CURVE * (square * upper)))
            tree[spot(0, i, c)] = (0.5 * upper * (1.0 + turn)).astype(BF)
            steep = 0.5 * (1.0 + turn) + (0.5 * ROOT) * upper * (1.0 - turn * turn) * (
                1.0 + (3.0 * CURVE) * square
            )
            tree[spot(halves, i, c)] = steep.astype(BF)
            return inner_carry

        lax.fori_loop(0, units // BLOCK, columns, 0)
        return carry

    def stage_two(i, carry):
        here = at(i)

        def columns(c, inner_carry):
            cols = pl.ds(pl.multiple_of(c * BLOCK, 128), BLOCK)
            down_cols = pl.ds(pl.multiple_of(units + c * BLOCK, 128), BLOCK)
            slope = nn(cot[here, :], wfull[:, down_cols])
            low = (slope * tree[spot(halves, i, c)].astype(F32)).astype(BF)
            tree[spot(halves, i, c)] = low
            bup_acc[:, cols] += jnp.sum(low.astype(F32), axis=0, keepdims=True)
            return inner_carry

        lax.fori_loop(0, units // BLOCK, columns, 0)
        total = jnp.zeros((chunk, width), F32)
        for part in range(halves):
            total = total + nt(
                tree[spot(halves + part, i, 0)[0], :], wfull[:, part * width : (part + 1) * width]
            )
        g_send[here, :] = total.astype(BF)
        g_copy(i).start()
        return carry

    def drain(k, carry):
        for part in range(SUBS):
            for direction in range(2):
                _, here, onward = place(direction, k)

                @pl.when(onward & (k < nz - 1))
                def _():
                    z_copy(direction, k, part).wait_send()

                @pl.when(here & (k > 0))
                def _():
                    y_copy(direction, k, part).wait_send()

        return carry

    lax.fori_loop(0, nz, drain, 0)
    lax.fori_loop(0, 2, stage_one, 0)
    weights.own()
    weights.z_start()
    for d in (0, 2, 1, 3):
        downs.x_done(d)
    lax.fori_loop(2, ROWS_WAVE, stage_one, 0)
    downs.all_here()
    lax.fori_loop(0, ROWS_WAVE, stage_two, 0)
    for d in (2, 1, 3):
        weights.z_done(d)

    def group_cols(index, block):
        return pl.ds(pl.multiple_of(weights.flip(index) * span + block * 128, 128), 128)

    def products(cols):
        turned_act, turned_cot = act[:, cols].T, cot[:, cols].T
        for part in range(halves):
            lo = part * width
            yield lo, nn(turned_act, tree[(halves + part) * rows : (halves + part + 1) * rows, :])
            yield units + lo, nn(turned_cot, tree[part * rows : (part + 1) * rows, :])

    def each_block(act_on):
        for index in range(2):

            def one(block, carry):
                act_on(index, block)
                return carry

            lax.fori_loop(0, span // 128, one, 0)

    def far_one(index, block):
        target = pl.ds(pl.multiple_of(block * 128, 128), 128)
        for lo, value_block in products(group_cols((1, 3)[index], block)):
            far[index, target, lo : lo + width] = value_block.astype(BF)

    def near_one(index, block):
        target = pl.ds(pl.multiple_of(block * 128, 128), 128)
        for lo, value_block in products(group_cols((0, 2)[index], block)):
            here = slice(lo, lo + width)
            core_in[index, target, here] = (core_in[index, target, here].astype(F32) + value_block).astype(BF)

    def out_product(cols):
        return nn(gbranch[:, cols].T, att[:, own_heads])

    def far_two(index, block):
        target = pl.ds(pl.multiple_of(block * 128, 128), 128)
        far[index, target, 2 * units :] = out_product(group_cols((1, 3)[index], block)).astype(BF)

    def near_two(index, block):
        target = pl.ds(pl.multiple_of(block * 128, 128), 128)
        here = slice(2 * units, 2 * units + inner)
        core_in[index, target, here] = (
            core_in[index, target, here].astype(F32) + out_product(group_cols((0, 2)[index], block))
        ).astype(BF)

    def stage_c(i, carry):
        g_copy(i).wait_recv()
        here = at(i)
        grad = g_send[here, :].astype(F32) + g_recv[here, :].astype(F32)
        _, normed, inverse = norm_rows(mid[here, :], gain[1:2, :], shift[1:2, :])
        given = cot[here, :].astype(F32)
        grad_middle = given + norm_rows_back(grad, normed, inverse, gain[1:2, :])
        gmid[here, :] = grad_middle
        low = grad_middle.astype(BF)
        gbranch[here, :] = low
        sums[2:3, :] += jnp.sum(low.astype(F32), axis=0, keepdims=True)
        sums[3:4, :] += jnp.sum(given, axis=0, keepdims=True)
        sums[4:5, :] += jnp.sum(grad * normed, axis=0, keepdims=True)
        sums[5:6, :] += jnp.sum(grad, axis=0, keepdims=True)
        ga_send[here, :] = nn(low, wfull[:, own_wide]).astype(BF)
        for d in range(1, nz):
            a_copy(i, d).start()
        ga_all[pl.ds(pl.multiple_of(z * rows + i * chunk, 32), chunk), :] = ga_send[
            here, pl.ds(pl.multiple_of(z * PAIR, 128), PAIR)
        ]
        return carry

    lax.fori_loop(0, 1, stage_c, 0)
    each_block(far_one)
    for index in range(2):
        c_copy(0, index).start()
    lax.fori_loop(1, 2, stage_c, 0)
    for d in (0, 2, 1, 3):
        weights.x_done(d)
    def down(i, carry):
        total = jnp.zeros((chunk, width), F32)
        for part in range(halves):
            total = total + nt(
                tree[spot(part, i, 0)[0], :], wfull[:, units + part * width : units + (part + 1) * width]
            )
        down_part[at(i), :] = total.astype(BF)
        return carry

    lax.fori_loop(0, ROWS_WAVE, down, 0)
    lax.fori_loop(2, 3, stage_c, 0)
    for index in range(2):
        c_copy(0, index).wait_recv()
    each_block(near_one)
    lax.fori_loop(3, ROWS_WAVE, stage_c, 0)
    each_block(far_two)
    for index in range(2):
        c_copy(1, index).start()
    for index in range(2):
        c_copy(1, index).wait_recv()
    each_block(near_two)
    for part in range(halves):
        sums[part : part + 1, :] = bup_acc[:, part * width : (part + 1) * width]
    weights.all_here()
    weights.finish()
    for part in range(2):
        for index in range(2):
            c_copy(part, index).wait_send()

    def finish(i, carry):
        g_copy(i).wait_send()
        for d in range(1, nz):
            a_copy(i, d).wait_send()
            a_copy(i, d).wait_recv()
        return carry

    lax.fori_loop(0, ROWS_WAVE, finish, 0)
    plane_copy().wait_send()
    core_copy().wait_send()
    for owner in range(nz):
        pass_on(owner).wait_send()

    for owner in range(nz):

        @pl.when(z != owner)
        def _():
            att_copy(owner).wait_send()

    ups.finish()
    downs.finish()
    outer.finish()
    for d in range(1, nz):
        info_copy(d).wait_send()
        wz_copy(d).wait_send()
    for d in range(1, ns):
        ws_copy(d).wait_send()


def run_front(
    dims, tok, w_up, w_out, w_down, cot, wq3, info, bias_qv, slopes, gain, shift, b_out, b_up
):
    ns, nz, rows = dims
    width, units, inner, depth = tok.shape[1], w_up.shape[1], w_out.shape[1], wq3.shape[1]
    span, total, wide = nz * depth, 2 * units + inner, 3 * PAIR
    return pl.pallas_call(
        partial(front_kernel, dims),
        name="front",
        out_shape=(
            shape((width, TREE), BF),
            shape((TREE, PAIR), BF),
            shape((TREE, PAIR), BF),
            shape((TREE, PAIR), BF),
            shape((TREE, PAIR), BF),
            shape((16, 512), F32),
            shape((nz, 16, 128), F32),
            shape((width, nz * wide), BF),
            shape((2, span, total), BF),
            shape((TREE, PAIR), BF),
            shape((rows, width), BF),
            shape((rows, width), F32),
            shape((rows, width), F32),
            shape((8, width), F32),
        ),
        in_specs=[pl.BlockSpec(memory_space=pl.ANY)] * 5 + [vmem()] * 8,
        out_specs=[vmem()] * 14,
        scratch_shapes=[
            pltpu.VMEM((width, 2 * units + 2 * inner), BF),
            pltpu.VMEM((depth, nz * wide), BF),
            pltpu.VMEM((rows, 2 * inner), BF),
            pltpu.VMEM((TREE, width), BF),
            pltpu.VMEM((width, wide), BF),
            pltpu.VMEM((TRUNK, 2 * PAIR), BF),
            pltpu.VMEM((PAIR, TRUNK), BF),
            pltpu.VMEM((16, 128), F32),
            pltpu.VMEM((16, 128), F32),
            pltpu.VMEM((rows, width), BF),
            pltpu.VMEM((2, span, total), BF),
            pltpu.VMEM((rows, width), BF),
            pltpu.VMEM((rows, width), BF),
            pltpu.VMEM((rows, width), BF),
            pltpu.VMEM((rows, width), BF),
            pltpu.VMEM((rows, inner), BF),
            pltpu.VMEM((1, units), F32),
            dma(nz - 1),
            dma(nz - 1),
            dma(nz - 1),
            dma(nz - 1),
            dma(ns - 1),
            dma(ns - 1),
            dma(2, nz, SUBS),
            dma(2, nz, SUBS),
            dma(2, nz, SUBS),
            dma(2, nz, SUBS),
            dma(nz),
            dma(nz),
            dma(5),
            dma(nz),
            dma(nz),
            dma(2),
            dma(2),
            dma(ROWS_WAVE),
            dma(ROWS_WAVE),
            dma(nz - 1, ROWS_WAVE),
            dma(nz - 1, ROWS_WAVE),
            dma(2, 2),
            dma(2, 2),
            *spread_sems(nz),
            *spread_sems(nz),
            *spread_sems(nz),
            *spread_sems(nz),
        ],
        compiler_params=pltpu.CompilerParams(
            collective_id=0, has_side_effects=True, vmem_limit_bytes=FRONT_LIMIT
        ),
        cost_estimate=pl.CostEstimate(flops=40_000_000_000, bytes_accessed=20_000_000, transcendentals=0),
    )(tok, w_up, w_out, w_down, cot, wq3, info, bias_qv, slopes, gain, shift, b_out, b_up)


class Halve:
    def __init__(self, near, far, cols, dims, depth, bufs, sems):
        self.near, self.far, self.cols, self.depth = near, far, cols, depth
        self.nz = dims[1]
        self.s, self.z = lax.axis_index("shard"), lax.axis_index("ctx")
        self.x_in, self.a_in, self.b_out, self.b_in = bufs
        self.xs, self.xr, self.as_, self.ar, self.bs, self.br = sems

    def place(self, bits):
        low, high = lax.rem(self.z, 2), lax.div(self.z, 2)
        low = 1 - low if bits & 1 else low
        high = 1 - high if bits & 2 else high
        return 2 * high + low

    def block(self, bits):
        return pl.ds(pl.multiple_of(self.place(bits) * self.depth, self.depth), self.depth)

    def x_copy(self):
        low, high = lax.rem(self.s, 2), lax.div(self.s, 2)
        return rcopy(
            self.far.at[:, self.cols],
            self.x_in.at[:, self.cols],
            self.xs,
            self.xr,
            {"shard": 2 * (1 - high) + low},
        )

    def a_copy(self, index):
        return rcopy(
            self.near.at[self.block((1, 3)[index]), self.cols],
            self.a_in.at[index, :, self.cols],
            self.as_.at[index],
            self.ar.at[index],
            {"ctx": self.place(1)},
        )

    def b_copy(self):
        return rcopy(
            self.b_out.at[:, self.cols], self.b_in.at[:, self.cols], self.bs, self.br, {"ctx": self.place(2)}
        )

    def step_x(self):
        self.x_copy().wait_recv()

        def one(r, carry):
            here = pl.ds(pl.multiple_of(r * 32, 32), 32)
            self.near[here, self.cols] = (
                self.near[here, self.cols].astype(F32) + self.x_in[here, self.cols].astype(F32)
            ).astype(BF)
            return carry

        lax.fori_loop(0, self.near.shape[0] // 32, one, 0)
        self.a_copy(0).start()
        self.a_copy(1).start()

    def step_a(self):
        self.a_copy(0).wait_recv()
        self.a_copy(1).wait_recv()
        self.b_out[:, self.cols] = (
            self.near[self.block(2), self.cols].astype(F32) + self.a_in[1, :, self.cols].astype(F32)
        ).astype(BF)
        self.b_copy().start()

    def step_b(self):
        self.b_copy().wait_recv()
        return (
            self.near[self.block(0), self.cols].astype(F32)
            + self.a_in[0, :, self.cols].astype(F32)
            + self.b_in[:, self.cols].astype(F32)
        )

    def finish(self):
        self.x_copy().wait_send()
        self.a_copy(0).wait_send()
        self.a_copy(1).wait_send()
        self.b_copy().wait_send()


PIECES = 6


def back_kernel(
    dims,
    query,
    key,
    value,
    out_heads,
    lse,
    info_all,
    ga_all,
    act_turned,
    wqkv,
    partial_in,
    down_part,
    mid,
    b_down,
    gmid,
    tok,
    slopes,
    gain,
    shift,
    early,
    result,
    gtok,
    gup,
    gdown,
    gout,
    gwqkv,
    early_sum,
    late_sum,
    near,
    x_in,
    a_in,
    b_out,
    b_in,
    q_near,
    q_far,
    q_core,
    qx_in,
    q_all,
    dqkv,
    dk_trunk,
    dv_trunk,
    dk_seg,
    dv_seg,
    dk_up,
    dv_up,
    keys_aug,
    keys_turned,
    labels,
    parents,
    dq_all,
    n_send,
    n_recv,
    down_recv,
    wg_send,
    early_mine,
    early_recv,
    late,
    late_recv,
    d_sem,
    e_send,
    e_recv,
    f_send,
    f_recv,
    l_send,
    l_recv,
    p_send,
    p_recv,
    r_send,
    r_recv,
    ns_sem,
    nr_sem,
    xs_sem,
    xr_sem,
    as_sem,
    ar_sem,
    bs_sem,
    br_sem,
    qc_send,
    qc_recv,
    qx_sem,
    qz_send,
    qz_recv,
    n_local,
):
    ns, nz, rows = dims
    s, z, y = lax.axis_index("shard"), lax.axis_index("ctx"), lax.axis_index("tp")
    count = ns * nz
    me = s * nz + z
    chunk = rows // ROWS_WAVE
    width = tok.shape[1]
    depth = width // count
    span = nz * depth
    wide = 3 * PAIR
    other = {"tp": 1 - y}
    total_cols = near.shape[1]
    step_cols = total_cols // PIECES
    units = gup.shape[1]

    far = partial_in.at[1]
    load = pltpu.make_async_copy(partial_in.at[0], near, n_local)
    load.start()

    def peer(d):
        index = lax.rem(me + d, count)
        return index, {"shard": lax.div(index, nz), "ctx": lax.rem(index, nz)}

    greet([other] + [peer(d)[1] for d in range(1, count)])

    halves = [
        Halve(
            near,
            far,
            slice(i * step_cols, (i + 1) * step_cols),
            dims,
            depth,
            (x_in, a_in, b_out, b_in),
            (xs_sem.at[i], xr_sem.at[i], as_sem.at[i], ar_sem.at[i], bs_sem.at[i], br_sem.at[i]),
        )
        for i in range(PIECES)
    ]
    def shard_flip(bits):
        low, high = lax.rem(s, 2), lax.div(s, 2)
        low = 1 - low if bits & 1 else low
        high = 1 - high if bits & 2 else high
        return 2 * high + low

    def q_copy(index):
        return rcopy(
            wg_send.at[pl.ds(pl.multiple_of(shard_flip((1, 3)[index]) * span, 128), span), :],
            q_core.at[index],
            qc_send.at[index],
            qc_recv.at[index],
            {"shard": shard_flip(1)},
        )

    def qx_copy():
        return rcopy(q_far, qx_in, qx_sem.at[0], qx_sem.at[1], {"shard": shard_flip(2)})

    def qz_copy(d):
        to = lax.rem(z + d, nz)
        return rcopy(
            q_near.at[pl.ds(pl.multiple_of(to * depth, depth), depth), :],
            q_all.at[z],
            qz_send.at[d - 1],
            qz_recv.at[d - 1],
            {"ctx": to},
        )

    def q_spread():
        qx_copy().wait_recv()
        q_near[...] = (q_near[...].astype(F32) + qx_in[...].astype(F32)).astype(BF)
        for d in range(1, nz):
            qz_copy(d).start()
        q_all[z] = q_near[pl.ds(pl.multiple_of(z * depth, depth), depth), :]

    def down_copy():
        return rcopy(down_part, down_recv, d_sem.at[0], d_sem.at[1], other)

    owners = width // 128

    def owner_cols(index):
        return pl.ds(pl.multiple_of(index * 128, 128), 128)

    def early_copy(d):
        index, device = peer(d)
        return index, rcopy(
            early_mine.at[:, owner_cols(lax.rem(index, owners))],
            early_recv.at[me],
            e_send.at[d - 1],
            e_recv.at[d - 1],
            device,
        )

    def spread_copy(d):
        cols = owner_cols(lax.rem(me, owners))
        return rcopy(
            early_sum.at[:, cols], early_sum.at[:, cols], f_send.at[d - 1], f_recv.at[d - 1], peer(d)[1]
        )

    def spread_arrival(d):
        index = lax.rem(me + count - d, count)
        cols = owner_cols(lax.rem(index, owners))
        return index, rcopy(
            early_sum.at[:, cols], early_sum.at[:, cols], f_send.at[d - 1], f_recv.at[d - 1], other
        )

    def late_copy(d):
        return rcopy(late, late_recv.at[me], l_send.at[d - 1], l_recv.at[d - 1], peer(d)[1])

    def over_peers(act):
        def one(d, carry):
            act(d)
            return carry

        lax.fori_loop(1, count, one, 0)

    for half in halves:
        half.x_copy().start()
    down_copy().start()

    fill_labels(info_all, rows // BRANCH, labels, parents)
    fill_trunk_keys(key, keys_aug)
    keys_turned[...] = key[0:TRUNK, :].T
    dk_trunk[...] = jnp.zeros(dk_trunk.shape, F32)
    dv_trunk[...] = jnp.zeros(dv_trunk.shape, F32)
    tile_mask = causal(BRANCH)

    def row_products(here, count_rows):
        turned = (ga_all[here, :].astype(F32) * out_heads[here, :].astype(F32)).T
        return jnp.concatenate(
            [
                jnp.sum(turned[:HD, :], axis=0, keepdims=True),
                jnp.sum(turned[HD:, :], axis=0, keepdims=True),
            ],
            axis=1,
        )

    def part_back(key_aug, value_rows, asked, given, level, drow, mask):
        logits = nt(key_aug, asked) * LOG2E - level
        if mask is not None:
            logits = jnp.where(mask, logits, NEG)
        probs = jnp.exp2(logits)
        grads = (probs * (nt(value_rows, given) - drow)).astype(BF)
        return probs.astype(BF), grads

    def segment(slot, carry):
        here = pl.ds(pl.multiple_of(TRUNK + slot * BRANCH, 128), BRANCH)
        seg = pl.ds(pl.multiple_of(slot * BRANCH, 128), BRANCH)
        stacked = stack_heads(query[here, :])
        asked = jnp.concatenate([stacked, query_features(slopes, BRANCH)], axis=1)
        given = stack_heads(ga_all[here, :])
        leaf, key_up, value_up = parent_pick(slot, labels, parents, key, value)
        own_feats, up_feats = segment_key_features(leaf)
        level = lse[pl.ds(4 + slot, 1), 0 : 2 * BRANCH]
        drow = row_products(here, BRANCH)
        probs, grads = part_back(keys_aug[...], value[0:TRUNK, :], asked, given, level, drow, None)
        dv_trunk[...] += nn(probs, given)
        dk_trunk[...] += nn(grads, stacked)
        turned = nn(keys_turned[...], grads)
        key_own = key[here, :]
        probs, grads = part_back(
            jnp.concatenate([key_own, own_feats], axis=1), value[here, :], asked, given, level, drow, tile_mask
        )
        dv_seg[seg, :] = nn(probs, given)
        dk_seg[seg, :] = nn(grads, stacked)
        turned = turned + nn(key_own.T, grads)
        probs, grads = part_back(
            jnp.concatenate([key_up, up_feats], axis=1), value_up, asked, given, level, drow, None
        )
        dv_up[seg, :] = nn(probs, given)
        dk_up[seg, :] = nn(grads, stacked)
        turned = turned + nn(key_up.T, grads)
        dqkv[here, 0:PAIR] = (unstack_turned(turned, BRANCH) * HD ** (-0.5)).astype(BF)
        return carry

    def dq_copy(to):
        return rcopy(
            dqkv.at[to * rows : (to + 1) * rows, 0:PAIR],
            dq_all.at[:, pl.ds(pl.multiple_of(z * wide, 128), PAIR)],
            r_send.at[to],
            r_recv.at[z],
            {"ctx": to},
        )

    def send_dq(to):
        @pl.when(z != to)
        def _():
            dq_copy(to).start()

    def piece_copy(to, i):
        return rcopy(
            dqkv.at[to * rows + i * chunk : to * rows + (i + 1) * chunk, PAIR:],
            dq_all.at[i * chunk : (i + 1) * chunk, pl.ds(pl.multiple_of(z * wide + PAIR, 128), 2 * PAIR)],
            p_send.at[to, i],
            p_recv.at[z, i],
            {"ctx": to},
        )

    wave_rows = TRUNK // 4
    wave_mask = causal(wave_rows)
    for tile in range(4):
        lo, hi = tile * wave_rows, (tile + 1) * wave_rows
        stacked = stack_heads(query[lo:hi, :])
        asked = jnp.concatenate([stacked, query_features(slopes, wave_rows)], axis=1)
        given = stack_heads(ga_all[lo:hi, :])
        level = lse[tile : tile + 1, :]
        drow = row_products(pl.ds(lo, wave_rows), wave_rows)
        probs, grads = part_back(
            keys_aug[lo:hi, :], value[lo:hi, :], asked, given, level, drow, wave_mask
        )
        dv_trunk[lo:hi, :] += nn(probs, given)
        dk_trunk[lo:hi, :] += nn(grads, stacked)
        turned = nn(keys_turned[:, lo:hi], grads)
        if tile:
            probs, grads = part_back(
                keys_aug[0:lo, :], value[0:lo, :], asked, given, level, drow, None
            )
            dv_trunk[0:lo, :] += nn(probs, given)
            dk_trunk[0:lo, :] += nn(grads, stacked)
            turned = turned + nn(keys_turned[:, 0:lo], grads)
        dqkv[lo:hi, 0:PAIR] = (unstack_turned(turned, wave_rows) * HD ** (-0.5)).astype(BF)
    send_dq(0)

    def segments(lo, hi):
        lax.fori_loop((lo - TRUNK) // BRANCH, (hi - TRUNK) // BRANCH, segment, 0)

    segments(2 * rows, 3 * rows)
    send_dq(2)
    segments(TRUNK, 2 * rows)
    send_dq(1)
    load.wait()
    halves[0].step_x()
    segments(3 * rows, 4 * rows)
    halves[1].step_x()
    send_dq(3)

    def gather_up(slot, carry):
        here = pl.ds(pl.multiple_of(TRUNK + slot * BRANCH, 128), BRANCH)
        seg = pl.ds(pl.multiple_of(slot * BRANCH, 128), BRANCH)
        mine = labels[pl.ds(slot, 1), :]
        dk, dv = dk_seg[seg, :], dv_seg[seg, :]
        for below in range(SLOTS):
            same = (parents[below : below + 1, :] == mine).astype(F32)
            at = below * BRANCH
            dk = dk + same * dk_up[at : at + BRANCH, :]
            dv = dv + same * dv_up[at : at + BRANCH, :]
        dqkv[here, PAIR : 2 * PAIR] = dk.astype(BF)
        dqkv[here, 2 * PAIR :] = dv.astype(BF)
        return carry

    lax.fori_loop(0, SLOTS, gather_up, 0)
    dqkv[0:TRUNK, PAIR : 2 * PAIR] = dk_trunk[...].astype(BF)
    dqkv[0:TRUNK, 2 * PAIR :] = dv_trunk[...].astype(BF)
    for i in range(ROWS_WAVE):
        for to in range(nz):

            @pl.when(z != to)
            def _():
                piece_copy(to, i).start()

    for to in range(nz):

        @pl.when(z == to)
        def _():
            dq_all[:, pl.ds(pl.multiple_of(z * wide, 128), wide)] = dqkv[to * rows : (to + 1) * rows, :]

    def weight(block, carry):
        here = pl.ds(pl.multiple_of(block * 128, 128), 128)
        wg_send[here, :] = nn(act_turned[here, :], dqkv[...]).astype(BF)
        return carry

    lax.fori_loop(0, width // 128, weight, 0)
    q_copy(0).start()
    q_copy(1).start()

    early_mine[...] = early[...]
    early_mine[6:7, pl.ds(pl.multiple_of(z * PAIR, 128), PAIR)] = jnp.sum(
        dqkv[:, 0:PAIR].astype(F32), axis=0, keepdims=True
    )
    early_mine[6:7, pl.ds(pl.multiple_of((nz + z) * PAIR, 128), PAIR)] = jnp.sum(
        dqkv[:, 2 * PAIR :].astype(F32), axis=0, keepdims=True
    )

    def early_send(d):
        index, copy = early_copy(d)

        @pl.when(index < owners)
        def _():
            copy.start()

    over_peers(early_send)
    early_recv[me] = early_mine[:, owner_cols(lax.rem(me, owners))]

    def at(i):
        return pl.ds(pl.multiple_of(i * chunk, 32), chunk)

    def n_copy(i):
        return rcopy(n_send.at[at(i), :], n_recv.at[at(i), :], ns_sem.at[i], nr_sem.at[i], other)

    def core_join():
        for index in range(2):
            q_copy(index).wait_recv()
            mine = pl.ds(pl.multiple_of(shard_flip((0, 2)[index]) * span, 128), span)
            (q_near, q_far)[index][...] = (wg_send[mine, :].astype(F32) + q_core[index].astype(F32)).astype(BF)
        qx_copy().start()

    def first(i):
        for owner in range(nz):

            @pl.when(z != owner)
            def _():
                if i == 0:
                    rcopy(
                        dqkv.at[0:rows, 0:PAIR],
                        dq_all.at[:, owner * wide : owner * wide + PAIR],
                        r_send.at[owner],
                        r_recv.at[owner],
                        {"ctx": owner},
                    ).wait_recv()
                rcopy(
                    dqkv.at[0:chunk, PAIR:],
                    dq_all.at[i * chunk : (i + 1) * chunk, owner * wide + PAIR : (owner + 1) * wide],
                    p_send.at[owner, i],
                    p_recv.at[owner, i],
                    {"ctx": owner},
                ).wait_recv()

        n_send[at(i), :] = nt(dq_all[at(i), :], wqkv[...]).astype(BF)
        n_copy(i).start()

    def second(i, carry):
        n_copy(i).wait_recv()
        here = at(i)
        grad = n_send[here, :].astype(F32) + n_recv[here, :].astype(F32)
        _, normed, inverse = norm_rows(tok[here, :].astype(F32), gain[0:1, :], shift[0:1, :])
        gtok[here, :] = gmid[here, :] + norm_rows_back(grad, normed, inverse, gain[0:1, :])
        late[0:1, :] += jnp.sum(grad * normed, axis=0, keepdims=True)
        late[1:2, :] += jnp.sum(grad, axis=0, keepdims=True)
        return carry

    def output(i, carry):
        here = at(i)
        result[here, :] = (
            mid[here, :] + b_down[...] + (down_part[here, :].astype(F32) + down_recv[here, :].astype(F32))
        ).astype(BF)
        return carry

    late[...] = jnp.zeros(late.shape, F32)
    core_join()
    halves[2].step_x()
    first(0)
    first(1)
    halves[3].step_x()
    first(2)
    halves[4].step_x()
    first(3)
    halves[5].step_x()
    down_copy().wait_recv()
    lax.fori_loop(0, ROWS_WAVE, output, 0)

    @pl.when(me < owners)
    def _():
        over_peers(lambda d: early_copy(d)[1].wait_recv())
        total = early_recv[0]
        for index in range(1, count):
            total = total + early_recv[index]
        early_sum[:, owner_cols(lax.rem(me, owners))] = total
        over_peers(lambda d: spread_copy(d).start())

    q_spread()
    halves[0].step_a()
    halves[1].step_a()
    lax.fori_loop(0, 2, second, 0)
    halves[2].step_a()
    lax.fori_loop(2, ROWS_WAVE, second, 0)
    over_peers(lambda d: late_copy(d).start())
    late_recv[me] = late[...]
    halves[3].step_a()
    halves[4].step_a()
    halves[5].step_a()

    for d in range(1, nz):
        qz_copy(d).wait_recv()
    for owner in range(nz):
        for part in range(3):
            gwqkv[part, :, owner * PAIR : (owner + 1) * PAIR] = q_all[
                owner, :, part * PAIR : (part + 1) * PAIR
            ].astype(F32)
    bounds = (0, units, 2 * units, total_cols)
    for i, half in enumerate(halves):
        block = half.step_b()
        lo, hi = i * step_cols, (i + 1) * step_cols
        for target, start_at, end_at in (
            (gup, bounds[0], bounds[1]),
            (gdown, bounds[1], bounds[2]),
            (gout, bounds[2], bounds[3]),
        ):
            a, b = max(lo, start_at), min(hi, end_at)
            if a < b:
                target[:, a - start_at : b - start_at] = block[:, a - lo : b - lo]

    def early_wait(d):
        index, copy = spread_arrival(d)

        @pl.when(index < owners)
        def _():
            copy.wait_recv()

    over_peers(early_wait)
    over_peers(lambda d: late_copy(d).wait_recv())
    total = late_recv[0]
    for index in range(1, count):
        total = total + late_recv[index]
    late_sum[...] = total

    down_copy().wait_send()
    for half in halves:
        half.finish()
    qx_copy().wait_send()
    for d in range(1, nz):
        qz_copy(d).wait_send()
    q_copy(0).wait_send()
    q_copy(1).wait_send()

    def early_drain(d):
        index, copy = early_copy(d)

        @pl.when(index < owners)
        def _():
            copy.wait_send()

    over_peers(early_drain)

    @pl.when(me < owners)
    def _():
        over_peers(lambda d: spread_copy(d).wait_send())

    over_peers(lambda d: late_copy(d).wait_send())

    def finish(i, carry):
        n_copy(i).wait_send()
        return carry

    lax.fori_loop(0, ROWS_WAVE, finish, 0)
    for owner in range(nz):

        @pl.when(z != owner)
        def _():
            dq_copy(owner).wait_send()
            for i in range(ROWS_WAVE):
                piece_copy(owner, i).wait_send()


def run_back(dims, units, *inputs):
    ns, nz, rows = dims
    width = inputs[14].shape[1]
    _, span, total = inputs[9].shape
    count = ns * nz
    depth = width // count
    wide = 3 * PAIR
    anywhere = pl.BlockSpec(memory_space=pl.ANY)
    return pl.pallas_call(
        partial(back_kernel, dims),
        name="tree_backward",
        out_shape=(
            shape((rows, width), BF),
            shape((rows, width), F32),
            shape((depth, units), F32),
            shape((depth, units), F32),
            shape((depth, total - 2 * units), F32),
            shape((3, depth, nz * PAIR), F32),
            shape((8, width), F32),
            shape((2, width), F32),
        ),
        in_specs=[vmem()] * 9 + [anywhere] + [vmem()] * 9,
        out_specs=[vmem()] * 8,
        scratch_shapes=[
            pltpu.VMEM((span, total), BF),
            pltpu.VMEM((span, total), BF),
            pltpu.VMEM((2, depth, total), BF),
            pltpu.VMEM((depth, total), BF),
            pltpu.VMEM((depth, total), BF),
            pltpu.VMEM((span, wide), BF),
            pltpu.VMEM((span, wide), BF),
            pltpu.VMEM((2, span, wide), BF),
            pltpu.VMEM((span, wide), BF),
            pltpu.VMEM((nz, depth, wide), BF),
            pltpu.VMEM((TREE, wide), BF),
            pltpu.VMEM((TRUNK, PAIR), F32),
            pltpu.VMEM((TRUNK, PAIR), F32),
            pltpu.VMEM((TREE - TRUNK, PAIR), F32),
            pltpu.VMEM((TREE - TRUNK, PAIR), F32),
            pltpu.VMEM((TREE - TRUNK, PAIR), F32),
            pltpu.VMEM((TREE - TRUNK, PAIR), F32),
            pltpu.VMEM((TRUNK, 2 * PAIR), BF),
            pltpu.VMEM((PAIR, TRUNK), BF),
            pltpu.VMEM((16, 128), F32),
            pltpu.VMEM((16, 128), F32),
            pltpu.VMEM((rows, nz * wide), BF),
            pltpu.VMEM((rows, width), BF),
            pltpu.VMEM((rows, width), BF),
            pltpu.VMEM((rows, width), BF),
            pltpu.VMEM((width, wide), BF),
            pltpu.VMEM((8, width), F32),
            pltpu.VMEM((count, 8, 128), F32),
            pltpu.VMEM((2, width), F32),
            pltpu.VMEM((count, 2, width), F32),
            dma(2),
            dma(count - 1),
            dma(count - 1),
            dma(count - 1),
            dma(count - 1),
            dma(count - 1),
            dma(count - 1),
            dma(nz, ROWS_WAVE),
            dma(nz, ROWS_WAVE),
            dma(nz),
            dma(nz),
            dma(ROWS_WAVE),
            dma(ROWS_WAVE),
            dma(PIECES),
            dma(PIECES),
            dma(PIECES, 2),
            dma(PIECES, 2),
            dma(PIECES),
            dma(PIECES),
            dma(2),
            dma(2),
            dma(2),
            dma(nz - 1),
            dma(nz - 1),
            pltpu.SemaphoreType.DMA,
        ],
        compiler_params=pltpu.CompilerParams(
            collective_id=2, has_side_effects=True, vmem_limit_bytes=60 << 20
        ),
        cost_estimate=pl.CostEstimate(flops=40_000_000_000, bytes_accessed=20_000_000, transcendentals=0),
    )(*inputs)


def place_kernel(early, late, *refs):
    count = (len(refs) - 7) // 2
    sources, targets = refs[:count], refs[count : 2 * count]
    b_qv, b_out, b_up, b_down, gains, shifts, sems = refs[2 * count :]
    copies = [pltpu.make_async_copy(a, b, sems.at[k]) for k, (a, b) in enumerate(zip(sources, targets))]
    for copy in copies:
        copy.start()
    wide, width = b_qv.shape[1], b_out.shape[1]
    for row in range(2):
        b_qv[row : row + 1, :] = early[6:7, row * wide : (row + 1) * wide]
    b_out[...] = early[2:3, :]
    for row in range(b_up.shape[1] // width):
        b_up[:, row * width : (row + 1) * width] = early[row : row + 1, :]
    b_down[...] = early[3:4, :]
    gains[0:1, :] = late[0:1, :]
    gains[1:2, :] = early[4:5, :]
    shifts[0:1, :] = late[1:2, :]
    shifts[1:2, :] = early[5:6, :]
    for copy in copies:
        copy.wait()


def run_place(early, late, wide, units, *arrays):
    width = early.shape[1]
    anywhere = pl.BlockSpec(memory_space=pl.ANY)
    return pl.pallas_call(
        place_kernel,
        name="place",
        out_shape=(
            *[shape(a.shape, a.dtype) for a in arrays],
            shape((2, wide), F32),
            shape((1, width), F32),
            shape((1, units), F32),
            shape((1, width), F32),
            shape((2, width), F32),
            shape((2, width), F32),
        ),
        in_specs=[vmem()] * 2 + [anywhere] * len(arrays),
        out_specs=[anywhere] * len(arrays) + [vmem()] * 6,
        scratch_shapes=[dma(len(arrays))],
        compiler_params=pltpu.CompilerParams(vmem_limit_bytes=60 << 20),
    )(early, late, *arrays)


def fast_device(
    tokens, cotangent, seg_ids, positions, parents, w_qkv, b_qv, w_out, b_out, w_up, b_up, w_down, b_down, ln_gain, ln_bias
):
    rows = tokens.shape[0]
    ns, nz, ntp = lax.axis_size("shard"), lax.axis_size("ctx"), lax.axis_size("tp")
    dims = (ns, nz, rows)

    labels = seg_ids.reshape(rows // BRANCH, BRANCH)[:, 0]
    match = labels[:, None] == jnp.arange(parents.shape[0], dtype=jnp.int32)[None, :]
    above = jnp.sum(jnp.where(match, parents[None, :], 0), axis=1)
    fill = 8 - rows // BRANCH
    lines = jnp.concatenate([jnp.pad(labels, (0, fill)), jnp.pad(above, (0, fill))]).astype(F32)
    info = jnp.broadcast_to(lines[:, None], (16, 128))
    per = HEADS // ntp
    index = lax.axis_index("tp") * per + lax.axis_index("ctx") * 2 + jnp.arange(2)
    slope = 2.0 ** (-8.0 * (index.astype(F32) + 1.0) / HEADS)
    one = lax.reduce_precision(slope, 8, 7)
    two = lax.reduce_precision(slope - one, 8, 7)
    three = lax.reduce_precision(slope - one - two, 8, 7)
    table = jnp.stack([one, two, three, one, two, three, jnp.ones_like(one)], axis=1)
    slopes = jnp.pad(table, ((0, 0), (0, 121)))

    units = b_up.shape[0]
    (
        act_turned, query, key, value, out_heads, lse, info_all, wqkv, partial_sums, ga_all, down_part, mid, gmid, sums
    ) = run_front(
        dims, tokens, w_up, w_out.T, w_down.T, cotangent, w_qkv, info, b_qv, slopes, ln_gain, ln_bias,
        b_out[None, :], b_up[None, :],
    )
    result, grad_tokens, gup, gdown, gout, grad_w_qkv, early, late = run_back(
        dims, units, query, key, value, out_heads, lse, info_all, ga_all, act_turned, wqkv, partial_sums, down_part,
        mid, b_down[None, :], gmid, tokens, slopes, ln_gain, ln_bias, sums,
    )
    result, grad_tokens, grad_w_qkv, gup, gdown, gout, b_qv_sum, b_out_sum, b_up_sum, b_down_sum, gains, shifts = run_place(
        early, late, nz * PAIR, units, result, grad_tokens, grad_w_qkv, gup, gdown, gout
    )
    return (
        result,
        grad_tokens,
        grad_w_qkv,
        b_qv_sum,
        gout.T,
        b_out_sum.reshape(-1),
        gup,
        b_up_sum.reshape(-1),
        gdown.T,
        b_down_sum.reshape(-1),
        gains,
        shifts,
    )


def norm_forward(inputs_in, gain_row, shift_row):
    centre = inputs_in - jnp.mean(inputs_in, axis=-1, keepdims=True)
    inverse = lax.rsqrt(jnp.mean(centre * centre, axis=-1, keepdims=True) + EPS)
    normed = centre * inverse
    return (normed * gain_row + shift_row, normed, inverse)


def norm_backward(grad_in, normed, inverse, gain_row):
    scaled = grad_in * gain_row
    mean_grad = jnp.mean(scaled, axis=-1, keepdims=True)
    mean_cross = jnp.mean(scaled * normed, axis=-1, keepdims=True)
    return inverse * (scaled - mean_grad - normed * mean_cross)


def ancestry(seg_vals, parents):
    first_up = jnp.take(parents, seg_vals)
    return (first_up, jnp.take(parents, first_up))


def block_scores(query_heads, key_heads, query_tags, key_tags, slopes):
    q_seg, q_first, q_second, q_pos = query_tags
    k_seg, k_pos = key_tags
    raw_scores = jnp.einsum(
        "qhd,khd->hqk", query_heads, key_heads, preferred_element_type=jnp.float32
    ) * HD ** (-0.5)
    distance = (q_pos[:, None] - k_pos[None, :]).astype(jnp.float32)
    scores = raw_scores - slopes[:, None, None] * distance[None]
    related = (
        (k_seg[None, :] == q_seg[:, None])
        | (k_seg[None, :] == q_first[:, None])
        | (k_seg[None, :] == q_second[:, None])
    )
    allowed = related & (k_pos[None, :] <= q_pos[:, None])
    return (scores, allowed[None])


def probabilities(scores, allowed, row_max, row_sum):
    shifted = jnp.where(allowed, scores - row_max[:, :, None], NEG)
    return jnp.exp(shifted) / row_sum[:, :, None]


def per_device(
    tokens,
    cotangent,
    seg_ids,
    positions,
    parents,
    w_qkv,
    b_qv,
    w_out,
    b_out,
    w_up,
    b_up,
    w_down,
    b_down,
    ln_gain,
    ln_bias,
):
    num_rows = tokens.shape[0]
    head_count = HEADS // lax.axis_size("tp")
    head_width = head_count * HD
    head_index = (lax.axis_index("tp") * head_count + jnp.arange(head_count)).astype(jnp.float32)
    slopes = 2.0 ** (-8.0 * (head_index + 1.0) / HEADS)
    scale = HD ** (-0.5)
    full_qkv, full_out = (
        lax.all_gather(w_qkv, ("shard", "ctx"), axis=1, tiled=True),
        lax.all_gather(w_out, ("shard", "ctx"), axis=1, tiled=True),
    )
    group_seg, group_pos = (
        lax.all_gather(seg_ids, "ctx", axis=0, tiled=True),
        lax.all_gather(positions, "ctx", axis=0, tiled=True),
    )
    own_first, own_second = ancestry(seg_ids, parents)
    own_tags = (seg_ids, own_first, own_second, positions)
    inputs = tokens.astype(jnp.float32)
    norm_one, normed_one, inverse_one = norm_forward(inputs, ln_gain[0], ln_bias[0])
    act_one = norm_one.astype(jnp.bfloat16)
    projected = jnp.einsum("td,cde->cte", act_one, full_qkv, preferred_element_type=jnp.float32)
    qkv_bias = jnp.stack([b_qv[0], jnp.zeros((head_width,), jnp.float32), b_qv[1]])
    qkv_low = (projected + qkv_bias[:, None, :]).astype(jnp.bfloat16)
    query_flat, key_flat, value_flat = (qkv_low[0], qkv_low[1], qkv_low[2])
    group_keys, group_values = (
        lax.all_gather(key_flat, "ctx", axis=0, tiled=True),
        lax.all_gather(value_flat, "ctx", axis=0, tiled=True),
    )
    group_rows = group_keys.shape[0]
    block_count = group_rows // KEY_BLOCK
    key_blocks = group_keys.reshape(block_count, KEY_BLOCK, head_count, HD)
    value_blocks = group_values.reshape(block_count, KEY_BLOCK, head_count, HD)
    seg_blocks = group_seg.reshape(block_count, KEY_BLOCK)
    pos_blocks = group_pos.reshape(block_count, KEY_BLOCK)
    query_heads = query_flat.reshape(num_rows, head_count, HD)

    def stats_step(carry_in, block_parts):
        row_max, row_sum = carry_in
        key_part, seg_part, pos_part = block_parts
        scores, allowed = block_scores(
            query_heads, key_part, own_tags, (seg_part, pos_part), slopes
        )
        new_max = jnp.maximum(row_max, jnp.max(jnp.where(allowed, scores, NEG), axis=-1))
        shifted = jnp.where(allowed, scores - new_max[:, :, None], NEG)
        row_sum = row_sum * jnp.exp(row_max - new_max) + jnp.sum(jnp.exp(shifted), axis=-1)
        return ((new_max, row_sum), None)

    start_stats = (
        jnp.full((head_count, num_rows), NEG, jnp.float32),
        jnp.zeros((head_count, num_rows), jnp.float32),
    )
    (row_max, row_sum), _ = lax.scan(stats_step, start_stats, (key_blocks, seg_blocks, pos_blocks))

    def output_step(out_accum, block_parts):
        key_part, value_part, seg_part, pos_part = block_parts
        scores, allowed = block_scores(
            query_heads, key_part, own_tags, (seg_part, pos_part), slopes
        )
        prob_low = probabilities(scores, allowed, row_max, row_sum).astype(jnp.bfloat16)
        return (
            out_accum
            + jnp.einsum("hqk,khd->qhd", prob_low, value_part, preferred_element_type=jnp.float32),
            None,
        )

    attended, _ = lax.scan(
        output_step,
        jnp.zeros((num_rows, head_count, HD), jnp.float32),
        (key_blocks, value_blocks, seg_blocks, pos_blocks),
    )
    attended_low = attended.reshape(num_rows, head_width).astype(jnp.bfloat16)
    branch_one = (
        lax.psum(
            jnp.dot(attended_low, full_out, preferred_element_type=jnp.float32).astype(
                jnp.bfloat16
            ),
            "tp",
        ).astype(jnp.float32)
        + b_out
    )
    middle = inputs + branch_one
    full_up, full_down = (
        lax.all_gather(w_up, ("shard", "ctx"), axis=0, tiled=True),
        lax.all_gather(w_down, ("shard", "ctx"), axis=1, tiled=True),
    )
    norm_two, normed_two, inverse_two = norm_forward(middle, ln_gain[1], ln_bias[1])
    act_two = norm_two.astype(jnp.bfloat16)
    upper_in = jnp.dot(act_two, full_up, preferred_element_type=jnp.float32) + b_up
    gelu_vals, gelu_pull = jax.vjp(partial(jax.nn.gelu, approximate=True), upper_in)
    hidden = gelu_vals.astype(jnp.bfloat16)
    branch_two = (
        lax.psum(
            jnp.dot(hidden, full_down, preferred_element_type=jnp.float32).astype(jnp.bfloat16),
            "tp",
        ).astype(jnp.float32)
        + b_down
    )
    result = (middle + branch_two).astype(jnp.bfloat16)
    grad_out = cotangent.astype(jnp.float32)
    grad_hidden = jnp.einsum("td,fd->tf", cotangent, full_down, preferred_element_type=jnp.float32)
    grad_upper = gelu_pull(grad_hidden)[0].astype(jnp.bfloat16)
    down_term = jnp.einsum("tf,td->fd", hidden, cotangent, preferred_element_type=jnp.float32)
    up_term = jnp.einsum("td,tf->df", act_two, grad_upper, preferred_element_type=jnp.float32)
    grad_w_up, grad_w_down = (
        lax.psum_scatter(up_term, ("shard", "ctx"), scatter_dimension=0, tiled=True),
        lax.psum_scatter(down_term, ("shard", "ctx"), scatter_dimension=1, tiled=True),
    )
    grad_norm_two = lax.psum(
        jnp.einsum("tf,df->td", grad_upper, full_up, preferred_element_type=jnp.float32).astype(
            jnp.bfloat16
        ),
        "tp",
    ).astype(jnp.float32)
    grad_middle = grad_out + norm_backward(grad_norm_two, normed_two, inverse_two, ln_gain[1])
    grad_branch = grad_middle.astype(jnp.bfloat16)
    out_term = jnp.einsum(
        "te,td->ed", attended_low, grad_branch, preferred_element_type=jnp.float32
    )
    grad_att = jnp.einsum(
        "td,ed->te", grad_branch, full_out, preferred_element_type=jnp.float32
    ).astype(jnp.bfloat16)
    grad_heads = grad_att.reshape(num_rows, head_count, HD)
    row_terms = jnp.einsum("qhd,qhd->hq", grad_heads.astype(jnp.float32), attended)

    def joint_step(grad_accum, block_parts):
        key_part, value_part, seg_part, pos_part = block_parts
        scores, allowed = block_scores(
            query_heads, key_part, own_tags, (seg_part, pos_part), slopes
        )
        prob_vals = probabilities(scores, allowed, row_max, row_sum)
        grad_probs = jnp.einsum(
            "qhd,khd->hqk", grad_heads, value_part, preferred_element_type=jnp.float32
        )
        grad_scores = (prob_vals * (grad_probs - row_terms[:, :, None])).astype(jnp.bfloat16)
        grad_accum = (
            grad_accum
            + jnp.einsum("hqk,khd->qhd", grad_scores, key_part, preferred_element_type=jnp.float32)
            * scale
        )
        key_part_grad = (
            jnp.einsum("hqk,qhd->khd", grad_scores, query_heads, preferred_element_type=jnp.float32)
            * scale
        )
        value_part_grad = jnp.einsum(
            "hqk,qhd->khd",
            prob_vals.astype(jnp.bfloat16),
            grad_heads,
            preferred_element_type=jnp.float32,
        )
        return (
            grad_accum,
            (
                key_part_grad.reshape(KEY_BLOCK, head_width),
                value_part_grad.reshape(KEY_BLOCK, head_width),
            ),
        )

    grad_query_sum, (key_terms, value_terms) = lax.scan(
        joint_step,
        jnp.zeros((num_rows, head_count, HD), jnp.float32),
        (key_blocks, value_blocks, seg_blocks, pos_blocks),
    )
    key_grad_sum, value_grad_sum = (
        lax.psum_scatter(
            key_terms.reshape(group_rows, head_width).astype(jnp.bfloat16),
            "ctx",
            scatter_dimension=0,
            tiled=True,
        ).astype(jnp.float32),
        lax.psum_scatter(
            value_terms.reshape(group_rows, head_width).astype(jnp.bfloat16),
            "ctx",
            scatter_dimension=0,
            tiled=True,
        ).astype(jnp.float32),
    )
    grad_query_low = grad_query_sum.reshape(num_rows, head_width).astype(jnp.bfloat16)
    grad_key_low = key_grad_sum.astype(jnp.bfloat16)
    grad_value_low = value_grad_sum.astype(jnp.bfloat16)
    grad_qkv = jnp.stack([grad_query_low, grad_key_low, grad_value_low])
    grad_norm_one = lax.psum(
        jnp.einsum("cte,cde->td", grad_qkv, full_qkv, preferred_element_type=jnp.float32).astype(
            jnp.bfloat16
        ),
        "tp",
    ).astype(jnp.float32)
    grad_tokens = grad_middle + norm_backward(grad_norm_one, normed_one, inverse_one, ln_gain[0])
    qkv_term = jnp.einsum("td,cte->cde", act_one, grad_qkv, preferred_element_type=jnp.float32)
    grad_w_qkv, grad_w_out = (
        lax.psum_scatter(qkv_term, ("shard", "ctx"), scatter_dimension=1, tiled=True),
        lax.psum_scatter(out_term, ("shard", "ctx"), scatter_dimension=1, tiled=True),
    )
    bias_qv_part = jnp.stack(
        [
            jnp.sum(grad_query_low.astype(jnp.float32), axis=0),
            jnp.sum(grad_value_low.astype(jnp.float32), axis=0),
        ]
    )
    out_bias_part = jnp.sum(grad_branch.astype(jnp.float32), axis=0)
    up_bias_part = jnp.sum(grad_upper.astype(jnp.float32), axis=0)
    down_bias_part = jnp.sum(grad_out, axis=0)
    gain_part = jnp.stack(
        [jnp.sum(grad_norm_one * normed_one, axis=0), jnp.sum(grad_norm_two * normed_two, axis=0)]
    )
    shift_part = jnp.stack([jnp.sum(grad_norm_one, axis=0), jnp.sum(grad_norm_two, axis=0)])
    grad_b_qv, grad_b_out, grad_b_up, grad_b_down, grad_gain, grad_shift = lax.psum(
        (bias_qv_part, out_bias_part, up_bias_part, down_bias_part, gain_part, shift_part),
        ("shard", "ctx"),
    )
    return (
        result,
        grad_tokens,
        grad_w_qkv,
        grad_b_qv,
        grad_w_out,
        grad_b_out,
        grad_w_up,
        grad_b_up,
        grad_w_down,
        grad_b_down,
        grad_gain,
        grad_shift,
    )


def solution(mesh):
    placed = (
        P(("shard", "ctx"), None),
        P(("shard", "ctx"), None),
        P(("shard", "ctx")),
        P(("shard", "ctx")),
        P(),
        P(None, ("shard", "ctx"), "tp"),
        P(None, "tp"),
        P("tp", ("shard", "ctx")),
        P(),
        P(("shard", "ctx"), "tp"),
        P("tp"),
        P("tp", ("shard", "ctx")),
        P(),
        P(),
        P(),
    )
    sizes = dict(mesh.shape)
    paired = sizes["tp"] * sizes["ctx"] * 2 == HEADS and sizes["tp"] == 2 and sizes["shard"] == 4
    return jax.shard_map(
        fast_device if paired else per_device,
        mesh=mesh,
        in_specs=placed,
        out_specs=(
            P(("shard", "ctx"), None),
            P(("shard", "ctx"), None),
            P(None, ("shard", "ctx"), "tp"),
            P(None, "tp"),
            P("tp", ("shard", "ctx")),
            P(),
            P(("shard", "ctx"), "tp"),
            P("tp"),
            P("tp", ("shard", "ctx")),
            P(),
            P(),
            P(),
        ),
        check_vma=False,
    )
```

```python
from functools import partial

import jax
import jax.numpy as jnp
from jax import lax
from jax.experimental import pallas as pl
from jax.experimental.pallas import tpu as pltpu
from jax.sharding import PartitionSpec as P

HEADS = 16
HD = 64
KEY_BLOCK = 512
TRUNK = 1024
BRANCH = 128
SLOTS = 12
TREE = TRUNK + SLOTS * BRANCH
PAIR = 2 * HD

EPS = 1e-05
NEG = -1e30
LOG2E = 1.4426950408889634
MESH = pl.DeviceIdType.MESH
BF = jnp.bfloat16
F32 = jnp.float32
ROWS_WAVE = 4
FRONT_LIMIT = 62 << 20
BLOCK = 512
CURVE = 0.044715
ROOT = 0.7978845608028654
SUBS = 2


def nt(left, right):
    return lax.dot_general(left, right, (((1,), (1,)), ((), ())), preferred_element_type=F32)


def nn(left, right):
    return lax.dot_general(left, right, (((1,), (0,)), ((), ())), preferred_element_type=F32)


def rcopy(src, dst, send, recv, device):
    return pltpu.make_async_remote_copy(
        src_ref=src, dst_ref=dst, send_sem=send, recv_sem=recv, device_id=device, device_id_type=MESH
    )


def greet(devices):
    barrier = pltpu.get_barrier_semaphore()
    for device in devices:
        pl.semaphore_signal(barrier, inc=1, device_id=device, device_id_type=MESH)
    pl.semaphore_wait(barrier, len(devices))


def norm_rows(values, gain_row, shift_row):
    centre = values - jnp.mean(values, axis=-1, keepdims=True)
    inverse = lax.rsqrt(jnp.mean(centre * centre, axis=-1, keepdims=True) + EPS)
    normed = centre * inverse
    return normed * gain_row + shift_row, normed, inverse


def norm_rows_back(grad_in, normed, inverse, gain_row):
    scaled = grad_in * gain_row
    mean_grad = jnp.mean(scaled, axis=-1, keepdims=True)
    mean_cross = jnp.mean(scaled * normed, axis=-1, keepdims=True)
    return inverse * (scaled - mean_grad - normed * mean_cross)


def head_masks():
    lane = lax.broadcasted_iota(jnp.int32, (1, PAIR), 1)
    first = (lane < HD).astype(F32).astype(BF)
    second = (lane >= HD).astype(F32).astype(BF)
    return first, second


def stack_heads(rows):
    first, second = head_masks()
    return jnp.concatenate([rows * first, rows * second], axis=0)


def unstack_turned(turned, rows):
    return jnp.concatenate([turned[:HD, :rows], turned[HD:, rows:]], axis=0).T


def key_features(high, low, flag, rows):
    lane = lax.broadcasted_iota(jnp.int32, (rows, 128), 1)
    feats = jnp.where(lane < 3, high, jnp.where(lane < 6, low, jnp.where(lane == 6, flag, 0.0)))
    return feats.astype(BF)


def query_features(slope_ref, rows):
    return jnp.concatenate(
        [
            jnp.broadcast_to(slope_ref[0:1, :], (rows, 128)),
            jnp.broadcast_to(slope_ref[1:2, :], (rows, 128)),
        ],
        axis=0,
    ).astype(BF)


def fill_trunk_keys(key_ref, keys_aug):
    keys_aug[:, 0:PAIR] = key_ref[0:TRUNK, :]
    pos = lax.broadcasted_iota(jnp.int32, (TRUNK, 128), 0)
    low = pos & 255
    keys_aug[:, PAIR:] = key_features((pos - low).astype(F32), low.astype(F32), 0.0, TRUNK)


def fill_labels(info_all, blocks, labels, parents):
    labels[...] = jnp.full(labels.shape, -1.0, F32)
    parents[...] = jnp.full(parents.shape, -2.0, F32)
    for slot in range(SLOTS):
        block = TRUNK // BRANCH + slot
        owner, inner = block // blocks, block % blocks
        labels[slot : slot + 1, :] = info_all[owner, inner : inner + 1, :]
        parents[slot : slot + 1, :] = info_all[owner, 8 + inner : 9 + inner, :]


def parent_pick(slot, labels, parents, key_ref, value_ref):
    mine = parents[pl.ds(slot, 1), :]
    leaf = jnp.zeros((1, 128), F32)
    key_sum = jnp.zeros((BRANCH, PAIR), BF)
    value_sum = jnp.zeros((BRANCH, PAIR), BF)
    for other in range(SLOTS):
        same = (mine == labels[other : other + 1, :]).astype(F32)
        leaf = leaf + same
        same_low = same.astype(BF)
        at = TRUNK + other * BRANCH
        key_sum = key_sum + same_low * key_ref[at : at + BRANCH, :]
        value_sum = value_sum + same_low * value_ref[at : at + BRANCH, :]
    return leaf, key_sum, value_sum


def segment_key_features(leaf):
    row = lax.broadcasted_iota(jnp.int32, (BRANCH, 128), 0).astype(F32)
    own = key_features(float(TRUNK), row + leaf * float(BRANCH), 0.0, BRANCH)
    above = key_features(float(TRUNK), row, (leaf - 1.0) * 1e30, BRANCH)
    return own, above


def causal(rows):
    key = lax.broadcasted_iota(jnp.int32, (rows, rows), 0)
    query = lax.broadcasted_iota(jnp.int32, (rows, rows), 1)
    once = key <= query
    return jnp.concatenate([once, once], axis=1)


class Spread:
    def __init__(self, full, dims, depth, cols, sems, doubling=True):
        self.doubling = doubling
        self.full, self.depth, self.cols = full, depth, cols
        self.ns, self.nz, _ = dims
        self.s, self.z = lax.axis_index("shard"), lax.axis_index("ctx")
        self.zs, self.zr, self.xs, self.xr, self.cs, self.cr = sems

    def rows(self, shard, place):
        at = pl.multiple_of((shard * self.nz + place) * self.depth, self.depth)
        return self.full.at[pl.ds(at, self.depth), self.cols]

    def flip(self, bits):
        low = lax.rem(self.s, 2)
        high = lax.div(self.s, 2)
        if bits & 1:
            low = 1 - low
        if bits & 2:
            high = 1 - high
        return 2 * high + low

    def source(self, d):
        low, high = lax.rem(self.z, 2), lax.div(self.z, 2)
        low = 1 - low if d & 1 else low
        high = 1 - high if d & 2 else high
        return 2 * high + low

    def z_copy(self, d):
        ref = self.rows(self.s, self.source(2 if self.doubling and d == 3 else 0))
        to = self.source(1 if self.doubling and d == 3 else d)
        return rcopy(ref, ref, self.zs.at[d - 1], self.zr.at[d - 1], {"ctx": to})

    def x_copy(self, d):
        ref = self.rows(self.s, self.source(d))
        return rcopy(ref, ref, self.xs.at[d], self.xr.at[d], {"shard": self.flip(2)})

    def c_copy(self, far, d):
        ref = self.rows(self.flip(2) if far else self.s, self.source(d))
        return rcopy(ref, ref, self.cs.at[far, d], self.cr.at[far, d], {"shard": self.flip(1)})

    def z_start(self):
        self.z_copy(2).start()
        self.z_copy(1).start()
        if not self.doubling:
            self.z_copy(3).start()

    def own(self):
        self.x_copy(0).start()
        self.c_copy(0, 0).start()

    def z_done(self, d):
        ref = self.rows(self.s, self.source(d))
        rcopy(ref, ref, self.zs.at[d - 1], self.zr.at[d - 1], {"ctx": self.source(1)}).wait_recv()
        if self.doubling and d == 2:
            self.z_copy(3).start()
        self.x_copy(d).start()
        self.c_copy(0, d).start()

    def x_done(self, d):
        ref = self.rows(self.flip(2), self.source(d))
        rcopy(ref, ref, self.xs.at[d], self.xr.at[d], {"shard": self.flip(2)}).wait_recv()
        self.c_copy(1, d).start()

    def c_done(self, far, d):
        ref = self.rows(self.flip(3) if far else self.flip(1), self.source(d))
        rcopy(ref, ref, self.cs.at[far, d], self.cr.at[far, d], {"shard": self.flip(1)}).wait_recv()

    def all_here(self):
        for d in range(self.nz):
            self.c_done(0, d)
            self.c_done(1, d)

    def finish(self):
        for d in range(self.nz):
            if d:
                self.z_copy(d).wait_send()
            self.x_copy(d).wait_send()
            self.c_copy(0, d).wait_send()
            self.c_copy(1, d).wait_send()


def spread_sems(nz):
    return [dma(nz - 1), dma(nz - 1), dma(nz), dma(nz), dma(2, nz), dma(2, nz)]


def vmem():
    return pl.BlockSpec(memory_space=pltpu.VMEM)


def shape(dims, kind):
    return jax.ShapeDtypeStruct(dims, kind)


def dma(*dims):
    return pltpu.SemaphoreType.DMA(dims)


def front_kernel(
    dims,
    tok,
    w_up,
    w_out,
    w_down,
    cot_in,
    wq3,
    info,
    bias_qv,
    slopes,
    gain,
    shift,
    b_out,
    b_up,
    act_turned_o,
    query_o,
    key_o,
    value_o,
    out_heads_o,
    lse,
    info_all,
    wqkv_o,
    core_o,
    ga_o,
    down_o,
    mid_o,
    gmid_o,
    sums,
    act_turned,
    query,
    key,
    value,
    out_heads,
    wqkv,
    core_in,
    ga_all,
    down_part,
    mid,
    gmid,
    wfull,
    wq,
    att,
    tree,
    wcat,
    keys_aug,
    values_turned,
    labels,
    parents,
    cot,
    far,
    act,
    gbranch,
    g_send,
    g_recv,
    ga_send,
    bup_acc,
    info_send,
    info_recv,
    wz_send,
    wz_recv,
    ws_send,
    ws_recv,
    z_send,
    z_recv,
    y_send,
    y_recv,
    a_send,
    a_recv,
    local_sem,
    b_send,
    b_recv,
    t_send,
    t_recv,
    gs_sem,
    gr_sem,
    as_sem,
    ar_sem,
    cs_sem,
    cr_sem,
    store_sem,
    *spread,
):
    ns, nz, rows = dims
    s, z, y = lax.axis_index("shard"), lax.axis_index("ctx"), lax.axis_index("tp")
    half = rows // 2
    sub = half // SUBS
    depth = wq.shape[0]
    wide = 3 * PAIR
    my_rows = pl.ds(pl.multiple_of((s * nz + z) * depth, depth), depth)
    units, inner = w_up.shape[1], w_out.shape[1]
    own_cols = pl.multiple_of(2 * units + y * inner, 128)
    starts = [
        pltpu.make_async_copy(tok, tree.at[pl.ds(pl.multiple_of(z * rows, 128), rows), :], local_sem.at[0]),
        pltpu.make_async_copy(w_up, wfull.at[my_rows, 0:units], local_sem.at[1]),
        pltpu.make_async_copy(w_down, wfull.at[my_rows, units : 2 * units], local_sem.at[2]),
        pltpu.make_async_copy(w_out, wfull.at[my_rows, pl.ds(own_cols, inner)], local_sem.at[3]),
    ]
    given_load = pltpu.make_async_copy(cot_in, cot, local_sem.at[4])
    given_load.start()
    stores = [
        pltpu.make_async_copy(a, b, store_sem.at[k])
        for k, (a, b) in enumerate(
            (
                (act_turned, act_turned_o),
                (query, query_o),
                (key, key_o),
                (value, value_o),
                (out_heads, out_heads_o),
                (mid, mid_o),
                (gmid, gmid_o),
                (down_part, down_o),
                (core_in.at[:, :, 0 : 2 * units], core_o.at[:, :, 0 : 2 * units]),
                (core_in.at[:, :, 2 * units :], core_o.at[:, :, 2 * units :]),
                (wqkv, wqkv_o),
                (ga_all, ga_o),
            )
        )
    ]
    for one in starts:
        one.start()
    for to in range(nz):
        for part in range(3):
            wq[:, to * wide + part * PAIR : to * wide + (part + 1) * PAIR] = wq3[
                part, :, to * PAIR : (to + 1) * PAIR
            ]
    greet(
        [{"ctx": lax.rem(z + d, nz)} for d in range(1, nz)]
        + [{"shard": lax.rem(s + d, ns)} for d in range(1, ns)]
        + [{"tp": 1 - y}]
    )
    ups = Spread(wfull, dims, depth, slice(0, units), spread[:6])
    downs = Spread(wfull, dims, depth, slice(units, 2 * units), spread[6:12])
    weights = Spread(wqkv, dims, depth, slice(None), spread[18:])
    outer = Spread(wfull, dims, depth, pl.ds(own_cols, inner), spread[12:18], False)

    def info_copy(d):
        return rcopy(
            info, info_all.at[z], info_send.at[d - 1], info_recv.at[d - 1], {"ctx": lax.rem(z + d, nz)}
        )

    def wz_copy(d):
        to = lax.rem(z + d, nz)
        return rcopy(
            wq.at[:, pl.ds(pl.multiple_of(to * wide, 128), wide)],
            wcat.at[my_rows, :],
            wz_send.at[d - 1],
            wz_recv.at[d - 1],
            {"ctx": to},
        )

    shard_rows = pl.ds(s * (nz * depth), nz * depth)

    def ws_copy(d):
        return rcopy(
            wcat.at[shard_rows, :],
            wcat.at[shard_rows, :],
            ws_send.at[d - 1],
            ws_recv.at[d - 1],
            {"shard": lax.rem(s + d, ns)},
        )

    wqkv[my_rows, :] = wq[...]
    for d in range(1, nz):
        wz_copy(d).start()
    for d in range(1, nz):
        info_copy(d).start()
    wcat[my_rows, :] = wq[:, pl.ds(pl.multiple_of(z * wide, 128), wide)]
    info_all[z] = info[...]
    for one in starts:
        one.wait()

    def piece(block, second, part):
        at = block * rows + jnp.where(second, 1 - y, y) * half + part * sub
        return tree.at[pl.ds(pl.multiple_of(at, 32), sub), :]

    def z_copy(direction, k, part):
        block = z - k if direction == 0 else z + k
        to = z + 1 if direction == 0 else z - 1
        ref = piece(block, False, part)
        return rcopy(ref, ref, z_send.at[direction, k, part], z_recv.at[direction, k, part], {"ctx": to})

    def z_arrival(direction, k, part):
        block = z - k if direction == 0 else z + k
        ref = piece(block, False, part)
        return rcopy(
            ref, ref, z_send.at[direction, k - 1, part], z_recv.at[direction, k - 1, part], {"ctx": z}
        )

    def y_copy(direction, k, part):
        block = z - k if direction == 0 else z + k
        ref = piece(block, False, part)
        return rcopy(
            ref, ref, y_send.at[direction, k - 1, part], y_recv.at[direction, k - 1, part], {"tp": 1 - y}
        )

    def y_arrival(direction, k, part):
        block = z - k if direction == 0 else z + k
        ref = piece(block, True, part)
        return rcopy(
            ref, ref, y_send.at[direction, k - 1, part], y_recv.at[direction, k - 1, part], {"tp": 1 - y}
        )

    def place(direction, k):
        block = z - k if direction == 0 else z + k
        nxt = z + 1 if direction == 0 else z - 1
        here = (block >= 0) & (block < nz)
        onward = here & (nxt >= 0) & (nxt < nz)
        return block, here, onward

    def forward(k, first):
        for part in range(SUBS):
            for direction in range(2):
                _, here, onward = place(direction, k)
                if not first:

                    @pl.when(here)
                    def _():
                        z_arrival(direction, k, part).wait_recv()

                @pl.when(onward & (k < nz - 1))
                def _():
                    z_copy(direction, k, part).start()

                if not first:

                    @pl.when(here)
                    def _():
                        y_copy(direction, k, part).start()

    forward(0, True)
    outer.own()
    ups.own()
    downs.own()
    for d in range(1, nz):
        wz_copy(d).wait_recv()
    for d in range(1, ns):
        ws_copy(d).start()

    bias_at = pl.ds(pl.multiple_of(z * PAIR, 128), PAIR)
    bias_q = bias_qv[0:1, bias_at]
    bias_v = bias_qv[1:2, bias_at]

    def project(k):
        def side(direction, inner_carry):
            block = z + (2 * direction - 1) * k

            @pl.when((block >= 0) & (block < nz) & ((k > 0) | (direction == 0)))
            def _():
                def tile(t, carry):
                    here = pl.ds(pl.multiple_of(block * rows + t * 128, 128), 128)
                    act = norm_rows(tree[here, :].astype(F32), gain[0:1, :], shift[0:1, :])[0].astype(BF)
                    act_turned[:, here] = act.T
                    both = nn(act, wcat[...])
                    query[here, :] = (
                        (both[:, :PAIR] + bias_q).astype(BF).astype(F32) * HD ** (-0.5)
                    ).astype(BF)
                    key[here, :] = both[:, PAIR : 2 * PAIR].astype(BF)
                    value[here, :] = (both[:, 2 * PAIR :] + bias_v).astype(BF)
                    return carry

                lax.fori_loop(0, rows // 128, tile, 0)

            return inner_carry

        lax.fori_loop(0, 2, side, 0)

    def shared(k):
        for part in range(SUBS):
            for direction in range(2):
                _, here, _ = place(direction, k)

                @pl.when(here)
                def _():
                    y_arrival(direction, k, part).wait_recv()

    forward(1, False)
    for d in range(1, ns):
        ws_copy(d).wait_recv()
    project(0)

    def wave(k, carry):
        forward(k, False)

        @pl.when(k == nz - 2)
        def _():
            outer.z_start()
            ups.z_start()
            downs.z_start()

        shared(k - 1)
        project(k - 1)
        return carry

    lax.fori_loop(2, nz, wave, 0)
    for d in (1, 3, 2):
        outer.z_done(d)
    shared(nz - 1)
    project(nz - 1)
    for k in range(4):
        stores[k].start()
    for d in (0, 1, 3, 2):
        outer.x_done(d)
    ups.z_done(2)
    ups.z_done(1)

    for d in range(1, nz):
        info_copy(d).wait_recv()

    fill_labels(info_all, rows // BRANCH, labels, parents)
    fill_trunk_keys(key, keys_aug)
    values_turned[...] = value[0:TRUNK, :].T

    def att_cols(half_at, owner):
        return pl.ds(pl.multiple_of(half_at * inner + owner * PAIR, 128), PAIR)

    def att_copy(to):
        return rcopy(
            out_heads.at[pl.ds(to * rows, rows), :],
            att.at[:, att_cols(y, z)],
            a_send.at[to],
            a_recv.at[z],
            {"ctx": to},
        )

    def pass_on(owner):
        return rcopy(
            att.at[:, att_cols(y, owner)],
            att.at[:, att_cols(y, owner)],
            b_send.at[owner],
            b_recv.at[owner],
            {"tp": 1 - y},
        )

    half_rows = pl.ds(pl.multiple_of(lax.rem(s, 2) * (ns * nz * depth // 2), 128), ns * nz * depth // 2)
    far_rows = pl.ds(pl.multiple_of((1 - lax.rem(s, 2)) * (ns * nz * depth // 2), 128), ns * nz * depth // 2)
    far_cols = pl.ds(pl.multiple_of(2 * units + (1 - y) * inner, 128), inner)

    def plane_copy():
        ref = wfull.at[half_rows, pl.ds(own_cols, inner)]
        return rcopy(ref, ref, t_send.at[0], t_recv.at[0], {"tp": 1 - y})

    def plane_arrival():
        ref = wfull.at[half_rows, far_cols]
        return rcopy(ref, ref, t_send.at[0], t_recv.at[0], {"tp": 1 - y})

    def core_copy():
        ref = wfull.at[half_rows, far_cols]
        return rcopy(ref, ref, t_send.at[1], t_recv.at[1], {"shard": outer.flip(1)})

    def core_arrival():
        ref = wfull.at[far_rows, far_cols]
        return rcopy(ref, ref, t_send.at[1], t_recv.at[1], {"shard": outer.flip(1)})

    outer.all_here()
    plane_copy().start()

    def send_out(to):
        @pl.when(z != to)
        def _():
            att_copy(to).start()

        @pl.when(z == to)
        def _():
            att[:, att_cols(y, z)] = out_heads[to * rows : (to + 1) * rows, :]
            pass_on(z).start()

    tile_mask = causal(BRANCH)

    def segment(slot, carry):
        here = pl.ds(pl.multiple_of(TRUNK + slot * BRANCH, 128), BRANCH)
        asked = jnp.concatenate(
            [stack_heads(query[here, :]), query_features(slopes, BRANCH)], axis=1
        )
        leaf, key_up, value_up = parent_pick(slot, labels, parents, key, value)
        own_feats, up_feats = segment_key_features(leaf)
        trunk_part = nt(keys_aug[...], asked) * LOG2E
        own_part = nt(jnp.concatenate([key[here, :], own_feats], axis=1), asked) * LOG2E
        own_part = jnp.where(tile_mask, own_part, NEG)
        up_part = nt(jnp.concatenate([key_up, up_feats], axis=1), asked) * LOG2E
        top = jnp.maximum(
            jnp.max(trunk_part, axis=0, keepdims=True),
            jnp.maximum(
                jnp.max(own_part, axis=0, keepdims=True), jnp.max(up_part, axis=0, keepdims=True)
            ),
        )
        trunk_part = jnp.exp2(trunk_part - top)
        own_part = jnp.exp2(own_part - top)
        up_part = jnp.exp2(up_part - top)
        total = (
            jnp.sum(trunk_part, axis=0, keepdims=True)
            + jnp.sum(own_part, axis=0, keepdims=True)
            + jnp.sum(up_part, axis=0, keepdims=True)
        )
        turned = nn(values_turned[...], trunk_part.astype(BF))
        turned = turned + nn(value[here, :].T, own_part.astype(BF))
        turned = turned + nn(value_up.T, up_part.astype(BF))
        turned = turned / total
        out_heads[here, :] = unstack_turned(turned, BRANCH).astype(BF)
        lse[pl.ds(4 + slot, 1), 0 : 2 * BRANCH] = top + jnp.log2(total)
        return carry

    wave_rows = TRUNK // 4
    wave_mask = causal(wave_rows)

    def trunk_tile(tile):
        lo, hi = tile * wave_rows, (tile + 1) * wave_rows
        asked = jnp.concatenate(
            [stack_heads(query[lo:hi, :]), query_features(slopes, wave_rows)], axis=1
        )
        edge = jnp.where(wave_mask, nt(keys_aug[lo:hi, :], asked) * LOG2E, NEG)
        top = jnp.max(edge, axis=0, keepdims=True)
        if tile:
            body = nt(keys_aug[0:lo, :], asked) * LOG2E
            top = jnp.maximum(top, jnp.max(body, axis=0, keepdims=True))
            body = jnp.exp2(body - top)
        edge = jnp.exp2(edge - top)
        total = jnp.sum(edge, axis=0, keepdims=True)
        turned = nn(values_turned[:, lo:hi], edge.astype(BF))
        if tile:
            total = total + jnp.sum(body, axis=0, keepdims=True)
            turned = turned + nn(values_turned[:, 0:lo], body.astype(BF))
        turned = turned / total
        out_heads[lo:hi, :] = unstack_turned(turned, wave_rows).astype(BF)
        lse[tile : tile + 1, :] = top + jnp.log2(total)

    def segments(lo, hi):
        lax.fori_loop((lo - TRUNK) // BRANCH, (hi - TRUNK) // BRANCH, segment, 0)

    segments(2 * rows, 3 * rows)
    send_out(2)
    for tile in range(3):
        trunk_tile(tile)
    send_out(0)
    downs.z_done(2)
    segments(3 * rows, 4 * rows)
    send_out(3)
    trunk_tile(3)
    segments(TRUNK, 2 * rows)
    send_out(1)
    downs.z_done(1)
    ups.z_done(3)
    stores[4].start()
    plane_arrival().wait_recv()
    core_copy().start()
    downs.z_done(3)
    for owner in range(nz):

        @pl.when(z != owner)
        def _():
            rcopy(
                out_heads.at[0:rows, :],
                att.at[:, att_cols(y, owner)],
                a_send.at[owner],
                a_recv.at[owner],
                {"ctx": owner},
            ).wait_recv()
            pass_on(owner).start()

    mid[...] = tree[pl.ds(pl.multiple_of(z * rows, 128), rows), :].astype(F32) + b_out[...]
    for d in (0, 2, 1, 3):
        ups.x_done(d)
    given_load.wait()
    for owner in range(nz):
        ref = att.at[:, att_cols(1 - y, owner)]
        rcopy(ref, ref, b_send.at[owner], b_recv.at[owner], {"tp": 1 - y}).wait_recv()
    core_arrival().wait_recv()
    ups.all_here()
    other = {"tp": 1 - y}
    chunk = rows // ROWS_WAVE
    width = act.shape[1]
    halves = units // width
    own_heads = pl.ds(pl.multiple_of(y * inner, 128), inner)
    own_wide = pl.ds(own_cols, inner)
    sums[...] = jnp.zeros(sums.shape, F32)
    bup_acc[...] = jnp.zeros(bup_acc.shape, F32)

    def at(i):
        return pl.ds(pl.multiple_of(i * chunk, 32), chunk)

    def g_copy(i):
        return rcopy(g_send.at[at(i), :], g_recv.at[at(i), :], gs_sem.at[i], gr_sem.at[i], other)

    def a_copy(i, d):
        to = lax.rem(z + d, nz)
        return rcopy(
            ga_send.at[at(i), pl.ds(pl.multiple_of(to * PAIR, 128), PAIR)],
            ga_all.at[pl.ds(pl.multiple_of(z * rows + i * chunk, 32), chunk), :],
            as_sem.at[d - 1, i],
            ar_sem.at[d - 1, i],
            {"ctx": to},
        )

    span = nz * depth
    parts = ((0, 2 * units), (2 * units, 2 * units + inner))

    def c_copy(part, index):
        lo, hi = parts[part]
        return rcopy(
            far.at[index, :, lo:hi],
            core_in.at[index, :, lo:hi],
            cs_sem.at[part, index],
            cr_sem.at[part, index],
            {"shard": weights.flip(1)},
        )

    sums[...] = jnp.zeros(sums.shape, F32)
    bup_acc[...] = jnp.zeros(bup_acc.shape, F32)
    per = width // BLOCK

    def spot(first, i, c):
        row = (first + lax.div(c, per)) * rows + i * chunk
        col = lax.rem(c, per) * BLOCK
        return pl.ds(pl.multiple_of(row, 32), chunk), pl.ds(pl.multiple_of(col, 128), BLOCK)

    def stage_one(i, carry):
        here = at(i)
        middle = mid[here, :] + nt(att[here, :], wfull[:, 2 * units :])
        mid[here, :] = middle
        act[here, :] = norm_rows(middle, gain[1:2, :], shift[1:2, :])[0].astype(BF)

        def columns(c, inner_carry):
            cols = pl.ds(pl.multiple_of(c * BLOCK, 128), BLOCK)
            upper = nn(act[here, :], wfull[:, cols]) + b_up[:, cols]
            square = upper * upper
            turn = jnp.tanh(ROOT * (upper + CURVE * (square * upper)))
            tree[spot(0, i, c)] = (0.5 * upper * (1.0 + turn)).astype(BF)
            steep = 0.5 * (1.0 + turn) + (0.5 * ROOT) * upper * (1.0 - turn * turn) * (
                1.0 + (3.0 * CURVE) * square
            )
            tree[spot(halves, i, c)] = steep.astype(BF)
            return inner_carry

        lax.fori_loop(0, units // BLOCK, columns, 0)
        return carry

    def stage_two(i, carry):
        here = at(i)

        def columns(c, inner_carry):
            cols = pl.ds(pl.multiple_of(c * BLOCK, 128), BLOCK)
            down_cols = pl.ds(pl.multiple_of(units + c * BLOCK, 128), BLOCK)
            slope = nn(cot[here, :], wfull[:, down_cols])
            low = (slope * tree[spot(halves, i, c)].astype(F32)).astype(BF)
            tree[spot(halves, i, c)] = low
            bup_acc[:, cols] += jnp.sum(low.astype(F32), axis=0, keepdims=True)
            return inner_carry

        lax.fori_loop(0, units // BLOCK, columns, 0)
        total = jnp.zeros((chunk, width), F32)
        for part in range(halves):
            total = total + nt(
                tree[spot(halves + part, i, 0)[0], :], wfull[:, part * width : (part + 1) * width]
            )
        g_send[here, :] = total.astype(BF)
        g_copy(i).start()
        return carry

    def drain(k, carry):
        for part in range(SUBS):
            for direction in range(2):
                _, here, onward = place(direction, k)

                @pl.when(onward & (k < nz - 1))
                def _():
                    z_copy(direction, k, part).wait_send()

                @pl.when(here & (k > 0))
                def _():
                    y_copy(direction, k, part).wait_send()

        return carry

    lax.fori_loop(0, nz, drain, 0)
    lax.fori_loop(0, 2, stage_one, 0)
    weights.own()
    weights.z_start()
    for d in (0, 2, 1, 3):
        downs.x_done(d)
    lax.fori_loop(2, ROWS_WAVE, stage_one, 0)
    stores[5].start()
    downs.all_here()
    lax.fori_loop(0, ROWS_WAVE, stage_two, 0)
    for d in (2, 1, 3):
        weights.z_done(d)

    def group_cols(index, block):
        return pl.ds(pl.multiple_of(weights.flip(index) * span + block * 128, 128), 128)

    def products(cols):
        turned_act, turned_cot = act[:, cols].T, cot[:, cols].T
        for part in range(halves):
            lo = part * width
            yield lo, nn(turned_act, tree[(halves + part) * rows : (halves + part + 1) * rows, :])
            yield units + lo, nn(turned_cot, tree[part * rows : (part + 1) * rows, :])

    def each_block(act_on):
        for index in range(2):

            def one(block, carry):
                act_on(index, block)
                return carry

            lax.fori_loop(0, span // 128, one, 0)

    def far_one(index, block):
        target = pl.ds(pl.multiple_of(block * 128, 128), 128)
        for lo, value_block in products(group_cols((1, 3)[index], block)):
            far[index, target, lo : lo + width] = value_block.astype(BF)

    def near_one(index, block):
        target = pl.ds(pl.multiple_of(block * 128, 128), 128)
        for lo, value_block in products(group_cols((0, 2)[index], block)):
            here = slice(lo, lo + width)
            core_in[index, target, here] = (core_in[index, target, here].astype(F32) + value_block).astype(BF)

    def out_product(cols):
        return nn(gbranch[:, cols].T, att[:, own_heads])

    def far_two(index, block):
        target = pl.ds(pl.multiple_of(block * 128, 128), 128)
        far[index, target, 2 * units :] = out_product(group_cols((1, 3)[index], block)).astype(BF)

    def near_two(index, block):
        target = pl.ds(pl.multiple_of(block * 128, 128), 128)
        here = slice(2 * units, 2 * units + inner)
        core_in[index, target, here] = (
            core_in[index, target, here].astype(F32) + out_product(group_cols((0, 2)[index], block))
        ).astype(BF)

    def stage_c(i, carry):
        g_copy(i).wait_recv()
        here = at(i)
        grad = g_send[here, :].astype(F32) + g_recv[here, :].astype(F32)
        _, normed, inverse = norm_rows(mid[here, :], gain[1:2, :], shift[1:2, :])
        given = cot[here, :].astype(F32)
        grad_middle = given + norm_rows_back(grad, normed, inverse, gain[1:2, :])
        gmid[here, :] = grad_middle
        low = grad_middle.astype(BF)
        gbranch[here, :] = low
        sums[2:3, :] += jnp.sum(low.astype(F32), axis=0, keepdims=True)
        sums[3:4, :] += jnp.sum(given, axis=0, keepdims=True)
        sums[4:5, :] += jnp.sum(grad * normed, axis=0, keepdims=True)
        sums[5:6, :] += jnp.sum(grad, axis=0, keepdims=True)
        ga_send[here, :] = nn(low, wfull[:, own_wide]).astype(BF)
        for d in range(1, nz):
            a_copy(i, d).start()
        ga_all[pl.ds(pl.multiple_of(z * rows + i * chunk, 32), chunk), :] = ga_send[
            here, pl.ds(pl.multiple_of(z * PAIR, 128), PAIR)
        ]
        return carry

    lax.fori_loop(0, 1, stage_c, 0)
    each_block(far_one)
    for index in range(2):
        c_copy(0, index).start()
    lax.fori_loop(1, 2, stage_c, 0)
    for d in (0, 2, 1, 3):
        weights.x_done(d)
    def down(i, carry):
        total = jnp.zeros((chunk, width), F32)
        for part in range(halves):
            total = total + nt(
                tree[spot(part, i, 0)[0], :], wfull[:, units + part * width : units + (part + 1) * width]
            )
        down_part[at(i), :] = total.astype(BF)
        return carry

    lax.fori_loop(0, ROWS_WAVE, down, 0)
    stores[7].start()
    lax.fori_loop(2, 3, stage_c, 0)
    for index in range(2):
        c_copy(0, index).wait_recv()
    each_block(near_one)
    stores[8].start()
    lax.fori_loop(3, ROWS_WAVE, stage_c, 0)
    stores[6].start()
    each_block(far_two)
    for index in range(2):
        c_copy(1, index).start()
    for index in range(2):
        c_copy(1, index).wait_recv()
    each_block(near_two)
    stores[9].start()
    for part in range(halves):
        sums[part : part + 1, :] = bup_acc[:, part * width : (part + 1) * width]
    weights.all_here()
    stores[10].start()
    weights.finish()
    for part in range(2):
        for index in range(2):
            c_copy(part, index).wait_send()

    def finish(i, carry):
        g_copy(i).wait_send()
        for d in range(1, nz):
            a_copy(i, d).wait_send()
            a_copy(i, d).wait_recv()
        return carry

    lax.fori_loop(0, ROWS_WAVE, finish, 0)
    stores[11].start()
    plane_copy().wait_send()
    core_copy().wait_send()
    for owner in range(nz):
        pass_on(owner).wait_send()

    for owner in range(nz):

        @pl.when(z != owner)
        def _():
            att_copy(owner).wait_send()

    ups.finish()
    downs.finish()
    outer.finish()
    for d in range(1, nz):
        info_copy(d).wait_send()
        wz_copy(d).wait_send()
    for d in range(1, ns):
        ws_copy(d).wait_send()
    for store in stores:
        store.wait()


def run_front(
    dims, tok, w_up, w_out, w_down, cot, wq3, info, bias_qv, slopes, gain, shift, b_out, b_up
):
    ns, nz, rows = dims
    width, units, inner, depth = tok.shape[1], w_up.shape[1], w_out.shape[1], wq3.shape[1]
    span, total, wide = nz * depth, 2 * units + inner, 3 * PAIR
    anywhere = pl.BlockSpec(memory_space=pl.ANY)
    return pl.pallas_call(
        partial(front_kernel, dims),
        name="front",
        out_shape=(
            shape((width, TREE), BF),
            shape((TREE, PAIR), BF),
            shape((TREE, PAIR), BF),
            shape((TREE, PAIR), BF),
            shape((TREE, PAIR), BF),
            shape((16, 512), F32),
            shape((nz, 16, 128), F32),
            shape((width, nz * wide), BF),
            shape((2, span, total), BF),
            shape((TREE, PAIR), BF),
            shape((rows, width), BF),
            shape((rows, width), F32),
            shape((rows, width), F32),
            shape((8, width), F32),
        ),
        in_specs=[pl.BlockSpec(memory_space=pl.ANY)] * 5 + [vmem()] * 8,
        out_specs=[anywhere] * 5 + [vmem()] * 2 + [anywhere] * 6 + [vmem()],
        scratch_shapes=[
            pltpu.VMEM((width, TREE), BF),
            pltpu.VMEM((TREE, PAIR), BF),
            pltpu.VMEM((TREE, PAIR), BF),
            pltpu.VMEM((TREE, PAIR), BF),
            pltpu.VMEM((TREE, PAIR), BF),
            pltpu.VMEM((width, nz * wide), BF),
            pltpu.VMEM((2, span, total), BF),
            pltpu.VMEM((TREE, PAIR), BF),
            pltpu.VMEM((rows, width), BF),
            pltpu.VMEM((rows, width), F32),
            pltpu.VMEM((rows, width), F32),
            pltpu.VMEM((width, 2 * units + 2 * inner), BF),
            pltpu.VMEM((depth, nz * wide), BF),
            pltpu.VMEM((rows, 2 * inner), BF),
            pltpu.VMEM((TREE, width), BF),
            pltpu.VMEM((width, wide), BF),
            pltpu.VMEM((TRUNK, 2 * PAIR), BF),
            pltpu.VMEM((PAIR, TRUNK), BF),
            pltpu.VMEM((16, 128), F32),
            pltpu.VMEM((16, 128), F32),
            pltpu.VMEM((rows, width), BF),
            pltpu.VMEM((2, span, total), BF),
            pltpu.VMEM((rows, width), BF),
            pltpu.VMEM((rows, width), BF),
            pltpu.VMEM((rows, width), BF),
            pltpu.VMEM((rows, width), BF),
            pltpu.VMEM((rows, inner), BF),
            pltpu.VMEM((1, units), F32),
            dma(nz - 1),
            dma(nz - 1),
            dma(nz - 1),
            dma(nz - 1),
            dma(ns - 1),
            dma(ns - 1),
            dma(2, nz, SUBS),
            dma(2, nz, SUBS),
            dma(2, nz, SUBS),
            dma(2, nz, SUBS),
            dma(nz),
            dma(nz),
            dma(5),
            dma(nz),
            dma(nz),
            dma(2),
            dma(2),
            dma(ROWS_WAVE),
            dma(ROWS_WAVE),
            dma(nz - 1, ROWS_WAVE),
            dma(nz - 1, ROWS_WAVE),
            dma(2, 2),
            dma(2, 2),
            dma(12),
            *spread_sems(nz),
            *spread_sems(nz),
            *spread_sems(nz),
            *spread_sems(nz),
        ],
        compiler_params=pltpu.CompilerParams(
            collective_id=0, has_side_effects=True, vmem_limit_bytes=FRONT_LIMIT
        ),
        cost_estimate=pl.CostEstimate(flops=40_000_000_000, bytes_accessed=20_000_000, transcendentals=0),
    )(tok, w_up, w_out, w_down, cot, wq3, info, bias_qv, slopes, gain, shift, b_out, b_up)


class Halve:
    def __init__(self, near, far, cols, dims, depth, bufs, sems):
        self.near, self.far, self.cols, self.depth = near, far, cols, depth
        self.nz = dims[1]
        self.s, self.z = lax.axis_index("shard"), lax.axis_index("ctx")
        self.x_in, self.a_in, self.b_out, self.b_in = bufs
        self.xs, self.xr, self.as_, self.ar, self.bs, self.br = sems

    def place(self, bits):
        low, high = lax.rem(self.z, 2), lax.div(self.z, 2)
        low = 1 - low if bits & 1 else low
        high = 1 - high if bits & 2 else high
        return 2 * high + low

    def block(self, bits):
        return pl.ds(pl.multiple_of(self.place(bits) * self.depth, self.depth), self.depth)

    def x_copy(self):
        low, high = lax.rem(self.s, 2), lax.div(self.s, 2)
        return rcopy(
            self.far.at[:, self.cols],
            self.x_in.at[:, self.cols],
            self.xs,
            self.xr,
            {"shard": 2 * (1 - high) + low},
        )

    def a_copy(self, index):
        return rcopy(
            self.near.at[self.block((1, 3)[index]), self.cols],
            self.a_in.at[index, :, self.cols],
            self.as_.at[index],
            self.ar.at[index],
            {"ctx": self.place(1)},
        )

    def b_copy(self):
        return rcopy(
            self.b_out.at[:, self.cols], self.b_in.at[:, self.cols], self.bs, self.br, {"ctx": self.place(2)}
        )

    def step_x(self):
        self.x_copy().wait_recv()

        def one(r, carry):
            here = pl.ds(pl.multiple_of(r * 32, 32), 32)
            self.near[here, self.cols] = (
                self.near[here, self.cols].astype(F32) + self.x_in[here, self.cols].astype(F32)
            ).astype(BF)
            return carry

        lax.fori_loop(0, self.near.shape[0] // 32, one, 0)
        self.a_copy(0).start()
        self.a_copy(1).start()

    def step_a(self):
        self.a_copy(0).wait_recv()
        self.a_copy(1).wait_recv()
        self.b_out[:, self.cols] = (
            self.near[self.block(2), self.cols].astype(F32) + self.a_in[1, :, self.cols].astype(F32)
        ).astype(BF)
        self.b_copy().start()

    def step_b(self):
        self.b_copy().wait_recv()
        return (
            self.near[self.block(0), self.cols].astype(F32)
            + self.a_in[0, :, self.cols].astype(F32)
            + self.b_in[:, self.cols].astype(F32)
        )

    def finish(self):
        self.x_copy().wait_send()
        self.a_copy(0).wait_send()
        self.a_copy(1).wait_send()
        self.b_copy().wait_send()


PIECES = 6


def back_kernel(
    dims,
    query,
    key,
    value,
    out_heads,
    lse,
    info_all,
    ga_all,
    act_turned_in,
    wqkv_in,
    partial_in,
    down_in,
    mid_in,
    b_down,
    gmid_in,
    tok_in,
    slopes,
    gain,
    shift,
    early,
    result,
    gtok,
    gup,
    gdown,
    gout,
    gwqkv,
    early_sum,
    late_sum,
    act_turned,
    wqkv,
    down_part,
    mid,
    gmid,
    tok,
    near,
    x_in,
    a_in,
    b_out,
    b_in,
    q_near,
    q_far,
    q_core,
    qx_in,
    q_all,
    dqkv,
    dk_trunk,
    dv_trunk,
    dk_seg,
    dv_seg,
    dk_up,
    dv_up,
    keys_aug,
    keys_turned,
    labels,
    parents,
    dq_all,
    n_send,
    n_recv,
    down_recv,
    wg_send,
    early_mine,
    early_recv,
    late,
    late_recv,
    d_sem,
    e_send,
    e_recv,
    f_send,
    f_recv,
    l_send,
    l_recv,
    p_send,
    p_recv,
    r_send,
    r_recv,
    ns_sem,
    nr_sem,
    xs_sem,
    xr_sem,
    as_sem,
    ar_sem,
    bs_sem,
    br_sem,
    qc_send,
    qc_recv,
    qx_sem,
    qz_send,
    qz_recv,
    n_local,
    load_sem,
):
    ns, nz, rows = dims
    s, z, y = lax.axis_index("shard"), lax.axis_index("ctx"), lax.axis_index("tp")
    count = ns * nz
    me = s * nz + z
    chunk = rows // ROWS_WAVE
    width = tok.shape[1]
    depth = width // count
    span = nz * depth
    wide = 3 * PAIR
    other = {"tp": 1 - y}
    total_cols = near.shape[1]
    step_cols = total_cols // PIECES
    units = gup.shape[1]

    far = partial_in.at[1]
    load = pltpu.make_async_copy(partial_in.at[0], near, n_local)
    loads = [
        pltpu.make_async_copy(a, c, load_sem.at[k])
        for k, (a, c) in enumerate(
            (
                (down_in, down_part),
                (act_turned_in, act_turned),
                (wqkv_in, wqkv),
                (mid_in, mid),
                (gmid_in, gmid),
                (tok_in, tok),
            )
        )
    ]
    loads[0].start()
    load.start()
    for one in loads[1:]:
        one.start()

    def peer(d):
        index = lax.rem(me + d, count)
        return index, {"shard": lax.div(index, nz), "ctx": lax.rem(index, nz)}

    greet([other] + [peer(d)[1] for d in range(1, count)])

    halves = [
        Halve(
            near,
            far,
            slice(i * step_cols, (i + 1) * step_cols),
            dims,
            depth,
            (x_in, a_in, b_out, b_in),
            (xs_sem.at[i], xr_sem.at[i], as_sem.at[i], ar_sem.at[i], bs_sem.at[i], br_sem.at[i]),
        )
        for i in range(PIECES)
    ]
    def shard_flip(bits):
        low, high = lax.rem(s, 2), lax.div(s, 2)
        low = 1 - low if bits & 1 else low
        high = 1 - high if bits & 2 else high
        return 2 * high + low

    def q_copy(index):
        return rcopy(
            wg_send.at[pl.ds(pl.multiple_of(shard_flip((1, 3)[index]) * span, 128), span), :],
            q_core.at[index],
            qc_send.at[index],
            qc_recv.at[index],
            {"shard": shard_flip(1)},
        )

    def qx_copy():
        return rcopy(q_far, qx_in, qx_sem.at[0], qx_sem.at[1], {"shard": shard_flip(2)})

    def qz_copy(d):
        to = lax.rem(z + d, nz)
        return rcopy(
            q_near.at[pl.ds(pl.multiple_of(to * depth, depth), depth), :],
            q_all.at[z],
            qz_send.at[d - 1],
            qz_recv.at[d - 1],
            {"ctx": to},
        )

    def q_spread():
        qx_copy().wait_recv()
        q_near[...] = (q_near[...].astype(F32) + qx_in[...].astype(F32)).astype(BF)
        for d in range(1, nz):
            qz_copy(d).start()
        q_all[z] = q_near[pl.ds(pl.multiple_of(z * depth, depth), depth), :]

    def down_copy():
        return rcopy(down_part, down_recv, d_sem.at[0], d_sem.at[1], other)

    owners = width // 128

    def owner_cols(index):
        return pl.ds(pl.multiple_of(index * 128, 128), 128)

    def early_copy(d):
        index, device = peer(d)
        return index, rcopy(
            early_mine.at[:, owner_cols(lax.rem(index, owners))],
            early_recv.at[me],
            e_send.at[d - 1],
            e_recv.at[d - 1],
            device,
        )

    def spread_copy(d):
        cols = owner_cols(lax.rem(me, owners))
        return rcopy(
            early_sum.at[:, cols], early_sum.at[:, cols], f_send.at[d - 1], f_recv.at[d - 1], peer(d)[1]
        )

    def spread_arrival(d):
        index = lax.rem(me + count - d, count)
        cols = owner_cols(lax.rem(index, owners))
        return index, rcopy(
            early_sum.at[:, cols], early_sum.at[:, cols], f_send.at[d - 1], f_recv.at[d - 1], other
        )

    def late_copy(d):
        return rcopy(late, late_recv.at[me], l_send.at[d - 1], l_recv.at[d - 1], peer(d)[1])

    def over_peers(act):
        def one(d, carry):
            act(d)
            return carry

        lax.fori_loop(1, count, one, 0)

    for half in halves:
        half.x_copy().start()
    loads[0].wait()
    down_copy().start()

    fill_labels(info_all, rows // BRANCH, labels, parents)
    fill_trunk_keys(key, keys_aug)
    keys_turned[...] = key[0:TRUNK, :].T
    dk_trunk[...] = jnp.zeros(dk_trunk.shape, F32)
    dv_trunk[...] = jnp.zeros(dv_trunk.shape, F32)
    tile_mask = causal(BRANCH)

    def row_products(here, count_rows):
        turned = (ga_all[here, :].astype(F32) * out_heads[here, :].astype(F32)).T
        return jnp.concatenate(
            [
                jnp.sum(turned[:HD, :], axis=0, keepdims=True),
                jnp.sum(turned[HD:, :], axis=0, keepdims=True),
            ],
            axis=1,
        )

    def part_back(key_aug, value_rows, asked, given, level, drow, mask):
        logits = nt(key_aug, asked) * LOG2E - level
        if mask is not None:
            logits = jnp.where(mask, logits, NEG)
        probs = jnp.exp2(logits)
        grads = (probs * (nt(value_rows, given) - drow)).astype(BF)
        return probs.astype(BF), grads

    def segment(slot, carry):
        here = pl.ds(pl.multiple_of(TRUNK + slot * BRANCH, 128), BRANCH)
        seg = pl.ds(pl.multiple_of(slot * BRANCH, 128), BRANCH)
        stacked = stack_heads(query[here, :])
        asked = jnp.concatenate([stacked, query_features(slopes, BRANCH)], axis=1)
        given = stack_heads(ga_all[here, :])
        leaf, key_up, value_up = parent_pick(slot, labels, parents, key, value)
        own_feats, up_feats = segment_key_features(leaf)
        level = lse[pl.ds(4 + slot, 1), 0 : 2 * BRANCH]
        drow = row_products(here, BRANCH)
        probs, grads = part_back(keys_aug[...], value[0:TRUNK, :], asked, given, level, drow, None)
        dv_trunk[...] += nn(probs, given)
        dk_trunk[...] += nn(grads, stacked)
        turned = nn(keys_turned[...], grads)
        key_own = key[here, :]
        probs, grads = part_back(
            jnp.concatenate([key_own, own_feats], axis=1), value[here, :], asked, given, level, drow, tile_mask
        )
        dv_seg[seg, :] = nn(probs, given)
        dk_seg[seg, :] = nn(grads, stacked)
        turned = turned + nn(key_own.T, grads)
        probs, grads = part_back(
            jnp.concatenate([key_up, up_feats], axis=1), value_up, asked, given, level, drow, None
        )
        dv_up[seg, :] = nn(probs, given)
        dk_up[seg, :] = nn(grads, stacked)
        turned = turned + nn(key_up.T, grads)
        dqkv[here, 0:PAIR] = (unstack_turned(turned, BRANCH) * HD ** (-0.5)).astype(BF)
        return carry

    def dq_copy(to):
        return rcopy(
            dqkv.at[to * rows : (to + 1) * rows, 0:PAIR],
            dq_all.at[:, pl.ds(pl.multiple_of(z * wide, 128), PAIR)],
            r_send.at[to],
            r_recv.at[z],
            {"ctx": to},
        )

    def send_dq(to):
        @pl.when(z != to)
        def _():
            dq_copy(to).start()

    def piece_copy(to, i):
        return rcopy(
            dqkv.at[to * rows + i * chunk : to * rows + (i + 1) * chunk, PAIR:],
            dq_all.at[i * chunk : (i + 1) * chunk, pl.ds(pl.multiple_of(z * wide + PAIR, 128), 2 * PAIR)],
            p_send.at[to, i],
            p_recv.at[z, i],
            {"ctx": to},
        )

    wave_rows = TRUNK // 4
    wave_mask = causal(wave_rows)
    for tile in range(4):
        lo, hi = tile * wave_rows, (tile + 1) * wave_rows
        stacked = stack_heads(query[lo:hi, :])
        asked = jnp.concatenate([stacked, query_features(slopes, wave_rows)], axis=1)
        given = stack_heads(ga_all[lo:hi, :])
        level = lse[tile : tile + 1, :]
        drow = row_products(pl.ds(lo, wave_rows), wave_rows)
        probs, grads = part_back(
            keys_aug[lo:hi, :], value[lo:hi, :], asked, given, level, drow, wave_mask
        )
        dv_trunk[lo:hi, :] += nn(probs, given)
        dk_trunk[lo:hi, :] += nn(grads, stacked)
        turned = nn(keys_turned[:, lo:hi], grads)
        if tile:
            probs, grads = part_back(
                keys_aug[0:lo, :], value[0:lo, :], asked, given, level, drow, None
            )
            dv_trunk[0:lo, :] += nn(probs, given)
            dk_trunk[0:lo, :] += nn(grads, stacked)
            turned = turned + nn(keys_turned[:, 0:lo], grads)
        dqkv[lo:hi, 0:PAIR] = (unstack_turned(turned, wave_rows) * HD ** (-0.5)).astype(BF)
    send_dq(0)

    def segments(lo, hi):
        lax.fori_loop((lo - TRUNK) // BRANCH, (hi - TRUNK) // BRANCH, segment, 0)

    segments(2 * rows, 3 * rows)
    send_dq(2)
    segments(TRUNK, 2 * rows)
    send_dq(1)
    load.wait()
    halves[0].step_x()
    segments(3 * rows, 4 * rows)
    halves[1].step_x()
    send_dq(3)

    def gather_up(slot, carry):
        here = pl.ds(pl.multiple_of(TRUNK + slot * BRANCH, 128), BRANCH)
        seg = pl.ds(pl.multiple_of(slot * BRANCH, 128), BRANCH)
        mine = labels[pl.ds(slot, 1), :]
        dk, dv = dk_seg[seg, :], dv_seg[seg, :]
        for below in range(SLOTS):
            same = (parents[below : below + 1, :] == mine).astype(F32)
            at = below * BRANCH
            dk = dk + same * dk_up[at : at + BRANCH, :]
            dv = dv + same * dv_up[at : at + BRANCH, :]
        dqkv[here, PAIR : 2 * PAIR] = dk.astype(BF)
        dqkv[here, 2 * PAIR :] = dv.astype(BF)
        return carry

    lax.fori_loop(0, SLOTS, gather_up, 0)
    dqkv[0:TRUNK, PAIR : 2 * PAIR] = dk_trunk[...].astype(BF)
    dqkv[0:TRUNK, 2 * PAIR :] = dv_trunk[...].astype(BF)
    for i in range(ROWS_WAVE):
        for to in range(nz):

            @pl.when(z != to)
            def _():
                piece_copy(to, i).start()

    for to in range(nz):

        @pl.when(z == to)
        def _():
            dq_all[:, pl.ds(pl.multiple_of(z * wide, 128), wide)] = dqkv[to * rows : (to + 1) * rows, :]

    def weight(block, carry):
        here = pl.ds(pl.multiple_of(block * 128, 128), 128)
        wg_send[here, :] = nn(act_turned[here, :], dqkv[...]).astype(BF)
        return carry

    loads[1].wait()
    lax.fori_loop(0, width // 128, weight, 0)
    q_copy(0).start()
    q_copy(1).start()

    early_mine[...] = early[...]
    early_mine[6:7, pl.ds(pl.multiple_of(z * PAIR, 128), PAIR)] = jnp.sum(
        dqkv[:, 0:PAIR].astype(F32), axis=0, keepdims=True
    )
    early_mine[6:7, pl.ds(pl.multiple_of((nz + z) * PAIR, 128), PAIR)] = jnp.sum(
        dqkv[:, 2 * PAIR :].astype(F32), axis=0, keepdims=True
    )

    def early_send(d):
        index, copy = early_copy(d)

        @pl.when(index < owners)
        def _():
            copy.start()

    over_peers(early_send)
    early_recv[me] = early_mine[:, owner_cols(lax.rem(me, owners))]

    def at(i):
        return pl.ds(pl.multiple_of(i * chunk, 32), chunk)

    def n_copy(i):
        return rcopy(n_send.at[at(i), :], n_recv.at[at(i), :], ns_sem.at[i], nr_sem.at[i], other)

    def core_join():
        for index in range(2):
            q_copy(index).wait_recv()
            mine = pl.ds(pl.multiple_of(shard_flip((0, 2)[index]) * span, 128), span)
            (q_near, q_far)[index][...] = (wg_send[mine, :].astype(F32) + q_core[index].astype(F32)).astype(BF)
        qx_copy().start()

    def first(i):
        for owner in range(nz):

            @pl.when(z != owner)
            def _():
                if i == 0:
                    rcopy(
                        dqkv.at[0:rows, 0:PAIR],
                        dq_all.at[:, owner * wide : owner * wide + PAIR],
                        r_send.at[owner],
                        r_recv.at[owner],
                        {"ctx": owner},
                    ).wait_recv()
                rcopy(
                    dqkv.at[0:chunk, PAIR:],
                    dq_all.at[i * chunk : (i + 1) * chunk, owner * wide + PAIR : (owner + 1) * wide],
                    p_send.at[owner, i],
                    p_recv.at[owner, i],
                    {"ctx": owner},
                ).wait_recv()

        n_send[at(i), :] = nt(dq_all[at(i), :], wqkv[...]).astype(BF)
        n_copy(i).start()

    def second(i, carry):
        n_copy(i).wait_recv()
        here = at(i)
        grad = n_send[here, :].astype(F32) + n_recv[here, :].astype(F32)
        _, normed, inverse = norm_rows(tok[here, :].astype(F32), gain[0:1, :], shift[0:1, :])
        gtok[here, :] = gmid[here, :] + norm_rows_back(grad, normed, inverse, gain[0:1, :])
        late[0:1, :] += jnp.sum(grad * normed, axis=0, keepdims=True)
        late[1:2, :] += jnp.sum(grad, axis=0, keepdims=True)
        return carry

    def output(i, carry):
        here = at(i)
        result[here, :] = (
            mid[here, :] + b_down[...] + (down_part[here, :].astype(F32) + down_recv[here, :].astype(F32))
        ).astype(BF)
        return carry

    late[...] = jnp.zeros(late.shape, F32)
    for one in loads[2:]:
        one.wait()
    core_join()
    halves[2].step_x()
    first(0)
    first(1)
    halves[3].step_x()
    first(2)
    halves[4].step_x()
    first(3)
    halves[5].step_x()
    down_copy().wait_recv()
    lax.fori_loop(0, ROWS_WAVE, output, 0)

    @pl.when(me < owners)
    def _():
        over_peers(lambda d: early_copy(d)[1].wait_recv())
        total = early_recv[0]
        for index in range(1, count):
            total = total + early_recv[index]
        early_sum[:, owner_cols(lax.rem(me, owners))] = total
        over_peers(lambda d: spread_copy(d).start())

    q_spread()
    halves[0].step_a()
    halves[1].step_a()
    lax.fori_loop(0, 2, second, 0)
    halves[2].step_a()
    lax.fori_loop(2, ROWS_WAVE, second, 0)
    over_peers(lambda d: late_copy(d).start())
    late_recv[me] = late[...]
    halves[3].step_a()
    halves[4].step_a()
    halves[5].step_a()

    for d in range(1, nz):
        qz_copy(d).wait_recv()
    for owner in range(nz):
        for part in range(3):
            gwqkv[part, :, owner * PAIR : (owner + 1) * PAIR] = q_all[
                owner, :, part * PAIR : (part + 1) * PAIR
            ].astype(F32)
    bounds = (0, units, 2 * units, total_cols)
    for i, half in enumerate(halves):
        block = half.step_b()
        lo, hi = i * step_cols, (i + 1) * step_cols
        for target, start_at, end_at in (
            (gup, bounds[0], bounds[1]),
            (gdown, bounds[1], bounds[2]),
            (gout, bounds[2], bounds[3]),
        ):
            a, b = max(lo, start_at), min(hi, end_at)
            if a < b:
                target[:, a - start_at : b - start_at] = block[:, a - lo : b - lo]

    def early_wait(d):
        index, copy = spread_arrival(d)

        @pl.when(index < owners)
        def _():
            copy.wait_recv()

    over_peers(early_wait)
    over_peers(lambda d: late_copy(d).wait_recv())
    total = late_recv[0]
    for index in range(1, count):
        total = total + late_recv[index]
    late_sum[...] = total

    down_copy().wait_send()
    for half in halves:
        half.finish()
    qx_copy().wait_send()
    for d in range(1, nz):
        qz_copy(d).wait_send()
    q_copy(0).wait_send()
    q_copy(1).wait_send()

    def early_drain(d):
        index, copy = early_copy(d)

        @pl.when(index < owners)
        def _():
            copy.wait_send()

    over_peers(early_drain)

    @pl.when(me < owners)
    def _():
        over_peers(lambda d: spread_copy(d).wait_send())

    over_peers(lambda d: late_copy(d).wait_send())

    def finish(i, carry):
        n_copy(i).wait_send()
        return carry

    lax.fori_loop(0, ROWS_WAVE, finish, 0)
    for owner in range(nz):

        @pl.when(z != owner)
        def _():
            dq_copy(owner).wait_send()
            for i in range(ROWS_WAVE):
                piece_copy(owner, i).wait_send()


def run_back(dims, units, *inputs):
    ns, nz, rows = dims
    width = inputs[14].shape[1]
    _, span, total = inputs[9].shape
    count = ns * nz
    depth = width // count
    wide = 3 * PAIR
    anywhere = pl.BlockSpec(memory_space=pl.ANY)
    return pl.pallas_call(
        partial(back_kernel, dims),
        name="tree_backward",
        out_shape=(
            shape((rows, width), BF),
            shape((rows, width), F32),
            shape((depth, units), F32),
            shape((depth, units), F32),
            shape((depth, total - 2 * units), F32),
            shape((3, depth, nz * PAIR), F32),
            shape((8, width), F32),
            shape((2, width), F32),
        ),
        in_specs=[vmem()] * 7 + [anywhere] * 5 + [vmem()] + [anywhere] * 2 + [vmem()] * 4,
        out_specs=[vmem()] * 8,
        scratch_shapes=[
            *[pltpu.VMEM(inputs[k].shape, inputs[k].dtype) for k in (7, 8, 10, 11, 13, 14)],
            pltpu.VMEM((span, total), BF),
            pltpu.VMEM((span, total), BF),
            pltpu.VMEM((2, depth, total), BF),
            pltpu.VMEM((depth, total), BF),
            pltpu.VMEM((depth, total), BF),
            pltpu.VMEM((span, wide), BF),
            pltpu.VMEM((span, wide), BF),
            pltpu.VMEM((2, span, wide), BF),
            pltpu.VMEM((span, wide), BF),
            pltpu.VMEM((nz, depth, wide), BF),
            pltpu.VMEM((TREE, wide), BF),
            pltpu.VMEM((TRUNK, PAIR), F32),
            pltpu.VMEM((TRUNK, PAIR), F32),
            pltpu.VMEM((TREE - TRUNK, PAIR), F32),
            pltpu.VMEM((TREE - TRUNK, PAIR), F32),
            pltpu.VMEM((TREE - TRUNK, PAIR), F32),
            pltpu.VMEM((TREE - TRUNK, PAIR), F32),
            pltpu.VMEM((TRUNK, 2 * PAIR), BF),
            pltpu.VMEM((PAIR, TRUNK), BF),
            pltpu.VMEM((16, 128), F32),
            pltpu.VMEM((16, 128), F32),
            pltpu.VMEM((rows, nz * wide), BF),
            pltpu.VMEM((rows, width), BF),
            pltpu.VMEM((rows, width), BF),
            pltpu.VMEM((rows, width), BF),
            pltpu.VMEM((width, wide), BF),
            pltpu.VMEM((8, width), F32),
            pltpu.VMEM((count, 8, 128), F32),
            pltpu.VMEM((2, width), F32),
            pltpu.VMEM((count, 2, width), F32),
            dma(2),
            dma(count - 1),
            dma(count - 1),
            dma(count - 1),
            dma(count - 1),
            dma(count - 1),
            dma(count - 1),
            dma(nz, ROWS_WAVE),
            dma(nz, ROWS_WAVE),
            dma(nz),
            dma(nz),
            dma(ROWS_WAVE),
            dma(ROWS_WAVE),
            dma(PIECES),
            dma(PIECES),
            dma(PIECES, 2),
            dma(PIECES, 2),
            dma(PIECES),
            dma(PIECES),
            dma(2),
            dma(2),
            dma(2),
            dma(nz - 1),
            dma(nz - 1),
            pltpu.SemaphoreType.DMA,
            dma(6),
        ],
        compiler_params=pltpu.CompilerParams(
            collective_id=2, has_side_effects=True, vmem_limit_bytes=60 << 20
        ),
        cost_estimate=pl.CostEstimate(flops=40_000_000_000, bytes_accessed=20_000_000, transcendentals=0),
    )(*inputs)


def place_kernel(early, late, *refs):
    count = (len(refs) - 7) // 3
    sources, targets, middle = refs[:count], refs[count : 2 * count], refs[2 * count + 6 : -1]
    b_qv, b_out, b_up, b_down, gains, shifts = refs[2 * count : 2 * count + 6]
    sems = refs[-1]
    loads = [pltpu.make_async_copy(a, b, sems.at[0, k]) for k, (a, b) in enumerate(zip(sources, middle))]
    copies = [pltpu.make_async_copy(a, b, sems.at[1, k]) for k, (a, b) in enumerate(zip(middle, targets))]
    for load in loads:
        load.start()
    for load, copy in zip(loads, copies):
        load.wait()
        copy.start()
    wide, width = b_qv.shape[1], b_out.shape[1]
    for row in range(2):
        b_qv[row : row + 1, :] = early[6:7, row * wide : (row + 1) * wide]
    b_out[...] = early[2:3, :]
    for row in range(b_up.shape[1] // width):
        b_up[:, row * width : (row + 1) * width] = early[row : row + 1, :]
    b_down[...] = early[3:4, :]
    gains[0:1, :] = late[0:1, :]
    gains[1:2, :] = early[4:5, :]
    shifts[0:1, :] = late[1:2, :]
    shifts[1:2, :] = early[5:6, :]
    for copy in copies:
        copy.wait()


def run_place(early, late, wide, units, *arrays):
    width = early.shape[1]
    anywhere = pl.BlockSpec(memory_space=pl.ANY)
    return pl.pallas_call(
        place_kernel,
        name="place",
        out_shape=(
            *[shape(a.shape, a.dtype) for a in arrays],
            shape((2, wide), F32),
            shape((1, width), F32),
            shape((1, units), F32),
            shape((1, width), F32),
            shape((2, width), F32),
            shape((2, width), F32),
        ),
        in_specs=[vmem()] * 2 + [anywhere] * len(arrays),
        out_specs=[anywhere] * len(arrays) + [vmem()] * 6,
        scratch_shapes=[*[pltpu.VMEM(a.shape, a.dtype) for a in arrays], dma(2, len(arrays))],
        compiler_params=pltpu.CompilerParams(vmem_limit_bytes=60 << 20),
    )(early, late, *arrays)


def fast_device(
    tokens, cotangent, seg_ids, positions, parents, w_qkv, b_qv, w_out, b_out, w_up, b_up, w_down, b_down, ln_gain, ln_bias
):
    rows = tokens.shape[0]
    ns, nz, ntp = lax.axis_size("shard"), lax.axis_size("ctx"), lax.axis_size("tp")
    dims = (ns, nz, rows)

    labels = seg_ids.reshape(rows // BRANCH, BRANCH)[:, 0]
    match = labels[:, None] == jnp.arange(parents.shape[0], dtype=jnp.int32)[None, :]
    above = jnp.sum(jnp.where(match, parents[None, :], 0), axis=1)
    fill = 8 - rows // BRANCH
    lines = jnp.concatenate([jnp.pad(labels, (0, fill)), jnp.pad(above, (0, fill))]).astype(F32)
    info = jnp.broadcast_to(lines[:, None], (16, 128))
    per = HEADS // ntp
    index = lax.axis_index("tp") * per + lax.axis_index("ctx") * 2 + jnp.arange(2)
    slope = 2.0 ** (-8.0 * (index.astype(F32) + 1.0) / HEADS)
    one = lax.reduce_precision(slope, 8, 7)
    two = lax.reduce_precision(slope - one, 8, 7)
    three = lax.reduce_precision(slope - one - two, 8, 7)
    table = jnp.stack([one, two, three, one, two, three, jnp.ones_like(one)], axis=1)
    slopes = jnp.pad(table, ((0, 0), (0, 121)))

    units = b_up.shape[0]
    (
        act_turned, query, key, value, out_heads, lse, info_all, wqkv, partial_sums, ga_all, down_part, mid, gmid, sums
    ) = run_front(
        dims, tokens, w_up, w_out.T, w_down.T, cotangent, w_qkv, info, b_qv, slopes, ln_gain, ln_bias,
        b_out[None, :], b_up[None, :],
    )
    result, grad_tokens, gup, gdown, gout, grad_w_qkv, early, late = run_back(
        dims, units, query, key, value, out_heads, lse, info_all, ga_all, act_turned, wqkv, partial_sums, down_part,
        mid, b_down[None, :], gmid, tokens, slopes, ln_gain, ln_bias, sums,
    )
    result, grad_tokens, grad_w_qkv, gup, gdown, gout, b_qv_sum, b_out_sum, b_up_sum, b_down_sum, gains, shifts = run_place(
        early, late, nz * PAIR, units, result, grad_tokens, grad_w_qkv, gup, gdown, gout
    )
    return (
        result,
        grad_tokens,
        grad_w_qkv,
        b_qv_sum,
        gout.T,
        b_out_sum.reshape(-1),
        gup,
        b_up_sum.reshape(-1),
        gdown.T,
        b_down_sum.reshape(-1),
        gains,
        shifts,
    )


def norm_forward(inputs_in, gain_row, shift_row):
    centre = inputs_in - jnp.mean(inputs_in, axis=-1, keepdims=True)
    inverse = lax.rsqrt(jnp.mean(centre * centre, axis=-1, keepdims=True) + EPS)
    normed = centre * inverse
    return (normed * gain_row + shift_row, normed, inverse)


def norm_backward(grad_in, normed, inverse, gain_row):
    scaled = grad_in * gain_row
    mean_grad = jnp.mean(scaled, axis=-1, keepdims=True)
    mean_cross = jnp.mean(scaled * normed, axis=-1, keepdims=True)
    return inverse * (scaled - mean_grad - normed * mean_cross)


def ancestry(seg_vals, parents):
    first_up = jnp.take(parents, seg_vals)
    return (first_up, jnp.take(parents, first_up))


def block_scores(query_heads, key_heads, query_tags, key_tags, slopes):
    q_seg, q_first, q_second, q_pos = query_tags
    k_seg, k_pos = key_tags
    raw_scores = jnp.einsum(
        "qhd,khd->hqk", query_heads, key_heads, preferred_element_type=jnp.float32
    ) * HD ** (-0.5)
    distance = (q_pos[:, None] - k_pos[None, :]).astype(jnp.float32)
    scores = raw_scores - slopes[:, None, None] * distance[None]
    related = (
        (k_seg[None, :] == q_seg[:, None])
        | (k_seg[None, :] == q_first[:, None])
        | (k_seg[None, :] == q_second[:, None])
    )
    allowed = related & (k_pos[None, :] <= q_pos[:, None])
    return (scores, allowed[None])


def probabilities(scores, allowed, row_max, row_sum):
    shifted = jnp.where(allowed, scores - row_max[:, :, None], NEG)
    return jnp.exp(shifted) / row_sum[:, :, None]


def per_device(
    tokens,
    cotangent,
    seg_ids,
    positions,
    parents,
    w_qkv,
    b_qv,
    w_out,
    b_out,
    w_up,
    b_up,
    w_down,
    b_down,
    ln_gain,
    ln_bias,
):
    num_rows = tokens.shape[0]
    head_count = HEADS // lax.axis_size("tp")
    head_width = head_count * HD
    head_index = (lax.axis_index("tp") * head_count + jnp.arange(head_count)).astype(jnp.float32)
    slopes = 2.0 ** (-8.0 * (head_index + 1.0) / HEADS)
    scale = HD ** (-0.5)
    full_qkv, full_out = (
        lax.all_gather(w_qkv, ("shard", "ctx"), axis=1, tiled=True),
        lax.all_gather(w_out, ("shard", "ctx"), axis=1, tiled=True),
    )
    group_seg, group_pos = (
        lax.all_gather(seg_ids, "ctx", axis=0, tiled=True),
        lax.all_gather(positions, "ctx", axis=0, tiled=True),
    )
    own_first, own_second = ancestry(seg_ids, parents)
    own_tags = (seg_ids, own_first, own_second, positions)
    inputs = tokens.astype(jnp.float32)
    norm_one, normed_one, inverse_one = norm_forward(inputs, ln_gain[0], ln_bias[0])
    act_one = norm_one.astype(jnp.bfloat16)
    projected = jnp.einsum("td,cde->cte", act_one, full_qkv, preferred_element_type=jnp.float32)
    qkv_bias = jnp.stack([b_qv[0], jnp.zeros((head_width,), jnp.float32), b_qv[1]])
    qkv_low = (projected + qkv_bias[:, None, :]).astype(jnp.bfloat16)
    query_flat, key_flat, value_flat = (qkv_low[0], qkv_low[1], qkv_low[2])
    group_keys, group_values = (
        lax.all_gather(key_flat, "ctx", axis=0, tiled=True),
        lax.all_gather(value_flat, "ctx", axis=0, tiled=True),
    )
    group_rows = group_keys.shape[0]
    block_count = group_rows // KEY_BLOCK
    key_blocks = group_keys.reshape(block_count, KEY_BLOCK, head_count, HD)
    value_blocks = group_values.reshape(block_count, KEY_BLOCK, head_count, HD)
    seg_blocks = group_seg.reshape(block_count, KEY_BLOCK)
    pos_blocks = group_pos.reshape(block_count, KEY_BLOCK)
    query_heads = query_flat.reshape(num_rows, head_count, HD)

    def stats_step(carry_in, block_parts):
        row_max, row_sum = carry_in
        key_part, seg_part, pos_part = block_parts
        scores, allowed = block_scores(
            query_heads, key_part, own_tags, (seg_part, pos_part), slopes
        )
        new_max = jnp.maximum(row_max, jnp.max(jnp.where(allowed, scores, NEG), axis=-1))
        shifted = jnp.where(allowed, scores - new_max[:, :, None], NEG)
        row_sum = row_sum * jnp.exp(row_max - new_max) + jnp.sum(jnp.exp(shifted), axis=-1)
        return ((new_max, row_sum), None)

    start_stats = (
        jnp.full((head_count, num_rows), NEG, jnp.float32),
        jnp.zeros((head_count, num_rows), jnp.float32),
    )
    (row_max, row_sum), _ = lax.scan(stats_step, start_stats, (key_blocks, seg_blocks, pos_blocks))

    def output_step(out_accum, block_parts):
        key_part, value_part, seg_part, pos_part = block_parts
        scores, allowed = block_scores(
            query_heads, key_part, own_tags, (seg_part, pos_part), slopes
        )
        prob_low = probabilities(scores, allowed, row_max, row_sum).astype(jnp.bfloat16)
        return (
            out_accum
            + jnp.einsum("hqk,khd->qhd", prob_low, value_part, preferred_element_type=jnp.float32),
            None,
        )

    attended, _ = lax.scan(
        output_step,
        jnp.zeros((num_rows, head_count, HD), jnp.float32),
        (key_blocks, value_blocks, seg_blocks, pos_blocks),
    )
    attended_low = attended.reshape(num_rows, head_width).astype(jnp.bfloat16)
    branch_one = (
        lax.psum(
            jnp.dot(attended_low, full_out, preferred_element_type=jnp.float32).astype(
                jnp.bfloat16
            ),
            "tp",
        ).astype(jnp.float32)
        + b_out
    )
    middle = inputs + branch_one
    full_up, full_down = (
        lax.all_gather(w_up, ("shard", "ctx"), axis=0, tiled=True),
        lax.all_gather(w_down, ("shard", "ctx"), axis=1, tiled=True),
    )
    norm_two, normed_two, inverse_two = norm_forward(middle, ln_gain[1], ln_bias[1])
    act_two = norm_two.astype(jnp.bfloat16)
    upper_in = jnp.dot(act_two, full_up, preferred_element_type=jnp.float32) + b_up
    gelu_vals, gelu_pull = jax.vjp(partial(jax.nn.gelu, approximate=True), upper_in)
    hidden = gelu_vals.astype(jnp.bfloat16)
    branch_two = (
        lax.psum(
            jnp.dot(hidden, full_down, preferred_element_type=jnp.float32).astype(jnp.bfloat16),
            "tp",
        ).astype(jnp.float32)
        + b_down
    )
    result = (middle + branch_two).astype(jnp.bfloat16)
    grad_out = cotangent.astype(jnp.float32)
    grad_hidden = jnp.einsum("td,fd->tf", cotangent, full_down, preferred_element_type=jnp.float32)
    grad_upper = gelu_pull(grad_hidden)[0].astype(jnp.bfloat16)
    down_term = jnp.einsum("tf,td->fd", hidden, cotangent, preferred_element_type=jnp.float32)
    up_term = jnp.einsum("td,tf->df", act_two, grad_upper, preferred_element_type=jnp.float32)
    grad_w_up, grad_w_down = (
        lax.psum_scatter(up_term, ("shard", "ctx"), scatter_dimension=0, tiled=True),
        lax.psum_scatter(down_term, ("shard", "ctx"), scatter_dimension=1, tiled=True),
    )
    grad_norm_two = lax.psum(
        jnp.einsum("tf,df->td", grad_upper, full_up, preferred_element_type=jnp.float32).astype(
            jnp.bfloat16
        ),
        "tp",
    ).astype(jnp.float32)
    grad_middle = grad_out + norm_backward(grad_norm_two, normed_two, inverse_two, ln_gain[1])
    grad_branch = grad_middle.astype(jnp.bfloat16)
    out_term = jnp.einsum(
        "te,td->ed", attended_low, grad_branch, preferred_element_type=jnp.float32
    )
    grad_att = jnp.einsum(
        "td,ed->te", grad_branch, full_out, preferred_element_type=jnp.float32
    ).astype(jnp.bfloat16)
    grad_heads = grad_att.reshape(num_rows, head_count, HD)
    row_terms = jnp.einsum("qhd,qhd->hq", grad_heads.astype(jnp.float32), attended)

    def joint_step(grad_accum, block_parts):
        key_part, value_part, seg_part, pos_part = block_parts
        scores, allowed = block_scores(
            query_heads, key_part, own_tags, (seg_part, pos_part), slopes
        )
        prob_vals = probabilities(scores, allowed, row_max, row_sum)
        grad_probs = jnp.einsum(
            "qhd,khd->hqk", grad_heads, value_part, preferred_element_type=jnp.float32
        )
        grad_scores = (prob_vals * (grad_probs - row_terms[:, :, None])).astype(jnp.bfloat16)
        grad_accum = (
            grad_accum
            + jnp.einsum("hqk,khd->qhd", grad_scores, key_part, preferred_element_type=jnp.float32)
            * scale
        )
        key_part_grad = (
            jnp.einsum("hqk,qhd->khd", grad_scores, query_heads, preferred_element_type=jnp.float32)
            * scale
        )
        value_part_grad = jnp.einsum(
            "hqk,qhd->khd",
            prob_vals.astype(jnp.bfloat16),
            grad_heads,
            preferred_element_type=jnp.float32,
        )
        return (
            grad_accum,
            (
                key_part_grad.reshape(KEY_BLOCK, head_width),
                value_part_grad.reshape(KEY_BLOCK, head_width),
            ),
        )

    grad_query_sum, (key_terms, value_terms) = lax.scan(
        joint_step,
        jnp.zeros((num_rows, head_count, HD), jnp.float32),
        (key_blocks, value_blocks, seg_blocks, pos_blocks),
    )
    key_grad_sum, value_grad_sum = (
        lax.psum_scatter(
            key_terms.reshape(group_rows, head_width).astype(jnp.bfloat16),
            "ctx",
            scatter_dimension=0,
            tiled=True,
        ).astype(jnp.float32),
        lax.psum_scatter(
            value_terms.reshape(group_rows, head_width).astype(jnp.bfloat16),
            "ctx",
            scatter_dimension=0,
            tiled=True,
        ).astype(jnp.float32),
    )
    grad_query_low = grad_query_sum.reshape(num_rows, head_width).astype(jnp.bfloat16)
    grad_key_low = key_grad_sum.astype(jnp.bfloat16)
    grad_value_low = value_grad_sum.astype(jnp.bfloat16)
    grad_qkv = jnp.stack([grad_query_low, grad_key_low, grad_value_low])
    grad_norm_one = lax.psum(
        jnp.einsum("cte,cde->td", grad_qkv, full_qkv, preferred_element_type=jnp.float32).astype(
            jnp.bfloat16
        ),
        "tp",
    ).astype(jnp.float32)
    grad_tokens = grad_middle + norm_backward(grad_norm_one, normed_one, inverse_one, ln_gain[0])
    qkv_term = jnp.einsum("td,cte->cde", act_one, grad_qkv, preferred_element_type=jnp.float32)
    grad_w_qkv, grad_w_out = (
        lax.psum_scatter(qkv_term, ("shard", "ctx"), scatter_dimension=1, tiled=True),
        lax.psum_scatter(out_term, ("shard", "ctx"), scatter_dimension=1, tiled=True),
    )
    bias_qv_part = jnp.stack(
        [
            jnp.sum(grad_query_low.astype(jnp.float32), axis=0),
            jnp.sum(grad_value_low.astype(jnp.float32), axis=0),
        ]
    )
    out_bias_part = jnp.sum(grad_branch.astype(jnp.float32), axis=0)
    up_bias_part = jnp.sum(grad_upper.astype(jnp.float32), axis=0)
    down_bias_part = jnp.sum(grad_out, axis=0)
    gain_part = jnp.stack(
        [jnp.sum(grad_norm_one * normed_one, axis=0), jnp.sum(grad_norm_two * normed_two, axis=0)]
    )
    shift_part = jnp.stack([jnp.sum(grad_norm_one, axis=0), jnp.sum(grad_norm_two, axis=0)])
    grad_b_qv, grad_b_out, grad_b_up, grad_b_down, grad_gain, grad_shift = lax.psum(
        (bias_qv_part, out_bias_part, up_bias_part, down_bias_part, gain_part, shift_part),
        ("shard", "ctx"),
    )
    return (
        result,
        grad_tokens,
        grad_w_qkv,
        grad_b_qv,
        grad_w_out,
        grad_b_out,
        grad_w_up,
        grad_b_up,
        grad_w_down,
        grad_b_down,
        grad_gain,
        grad_shift,
    )


def solution(mesh):
    placed = (
        P(("shard", "ctx"), None),
        P(("shard", "ctx"), None),
        P(("shard", "ctx")),
        P(("shard", "ctx")),
        P(),
        P(None, ("shard", "ctx"), "tp"),
        P(None, "tp"),
        P("tp", ("shard", "ctx")),
        P(),
        P(("shard", "ctx"), "tp"),
        P("tp"),
        P("tp", ("shard", "ctx")),
        P(),
        P(),
        P(),
    )
    sizes = dict(mesh.shape)
    paired = sizes["tp"] * sizes["ctx"] * 2 == HEADS and sizes["tp"] == 2 and sizes["shard"] == 4
    return jax.shard_map(
        fast_device if paired else per_device,
        mesh=mesh,
        in_specs=placed,
        out_specs=(
            P(("shard", "ctx"), None),
            P(("shard", "ctx"), None),
            P(None, ("shard", "ctx"), "tp"),
            P(None, "tp"),
            P("tp", ("shard", "ctx")),
            P(),
            P(("shard", "ctx"), "tp"),
            P("tp"),
            P("tp", ("shard", "ctx")),
            P(),
            P(),
            P(),
        ),
        check_vma=False,
    )
```

```python
from functools import partial

import jax
import jax.numpy as jnp
import numpy as np
from jax import lax
from jax.experimental import pallas as pl
from jax.experimental.pallas import tpu as pltpu
from jax.sharding import PartitionSpec as P

HEADS = 16
HD = 64
KEY_BLOCK = 512
TRUNK = 1024
BRANCH = 128
SLOTS = 12
TREE = TRUNK + SLOTS * BRANCH
PAIR = 2 * HD

EPS = 1e-05
NEG = -1e30
LOG2E = 1.4426950408889634
MESH = pl.DeviceIdType.MESH
BF = jnp.bfloat16
F32 = jnp.float32
ROWS_WAVE = 4
FRONT_LIMIT = 62 << 20
BLOCK = 512
CURVE = 0.044715
ROOT = 0.7978845608028654
SUBS = 2


def nt(left, right):
    return lax.dot_general(left, right, (((1,), (1,)), ((), ())), preferred_element_type=F32)


def nn(left, right):
    return lax.dot_general(left, right, (((1,), (0,)), ((), ())), preferred_element_type=F32)


def rcopy(src, dst, send, recv, device):
    return pltpu.make_async_remote_copy(
        src_ref=src, dst_ref=dst, send_sem=send, recv_sem=recv, device_id=device, device_id_type=MESH
    )


def greet(devices):
    barrier = pltpu.get_barrier_semaphore()
    for device in devices:
        pl.semaphore_signal(barrier, inc=1, device_id=device, device_id_type=MESH)
    pl.semaphore_wait(barrier, len(devices))


def norm_rows(values, gain_row, shift_row):
    centre = values - jnp.mean(values, axis=-1, keepdims=True)
    inverse = lax.rsqrt(jnp.mean(centre * centre, axis=-1, keepdims=True) + EPS)
    normed = centre * inverse
    return normed * gain_row + shift_row, normed, inverse


def norm_rows_back(grad_in, normed, inverse, gain_row):
    scaled = grad_in * gain_row
    mean_grad = jnp.mean(scaled, axis=-1, keepdims=True)
    mean_cross = jnp.mean(scaled * normed, axis=-1, keepdims=True)
    return inverse * (scaled - mean_grad - normed * mean_cross)


def head_masks():
    lane = lax.broadcasted_iota(jnp.int32, (1, PAIR), 1)
    first = (lane < HD).astype(F32).astype(BF)
    second = (lane >= HD).astype(F32).astype(BF)
    return first, second


def stack_heads(rows):
    first, second = head_masks()
    return jnp.concatenate([rows * first, rows * second], axis=0)


def unstack_turned(turned, rows):
    return jnp.concatenate([turned[:HD, :rows], turned[HD:, rows:]], axis=0).T


def key_features(high, low, flag, rows):
    lane = lax.broadcasted_iota(jnp.int32, (rows, 128), 1)
    feats = jnp.where(lane < 3, high, jnp.where(lane < 6, low, jnp.where(lane == 6, flag, 0.0)))
    return feats.astype(BF)


def query_features(slope_ref, rows):
    return jnp.concatenate(
        [
            jnp.broadcast_to(slope_ref[0:1, :], (rows, 128)),
            jnp.broadcast_to(slope_ref[1:2, :], (rows, 128)),
        ],
        axis=0,
    ).astype(BF)


def fill_trunk_keys(key_ref, keys_aug):
    keys_aug[:, 0:PAIR] = key_ref[0:TRUNK, :]
    pos = lax.broadcasted_iota(jnp.int32, (TRUNK, 128), 0)
    low = pos & 255
    keys_aug[:, PAIR:] = key_features((pos - low).astype(F32), low.astype(F32), 0.0, TRUNK)


def fill_labels(info_all, blocks, labels, parents):
    labels[...] = jnp.full(labels.shape, -1.0, F32)
    parents[...] = jnp.full(parents.shape, -2.0, F32)
    for slot in range(SLOTS):
        block = TRUNK // BRANCH + slot
        owner, inner = block // blocks, block % blocks
        labels[slot : slot + 1, :] = info_all[owner, inner : inner + 1, :]
        parents[slot : slot + 1, :] = info_all[owner, 8 + inner : 9 + inner, :]


def parent_pick(slot, labels, parents, key_ref, value_ref):
    mine = parents[pl.ds(slot, 1), :]
    leaf = jnp.zeros((1, 128), F32)
    key_sum = jnp.zeros((BRANCH, PAIR), BF)
    value_sum = jnp.zeros((BRANCH, PAIR), BF)
    for other in range(SLOTS):
        same = (mine == labels[other : other + 1, :]).astype(F32)
        leaf = leaf + same
        same_low = same.astype(BF)
        at = TRUNK + other * BRANCH
        key_sum = key_sum + same_low * key_ref[at : at + BRANCH, :]
        value_sum = value_sum + same_low * value_ref[at : at + BRANCH, :]
    return leaf, key_sum, value_sum


def segment_key_features(leaf):
    row = lax.broadcasted_iota(jnp.int32, (BRANCH, 128), 0).astype(F32)
    own = key_features(float(TRUNK), row + leaf * float(BRANCH), 0.0, BRANCH)
    above = key_features(float(TRUNK), row, (leaf - 1.0) * 1e30, BRANCH)
    return own, above


def causal(rows):
    key = lax.broadcasted_iota(jnp.int32, (rows, rows), 0)
    query = lax.broadcasted_iota(jnp.int32, (rows, rows), 1)
    once = key <= query
    return jnp.concatenate([once, once], axis=1)


class Spread:
    def __init__(self, full, dims, depth, cols, sems, doubling=True):
        self.doubling = doubling
        self.full, self.depth, self.cols = full, depth, cols
        self.ns, self.nz, _ = dims
        self.s, self.z = lax.axis_index("shard"), lax.axis_index("ctx")
        self.zs, self.zr, self.xs, self.xr, self.cs, self.cr = sems

    def rows(self, shard, place):
        at = pl.multiple_of((shard * self.nz + place) * self.depth, self.depth)
        return self.full.at[pl.ds(at, self.depth), self.cols]

    def flip(self, bits):
        low = lax.rem(self.s, 2)
        high = lax.div(self.s, 2)
        if bits & 1:
            low = 1 - low
        if bits & 2:
            high = 1 - high
        return 2 * high + low

    def source(self, d):
        low, high = lax.rem(self.z, 2), lax.div(self.z, 2)
        low = 1 - low if d & 1 else low
        high = 1 - high if d & 2 else high
        return 2 * high + low

    def z_copy(self, d):
        ref = self.rows(self.s, self.source(2 if self.doubling and d == 3 else 0))
        to = self.source(1 if self.doubling and d == 3 else d)
        return rcopy(ref, ref, self.zs.at[d - 1], self.zr.at[d - 1], {"ctx": to})

    def x_copy(self, d):
        ref = self.rows(self.s, self.source(d))
        return rcopy(ref, ref, self.xs.at[d], self.xr.at[d], {"shard": self.flip(2)})

    def c_copy(self, far, d):
        ref = self.rows(self.flip(2) if far else self.s, self.source(d))
        return rcopy(ref, ref, self.cs.at[far, d], self.cr.at[far, d], {"shard": self.flip(1)})

    def z_start(self):
        self.z_copy(2).start()
        self.z_copy(1).start()
        if not self.doubling:
            self.z_copy(3).start()

    def own(self):
        self.x_copy(0).start()
        self.c_copy(0, 0).start()

    def z_done(self, d):
        ref = self.rows(self.s, self.source(d))
        rcopy(ref, ref, self.zs.at[d - 1], self.zr.at[d - 1], {"ctx": self.source(1)}).wait_recv()
        if self.doubling and d == 2:
            self.z_copy(3).start()
        self.x_copy(d).start()
        self.c_copy(0, d).start()

    def x_done(self, d):
        ref = self.rows(self.flip(2), self.source(d))
        rcopy(ref, ref, self.xs.at[d], self.xr.at[d], {"shard": self.flip(2)}).wait_recv()
        self.c_copy(1, d).start()

    def c_done(self, far, d):
        ref = self.rows(self.flip(3) if far else self.flip(1), self.source(d))
        rcopy(ref, ref, self.cs.at[far, d], self.cr.at[far, d], {"shard": self.flip(1)}).wait_recv()

    def all_here(self):
        for d in range(self.nz):
            self.c_done(0, d)
            self.c_done(1, d)

    def finish(self):
        for d in range(self.nz):
            if d:
                self.z_copy(d).wait_send()
            self.x_copy(d).wait_send()
            self.c_copy(0, d).wait_send()
            self.c_copy(1, d).wait_send()


def spread_sems(nz):
    return [dma(nz - 1), dma(nz - 1), dma(nz), dma(nz), dma(2, nz), dma(2, nz)]


def vmem():
    return pl.BlockSpec(memory_space=pltpu.VMEM)


def shape(dims, kind):
    return jax.ShapeDtypeStruct(dims, kind)


def dma(*dims):
    return pltpu.SemaphoreType.DMA(dims)


def front_kernel(
    dims,
    tok,
    w_up,
    w_out,
    w_down,
    cot_in,
    wq3,
    seg,
    above,
    bias_qv,
    slope_table,
    gain,
    shift,
    b_out,
    b_up,
    act_turned_o,
    query_o,
    key_o,
    value_o,
    out_heads_o,
    lse,
    info_all,
    wqkv_o,
    core_o,
    ga_o,
    down_o,
    mid_o,
    gmid_o,
    sums,
    act_turned,
    query,
    key,
    value,
    out_heads,
    wqkv,
    core_in,
    ga_all,
    down_part,
    mid,
    gmid,
    info,
    wfull,
    wq,
    att,
    tree,
    wcat,
    keys_aug,
    values_turned,
    labels,
    parents,
    cot,
    far,
    act,
    gbranch,
    g_send,
    g_recv,
    ga_send,
    bup_acc,
    info_send,
    info_recv,
    wz_send,
    wz_recv,
    ws_send,
    ws_recv,
    z_send,
    z_recv,
    y_send,
    y_recv,
    a_send,
    a_recv,
    local_sem,
    b_send,
    b_recv,
    t_send,
    t_recv,
    gs_sem,
    gr_sem,
    as_sem,
    ar_sem,
    cs_sem,
    cr_sem,
    store_sem,
    *spread,
):
    ns, nz, rows = dims
    s, z, y = lax.axis_index("shard"), lax.axis_index("ctx"), lax.axis_index("tp")
    slopes = slope_table.at[y * nz + z]
    half = rows // 2
    sub = half // SUBS
    depth = wq.shape[0]
    wide = 3 * PAIR
    my_rows = pl.ds(pl.multiple_of((s * nz + z) * depth, depth), depth)
    units, inner = w_up.shape[1], w_out.shape[1]
    own_cols = pl.multiple_of(2 * units + y * inner, 128)
    starts = [
        pltpu.make_async_copy(tok, tree.at[pl.ds(pl.multiple_of(z * rows, 128), rows), :], local_sem.at[0]),
        pltpu.make_async_copy(w_up, wfull.at[my_rows, 0:units], local_sem.at[1]),
        pltpu.make_async_copy(w_down, wfull.at[my_rows, units : 2 * units], local_sem.at[2]),
        pltpu.make_async_copy(w_out, wfull.at[my_rows, pl.ds(own_cols, inner)], local_sem.at[3]),
    ]
    given_load = pltpu.make_async_copy(cot_in, cot, local_sem.at[4])
    given_load.start()
    stores = [
        pltpu.make_async_copy(a, b, store_sem.at[k])
        for k, (a, b) in enumerate(
            (
                (act_turned, act_turned_o),
                (query, query_o),
                (key, key_o),
                (value, value_o),
                (out_heads, out_heads_o),
                (mid, mid_o),
                (gmid, gmid_o),
                (down_part, down_o),
                (core_in.at[:, :, 0 : 2 * units], core_o.at[:, :, 0 : 2 * units]),
                (core_in.at[:, :, 2 * units :], core_o.at[:, :, 2 * units :]),
                (wqkv, wqkv_o),
                (ga_all, ga_o),
            )
        )
    ]
    for one in starts:
        one.start()
    for to in range(nz):
        for part in range(3):
            wq[:, to * wide + part * PAIR : to * wide + (part + 1) * PAIR] = wq3[
                part, :, to * PAIR : (to + 1) * PAIR
            ]
    lane = lax.broadcasted_iota(jnp.int32, above.shape, 1)
    info[...] = jnp.zeros(info.shape, F32)
    for block in range(rows // BRANCH):
        label = seg[block : block + 1, 0:1]
        upper_label = jnp.sum(jnp.where(lane == label, above[...], 0), axis=1, keepdims=True)
        info[block : block + 1, :] = jnp.broadcast_to(label, (1, 128)).astype(F32)
        info[8 + block : 9 + block, :] = jnp.broadcast_to(upper_label, (1, 128)).astype(F32)
    greet(
        [{"ctx": lax.rem(z + d, nz)} for d in range(1, nz)]
        + [{"shard": lax.rem(s + d, ns)} for d in range(1, ns)]
        + [{"tp": 1 - y}]
    )
    ups = Spread(wfull, dims, depth, slice(0, units), spread[:6])
    downs = Spread(wfull, dims, depth, slice(units, 2 * units), spread[6:12])
    weights = Spread(wqkv, dims, depth, slice(None), spread[18:])
    outer = Spread(wfull, dims, depth, pl.ds(own_cols, inner), spread[12:18], False)

    def info_copy(d):
        return rcopy(
            info, info_all.at[z], info_send.at[d - 1], info_recv.at[d - 1], {"ctx": lax.rem(z + d, nz)}
        )

    def wz_copy(d):
        to = lax.rem(z + d, nz)
        return rcopy(
            wq.at[:, pl.ds(pl.multiple_of(to * wide, 128), wide)],
            wcat.at[my_rows, :],
            wz_send.at[d - 1],
            wz_recv.at[d - 1],
            {"ctx": to},
        )

    shard_rows = pl.ds(s * (nz * depth), nz * depth)

    def ws_copy(d):
        return rcopy(
            wcat.at[shard_rows, :],
            wcat.at[shard_rows, :],
            ws_send.at[d - 1],
            ws_recv.at[d - 1],
            {"shard": lax.rem(s + d, ns)},
        )

    wqkv[my_rows, :] = wq[...]
    for d in range(1, nz):
        wz_copy(d).start()
    for d in range(1, nz):
        info_copy(d).start()
    wcat[my_rows, :] = wq[:, pl.ds(pl.multiple_of(z * wide, 128), wide)]
    info_all[z] = info[...]
    for one in starts:
        one.wait()

    def piece(block, second, part):
        at = block * rows + jnp.where(second, 1 - y, y) * half + part * sub
        return tree.at[pl.ds(pl.multiple_of(at, 32), sub), :]

    def z_copy(direction, k, part):
        block = z - k if direction == 0 else z + k
        to = z + 1 if direction == 0 else z - 1
        ref = piece(block, False, part)
        return rcopy(ref, ref, z_send.at[direction, k, part], z_recv.at[direction, k, part], {"ctx": to})

    def z_arrival(direction, k, part):
        block = z - k if direction == 0 else z + k
        ref = piece(block, False, part)
        return rcopy(
            ref, ref, z_send.at[direction, k - 1, part], z_recv.at[direction, k - 1, part], {"ctx": z}
        )

    def y_copy(direction, k, part):
        block = z - k if direction == 0 else z + k
        ref = piece(block, False, part)
        return rcopy(
            ref, ref, y_send.at[direction, k - 1, part], y_recv.at[direction, k - 1, part], {"tp": 1 - y}
        )

    def y_arrival(direction, k, part):
        block = z - k if direction == 0 else z + k
        ref = piece(block, True, part)
        return rcopy(
            ref, ref, y_send.at[direction, k - 1, part], y_recv.at[direction, k - 1, part], {"tp": 1 - y}
        )

    def place(direction, k):
        block = z - k if direction == 0 else z + k
        nxt = z + 1 if direction == 0 else z - 1
        here = (block >= 0) & (block < nz)
        onward = here & (nxt >= 0) & (nxt < nz)
        return block, here, onward

    def forward(k, first):
        for part in range(SUBS):
            for direction in range(2):
                _, here, onward = place(direction, k)
                if not first:

                    @pl.when(here)
                    def _():
                        z_arrival(direction, k, part).wait_recv()

                @pl.when(onward & (k < nz - 1))
                def _():
                    z_copy(direction, k, part).start()

                if not first:

                    @pl.when(here)
                    def _():
                        y_copy(direction, k, part).start()

    forward(0, True)
    outer.own()
    ups.own()
    downs.own()
    for d in range(1, nz):
        wz_copy(d).wait_recv()
    for d in range(1, ns):
        ws_copy(d).start()

    bias_at = pl.ds(pl.multiple_of(z * PAIR, 128), PAIR)
    bias_q = bias_qv[0:1, bias_at]
    bias_v = bias_qv[1:2, bias_at]

    def project(k):
        def side(direction, inner_carry):
            block = z + (2 * direction - 1) * k

            @pl.when((block >= 0) & (block < nz) & ((k > 0) | (direction == 0)))
            def _():
                def tile(t, carry):
                    here = pl.ds(pl.multiple_of(block * rows + t * 128, 128), 128)
                    act = norm_rows(tree[here, :].astype(F32), gain[0:1, :], shift[0:1, :])[0].astype(BF)
                    act_turned[:, here] = act.T
                    both = nn(act, wcat[...])
                    query[here, :] = (
                        (both[:, :PAIR] + bias_q).astype(BF).astype(F32) * HD ** (-0.5)
                    ).astype(BF)
                    key[here, :] = both[:, PAIR : 2 * PAIR].astype(BF)
                    value[here, :] = (both[:, 2 * PAIR :] + bias_v).astype(BF)
                    return carry

                lax.fori_loop(0, rows // 128, tile, 0)

            return inner_carry

        lax.fori_loop(0, 2, side, 0)

    def shared(k):
        for part in range(SUBS):
            for direction in range(2):
                _, here, _ = place(direction, k)

                @pl.when(here)
                def _():
                    y_arrival(direction, k, part).wait_recv()

    forward(1, False)
    for d in range(1, ns):
        ws_copy(d).wait_recv()
    project(0)

    def wave(k, carry):
        forward(k, False)

        @pl.when(k == nz - 2)
        def _():
            outer.z_start()
            ups.z_start()
            downs.z_start()

        shared(k - 1)
        project(k - 1)
        return carry

    lax.fori_loop(2, nz, wave, 0)
    for d in (1, 3, 2):
        outer.z_done(d)
    shared(nz - 1)
    project(nz - 1)
    for k in range(4):
        stores[k].start()
    for d in (0, 1, 3, 2):
        outer.x_done(d)
    ups.z_done(2)
    ups.z_done(1)

    for d in range(1, nz):
        info_copy(d).wait_recv()

    fill_labels(info_all, rows // BRANCH, labels, parents)
    fill_trunk_keys(key, keys_aug)
    values_turned[...] = value[0:TRUNK, :].T

    def att_cols(half_at, owner):
        return pl.ds(pl.multiple_of(half_at * inner + owner * PAIR, 128), PAIR)

    def att_copy(to):
        return rcopy(
            out_heads.at[pl.ds(to * rows, rows), :],
            att.at[:, att_cols(y, z)],
            a_send.at[to],
            a_recv.at[z],
            {"ctx": to},
        )

    def pass_on(owner):
        return rcopy(
            att.at[:, att_cols(y, owner)],
            att.at[:, att_cols(y, owner)],
            b_send.at[owner],
            b_recv.at[owner],
            {"tp": 1 - y},
        )

    half_rows = pl.ds(pl.multiple_of(lax.rem(s, 2) * (ns * nz * depth // 2), 128), ns * nz * depth // 2)
    far_rows = pl.ds(pl.multiple_of((1 - lax.rem(s, 2)) * (ns * nz * depth // 2), 128), ns * nz * depth // 2)
    far_cols = pl.ds(pl.multiple_of(2 * units + (1 - y) * inner, 128), inner)

    def plane_copy():
        ref = wfull.at[half_rows, pl.ds(own_cols, inner)]
        return rcopy(ref, ref, t_send.at[0], t_recv.at[0], {"tp": 1 - y})

    def plane_arrival():
        ref = wfull.at[half_rows, far_cols]
        return rcopy(ref, ref, t_send.at[0], t_recv.at[0], {"tp": 1 - y})

    def core_copy():
        ref = wfull.at[half_rows, far_cols]
        return rcopy(ref, ref, t_send.at[1], t_recv.at[1], {"shard": outer.flip(1)})

    def core_arrival():
        ref = wfull.at[far_rows, far_cols]
        return rcopy(ref, ref, t_send.at[1], t_recv.at[1], {"shard": outer.flip(1)})

    outer.all_here()
    plane_copy().start()

    def send_out(to):
        @pl.when(z != to)
        def _():
            att_copy(to).start()

        @pl.when(z == to)
        def _():
            att[:, att_cols(y, z)] = out_heads[to * rows : (to + 1) * rows, :]
            pass_on(z).start()

    tile_mask = causal(BRANCH)

    def segment(slot, carry):
        here = pl.ds(pl.multiple_of(TRUNK + slot * BRANCH, 128), BRANCH)
        asked = jnp.concatenate(
            [stack_heads(query[here, :]), query_features(slopes, BRANCH)], axis=1
        )
        leaf, key_up, value_up = parent_pick(slot, labels, parents, key, value)
        own_feats, up_feats = segment_key_features(leaf)
        trunk_part = nt(keys_aug[...], asked) * LOG2E
        own_part = nt(jnp.concatenate([key[here, :], own_feats], axis=1), asked) * LOG2E
        own_part = jnp.where(tile_mask, own_part, NEG)
        up_part = nt(jnp.concatenate([key_up, up_feats], axis=1), asked) * LOG2E
        top = jnp.maximum(
            jnp.max(trunk_part, axis=0, keepdims=True),
            jnp.maximum(
                jnp.max(own_part, axis=0, keepdims=True), jnp.max(up_part, axis=0, keepdims=True)
            ),
        )
        trunk_part = jnp.exp2(trunk_part - top)
        own_part = jnp.exp2(own_part - top)
        up_part = jnp.exp2(up_part - top)
        total = (
            jnp.sum(trunk_part, axis=0, keepdims=True)
            + jnp.sum(own_part, axis=0, keepdims=True)
            + jnp.sum(up_part, axis=0, keepdims=True)
        )
        turned = nn(values_turned[...], trunk_part.astype(BF))
        turned = turned + nn(value[here, :].T, own_part.astype(BF))
        turned = turned + nn(value_up.T, up_part.astype(BF))
        turned = turned / total
        out_heads[here, :] = unstack_turned(turned, BRANCH).astype(BF)
        lse[pl.ds(4 + slot, 1), 0 : 2 * BRANCH] = top + jnp.log2(total)
        return carry

    wave_rows = TRUNK // 4
    wave_mask = causal(wave_rows)

    def trunk_tile(tile):
        lo, hi = tile * wave_rows, (tile + 1) * wave_rows
        asked = jnp.concatenate(
            [stack_heads(query[lo:hi, :]), query_features(slopes, wave_rows)], axis=1
        )
        edge = jnp.where(wave_mask, nt(keys_aug[lo:hi, :], asked) * LOG2E, NEG)
        top = jnp.max(edge, axis=0, keepdims=True)
        if tile:
            body = nt(keys_aug[0:lo, :], asked) * LOG2E
            top = jnp.maximum(top, jnp.max(body, axis=0, keepdims=True))
            body = jnp.exp2(body - top)
        edge = jnp.exp2(edge - top)
        total = jnp.sum(edge, axis=0, keepdims=True)
        turned = nn(values_turned[:, lo:hi], edge.astype(BF))
        if tile:
            total = total + jnp.sum(body, axis=0, keepdims=True)
            turned = turned + nn(values_turned[:, 0:lo], body.astype(BF))
        turned = turned / total
        out_heads[lo:hi, :] = unstack_turned(turned, wave_rows).astype(BF)
        lse[tile : tile + 1, :] = top + jnp.log2(total)

    def turn(n, carry):
        @pl.when(n == 5)
        def _():
            send_out(2)
            for tile in range(3):
                trunk_tile(tile)
            send_out(0)
            downs.z_done(2)

        @pl.when(n == 10)
        def _():
            send_out(3)
            trunk_tile(3)

        return segment(lax.rem(n + 2, SLOTS), carry)

    lax.fori_loop(0, SLOTS, turn, 0)
    send_out(1)
    downs.z_done(1)
    ups.z_done(3)
    stores[4].start()
    plane_arrival().wait_recv()
    core_copy().start()
    downs.z_done(3)
    for owner in range(nz):

        @pl.when(z != owner)
        def _():
            rcopy(
                out_heads.at[0:rows, :],
                att.at[:, att_cols(y, owner)],
                a_send.at[owner],
                a_recv.at[owner],
                {"ctx": owner},
            ).wait_recv()
            pass_on(owner).start()

    mid[...] = tree[pl.ds(pl.multiple_of(z * rows, 128), rows), :].astype(F32) + b_out[...]
    for d in (0, 2, 1, 3):
        ups.x_done(d)
    given_load.wait()
    for owner in range(nz):
        ref = att.at[:, att_cols(1 - y, owner)]
        rcopy(ref, ref, b_send.at[owner], b_recv.at[owner], {"tp": 1 - y}).wait_recv()
    core_arrival().wait_recv()
    ups.all_here()
    other = {"tp": 1 - y}
    chunk = rows // ROWS_WAVE
    width = act.shape[1]
    halves = units // width
    own_heads = pl.ds(pl.multiple_of(y * inner, 128), inner)
    own_wide = pl.ds(own_cols, inner)
    sums[...] = jnp.zeros(sums.shape, F32)
    bup_acc[...] = jnp.zeros(bup_acc.shape, F32)

    def at(i):
        return pl.ds(pl.multiple_of(i * chunk, 32), chunk)

    def g_copy(i):
        return rcopy(g_send.at[at(i), :], g_recv.at[at(i), :], gs_sem.at[i], gr_sem.at[i], other)

    def a_copy(i, d):
        to = lax.rem(z + d, nz)
        return rcopy(
            ga_send.at[at(i), pl.ds(pl.multiple_of(to * PAIR, 128), PAIR)],
            ga_all.at[pl.ds(pl.multiple_of(z * rows + i * chunk, 32), chunk), :],
            as_sem.at[d - 1, i],
            ar_sem.at[d - 1, i],
            {"ctx": to},
        )

    span = nz * depth
    parts = ((0, 2 * units), (2 * units, 2 * units + inner))

    def c_copy(part, index):
        lo, hi = parts[part]
        return rcopy(
            far.at[index, :, lo:hi],
            core_in.at[index, :, lo:hi],
            cs_sem.at[part, index],
            cr_sem.at[part, index],
            {"shard": weights.flip(1)},
        )

    sums[...] = jnp.zeros(sums.shape, F32)
    bup_acc[...] = jnp.zeros(bup_acc.shape, F32)
    per = width // BLOCK

    def spot(first, i, c, size):
        row = (first + lax.div(c, per)) * rows + i * size
        col = lax.rem(c, per) * BLOCK
        return pl.ds(pl.multiple_of(row, 32), size), pl.ds(pl.multiple_of(col, 128), BLOCK)

    large = 2 * chunk

    def large_at(i):
        return pl.ds(pl.multiple_of(i * large, 64), large)

    def stage_one(i, carry):
        here = large_at(i)
        middle = mid[here, :] + nt(att[here, :], wfull[:, 2 * units :])
        mid[here, :] = middle
        act[here, :] = norm_rows(middle, gain[1:2, :], shift[1:2, :])[0].astype(BF)

        def columns(c, inner_carry):
            cols = pl.ds(pl.multiple_of(c * BLOCK, 128), BLOCK)
            upper = nn(act[here, :], wfull[:, cols]) + b_up[:, cols]
            square = upper * upper
            turn = jnp.tanh(ROOT * (upper + CURVE * (square * upper)))
            tree[spot(0, i, c, large)] = (0.5 * upper * (1.0 + turn)).astype(BF)
            steep = 0.5 * (1.0 + turn) + (0.5 * ROOT) * upper * (1.0 - turn * turn) * (
                1.0 + (3.0 * CURVE) * square
            )
            tree[spot(halves, i, c, large)] = steep.astype(BF)
            return inner_carry

        lax.fori_loop(0, units // BLOCK, columns, 0)
        return carry

    def stage_two(i, carry):
        here = large_at(i)

        def columns(c, inner_carry):
            cols = pl.ds(pl.multiple_of(c * BLOCK, 128), BLOCK)
            down_cols = pl.ds(pl.multiple_of(units + c * BLOCK, 128), BLOCK)
            slope = nn(cot[here, :], wfull[:, down_cols])
            low = (slope * tree[spot(halves, i, c, large)].astype(F32)).astype(BF)
            tree[spot(halves, i, c, large)] = low
            bup_acc[:, cols] += jnp.sum(low.astype(F32), axis=0, keepdims=True)
            return inner_carry

        lax.fori_loop(0, units // BLOCK, columns, 0)
        total = jnp.zeros((large, width), F32)
        for part in range(halves):
            total = total + nt(
                tree[spot(halves + part, i, 0, large)[0], :], wfull[:, part * width : (part + 1) * width]
            )
        g_send[here, :] = total.astype(BF)
        g_copy(2 * i).start()
        g_copy(2 * i + 1).start()
        return carry

    def drain(k, carry):
        for part in range(SUBS):
            for direction in range(2):
                _, here, onward = place(direction, k)

                @pl.when(onward & (k < nz - 1))
                def _():
                    z_copy(direction, k, part).wait_send()

                @pl.when(here & (k > 0))
                def _():
                    y_copy(direction, k, part).wait_send()

        return carry

    lax.fori_loop(0, nz, drain, 0)
    lax.fori_loop(0, 1, stage_one, 0)
    weights.own()
    weights.z_start()
    for d in (0, 2, 1, 3):
        downs.x_done(d)
    lax.fori_loop(1, ROWS_WAVE // 2, stage_one, 0)
    stores[5].start()
    downs.all_here()
    lax.fori_loop(0, ROWS_WAVE // 2, stage_two, 0)
    for d in (2, 1, 3):
        weights.z_done(d)

    def group_cols(index, block):
        return pl.ds(pl.multiple_of(weights.flip(index) * span + block * 128, 128), 128)

    def products(cols):
        turned_act, turned_cot = act[:, cols].T, cot[:, cols].T
        for part in range(halves):
            lo = part * width
            yield lo, nn(turned_act, tree[(halves + part) * rows : (halves + part + 1) * rows, :])
            yield units + lo, nn(turned_cot, tree[part * rows : (part + 1) * rows, :])

    def each_block(act_on):
        for index in range(2):

            def one(block, carry):
                act_on(index, block)
                return carry

            lax.fori_loop(0, span // 128, one, 0)

    def far_one(index, block):
        target = pl.ds(pl.multiple_of(block * 128, 128), 128)
        for lo, value_block in products(group_cols((1, 3)[index], block)):
            far[index, target, lo : lo + width] = value_block.astype(BF)

    def near_one(index, block):
        target = pl.ds(pl.multiple_of(block * 128, 128), 128)
        for lo, value_block in products(group_cols((0, 2)[index], block)):
            here = slice(lo, lo + width)
            core_in[index, target, here] = (core_in[index, target, here].astype(F32) + value_block).astype(BF)

    def out_product(cols):
        return nn(gbranch[:, cols].T, att[:, own_heads])

    def far_two(index, block):
        target = pl.ds(pl.multiple_of(block * 128, 128), 128)
        far[index, target, 2 * units :] = out_product(group_cols((1, 3)[index], block)).astype(BF)

    def near_two(index, block):
        target = pl.ds(pl.multiple_of(block * 128, 128), 128)
        here = slice(2 * units, 2 * units + inner)
        core_in[index, target, here] = (
            core_in[index, target, here].astype(F32) + out_product(group_cols((0, 2)[index], block))
        ).astype(BF)

    def stage_c(i, carry):
        g_copy(i).wait_recv()
        here = at(i)
        grad = g_send[here, :].astype(F32) + g_recv[here, :].astype(F32)
        _, normed, inverse = norm_rows(mid[here, :], gain[1:2, :], shift[1:2, :])
        given = cot[here, :].astype(F32)
        grad_middle = given + norm_rows_back(grad, normed, inverse, gain[1:2, :])
        gmid[here, :] = grad_middle
        low = grad_middle.astype(BF)
        gbranch[here, :] = low
        sums[2:3, :] += jnp.sum(low.astype(F32), axis=0, keepdims=True)
        sums[3:4, :] += jnp.sum(given, axis=0, keepdims=True)
        sums[4:5, :] += jnp.sum(grad * normed, axis=0, keepdims=True)
        sums[5:6, :] += jnp.sum(grad, axis=0, keepdims=True)
        ga_send[here, :] = nn(low, wfull[:, own_wide]).astype(BF)
        for d in range(1, nz):
            a_copy(i, d).start()
        ga_all[pl.ds(pl.multiple_of(z * rows + i * chunk, 32), chunk), :] = ga_send[
            here, pl.ds(pl.multiple_of(z * PAIR, 128), PAIR)
        ]
        return carry

    lax.fori_loop(0, 1, stage_c, 0)
    each_block(far_one)
    for index in range(2):
        c_copy(0, index).start()
    lax.fori_loop(1, 2, stage_c, 0)
    for d in (0, 2, 1, 3):
        weights.x_done(d)
    def down(i, carry):
        total = jnp.zeros((large, width), F32)
        for part in range(halves):
            total = total + nt(
                tree[spot(part, i, 0, large)[0], :], wfull[:, units + part * width : units + (part + 1) * width]
            )
        down_part[large_at(i), :] = total.astype(BF)
        return carry

    lax.fori_loop(0, ROWS_WAVE // 2, down, 0)
    stores[7].start()
    lax.fori_loop(2, 3, stage_c, 0)
    for index in range(2):
        c_copy(0, index).wait_recv()
    each_block(near_one)
    stores[8].start()
    lax.fori_loop(3, ROWS_WAVE, stage_c, 0)
    stores[6].start()
    each_block(far_two)
    for index in range(2):
        c_copy(1, index).start()
    for index in range(2):
        c_copy(1, index).wait_recv()
    each_block(near_two)
    stores[9].start()
    for part in range(halves):
        sums[part : part + 1, :] = bup_acc[:, part * width : (part + 1) * width]
    weights.all_here()
    stores[10].start()
    weights.finish()
    for part in range(2):
        for index in range(2):
            c_copy(part, index).wait_send()

    def finish(i, carry):
        g_copy(i).wait_send()
        for d in range(1, nz):
            a_copy(i, d).wait_send()
            a_copy(i, d).wait_recv()
        return carry

    lax.fori_loop(0, ROWS_WAVE, finish, 0)
    stores[11].start()
    plane_copy().wait_send()
    core_copy().wait_send()
    for owner in range(nz):
        pass_on(owner).wait_send()

    for owner in range(nz):

        @pl.when(z != owner)
        def _():
            att_copy(owner).wait_send()

    ups.finish()
    downs.finish()
    outer.finish()
    for d in range(1, nz):
        info_copy(d).wait_send()
        wz_copy(d).wait_send()
    for d in range(1, ns):
        ws_copy(d).wait_send()
    for store in stores:
        store.wait()


def run_front(
    dims, tok, w_up, w_out, w_down, cot, wq3, seg, above, bias_qv, slopes, gain, shift, b_out, b_up
):
    ns, nz, rows = dims
    width, units, inner, depth = tok.shape[1], w_up.shape[1], w_out.shape[1], wq3.shape[1]
    span, total, wide = nz * depth, 2 * units + inner, 3 * PAIR
    anywhere = pl.BlockSpec(memory_space=pl.ANY)
    return pl.pallas_call(
        partial(front_kernel, dims),
        name="front",
        out_shape=(
            shape((width, TREE), BF),
            shape((TREE, PAIR), BF),
            shape((TREE, PAIR), BF),
            shape((TREE, PAIR), BF),
            shape((TREE, PAIR), BF),
            shape((16, 512), F32),
            shape((nz, 16, 128), F32),
            shape((width, nz * wide), BF),
            shape((2, span, total), BF),
            shape((TREE, PAIR), BF),
            shape((rows, width), BF),
            shape((rows, width), F32),
            shape((rows, width), F32),
            shape((8, width), F32),
        ),
        in_specs=[anywhere] * 5 + [vmem()] * 9,
        out_specs=[anywhere] * 5 + [vmem()] * 2 + [anywhere] * 6 + [vmem()],
        scratch_shapes=[
            pltpu.VMEM((width, TREE), BF),
            pltpu.VMEM((TREE, PAIR), BF),
            pltpu.VMEM((TREE, PAIR), BF),
            pltpu.VMEM((TREE, PAIR), BF),
            pltpu.VMEM((TREE, PAIR), BF),
            pltpu.VMEM((width, nz * wide), BF),
            pltpu.VMEM((2, span, total), BF),
            pltpu.VMEM((TREE, PAIR), BF),
            pltpu.VMEM((rows, width), BF),
            pltpu.VMEM((rows, width), F32),
            pltpu.VMEM((rows, width), F32),
            pltpu.VMEM((16, 128), F32),
            pltpu.VMEM((width, 2 * units + 2 * inner), BF),
            pltpu.VMEM((depth, nz * wide), BF),
            pltpu.VMEM((rows, 2 * inner), BF),
            pltpu.VMEM((TREE, width), BF),
            pltpu.VMEM((width, wide), BF),
            pltpu.VMEM((TRUNK, 2 * PAIR), BF),
            pltpu.VMEM((PAIR, TRUNK), BF),
            pltpu.VMEM((16, 128), F32),
            pltpu.VMEM((16, 128), F32),
            pltpu.VMEM((rows, width), BF),
            pltpu.VMEM((2, span, total), BF),
            pltpu.VMEM((rows, width), BF),
            pltpu.VMEM((rows, width), BF),
            pltpu.VMEM((rows, width), BF),
            pltpu.VMEM((rows, width), BF),
            pltpu.VMEM((rows, inner), BF),
            pltpu.VMEM((1, units), F32),
            dma(nz - 1),
            dma(nz - 1),
            dma(nz - 1),
            dma(nz - 1),
            dma(ns - 1),
            dma(ns - 1),
            dma(2, nz, SUBS),
            dma(2, nz, SUBS),
            dma(2, nz, SUBS),
            dma(2, nz, SUBS),
            dma(nz),
            dma(nz),
            dma(5),
            dma(nz),
            dma(nz),
            dma(2),
            dma(2),
            dma(ROWS_WAVE),
            dma(ROWS_WAVE),
            dma(nz - 1, ROWS_WAVE),
            dma(nz - 1, ROWS_WAVE),
            dma(2, 2),
            dma(2, 2),
            dma(12),
            *spread_sems(nz),
            *spread_sems(nz),
            *spread_sems(nz),
            *spread_sems(nz),
        ],
        compiler_params=pltpu.CompilerParams(
            collective_id=0, has_side_effects=True, vmem_limit_bytes=FRONT_LIMIT
        ),
        cost_estimate=pl.CostEstimate(flops=40_000_000_000, bytes_accessed=20_000_000, transcendentals=0),
    )(tok, w_up, w_out, w_down, cot, wq3, seg, above, bias_qv, slopes, gain, shift, b_out, b_up)


class Halve:
    def __init__(self, near, far, cols, dims, depth, bufs, sems):
        self.near, self.far, self.cols, self.depth = near, far, cols, depth
        self.nz = dims[1]
        self.s, self.z = lax.axis_index("shard"), lax.axis_index("ctx")
        self.x_in, self.a_in, self.b_out, self.b_in = bufs
        self.xs, self.xr, self.as_, self.ar, self.bs, self.br = sems

    def place(self, bits):
        low, high = lax.rem(self.z, 2), lax.div(self.z, 2)
        low = 1 - low if bits & 1 else low
        high = 1 - high if bits & 2 else high
        return 2 * high + low

    def block(self, bits):
        return pl.ds(pl.multiple_of(self.place(bits) * self.depth, self.depth), self.depth)

    def x_copy(self):
        low, high = lax.rem(self.s, 2), lax.div(self.s, 2)
        return rcopy(
            self.far.at[:, self.cols],
            self.x_in.at[:, self.cols],
            self.xs,
            self.xr,
            {"shard": 2 * (1 - high) + low},
        )

    def a_copy(self, index):
        return rcopy(
            self.near.at[self.block((1, 3)[index]), self.cols],
            self.a_in.at[index, :, self.cols],
            self.as_.at[index],
            self.ar.at[index],
            {"ctx": self.place(1)},
        )

    def b_copy(self):
        return rcopy(
            self.b_out.at[:, self.cols], self.b_in.at[:, self.cols], self.bs, self.br, {"ctx": self.place(2)}
        )

    def step_x(self):
        self.x_copy().wait_recv()

        def one(r, carry):
            here = pl.ds(pl.multiple_of(r * 32, 32), 32)
            self.near[here, self.cols] = (
                self.near[here, self.cols].astype(F32) + self.x_in[here, self.cols].astype(F32)
            ).astype(BF)
            return carry

        lax.fori_loop(0, self.near.shape[0] // 32, one, 0)
        self.a_copy(0).start()
        self.a_copy(1).start()

    def step_a(self):
        self.a_copy(0).wait_recv()
        self.a_copy(1).wait_recv()
        self.b_out[:, self.cols] = (
            self.near[self.block(2), self.cols].astype(F32) + self.a_in[1, :, self.cols].astype(F32)
        ).astype(BF)
        self.b_copy().start()

    def step_b(self):
        self.b_copy().wait_recv()
        return (
            self.near[self.block(0), self.cols].astype(F32)
            + self.a_in[0, :, self.cols].astype(F32)
            + self.b_in[:, self.cols].astype(F32)
        )

    def finish(self):
        self.x_copy().wait_send()
        self.a_copy(0).wait_send()
        self.a_copy(1).wait_send()
        self.b_copy().wait_send()


PIECES = 6


def back_kernel(
    dims,
    query,
    key,
    value,
    out_heads,
    lse,
    info_all,
    ga_all,
    act_turned_in,
    wqkv_in,
    partial_in,
    down_in,
    mid_in,
    b_down,
    gmid_in,
    tok_in,
    slope_table,
    gain,
    shift,
    early,
    result,
    gtok,
    gup,
    gdown,
    gout,
    gwqkv,
    early_sum,
    late_sum,
    act_turned,
    wqkv,
    down_part,
    mid,
    gmid,
    tok,
    near,
    x_in,
    a_in,
    b_out,
    b_in,
    q_near,
    q_far,
    q_core,
    qx_in,
    q_all,
    dqkv,
    dk_trunk,
    dv_trunk,
    dk_seg,
    dv_seg,
    dk_up,
    dv_up,
    keys_aug,
    keys_turned,
    labels,
    parents,
    dq_all,
    n_send,
    n_recv,
    down_recv,
    wg_send,
    early_mine,
    early_recv,
    late,
    late_recv,
    d_sem,
    e_send,
    e_recv,
    f_send,
    f_recv,
    l_send,
    l_recv,
    p_send,
    p_recv,
    r_send,
    r_recv,
    ns_sem,
    nr_sem,
    xs_sem,
    xr_sem,
    as_sem,
    ar_sem,
    bs_sem,
    br_sem,
    qc_send,
    qc_recv,
    qx_sem,
    qz_send,
    qz_recv,
    n_local,
    load_sem,
):
    ns, nz, rows = dims
    s, z, y = lax.axis_index("shard"), lax.axis_index("ctx"), lax.axis_index("tp")
    count = ns * nz
    me = s * nz + z
    chunk = rows // ROWS_WAVE
    width = tok.shape[1]
    depth = width // count
    span = nz * depth
    wide = 3 * PAIR
    other = {"tp": 1 - y}
    slopes = slope_table.at[y * nz + z]
    total_cols = near.shape[1]
    step_cols = total_cols // PIECES
    units = gup.shape[1]

    far = partial_in.at[1]
    load = pltpu.make_async_copy(partial_in.at[0], near, n_local)
    loads = [
        pltpu.make_async_copy(a, c, load_sem.at[k])
        for k, (a, c) in enumerate(
            (
                (down_in, down_part),
                (act_turned_in, act_turned),
                (wqkv_in, wqkv),
                (mid_in, mid),
                (gmid_in, gmid),
                (tok_in, tok),
            )
        )
    ]
    loads[0].start()
    load.start()
    for one in loads[1:]:
        one.start()

    def peer(d):
        index = lax.rem(me + d, count)
        return index, {"shard": lax.div(index, nz), "ctx": lax.rem(index, nz)}

    greet([other] + [peer(d)[1] for d in range(1, count)])

    halves = [
        Halve(
            near,
            far,
            slice(i * step_cols, (i + 1) * step_cols),
            dims,
            depth,
            (x_in, a_in, b_out, b_in),
            (xs_sem.at[i], xr_sem.at[i], as_sem.at[i], ar_sem.at[i], bs_sem.at[i], br_sem.at[i]),
        )
        for i in range(PIECES)
    ]
    def shard_flip(bits):
        low, high = lax.rem(s, 2), lax.div(s, 2)
        low = 1 - low if bits & 1 else low
        high = 1 - high if bits & 2 else high
        return 2 * high + low

    def q_copy(index):
        return rcopy(
            wg_send.at[pl.ds(pl.multiple_of(shard_flip((1, 3)[index]) * span, 128), span), :],
            q_core.at[index],
            qc_send.at[index],
            qc_recv.at[index],
            {"shard": shard_flip(1)},
        )

    def qx_copy():
        return rcopy(q_far, qx_in, qx_sem.at[0], qx_sem.at[1], {"shard": shard_flip(2)})

    def qz_copy(d):
        to = lax.rem(z + d, nz)
        return rcopy(
            q_near.at[pl.ds(pl.multiple_of(to * depth, depth), depth), :],
            q_all.at[z],
            qz_send.at[d - 1],
            qz_recv.at[d - 1],
            {"ctx": to},
        )

    def q_spread():
        qx_copy().wait_recv()
        q_near[...] = (q_near[...].astype(F32) + qx_in[...].astype(F32)).astype(BF)
        for d in range(1, nz):
            qz_copy(d).start()
        q_all[z] = q_near[pl.ds(pl.multiple_of(z * depth, depth), depth), :]

    def down_copy():
        return rcopy(down_part, down_recv, d_sem.at[0], d_sem.at[1], other)

    owners = width // 128

    def owner_cols(index):
        return pl.ds(pl.multiple_of(index * 128, 128), 128)

    def early_copy(d):
        index, device = peer(d)
        return index, rcopy(
            early_mine.at[:, owner_cols(lax.rem(index, owners))],
            early_recv.at[me],
            e_send.at[d - 1],
            e_recv.at[d - 1],
            device,
        )

    def spread_copy(d):
        cols = owner_cols(lax.rem(me, owners))
        return rcopy(
            early_sum.at[:, cols], early_sum.at[:, cols], f_send.at[d - 1], f_recv.at[d - 1], peer(d)[1]
        )

    def spread_arrival(d):
        index = lax.rem(me + count - d, count)
        cols = owner_cols(lax.rem(index, owners))
        return index, rcopy(
            early_sum.at[:, cols], early_sum.at[:, cols], f_send.at[d - 1], f_recv.at[d - 1], other
        )

    def late_copy(d):
        return rcopy(late, late_recv.at[me], l_send.at[d - 1], l_recv.at[d - 1], peer(d)[1])

    def over_peers(act):
        def one(d, carry):
            act(d)
            return carry

        lax.fori_loop(1, count, one, 0)

    for half in halves:
        half.x_copy().start()
    loads[0].wait()
    down_copy().start()

    fill_labels(info_all, rows // BRANCH, labels, parents)
    fill_trunk_keys(key, keys_aug)
    keys_turned[...] = key[0:TRUNK, :].T
    dk_trunk[...] = jnp.zeros(dk_trunk.shape, F32)
    dv_trunk[...] = jnp.zeros(dv_trunk.shape, F32)
    tile_mask = causal(BRANCH)

    def row_products(here, count_rows):
        turned = (ga_all[here, :].astype(F32) * out_heads[here, :].astype(F32)).T
        return jnp.concatenate(
            [
                jnp.sum(turned[:HD, :], axis=0, keepdims=True),
                jnp.sum(turned[HD:, :], axis=0, keepdims=True),
            ],
            axis=1,
        )

    def part_back(key_aug, value_rows, asked, given, level, drow, mask):
        logits = nt(key_aug, asked) * LOG2E - level
        if mask is not None:
            logits = jnp.where(mask, logits, NEG)
        probs = jnp.exp2(logits)
        grads = (probs * (nt(value_rows, given) - drow)).astype(BF)
        return probs.astype(BF), grads

    def segment(slot, carry):
        here = pl.ds(pl.multiple_of(TRUNK + slot * BRANCH, 128), BRANCH)
        seg = pl.ds(pl.multiple_of(slot * BRANCH, 128), BRANCH)
        stacked = stack_heads(query[here, :])
        asked = jnp.concatenate([stacked, query_features(slopes, BRANCH)], axis=1)
        given = stack_heads(ga_all[here, :])
        leaf, key_up, value_up = parent_pick(slot, labels, parents, key, value)
        own_feats, up_feats = segment_key_features(leaf)
        level = lse[pl.ds(4 + slot, 1), 0 : 2 * BRANCH]
        drow = row_products(here, BRANCH)
        probs, grads = part_back(keys_aug[...], value[0:TRUNK, :], asked, given, level, drow, None)
        dv_trunk[...] += nn(probs, given)
        dk_trunk[...] += nn(grads, stacked)
        turned = nn(keys_turned[...], grads)
        key_own = key[here, :]
        probs, grads = part_back(
            jnp.concatenate([key_own, own_feats], axis=1), value[here, :], asked, given, level, drow, tile_mask
        )
        dv_seg[seg, :] = nn(probs, given)
        dk_seg[seg, :] = nn(grads, stacked)
        turned = turned + nn(key_own.T, grads)
        probs, grads = part_back(
            jnp.concatenate([key_up, up_feats], axis=1), value_up, asked, given, level, drow, None
        )
        dv_up[seg, :] = nn(probs, given)
        dk_up[seg, :] = nn(grads, stacked)
        turned = turned + nn(key_up.T, grads)
        dqkv[here, 0:PAIR] = (unstack_turned(turned, BRANCH) * HD ** (-0.5)).astype(BF)
        return carry

    def dq_copy(to):
        return rcopy(
            dqkv.at[to * rows : (to + 1) * rows, 0:PAIR],
            dq_all.at[:, pl.ds(pl.multiple_of(z * wide, 128), PAIR)],
            r_send.at[to],
            r_recv.at[z],
            {"ctx": to},
        )

    def send_dq(to):
        @pl.when(z != to)
        def _():
            dq_copy(to).start()

    def piece_copy(to, i):
        return rcopy(
            dqkv.at[to * rows + i * chunk : to * rows + (i + 1) * chunk, PAIR:],
            dq_all.at[i * chunk : (i + 1) * chunk, pl.ds(pl.multiple_of(z * wide + PAIR, 128), 2 * PAIR)],
            p_send.at[to, i],
            p_recv.at[z, i],
            {"ctx": to},
        )

    wave_rows = TRUNK // 4
    wave_mask = causal(wave_rows)
    for tile in range(4):
        lo, hi = tile * wave_rows, (tile + 1) * wave_rows
        stacked = stack_heads(query[lo:hi, :])
        asked = jnp.concatenate([stacked, query_features(slopes, wave_rows)], axis=1)
        given = stack_heads(ga_all[lo:hi, :])
        level = lse[tile : tile + 1, :]
        drow = row_products(pl.ds(lo, wave_rows), wave_rows)
        probs, grads = part_back(
            keys_aug[lo:hi, :], value[lo:hi, :], asked, given, level, drow, wave_mask
        )
        dv_trunk[lo:hi, :] += nn(probs, given)
        dk_trunk[lo:hi, :] += nn(grads, stacked)
        turned = nn(keys_turned[:, lo:hi], grads)
        if tile:
            probs, grads = part_back(
                keys_aug[0:lo, :], value[0:lo, :], asked, given, level, drow, None
            )
            dv_trunk[0:lo, :] += nn(probs, given)
            dk_trunk[0:lo, :] += nn(grads, stacked)
            turned = turned + nn(keys_turned[:, 0:lo], grads)
        dqkv[lo:hi, 0:PAIR] = (unstack_turned(turned, wave_rows) * HD ** (-0.5)).astype(BF)
    send_dq(0)

    def turn(n, carry):
        @pl.when(n == 5)
        def _():
            send_dq(2)

        @pl.when(n == 7)
        def _():
            send_dq(1)
            load.wait()
            halves[0].step_x()

        return segment(jnp.where(n < 5, n + 2, jnp.where(n < 7, n - 5, n)), carry)

    lax.fori_loop(0, SLOTS, turn, 0)
    halves[1].step_x()
    send_dq(3)

    def gather_up(slot, carry):
        here = pl.ds(pl.multiple_of(TRUNK + slot * BRANCH, 128), BRANCH)
        seg = pl.ds(pl.multiple_of(slot * BRANCH, 128), BRANCH)
        mine = labels[pl.ds(slot, 1), :]
        dk, dv = dk_seg[seg, :], dv_seg[seg, :]
        for below in range(SLOTS):
            same = (parents[below : below + 1, :] == mine).astype(F32)
            at = below * BRANCH
            dk = dk + same * dk_up[at : at + BRANCH, :]
            dv = dv + same * dv_up[at : at + BRANCH, :]
        dqkv[here, PAIR : 2 * PAIR] = dk.astype(BF)
        dqkv[here, 2 * PAIR :] = dv.astype(BF)
        return carry

    lax.fori_loop(0, SLOTS, gather_up, 0)
    dqkv[0:TRUNK, PAIR : 2 * PAIR] = dk_trunk[...].astype(BF)
    dqkv[0:TRUNK, 2 * PAIR :] = dv_trunk[...].astype(BF)
    for i in range(ROWS_WAVE):
        for to in range(nz):

            @pl.when(z != to)
            def _():
                piece_copy(to, i).start()

    for to in range(nz):

        @pl.when(z == to)
        def _():
            dq_all[:, pl.ds(pl.multiple_of(z * wide, 128), wide)] = dqkv[to * rows : (to + 1) * rows, :]

    def weight(block, carry):
        here = pl.ds(pl.multiple_of(block * 128, 128), 128)
        wg_send[here, :] = nn(act_turned[here, :], dqkv[...]).astype(BF)
        return carry

    loads[1].wait()
    lax.fori_loop(0, width // 128, weight, 0)
    q_copy(0).start()
    q_copy(1).start()

    early_mine[...] = early[...]
    early_mine[6:7, pl.ds(pl.multiple_of(z * PAIR, 128), PAIR)] = jnp.sum(
        dqkv[:, 0:PAIR].astype(F32), axis=0, keepdims=True
    )
    early_mine[6:7, pl.ds(pl.multiple_of((nz + z) * PAIR, 128), PAIR)] = jnp.sum(
        dqkv[:, 2 * PAIR :].astype(F32), axis=0, keepdims=True
    )

    def early_send(d):
        index, copy = early_copy(d)

        @pl.when(index < owners)
        def _():
            copy.start()

    over_peers(early_send)
    early_recv[me] = early_mine[:, owner_cols(lax.rem(me, owners))]

    def at(i):
        return pl.ds(pl.multiple_of(i * chunk, 32), chunk)

    def n_copy(i):
        return rcopy(n_send.at[at(i), :], n_recv.at[at(i), :], ns_sem.at[i], nr_sem.at[i], other)

    def core_join():
        for index in range(2):
            q_copy(index).wait_recv()
            mine = pl.ds(pl.multiple_of(shard_flip((0, 2)[index]) * span, 128), span)
            (q_near, q_far)[index][...] = (wg_send[mine, :].astype(F32) + q_core[index].astype(F32)).astype(BF)
        qx_copy().start()

    def first(i):
        for owner in range(nz):

            @pl.when(z != owner)
            def _():
                if i == 0:
                    rcopy(
                        dqkv.at[0:rows, 0:PAIR],
                        dq_all.at[:, owner * wide : owner * wide + PAIR],
                        r_send.at[owner],
                        r_recv.at[owner],
                        {"ctx": owner},
                    ).wait_recv()
                rcopy(
                    dqkv.at[0:chunk, PAIR:],
                    dq_all.at[i * chunk : (i + 1) * chunk, owner * wide + PAIR : (owner + 1) * wide],
                    p_send.at[owner, i],
                    p_recv.at[owner, i],
                    {"ctx": owner},
                ).wait_recv()

        n_send[at(i), :] = nt(dq_all[at(i), :], wqkv[...]).astype(BF)
        n_copy(i).start()

    def second(i, carry):
        n_copy(i).wait_recv()
        here = at(i)
        grad = n_send[here, :].astype(F32) + n_recv[here, :].astype(F32)
        _, normed, inverse = norm_rows(tok[here, :].astype(F32), gain[0:1, :], shift[0:1, :])
        gtok[here, :] = gmid[here, :] + norm_rows_back(grad, normed, inverse, gain[0:1, :])
        late[0:1, :] += jnp.sum(grad * normed, axis=0, keepdims=True)
        late[1:2, :] += jnp.sum(grad, axis=0, keepdims=True)
        return carry

    def output(i, carry):
        here = at(i)
        result[here, :] = (
            mid[here, :] + b_down[...] + (down_part[here, :].astype(F32) + down_recv[here, :].astype(F32))
        ).astype(BF)
        return carry

    late[...] = jnp.zeros(late.shape, F32)
    for one in loads[2:]:
        one.wait()
    core_join()
    halves[2].step_x()
    first(0)
    first(1)
    halves[3].step_x()
    first(2)
    halves[4].step_x()
    first(3)
    halves[5].step_x()
    down_copy().wait_recv()
    lax.fori_loop(0, ROWS_WAVE, output, 0)

    @pl.when(me < owners)
    def _():
        over_peers(lambda d: early_copy(d)[1].wait_recv())
        total = early_recv[0]
        for index in range(1, count):
            total = total + early_recv[index]
        early_sum[:, owner_cols(lax.rem(me, owners))] = total
        over_peers(lambda d: spread_copy(d).start())

    q_spread()
    halves[0].step_a()
    halves[1].step_a()
    lax.fori_loop(0, 2, second, 0)
    halves[2].step_a()
    lax.fori_loop(2, ROWS_WAVE, second, 0)
    over_peers(lambda d: late_copy(d).start())
    late_recv[me] = late[...]
    halves[3].step_a()
    halves[4].step_a()
    halves[5].step_a()

    for d in range(1, nz):
        qz_copy(d).wait_recv()
    for owner in range(nz):
        for part in range(3):
            gwqkv[part, :, owner * PAIR : (owner + 1) * PAIR] = q_all[
                owner, :, part * PAIR : (part + 1) * PAIR
            ].astype(F32)
    bounds = (0, units, 2 * units, total_cols)
    for i, half in enumerate(halves):
        block = half.step_b()
        lo, hi = i * step_cols, (i + 1) * step_cols
        for target, start_at, end_at in (
            (gup, bounds[0], bounds[1]),
            (gdown, bounds[1], bounds[2]),
            (gout, bounds[2], bounds[3]),
        ):
            a, b = max(lo, start_at), min(hi, end_at)
            if a < b:
                target[:, a - start_at : b - start_at] = block[:, a - lo : b - lo]

    def early_wait(d):
        index, copy = spread_arrival(d)

        @pl.when(index < owners)
        def _():
            copy.wait_recv()

    over_peers(early_wait)
    over_peers(lambda d: late_copy(d).wait_recv())
    total = late_recv[0]
    for index in range(1, count):
        total = total + late_recv[index]
    late_sum[...] = total

    down_copy().wait_send()
    for half in halves:
        half.finish()
    qx_copy().wait_send()
    for d in range(1, nz):
        qz_copy(d).wait_send()
    q_copy(0).wait_send()
    q_copy(1).wait_send()

    def early_drain(d):
        index, copy = early_copy(d)

        @pl.when(index < owners)
        def _():
            copy.wait_send()

    over_peers(early_drain)

    @pl.when(me < owners)
    def _():
        over_peers(lambda d: spread_copy(d).wait_send())

    over_peers(lambda d: late_copy(d).wait_send())

    def finish(i, carry):
        n_copy(i).wait_send()
        return carry

    lax.fori_loop(0, ROWS_WAVE, finish, 0)
    for owner in range(nz):

        @pl.when(z != owner)
        def _():
            dq_copy(owner).wait_send()
            for i in range(ROWS_WAVE):
                piece_copy(owner, i).wait_send()


def run_back(dims, units, *inputs):
    ns, nz, rows = dims
    width = inputs[14].shape[1]
    _, span, total = inputs[9].shape
    count = ns * nz
    depth = width // count
    wide = 3 * PAIR
    anywhere = pl.BlockSpec(memory_space=pl.ANY)
    return pl.pallas_call(
        partial(back_kernel, dims),
        name="tree_backward",
        out_shape=(
            shape((rows, width), BF),
            shape((rows, width), F32),
            shape((depth, units), F32),
            shape((depth, units), F32),
            shape((depth, total - 2 * units), F32),
            shape((3, depth, nz * PAIR), F32),
            shape((8, width), F32),
            shape((2, width), F32),
        ),
        in_specs=[vmem()] * 7 + [anywhere] * 5 + [vmem()] + [anywhere] * 2 + [vmem()] * 4,
        out_specs=[vmem()] * 8,
        scratch_shapes=[
            *[pltpu.VMEM(inputs[k].shape, inputs[k].dtype) for k in (7, 8, 10, 11, 13, 14)],
            pltpu.VMEM((span, total), BF),
            pltpu.VMEM((span, total), BF),
            pltpu.VMEM((2, depth, total), BF),
            pltpu.VMEM((depth, total), BF),
            pltpu.VMEM((depth, total), BF),
            pltpu.VMEM((span, wide), BF),
            pltpu.VMEM((span, wide), BF),
            pltpu.VMEM((2, span, wide), BF),
            pltpu.VMEM((span, wide), BF),
            pltpu.VMEM((nz, depth, wide), BF),
            pltpu.VMEM((TREE, wide), BF),
            pltpu.VMEM((TRUNK, PAIR), F32),
            pltpu.VMEM((TRUNK, PAIR), F32),
            pltpu.VMEM((TREE - TRUNK, PAIR), F32),
            pltpu.VMEM((TREE - TRUNK, PAIR), F32),
            pltpu.VMEM((TREE - TRUNK, PAIR), F32),
            pltpu.VMEM((TREE - TRUNK, PAIR), F32),
            pltpu.VMEM((TRUNK, 2 * PAIR), BF),
            pltpu.VMEM((PAIR, TRUNK), BF),
            pltpu.VMEM((16, 128), F32),
            pltpu.VMEM((16, 128), F32),
            pltpu.VMEM((rows, nz * wide), BF),
            pltpu.VMEM((rows, width), BF),
            pltpu.VMEM((rows, width), BF),
            pltpu.VMEM((rows, width), BF),
            pltpu.VMEM((width, wide), BF),
            pltpu.VMEM((8, width), F32),
            pltpu.VMEM((count, 8, 128), F32),
            pltpu.VMEM((2, width), F32),
            pltpu.VMEM((count, 2, width), F32),
            dma(2),
            dma(count - 1),
            dma(count - 1),
            dma(count - 1),
            dma(count - 1),
            dma(count - 1),
            dma(count - 1),
            dma(nz, ROWS_WAVE),
            dma(nz, ROWS_WAVE),
            dma(nz),
            dma(nz),
            dma(ROWS_WAVE),
            dma(ROWS_WAVE),
            dma(PIECES),
            dma(PIECES),
            dma(PIECES, 2),
            dma(PIECES, 2),
            dma(PIECES),
            dma(PIECES),
            dma(2),
            dma(2),
            dma(2),
            dma(nz - 1),
            dma(nz - 1),
            pltpu.SemaphoreType.DMA,
            dma(6),
        ],
        compiler_params=pltpu.CompilerParams(
            collective_id=2, has_side_effects=True, vmem_limit_bytes=60 << 20
        ),
        cost_estimate=pl.CostEstimate(flops=40_000_000_000, bytes_accessed=20_000_000, transcendentals=0),
    )(*inputs)


def place_kernel(early, late, *refs):
    count = (len(refs) - 7) // 3
    sources, targets, middle = refs[:count], refs[count : 2 * count], refs[2 * count + 6 : -1]
    b_qv, b_out, b_up, b_down, gains, shifts = refs[2 * count : 2 * count + 6]
    sems = refs[-1]
    loads = [pltpu.make_async_copy(a, b, sems.at[0, k]) for k, (a, b) in enumerate(zip(sources, middle))]
    copies = [pltpu.make_async_copy(a, b, sems.at[1, k]) for k, (a, b) in enumerate(zip(middle, targets))]
    for load in loads:
        load.start()
    for load, copy in zip(loads, copies):
        load.wait()
        copy.start()
    wide, width = b_qv.shape[1], b_out.shape[1]
    for row in range(2):
        b_qv[row : row + 1, :] = early[6:7, row * wide : (row + 1) * wide]
    b_out[...] = early[2:3, :]
    for row in range(b_up.shape[1] // width):
        b_up[:, row * width : (row + 1) * width] = early[row : row + 1, :]
    b_down[...] = early[3:4, :]
    gains[0:1, :] = late[0:1, :]
    gains[1:2, :] = early[4:5, :]
    shifts[0:1, :] = late[1:2, :]
    shifts[1:2, :] = early[5:6, :]
    for copy in copies:
        copy.wait()


def run_place(early, late, wide, units, *arrays):
    width = early.shape[1]
    anywhere = pl.BlockSpec(memory_space=pl.ANY)
    return pl.pallas_call(
        place_kernel,
        name="place",
        out_shape=(
            *[shape(a.shape, a.dtype) for a in arrays],
            shape((2, wide), F32),
            shape((1, width), F32),
            shape((1, units), F32),
            shape((1, width), F32),
            shape((2, width), F32),
            shape((2, width), F32),
        ),
        in_specs=[vmem()] * 2 + [anywhere] * len(arrays),
        out_specs=[anywhere] * len(arrays) + [vmem()] * 6,
        scratch_shapes=[*[pltpu.VMEM(a.shape, a.dtype) for a in arrays], dma(2, len(arrays))],
        compiler_params=pltpu.CompilerParams(vmem_limit_bytes=60 << 20),
    )(early, late, *arrays)


def position_slopes(ntp, nz):
    index = np.arange(HEADS, dtype=np.float32).reshape(ntp * nz, 2)
    slope = np.exp2(-8.0 * (index + 1.0) / HEADS).astype(np.float32)
    table = np.zeros((ntp * nz, 2, 128), np.float32)
    left = slope
    for part in range(3):
        piece = left.astype(BF).astype(np.float32)
        table[:, :, part] = piece
        table[:, :, part + 3] = piece
        left = left - piece
    table[:, :, 6] = 1.0
    return table


def fast_device(
    tokens, cotangent, seg_ids, positions, parents, w_qkv, b_qv, w_out, b_out, w_up, b_up, w_down, b_down, ln_gain, ln_bias
):
    rows = tokens.shape[0]
    ns, nz, ntp = lax.axis_size("shard"), lax.axis_size("ctx"), lax.axis_size("tp")
    dims = (ns, nz, rows)

    slopes = jnp.asarray(position_slopes(ntp, nz))
    units = b_up.shape[0]
    (
        act_turned, query, key, value, out_heads, lse, info_all, wqkv, partial_sums, ga_all, down_part, mid, gmid, sums
    ) = run_front(
        dims, tokens, w_up, w_out.T, w_down.T, cotangent, w_qkv, seg_ids.reshape(rows // BRANCH, BRANCH),
        parents[None, :], b_qv, slopes, ln_gain, ln_bias,
        b_out[None, :], b_up[None, :],
    )
    result, grad_tokens, gup, gdown, gout, grad_w_qkv, early, late = run_back(
        dims, units, query, key, value, out_heads, lse, info_all, ga_all, act_turned, wqkv, partial_sums, down_part,
        mid, b_down[None, :], gmid, tokens, slopes, ln_gain, ln_bias, sums,
    )
    result, grad_tokens, grad_w_qkv, gup, gdown, gout, b_qv_sum, b_out_sum, b_up_sum, b_down_sum, gains, shifts = run_place(
        early, late, nz * PAIR, units, result, grad_tokens, grad_w_qkv, gup, gdown, gout
    )
    return (
        result,
        grad_tokens,
        grad_w_qkv,
        b_qv_sum,
        gout.T,
        b_out_sum.reshape(-1),
        gup,
        b_up_sum.reshape(-1),
        gdown.T,
        b_down_sum.reshape(-1),
        gains,
        shifts,
    )


def norm_forward(inputs_in, gain_row, shift_row):
    centre = inputs_in - jnp.mean(inputs_in, axis=-1, keepdims=True)
    inverse = lax.rsqrt(jnp.mean(centre * centre, axis=-1, keepdims=True) + EPS)
    normed = centre * inverse
    return (normed * gain_row + shift_row, normed, inverse)


def norm_backward(grad_in, normed, inverse, gain_row):
    scaled = grad_in * gain_row
    mean_grad = jnp.mean(scaled, axis=-1, keepdims=True)
    mean_cross = jnp.mean(scaled * normed, axis=-1, keepdims=True)
    return inverse * (scaled - mean_grad - normed * mean_cross)


def ancestry(seg_vals, parents):
    first_up = jnp.take(parents, seg_vals)
    return (first_up, jnp.take(parents, first_up))


def block_scores(query_heads, key_heads, query_tags, key_tags, slopes):
    q_seg, q_first, q_second, q_pos = query_tags
    k_seg, k_pos = key_tags
    raw_scores = jnp.einsum(
        "qhd,khd->hqk", query_heads, key_heads, preferred_element_type=jnp.float32
    ) * HD ** (-0.5)
    distance = (q_pos[:, None] - k_pos[None, :]).astype(jnp.float32)
    scores = raw_scores - slopes[:, None, None] * distance[None]
    related = (
        (k_seg[None, :] == q_seg[:, None])
        | (k_seg[None, :] == q_first[:, None])
        | (k_seg[None, :] == q_second[:, None])
    )
    allowed = related & (k_pos[None, :] <= q_pos[:, None])
    return (scores, allowed[None])


def probabilities(scores, allowed, row_max, row_sum):
    shifted = jnp.where(allowed, scores - row_max[:, :, None], NEG)
    return jnp.exp(shifted) / row_sum[:, :, None]


def per_device(
    tokens,
    cotangent,
    seg_ids,
    positions,
    parents,
    w_qkv,
    b_qv,
    w_out,
    b_out,
    w_up,
    b_up,
    w_down,
    b_down,
    ln_gain,
    ln_bias,
):
    num_rows = tokens.shape[0]
    head_count = HEADS // lax.axis_size("tp")
    head_width = head_count * HD
    head_index = (lax.axis_index("tp") * head_count + jnp.arange(head_count)).astype(jnp.float32)
    slopes = 2.0 ** (-8.0 * (head_index + 1.0) / HEADS)
    scale = HD ** (-0.5)
    full_qkv, full_out = (
        lax.all_gather(w_qkv, ("shard", "ctx"), axis=1, tiled=True),
        lax.all_gather(w_out, ("shard", "ctx"), axis=1, tiled=True),
    )
    group_seg, group_pos = (
        lax.all_gather(seg_ids, "ctx", axis=0, tiled=True),
        lax.all_gather(positions, "ctx", axis=0, tiled=True),
    )
    own_first, own_second = ancestry(seg_ids, parents)
    own_tags = (seg_ids, own_first, own_second, positions)
    inputs = tokens.astype(jnp.float32)
    norm_one, normed_one, inverse_one = norm_forward(inputs, ln_gain[0], ln_bias[0])
    act_one = norm_one.astype(jnp.bfloat16)
    projected = jnp.einsum("td,cde->cte", act_one, full_qkv, preferred_element_type=jnp.float32)
    qkv_bias = jnp.stack([b_qv[0], jnp.zeros((head_width,), jnp.float32), b_qv[1]])
    qkv_low = (projected + qkv_bias[:, None, :]).astype(jnp.bfloat16)
    query_flat, key_flat, value_flat = (qkv_low[0], qkv_low[1], qkv_low[2])
    group_keys, group_values = (
        lax.all_gather(key_flat, "ctx", axis=0, tiled=True),
        lax.all_gather(value_flat, "ctx", axis=0, tiled=True),
    )
    group_rows = group_keys.shape[0]
    block_count = group_rows // KEY_BLOCK
    key_blocks = group_keys.reshape(block_count, KEY_BLOCK, head_count, HD)
    value_blocks = group_values.reshape(block_count, KEY_BLOCK, head_count, HD)
    seg_blocks = group_seg.reshape(block_count, KEY_BLOCK)
    pos_blocks = group_pos.reshape(block_count, KEY_BLOCK)
    query_heads = query_flat.reshape(num_rows, head_count, HD)

    def stats_step(carry_in, block_parts):
        row_max, row_sum = carry_in
        key_part, seg_part, pos_part = block_parts
        scores, allowed = block_scores(
            query_heads, key_part, own_tags, (seg_part, pos_part), slopes
        )
        new_max = jnp.maximum(row_max, jnp.max(jnp.where(allowed, scores, NEG), axis=-1))
        shifted = jnp.where(allowed, scores - new_max[:, :, None], NEG)
        row_sum = row_sum * jnp.exp(row_max - new_max) + jnp.sum(jnp.exp(shifted), axis=-1)
        return ((new_max, row_sum), None)

    start_stats = (
        jnp.full((head_count, num_rows), NEG, jnp.float32),
        jnp.zeros((head_count, num_rows), jnp.float32),
    )
    (row_max, row_sum), _ = lax.scan(stats_step, start_stats, (key_blocks, seg_blocks, pos_blocks))

    def output_step(out_accum, block_parts):
        key_part, value_part, seg_part, pos_part = block_parts
        scores, allowed = block_scores(
            query_heads, key_part, own_tags, (seg_part, pos_part), slopes
        )
        prob_low = probabilities(scores, allowed, row_max, row_sum).astype(jnp.bfloat16)
        return (
            out_accum
            + jnp.einsum("hqk,khd->qhd", prob_low, value_part, preferred_element_type=jnp.float32),
            None,
        )

    attended, _ = lax.scan(
        output_step,
        jnp.zeros((num_rows, head_count, HD), jnp.float32),
        (key_blocks, value_blocks, seg_blocks, pos_blocks),
    )
    attended_low = attended.reshape(num_rows, head_width).astype(jnp.bfloat16)
    branch_one = (
        lax.psum(
            jnp.dot(attended_low, full_out, preferred_element_type=jnp.float32).astype(
                jnp.bfloat16
            ),
            "tp",
        ).astype(jnp.float32)
        + b_out
    )
    middle = inputs + branch_one
    full_up, full_down = (
        lax.all_gather(w_up, ("shard", "ctx"), axis=0, tiled=True),
        lax.all_gather(w_down, ("shard", "ctx"), axis=1, tiled=True),
    )
    norm_two, normed_two, inverse_two = norm_forward(middle, ln_gain[1], ln_bias[1])
    act_two = norm_two.astype(jnp.bfloat16)
    upper_in = jnp.dot(act_two, full_up, preferred_element_type=jnp.float32) + b_up
    gelu_vals, gelu_pull = jax.vjp(partial(jax.nn.gelu, approximate=True), upper_in)
    hidden = gelu_vals.astype(jnp.bfloat16)
    branch_two = (
        lax.psum(
            jnp.dot(hidden, full_down, preferred_element_type=jnp.float32).astype(jnp.bfloat16),
            "tp",
        ).astype(jnp.float32)
        + b_down
    )
    result = (middle + branch_two).astype(jnp.bfloat16)
    grad_out = cotangent.astype(jnp.float32)
    grad_hidden = jnp.einsum("td,fd->tf", cotangent, full_down, preferred_element_type=jnp.float32)
    grad_upper = gelu_pull(grad_hidden)[0].astype(jnp.bfloat16)
    down_term = jnp.einsum("tf,td->fd", hidden, cotangent, preferred_element_type=jnp.float32)
    up_term = jnp.einsum("td,tf->df", act_two, grad_upper, preferred_element_type=jnp.float32)
    grad_w_up, grad_w_down = (
        lax.psum_scatter(up_term, ("shard", "ctx"), scatter_dimension=0, tiled=True),
        lax.psum_scatter(down_term, ("shard", "ctx"), scatter_dimension=1, tiled=True),
    )
    grad_norm_two = lax.psum(
        jnp.einsum("tf,df->td", grad_upper, full_up, preferred_element_type=jnp.float32).astype(
            jnp.bfloat16
        ),
        "tp",
    ).astype(jnp.float32)
    grad_middle = grad_out + norm_backward(grad_norm_two, normed_two, inverse_two, ln_gain[1])
    grad_branch = grad_middle.astype(jnp.bfloat16)
    out_term = jnp.einsum(
        "te,td->ed", attended_low, grad_branch, preferred_element_type=jnp.float32
    )
    grad_att = jnp.einsum(
        "td,ed->te", grad_branch, full_out, preferred_element_type=jnp.float32
    ).astype(jnp.bfloat16)
    grad_heads = grad_att.reshape(num_rows, head_count, HD)
    row_terms = jnp.einsum("qhd,qhd->hq", grad_heads.astype(jnp.float32), attended)

    def joint_step(grad_accum, block_parts):
        key_part, value_part, seg_part, pos_part = block_parts
        scores, allowed = block_scores(
            query_heads, key_part, own_tags, (seg_part, pos_part), slopes
        )
        prob_vals = probabilities(scores, allowed, row_max, row_sum)
        grad_probs = jnp.einsum(
            "qhd,khd->hqk", grad_heads, value_part, preferred_element_type=jnp.float32
        )
        grad_scores = (prob_vals * (grad_probs - row_terms[:, :, None])).astype(jnp.bfloat16)
        grad_accum = (
            grad_accum
            + jnp.einsum("hqk,khd->qhd", grad_scores, key_part, preferred_element_type=jnp.float32)
            * scale
        )
        key_part_grad = (
            jnp.einsum("hqk,qhd->khd", grad_scores, query_heads, preferred_element_type=jnp.float32)
            * scale
        )
        value_part_grad = jnp.einsum(
            "hqk,qhd->khd",
            prob_vals.astype(jnp.bfloat16),
            grad_heads,
            preferred_element_type=jnp.float32,
        )
        return (
            grad_accum,
            (
                key_part_grad.reshape(KEY_BLOCK, head_width),
                value_part_grad.reshape(KEY_BLOCK, head_width),
            ),
        )

    grad_query_sum, (key_terms, value_terms) = lax.scan(
        joint_step,
        jnp.zeros((num_rows, head_count, HD), jnp.float32),
        (key_blocks, value_blocks, seg_blocks, pos_blocks),
    )
    key_grad_sum, value_grad_sum = (
        lax.psum_scatter(
            key_terms.reshape(group_rows, head_width).astype(jnp.bfloat16),
            "ctx",
            scatter_dimension=0,
            tiled=True,
        ).astype(jnp.float32),
        lax.psum_scatter(
            value_terms.reshape(group_rows, head_width).astype(jnp.bfloat16),
            "ctx",
            scatter_dimension=0,
            tiled=True,
        ).astype(jnp.float32),
    )
    grad_query_low = grad_query_sum.reshape(num_rows, head_width).astype(jnp.bfloat16)
    grad_key_low = key_grad_sum.astype(jnp.bfloat16)
    grad_value_low = value_grad_sum.astype(jnp.bfloat16)
    grad_qkv = jnp.stack([grad_query_low, grad_key_low, grad_value_low])
    grad_norm_one = lax.psum(
        jnp.einsum("cte,cde->td", grad_qkv, full_qkv, preferred_element_type=jnp.float32).astype(
            jnp.bfloat16
        ),
        "tp",
    ).astype(jnp.float32)
    grad_tokens = grad_middle + norm_backward(grad_norm_one, normed_one, inverse_one, ln_gain[0])
    qkv_term = jnp.einsum("td,cte->cde", act_one, grad_qkv, preferred_element_type=jnp.float32)
    grad_w_qkv, grad_w_out = (
        lax.psum_scatter(qkv_term, ("shard", "ctx"), scatter_dimension=1, tiled=True),
        lax.psum_scatter(out_term, ("shard", "ctx"), scatter_dimension=1, tiled=True),
    )
    bias_qv_part = jnp.stack(
        [
            jnp.sum(grad_query_low.astype(jnp.float32), axis=0),
            jnp.sum(grad_value_low.astype(jnp.float32), axis=0),
        ]
    )
    out_bias_part = jnp.sum(grad_branch.astype(jnp.float32), axis=0)
    up_bias_part = jnp.sum(grad_upper.astype(jnp.float32), axis=0)
    down_bias_part = jnp.sum(grad_out, axis=0)
    gain_part = jnp.stack(
        [jnp.sum(grad_norm_one * normed_one, axis=0), jnp.sum(grad_norm_two * normed_two, axis=0)]
    )
    shift_part = jnp.stack([jnp.sum(grad_norm_one, axis=0), jnp.sum(grad_norm_two, axis=0)])
    grad_b_qv, grad_b_out, grad_b_up, grad_b_down, grad_gain, grad_shift = lax.psum(
        (bias_qv_part, out_bias_part, up_bias_part, down_bias_part, gain_part, shift_part),
        ("shard", "ctx"),
    )
    return (
        result,
        grad_tokens,
        grad_w_qkv,
        grad_b_qv,
        grad_w_out,
        grad_b_out,
        grad_w_up,
        grad_b_up,
        grad_w_down,
        grad_b_down,
        grad_gain,
        grad_shift,
    )


def solution(mesh):
    placed = (
        P(("shard", "ctx"), None),
        P(("shard", "ctx"), None),
        P(("shard", "ctx")),
        P(("shard", "ctx")),
        P(),
        P(None, ("shard", "ctx"), "tp"),
        P(None, "tp"),
        P("tp", ("shard", "ctx")),
        P(),
        P(("shard", "ctx"), "tp"),
        P("tp"),
        P("tp", ("shard", "ctx")),
        P(),
        P(),
        P(),
    )
    sizes = dict(mesh.shape)
    paired = sizes["tp"] * sizes["ctx"] * 2 == HEADS and sizes["tp"] == 2 and sizes["shard"] == 4
    return jax.shard_map(
        fast_device if paired else per_device,
        mesh=mesh,
        in_specs=placed,
        out_specs=(
            P(("shard", "ctx"), None),
            P(("shard", "ctx"), None),
            P(None, ("shard", "ctx"), "tp"),
            P(None, "tp"),
            P("tp", ("shard", "ctx")),
            P(),
            P(("shard", "ctx"), "tp"),
            P("tp"),
            P("tp", ("shard", "ctx")),
            P(),
            P(),
            P(),
        ),
        check_vma=False,
    )
```

```python
from functools import partial

import jax
import jax.numpy as jnp
import numpy as np
from jax import lax
from jax.experimental import pallas as pl
from jax.experimental.pallas import tpu as pltpu
from jax.sharding import PartitionSpec as P

HEADS = 16
HD = 64
KEY_BLOCK = 512
TRUNK = 1024
BRANCH = 128
SLOTS = 12
TREE = TRUNK + SLOTS * BRANCH
PAIR = 2 * HD

EPS = 1e-05
NEG = -1e30
LOG2E = 1.4426950408889634
MESH = pl.DeviceIdType.MESH
BF = jnp.bfloat16
F32 = jnp.float32
ROWS_WAVE = 4
FRONT_LIMIT = 62 << 20
BLOCK = 512
CURVE = 0.044715
ROOT = 0.7978845608028654
SUBS = 2


def nt(left, right):
    return lax.dot_general(left, right, (((1,), (1,)), ((), ())), preferred_element_type=F32)


def nn(left, right):
    return lax.dot_general(left, right, (((1,), (0,)), ((), ())), preferred_element_type=F32)


def rcopy(src, dst, send, recv, device):
    return pltpu.make_async_remote_copy(
        src_ref=src, dst_ref=dst, send_sem=send, recv_sem=recv, device_id=device, device_id_type=MESH
    )


def greet(devices):
    barrier = pltpu.get_barrier_semaphore()
    for device in devices:
        pl.semaphore_signal(barrier, inc=1, device_id=device, device_id_type=MESH)
    pl.semaphore_wait(barrier, len(devices))


def norm_rows(values, gain_row, shift_row):
    centre = values - jnp.mean(values, axis=-1, keepdims=True)
    inverse = lax.rsqrt(jnp.mean(centre * centre, axis=-1, keepdims=True) + EPS)
    normed = centre * inverse
    return normed * gain_row + shift_row, normed, inverse


def norm_rows_back(grad_in, normed, inverse, gain_row):
    scaled = grad_in * gain_row
    mean_grad = jnp.mean(scaled, axis=-1, keepdims=True)
    mean_cross = jnp.mean(scaled * normed, axis=-1, keepdims=True)
    return inverse * (scaled - mean_grad - normed * mean_cross)


def head_masks():
    lane = lax.broadcasted_iota(jnp.int32, (1, PAIR), 1)
    first = (lane < HD).astype(F32).astype(BF)
    second = (lane >= HD).astype(F32).astype(BF)
    return first, second


def stack_heads(rows):
    first, second = head_masks()
    return jnp.concatenate([rows * first, rows * second], axis=0)


def unstack_turned(turned, rows):
    return jnp.concatenate([turned[:HD, :rows], turned[HD:, rows:]], axis=0).T


def key_features(high, low, flag, rows):
    lane = lax.broadcasted_iota(jnp.int32, (rows, 128), 1)
    feats = jnp.where(lane < 3, high, jnp.where(lane < 6, low, jnp.where(lane == 6, flag, 0.0)))
    return feats.astype(BF)


def query_features(slope_ref, rows):
    return jnp.concatenate(
        [
            jnp.broadcast_to(slope_ref[0:1, :], (rows, 128)),
            jnp.broadcast_to(slope_ref[1:2, :], (rows, 128)),
        ],
        axis=0,
    ).astype(BF)


def fill_trunk_keys(key_ref, keys_aug):
    keys_aug[:, 0:PAIR] = key_ref[0:TRUNK, :]
    pos = lax.broadcasted_iota(jnp.int32, (TRUNK, 128), 0)
    low = pos & 255
    keys_aug[:, PAIR:] = key_features((pos - low).astype(F32), low.astype(F32), 0.0, TRUNK)


def fill_labels(info_all, blocks, labels, parents):
    labels[...] = jnp.full(labels.shape, -1.0, F32)
    parents[...] = jnp.full(parents.shape, -2.0, F32)
    for slot in range(SLOTS):
        block = TRUNK // BRANCH + slot
        owner, inner = block // blocks, block % blocks
        labels[slot : slot + 1, :] = info_all[owner, inner : inner + 1, :]
        parents[slot : slot + 1, :] = info_all[owner, 8 + inner : 9 + inner, :]


def parent_pick(slot, labels, parents, key_ref, value_ref):
    mine = parents[pl.ds(slot, 1), :]
    leaf = jnp.zeros((1, 128), F32)
    key_sum = jnp.zeros((BRANCH, PAIR), BF)
    value_sum = jnp.zeros((BRANCH, PAIR), BF)
    for other in range(SLOTS):
        same = (mine == labels[other : other + 1, :]).astype(F32)
        leaf = leaf + same
        same_low = same.astype(BF)
        at = TRUNK + other * BRANCH
        key_sum = key_sum + same_low * key_ref[at : at + BRANCH, :]
        value_sum = value_sum + same_low * value_ref[at : at + BRANCH, :]
    return leaf, key_sum, value_sum


def segment_key_features(leaf):
    row = lax.broadcasted_iota(jnp.int32, (BRANCH, 128), 0).astype(F32)
    own = key_features(float(TRUNK), row + leaf * float(BRANCH), 0.0, BRANCH)
    above = key_features(float(TRUNK), row, (leaf - 1.0) * 1e30, BRANCH)
    return own, above


def causal(rows):
    key = lax.broadcasted_iota(jnp.int32, (rows, rows), 0)
    query = lax.broadcasted_iota(jnp.int32, (rows, rows), 1)
    once = key <= query
    return jnp.concatenate([once, once], axis=1)


class Spread:
    def __init__(self, full, dims, depth, cols, sems, doubling=True):
        self.doubling = doubling
        self.full, self.depth, self.cols = full, depth, cols
        self.ns, self.nz, _ = dims
        self.s, self.z = lax.axis_index("shard"), lax.axis_index("ctx")
        self.zs, self.zr, self.xs, self.xr, self.cs, self.cr = sems

    def rows(self, shard, place):
        at = pl.multiple_of((shard * self.nz + place) * self.depth, self.depth)
        return self.full.at[pl.ds(at, self.depth), self.cols]

    def flip(self, bits):
        low = lax.rem(self.s, 2)
        high = lax.div(self.s, 2)
        if bits & 1:
            low = 1 - low
        if bits & 2:
            high = 1 - high
        return 2 * high + low

    def source(self, d):
        low, high = lax.rem(self.z, 2), lax.div(self.z, 2)
        low = 1 - low if d & 1 else low
        high = 1 - high if d & 2 else high
        return 2 * high + low

    def z_copy(self, d):
        ref = self.rows(self.s, self.source(2 if self.doubling and d == 3 else 0))
        to = self.source(1 if self.doubling and d == 3 else d)
        return rcopy(ref, ref, self.zs.at[d - 1], self.zr.at[d - 1], {"ctx": to})

    def x_copy(self, d):
        ref = self.rows(self.s, self.source(d))
        return rcopy(ref, ref, self.xs.at[d], self.xr.at[d], {"shard": self.flip(2)})

    def c_copy(self, far, d):
        ref = self.rows(self.flip(2) if far else self.s, self.source(d))
        return rcopy(ref, ref, self.cs.at[far, d], self.cr.at[far, d], {"shard": self.flip(1)})

    def z_start(self):
        self.z_copy(2).start()
        self.z_copy(1).start()
        if not self.doubling:
            self.z_copy(3).start()

    def own(self):
        self.x_copy(0).start()
        self.c_copy(0, 0).start()

    def z_done(self, d):
        ref = self.rows(self.s, self.source(d))
        rcopy(ref, ref, self.zs.at[d - 1], self.zr.at[d - 1], {"ctx": self.source(1)}).wait_recv()
        if self.doubling and d == 2:
            self.z_copy(3).start()
        self.x_copy(d).start()
        self.c_copy(0, d).start()

    def x_done(self, d):
        ref = self.rows(self.flip(2), self.source(d))
        rcopy(ref, ref, self.xs.at[d], self.xr.at[d], {"shard": self.flip(2)}).wait_recv()
        self.c_copy(1, d).start()

    def c_done(self, far, d):
        ref = self.rows(self.flip(3) if far else self.flip(1), self.source(d))
        rcopy(ref, ref, self.cs.at[far, d], self.cr.at[far, d], {"shard": self.flip(1)}).wait_recv()

    def all_here(self):
        for d in range(self.nz):
            self.c_done(0, d)
            self.c_done(1, d)

    def finish(self):
        for d in range(self.nz):
            if d:
                self.z_copy(d).wait_send()
            self.x_copy(d).wait_send()
            self.c_copy(0, d).wait_send()
            self.c_copy(1, d).wait_send()


def spread_sems(nz):
    return [dma(nz - 1), dma(nz - 1), dma(nz), dma(nz), dma(2, nz), dma(2, nz)]


def vmem():
    return pl.BlockSpec(memory_space=pltpu.VMEM)


def shape(dims, kind):
    return jax.ShapeDtypeStruct(dims, kind)


def dma(*dims):
    return pltpu.SemaphoreType.DMA(dims)


def front_kernel(
    dims,
    tok,
    w_up,
    w_out,
    w_down,
    cot_in,
    wq3,
    seg,
    above,
    bias_qv,
    slope_table,
    gain,
    shift,
    b_out,
    b_up,
    act_turned_o,
    query_o,
    key_o,
    value_o,
    out_heads_o,
    lse,
    info_all,
    wqkv_o,
    core_o,
    ga_o,
    down_o,
    mid_o,
    gmid_o,
    sums,
    act_turned,
    query,
    key,
    value,
    out_heads,
    wqkv,
    core_in,
    ga_all,
    down_part,
    mid,
    gmid,
    info,
    wfull,
    wq,
    att,
    tree,
    wcat,
    keys_aug,
    values_turned,
    labels,
    parents,
    cot,
    far,
    act,
    gbranch,
    g_send,
    g_recv,
    ga_send,
    bup_acc,
    info_send,
    info_recv,
    wz_send,
    wz_recv,
    ws_send,
    ws_recv,
    z_send,
    z_recv,
    y_send,
    y_recv,
    a_send,
    a_recv,
    local_sem,
    b_send,
    b_recv,
    t_send,
    t_recv,
    gs_sem,
    gr_sem,
    as_sem,
    ar_sem,
    cs_sem,
    cr_sem,
    store_sem,
    *spread,
):
    ns, nz, rows = dims
    s, z, y = lax.axis_index("shard"), lax.axis_index("ctx"), lax.axis_index("tp")
    slopes = slope_table.at[y * nz + z]
    half = rows // 2
    sub = half // SUBS
    depth = wq.shape[0]
    wide = 3 * PAIR
    my_rows = pl.ds(pl.multiple_of((s * nz + z) * depth, depth), depth)
    units, inner = w_up.shape[1], w_out.shape[1]
    own_cols = pl.multiple_of(2 * units + y * inner, 128)
    starts = [
        pltpu.make_async_copy(tok, tree.at[pl.ds(pl.multiple_of(z * rows, 128), rows), :], local_sem.at[0]),
        pltpu.make_async_copy(w_up, wfull.at[my_rows, 0:units], local_sem.at[1]),
        pltpu.make_async_copy(w_down, wfull.at[my_rows, units : 2 * units], local_sem.at[2]),
        pltpu.make_async_copy(w_out, wfull.at[my_rows, pl.ds(own_cols, inner)], local_sem.at[3]),
    ]
    given_load = pltpu.make_async_copy(cot_in, cot, local_sem.at[4])
    given_load.start()
    stores = [
        pltpu.make_async_copy(a, b, store_sem.at[k])
        for k, (a, b) in enumerate(
            (
                (act_turned, act_turned_o),
                (query, query_o),
                (key, key_o),
                (value, value_o),
                (out_heads, out_heads_o),
                (mid, mid_o),
                (gmid, gmid_o),
                (down_part, down_o),
                (core_in.at[:, :, 0 : 2 * units], core_o.at[:, :, 0 : 2 * units]),
                (core_in.at[:, :, 2 * units :], core_o.at[:, :, 2 * units :]),
                (wqkv, wqkv_o),
                (ga_all, ga_o),
            )
        )
    ]
    for one in starts:
        one.start()
    for to in range(nz):
        for part in range(3):
            wq[:, to * wide + part * PAIR : to * wide + (part + 1) * PAIR] = wq3[
                part, :, to * PAIR : (to + 1) * PAIR
            ]
    lane = lax.broadcasted_iota(jnp.int32, above.shape, 1)
    info[...] = jnp.zeros(info.shape, F32)
    for block in range(rows // BRANCH):
        label = seg[block : block + 1, 0:1]
        upper_label = jnp.sum(jnp.where(lane == label, above[...], 0), axis=1, keepdims=True)
        info[block : block + 1, :] = jnp.broadcast_to(label, (1, 128)).astype(F32)
        info[8 + block : 9 + block, :] = jnp.broadcast_to(upper_label, (1, 128)).astype(F32)
    greet(
        [{"ctx": lax.rem(z + d, nz)} for d in range(1, nz)]
        + [{"shard": lax.rem(s + d, ns)} for d in range(1, ns)]
        + [{"tp": 1 - y}]
    )
    ups = Spread(wfull, dims, depth, slice(0, units), spread[:6])
    downs = Spread(wfull, dims, depth, slice(units, 2 * units), spread[6:12])
    weights = Spread(wqkv, dims, depth, slice(None), spread[18:])
    outer = Spread(wfull, dims, depth, pl.ds(own_cols, inner), spread[12:18], False)

    def info_copy(d):
        return rcopy(
            info, info_all.at[z], info_send.at[d - 1], info_recv.at[d - 1], {"ctx": lax.rem(z + d, nz)}
        )

    def wz_copy(d):
        to = lax.rem(z + d, nz)
        return rcopy(
            wq.at[:, pl.ds(pl.multiple_of(to * wide, 128), wide)],
            wcat.at[my_rows, :],
            wz_send.at[d - 1],
            wz_recv.at[d - 1],
            {"ctx": to},
        )

    shard_rows = pl.ds(s * (nz * depth), nz * depth)

    def ws_copy(d):
        return rcopy(
            wcat.at[shard_rows, :],
            wcat.at[shard_rows, :],
            ws_send.at[d - 1],
            ws_recv.at[d - 1],
            {"shard": lax.rem(s + d, ns)},
        )

    wqkv[my_rows, :] = wq[...]
    for d in range(1, nz):
        wz_copy(d).start()
    for d in range(1, nz):
        info_copy(d).start()
    wcat[my_rows, :] = wq[:, pl.ds(pl.multiple_of(z * wide, 128), wide)]
    info_all[z] = info[...]
    for one in starts:
        one.wait()

    def piece(block, second, part):
        at = block * rows + jnp.where(second, 1 - y, y) * half + part * sub
        return tree.at[pl.ds(pl.multiple_of(at, 32), sub), :]

    def z_copy(direction, k, part):
        block = z - k if direction == 0 else z + k
        to = z + 1 if direction == 0 else z - 1
        ref = piece(block, False, part)
        return rcopy(ref, ref, z_send.at[direction, k, part], z_recv.at[direction, k, part], {"ctx": to})

    def z_arrival(direction, k, part):
        block = z - k if direction == 0 else z + k
        ref = piece(block, False, part)
        return rcopy(
            ref, ref, z_send.at[direction, k - 1, part], z_recv.at[direction, k - 1, part], {"ctx": z}
        )

    def y_copy(direction, k, part):
        block = z - k if direction == 0 else z + k
        ref = piece(block, False, part)
        return rcopy(
            ref, ref, y_send.at[direction, k - 1, part], y_recv.at[direction, k - 1, part], {"tp": 1 - y}
        )

    def y_arrival(direction, k, part):
        block = z - k if direction == 0 else z + k
        ref = piece(block, True, part)
        return rcopy(
            ref, ref, y_send.at[direction, k - 1, part], y_recv.at[direction, k - 1, part], {"tp": 1 - y}
        )

    def place(direction, k):
        block = z - k if direction == 0 else z + k
        nxt = z + 1 if direction == 0 else z - 1
        here = (block >= 0) & (block < nz)
        onward = here & (nxt >= 0) & (nxt < nz)
        return block, here, onward

    def forward(k, first):
        for part in range(SUBS):
            for direction in range(2):
                _, here, onward = place(direction, k)
                if not first:

                    @pl.when(here)
                    def _():
                        z_arrival(direction, k, part).wait_recv()

                @pl.when(onward & (k < nz - 1))
                def _():
                    z_copy(direction, k, part).start()

                if not first:

                    @pl.when(here)
                    def _():
                        y_copy(direction, k, part).start()

    forward(0, True)
    outer.own()
    ups.own()
    downs.own()
    for d in range(1, nz):
        wz_copy(d).wait_recv()
    for d in range(1, ns):
        ws_copy(d).start()

    bias_at = pl.ds(pl.multiple_of(z * PAIR, 128), PAIR)
    bias_q = bias_qv[0:1, bias_at]
    bias_v = bias_qv[1:2, bias_at]

    def project(k):
        def side(direction, inner_carry):
            block = z + (2 * direction - 1) * k

            @pl.when((block >= 0) & (block < nz) & ((k > 0) | (direction == 0)))
            def _():
                def tile(t, carry):
                    here = pl.ds(pl.multiple_of(block * rows + t * 128, 128), 128)
                    act = norm_rows(tree[here, :].astype(F32), gain[0:1, :], shift[0:1, :])[0].astype(BF)
                    act_turned[:, here] = act.T
                    both = nn(act, wcat[...])
                    query[here, :] = (
                        (both[:, :PAIR] + bias_q).astype(BF).astype(F32) * HD ** (-0.5)
                    ).astype(BF)
                    key[here, :] = both[:, PAIR : 2 * PAIR].astype(BF)
                    value[here, :] = (both[:, 2 * PAIR :] + bias_v).astype(BF)
                    return carry

                lax.fori_loop(0, rows // 128, tile, 0)

            return inner_carry

        lax.fori_loop(0, 2, side, 0)

    def shared(k):
        for part in range(SUBS):
            for direction in range(2):
                _, here, _ = place(direction, k)

                @pl.when(here)
                def _():
                    y_arrival(direction, k, part).wait_recv()

    forward(1, False)
    for d in range(1, ns):
        ws_copy(d).wait_recv()
    project(0)

    def wave(k, carry):
        forward(k, False)

        @pl.when(k == nz - 2)
        def _():
            outer.z_start()
            ups.z_start()
            downs.z_start()

        shared(k - 1)
        project(k - 1)
        return carry

    lax.fori_loop(2, nz, wave, 0)
    for d in (1, 3, 2):
        outer.z_done(d)
    shared(nz - 1)
    project(nz - 1)
    for k in range(4):
        stores[k].start()
    for d in (0, 1, 3, 2):
        outer.x_done(d)
    ups.z_done(2)
    ups.z_done(1)

    for d in range(1, nz):
        info_copy(d).wait_recv()

    fill_labels(info_all, rows // BRANCH, labels, parents)
    fill_trunk_keys(key, keys_aug)
    values_turned[...] = value[0:TRUNK, :].T

    def att_cols(half_at, owner):
        return pl.ds(pl.multiple_of(half_at * inner + owner * PAIR, 128), PAIR)

    def att_copy(to):
        return rcopy(
            out_heads.at[pl.ds(to * rows, rows), :],
            att.at[:, att_cols(y, z)],
            a_send.at[to],
            a_recv.at[z],
            {"ctx": to},
        )

    def pass_on(owner):
        return rcopy(
            att.at[:, att_cols(y, owner)],
            att.at[:, att_cols(y, owner)],
            b_send.at[owner],
            b_recv.at[owner],
            {"tp": 1 - y},
        )

    half_rows = pl.ds(pl.multiple_of(lax.rem(s, 2) * (ns * nz * depth // 2), 128), ns * nz * depth // 2)
    far_rows = pl.ds(pl.multiple_of((1 - lax.rem(s, 2)) * (ns * nz * depth // 2), 128), ns * nz * depth // 2)
    far_cols = pl.ds(pl.multiple_of(2 * units + (1 - y) * inner, 128), inner)

    def plane_copy():
        ref = wfull.at[half_rows, pl.ds(own_cols, inner)]
        return rcopy(ref, ref, t_send.at[0], t_recv.at[0], {"tp": 1 - y})

    def plane_arrival():
        ref = wfull.at[half_rows, far_cols]
        return rcopy(ref, ref, t_send.at[0], t_recv.at[0], {"tp": 1 - y})

    def core_copy():
        ref = wfull.at[half_rows, far_cols]
        return rcopy(ref, ref, t_send.at[1], t_recv.at[1], {"shard": outer.flip(1)})

    def core_arrival():
        ref = wfull.at[far_rows, far_cols]
        return rcopy(ref, ref, t_send.at[1], t_recv.at[1], {"shard": outer.flip(1)})

    outer.all_here()
    plane_copy().start()

    def send_out(to):
        @pl.when(z != to)
        def _():
            att_copy(to).start()

        @pl.when(z == to)
        def _():
            att[:, att_cols(y, z)] = out_heads[to * rows : (to + 1) * rows, :]
            pass_on(z).start()

    tile_mask = causal(BRANCH)

    def segment(slot, carry):
        here = pl.ds(pl.multiple_of(TRUNK + slot * BRANCH, 128), BRANCH)
        asked = jnp.concatenate(
            [stack_heads(query[here, :]), query_features(slopes, BRANCH)], axis=1
        )
        leaf, key_up, value_up = parent_pick(slot, labels, parents, key, value)
        own_feats, up_feats = segment_key_features(leaf)
        trunk_part = nt(keys_aug[...], asked) * LOG2E
        own_part = nt(jnp.concatenate([key[here, :], own_feats], axis=1), asked) * LOG2E
        own_part = jnp.where(tile_mask, own_part, NEG)
        up_part = nt(jnp.concatenate([key_up, up_feats], axis=1), asked) * LOG2E
        top = jnp.maximum(
            jnp.max(trunk_part, axis=0, keepdims=True),
            jnp.maximum(
                jnp.max(own_part, axis=0, keepdims=True), jnp.max(up_part, axis=0, keepdims=True)
            ),
        )
        trunk_part = jnp.exp2(trunk_part - top)
        own_part = jnp.exp2(own_part - top)
        up_part = jnp.exp2(up_part - top)
        total = (
            jnp.sum(trunk_part, axis=0, keepdims=True)
            + jnp.sum(own_part, axis=0, keepdims=True)
            + jnp.sum(up_part, axis=0, keepdims=True)
        )
        turned = nn(values_turned[...], trunk_part.astype(BF))
        turned = turned + nn(value[here, :].T, own_part.astype(BF))
        turned = turned + nn(value_up.T, up_part.astype(BF))
        turned = turned / total
        out_heads[here, :] = unstack_turned(turned, BRANCH).astype(BF)
        lse[pl.ds(4 + slot, 1), 0 : 2 * BRANCH] = top + jnp.log2(total)
        return carry

    wave_rows = TRUNK // 4
    wave_mask = causal(wave_rows)

    def trunk_tile(tile):
        lo, hi = tile * wave_rows, (tile + 1) * wave_rows
        asked = jnp.concatenate(
            [stack_heads(query[lo:hi, :]), query_features(slopes, wave_rows)], axis=1
        )
        edge = jnp.where(wave_mask, nt(keys_aug[lo:hi, :], asked) * LOG2E, NEG)
        top = jnp.max(edge, axis=0, keepdims=True)
        if tile:
            body = nt(keys_aug[0:lo, :], asked) * LOG2E
            top = jnp.maximum(top, jnp.max(body, axis=0, keepdims=True))
            body = jnp.exp2(body - top)
        edge = jnp.exp2(edge - top)
        total = jnp.sum(edge, axis=0, keepdims=True)
        turned = nn(values_turned[:, lo:hi], edge.astype(BF))
        if tile:
            total = total + jnp.sum(body, axis=0, keepdims=True)
            turned = turned + nn(values_turned[:, 0:lo], body.astype(BF))
        turned = turned / total
        out_heads[lo:hi, :] = unstack_turned(turned, wave_rows).astype(BF)
        lse[tile : tile + 1, :] = top + jnp.log2(total)

    def turn(n, carry):
        @pl.when(n == 5)
        def _():
            send_out(2)
            for tile in range(3):
                trunk_tile(tile)
            send_out(0)
            downs.z_done(2)

        @pl.when(n == 10)
        def _():
            send_out(3)
            trunk_tile(3)

        return segment(lax.rem(n + 2, SLOTS), carry)

    lax.fori_loop(0, SLOTS, turn, 0)
    send_out(1)
    downs.z_done(1)
    ups.z_done(3)
    stores[4].start()
    plane_arrival().wait_recv()
    core_copy().start()
    downs.z_done(3)
    for owner in range(nz):

        @pl.when(z != owner)
        def _():
            rcopy(
                out_heads.at[0:rows, :],
                att.at[:, att_cols(y, owner)],
                a_send.at[owner],
                a_recv.at[owner],
                {"ctx": owner},
            ).wait_recv()
            pass_on(owner).start()

    mid[...] = tree[pl.ds(pl.multiple_of(z * rows, 128), rows), :].astype(F32) + b_out[...]
    for d in (0, 2, 1, 3):
        ups.x_done(d)
    given_load.wait()
    for owner in range(nz):
        ref = att.at[:, att_cols(1 - y, owner)]
        rcopy(ref, ref, b_send.at[owner], b_recv.at[owner], {"tp": 1 - y}).wait_recv()
    core_arrival().wait_recv()
    ups.all_here()
    other = {"tp": 1 - y}
    chunk = rows // ROWS_WAVE
    width = act.shape[1]
    halves = units // width
    own_heads = pl.ds(pl.multiple_of(y * inner, 128), inner)
    own_wide = pl.ds(own_cols, inner)
    sums[...] = jnp.zeros(sums.shape, F32)
    bup_acc[...] = jnp.zeros(bup_acc.shape, F32)

    def at(i):
        return pl.ds(pl.multiple_of(i * chunk, 32), chunk)

    def g_copy(i):
        return rcopy(g_send.at[at(i), :], g_recv.at[at(i), :], gs_sem.at[i], gr_sem.at[i], other)

    def a_copy(i, d):
        to = lax.rem(z + d, nz)
        return rcopy(
            ga_send.at[at(i), pl.ds(pl.multiple_of(to * PAIR, 128), PAIR)],
            ga_all.at[pl.ds(pl.multiple_of(z * rows + i * chunk, 32), chunk), :],
            as_sem.at[d - 1, i],
            ar_sem.at[d - 1, i],
            {"ctx": to},
        )

    span = nz * depth
    parts = ((0, 2 * units), (2 * units, 2 * units + inner))

    def c_copy(part, index):
        lo, hi = parts[part]
        return rcopy(
            far.at[index, :, lo:hi],
            core_in.at[index, :, lo:hi],
            cs_sem.at[part, index],
            cr_sem.at[part, index],
            {"shard": weights.flip(1)},
        )

    sums[...] = jnp.zeros(sums.shape, F32)
    bup_acc[...] = jnp.zeros(bup_acc.shape, F32)
    per = width // BLOCK

    def spot(first, i, c, size):
        row = (first + lax.div(c, per)) * rows + i * size
        col = lax.rem(c, per) * BLOCK
        return pl.ds(pl.multiple_of(row, 32), size), pl.ds(pl.multiple_of(col, 128), BLOCK)

    large = 2 * chunk

    def large_at(i):
        return pl.ds(pl.multiple_of(i * large, 64), large)

    def stage_one(i, carry):
        here = large_at(i)
        middle = mid[here, :] + nt(att[here, :], wfull[:, 2 * units :])
        mid[here, :] = middle
        act[here, :] = norm_rows(middle, gain[1:2, :], shift[1:2, :])[0].astype(BF)

        def columns(c, inner_carry):
            cols = pl.ds(pl.multiple_of(c * BLOCK, 128), BLOCK)
            upper = nn(act[here, :], wfull[:, cols]) + b_up[:, cols]
            square = upper * upper
            turn = jnp.tanh(ROOT * (upper + CURVE * (square * upper)))
            tree[spot(0, i, c, large)] = (0.5 * upper * (1.0 + turn)).astype(BF)
            steep = 0.5 * (1.0 + turn) + (0.5 * ROOT) * upper * (1.0 - turn * turn) * (
                1.0 + (3.0 * CURVE) * square
            )
            tree[spot(halves, i, c, large)] = steep.astype(BF)
            return inner_carry

        lax.fori_loop(0, units // BLOCK, columns, 0)
        return carry

    def stage_two(i, carry):
        here = large_at(i)

        def columns(c, inner_carry):
            cols = pl.ds(pl.multiple_of(c * BLOCK, 128), BLOCK)
            down_cols = pl.ds(pl.multiple_of(units + c * BLOCK, 128), BLOCK)
            slope = nn(cot[here, :], wfull[:, down_cols])
            low = (slope * tree[spot(halves, i, c, large)].astype(F32)).astype(BF)
            tree[spot(halves, i, c, large)] = low
            bup_acc[:, cols] += jnp.sum(low.astype(F32), axis=0, keepdims=True)
            return inner_carry

        lax.fori_loop(0, units // BLOCK, columns, 0)
        total = jnp.zeros((large, width), F32)
        for part in range(halves):
            total = total + nt(
                tree[spot(halves + part, i, 0, large)[0], :], wfull[:, part * width : (part + 1) * width]
            )
        g_send[here, :] = total.astype(BF)
        g_copy(2 * i).start()
        g_copy(2 * i + 1).start()
        return carry

    def drain(k, carry):
        for part in range(SUBS):
            for direction in range(2):
                _, here, onward = place(direction, k)

                @pl.when(onward & (k < nz - 1))
                def _():
                    z_copy(direction, k, part).wait_send()

                @pl.when(here & (k > 0))
                def _():
                    y_copy(direction, k, part).wait_send()

        return carry

    lax.fori_loop(0, nz, drain, 0)
    lax.fori_loop(0, 1, stage_one, 0)
    weights.own()
    weights.z_start()
    for d in (0, 2, 1, 3):
        downs.x_done(d)
    lax.fori_loop(1, ROWS_WAVE // 2, stage_one, 0)
    stores[5].start()
    downs.all_here()
    lax.fori_loop(0, ROWS_WAVE // 2, stage_two, 0)
    for d in (2, 1, 3):
        weights.z_done(d)

    def group_cols(index, block):
        return pl.ds(pl.multiple_of(weights.flip(index) * span + block * 128, 128), 128)

    def products(cols):
        turned_act, turned_cot = act[:, cols].T, cot[:, cols].T
        for part in range(halves):
            lo = part * width
            yield lo, nn(turned_act, tree[(halves + part) * rows : (halves + part + 1) * rows, :])
            yield units + lo, nn(turned_cot, tree[part * rows : (part + 1) * rows, :])

    def each_block(act_on):
        for index in range(2):

            def one(block, carry):
                act_on(index, block)
                return carry

            lax.fori_loop(0, span // 128, one, 0)

    def far_one(index, block):
        target = pl.ds(pl.multiple_of(block * 128, 128), 128)
        for lo, value_block in products(group_cols((1, 3)[index], block)):
            far[index, target, lo : lo + width] = value_block.astype(BF)

    def near_one(index, block):
        target = pl.ds(pl.multiple_of(block * 128, 128), 128)
        for lo, value_block in products(group_cols((0, 2)[index], block)):
            here = slice(lo, lo + width)
            core_in[index, target, here] = (core_in[index, target, here].astype(F32) + value_block).astype(BF)

    def out_product(cols):
        return nn(gbranch[:, cols].T, att[:, own_heads])

    def far_two(index, block):
        target = pl.ds(pl.multiple_of(block * 128, 128), 128)
        far[index, target, 2 * units :] = out_product(group_cols((1, 3)[index], block)).astype(BF)

    def near_two(index, block):
        target = pl.ds(pl.multiple_of(block * 128, 128), 128)
        here = slice(2 * units, 2 * units + inner)
        core_in[index, target, here] = (
            core_in[index, target, here].astype(F32) + out_product(group_cols((0, 2)[index], block))
        ).astype(BF)

    def stage_c(i, carry):
        g_copy(i).wait_recv()
        here = at(i)
        grad = g_send[here, :].astype(F32) + g_recv[here, :].astype(F32)
        _, normed, inverse = norm_rows(mid[here, :], gain[1:2, :], shift[1:2, :])
        given = cot[here, :].astype(F32)
        grad_middle = given + norm_rows_back(grad, normed, inverse, gain[1:2, :])
        gmid[here, :] = grad_middle
        low = grad_middle.astype(BF)
        gbranch[here, :] = low
        sums[2:3, :] += jnp.sum(low.astype(F32), axis=0, keepdims=True)
        sums[3:4, :] += jnp.sum(given, axis=0, keepdims=True)
        sums[4:5, :] += jnp.sum(grad * normed, axis=0, keepdims=True)
        sums[5:6, :] += jnp.sum(grad, axis=0, keepdims=True)
        ga_send[here, :] = nn(low, wfull[:, own_wide]).astype(BF)
        for d in range(1, nz):
            a_copy(i, d).start()
        ga_all[pl.ds(pl.multiple_of(z * rows + i * chunk, 32), chunk), :] = ga_send[
            here, pl.ds(pl.multiple_of(z * PAIR, 128), PAIR)
        ]
        return carry

    lax.fori_loop(0, 1, stage_c, 0)
    each_block(far_one)
    for index in range(2):
        c_copy(0, index).start()
    lax.fori_loop(1, 2, stage_c, 0)
    for d in (0, 2, 1, 3):
        weights.x_done(d)
    def down(i, carry):
        total = jnp.zeros((large, width), F32)
        for part in range(halves):
            total = total + nt(
                tree[spot(part, i, 0, large)[0], :], wfull[:, units + part * width : units + (part + 1) * width]
            )
        down_part[large_at(i), :] = total.astype(BF)
        return carry

    lax.fori_loop(0, ROWS_WAVE // 2, down, 0)
    stores[7].start()
    lax.fori_loop(2, 3, stage_c, 0)
    for index in range(2):
        c_copy(0, index).wait_recv()
    each_block(near_one)
    stores[8].start()
    lax.fori_loop(3, ROWS_WAVE, stage_c, 0)
    stores[6].start()
    each_block(far_two)
    for index in range(2):
        c_copy(1, index).start()
    for index in range(2):
        c_copy(1, index).wait_recv()
    each_block(near_two)
    stores[9].start()
    for part in range(halves):
        sums[part : part + 1, :] = bup_acc[:, part * width : (part + 1) * width]
    weights.all_here()
    stores[10].start()
    weights.finish()
    for part in range(2):
        for index in range(2):
            c_copy(part, index).wait_send()

    def finish(i, carry):
        g_copy(i).wait_send()
        for d in range(1, nz):
            a_copy(i, d).wait_send()
            a_copy(i, d).wait_recv()
        return carry

    lax.fori_loop(0, ROWS_WAVE, finish, 0)
    stores[11].start()
    plane_copy().wait_send()
    core_copy().wait_send()
    for owner in range(nz):
        pass_on(owner).wait_send()

    for owner in range(nz):

        @pl.when(z != owner)
        def _():
            att_copy(owner).wait_send()

    ups.finish()
    downs.finish()
    outer.finish()
    for d in range(1, nz):
        info_copy(d).wait_send()
        wz_copy(d).wait_send()
    for d in range(1, ns):
        ws_copy(d).wait_send()
    for store in stores:
        store.wait()


def run_front(
    dims, tok, w_up, w_out, w_down, cot, wq3, seg, above, bias_qv, slopes, gain, shift, b_out, b_up
):
    ns, nz, rows = dims
    width, units, inner, depth = tok.shape[1], w_up.shape[1], w_out.shape[1], wq3.shape[1]
    span, total, wide = nz * depth, 2 * units + inner, 3 * PAIR
    anywhere = pl.BlockSpec(memory_space=pl.ANY)
    return pl.pallas_call(
        partial(front_kernel, dims),
        name="front",
        out_shape=(
            shape((width, TREE), BF),
            shape((TREE, PAIR), BF),
            shape((TREE, PAIR), BF),
            shape((TREE, PAIR), BF),
            shape((TREE, PAIR), BF),
            shape((16, 512), F32),
            shape((nz, 16, 128), F32),
            shape((width, nz * wide), BF),
            shape((2, span, total), BF),
            shape((TREE, PAIR), BF),
            shape((rows, width), BF),
            shape((rows, width), F32),
            shape((rows, width), F32),
            shape((8, width), F32),
        ),
        in_specs=[anywhere] * 5 + [vmem()] * 9,
        out_specs=[anywhere] * 5 + [vmem()] * 2 + [anywhere] * 6 + [vmem()],
        scratch_shapes=[
            pltpu.VMEM((width, TREE), BF),
            pltpu.VMEM((TREE, PAIR), BF),
            pltpu.VMEM((TREE, PAIR), BF),
            pltpu.VMEM((TREE, PAIR), BF),
            pltpu.VMEM((TREE, PAIR), BF),
            pltpu.VMEM((width, nz * wide), BF),
            pltpu.VMEM((2, span, total), BF),
            pltpu.VMEM((TREE, PAIR), BF),
            pltpu.VMEM((rows, width), BF),
            pltpu.VMEM((rows, width), F32),
            pltpu.VMEM((rows, width), F32),
            pltpu.VMEM((16, 128), F32),
            pltpu.VMEM((width, 2 * units + 2 * inner), BF),
            pltpu.VMEM((depth, nz * wide), BF),
            pltpu.VMEM((rows, 2 * inner), BF),
            pltpu.VMEM((TREE, width), BF),
            pltpu.VMEM((width, wide), BF),
            pltpu.VMEM((TRUNK, 2 * PAIR), BF),
            pltpu.VMEM((PAIR, TRUNK), BF),
            pltpu.VMEM((16, 128), F32),
            pltpu.VMEM((16, 128), F32),
            pltpu.VMEM((rows, width), BF),
            pltpu.VMEM((2, span, total), BF),
            pltpu.VMEM((rows, width), BF),
            pltpu.VMEM((rows, width), BF),
            pltpu.VMEM((rows, width), BF),
            pltpu.VMEM((rows, width), BF),
            pltpu.VMEM((rows, inner), BF),
            pltpu.VMEM((1, units), F32),
            dma(nz - 1),
            dma(nz - 1),
            dma(nz - 1),
            dma(nz - 1),
            dma(ns - 1),
            dma(ns - 1),
            dma(2, nz, SUBS),
            dma(2, nz, SUBS),
            dma(2, nz, SUBS),
            dma(2, nz, SUBS),
            dma(nz),
            dma(nz),
            dma(5),
            dma(nz),
            dma(nz),
            dma(2),
            dma(2),
            dma(ROWS_WAVE),
            dma(ROWS_WAVE),
            dma(nz - 1, ROWS_WAVE),
            dma(nz - 1, ROWS_WAVE),
            dma(2, 2),
            dma(2, 2),
            dma(12),
            *spread_sems(nz),
            *spread_sems(nz),
            *spread_sems(nz),
            *spread_sems(nz),
        ],
        compiler_params=pltpu.CompilerParams(
            collective_id=0, has_side_effects=True, vmem_limit_bytes=FRONT_LIMIT
        ),
        cost_estimate=pl.CostEstimate(flops=40_000_000_000, bytes_accessed=20_000_000, transcendentals=0),
    )(tok, w_up, w_out, w_down, cot, wq3, seg, above, bias_qv, slopes, gain, shift, b_out, b_up)


class Halve:
    def __init__(self, near, far, cols, dims, depth, bufs, sems):
        self.near, self.far, self.cols, self.depth = near, far, cols, depth
        self.nz = dims[1]
        self.s, self.z = lax.axis_index("shard"), lax.axis_index("ctx")
        self.x_in, self.a_in, self.b_out, self.b_in = bufs
        self.xs, self.xr, self.as_, self.ar, self.bs, self.br = sems

    def place(self, bits):
        low, high = lax.rem(self.z, 2), lax.div(self.z, 2)
        low = 1 - low if bits & 1 else low
        high = 1 - high if bits & 2 else high
        return 2 * high + low

    def block(self, bits):
        return pl.ds(pl.multiple_of(self.place(bits) * self.depth, self.depth), self.depth)

    def x_copy(self):
        low, high = lax.rem(self.s, 2), lax.div(self.s, 2)
        return rcopy(
            self.far.at[:, self.cols],
            self.x_in.at[:, self.cols],
            self.xs,
            self.xr,
            {"shard": 2 * (1 - high) + low},
        )

    def a_copy(self, index):
        return rcopy(
            self.near.at[self.block((1, 3)[index]), self.cols],
            self.a_in.at[index, :, self.cols],
            self.as_.at[index],
            self.ar.at[index],
            {"ctx": self.place(1)},
        )

    def b_copy(self):
        return rcopy(
            self.b_out.at[:, self.cols], self.b_in.at[:, self.cols], self.bs, self.br, {"ctx": self.place(2)}
        )

    def step_x(self):
        self.x_copy().wait_recv()

        def one(r, carry):
            here = pl.ds(pl.multiple_of(r * 32, 32), 32)
            self.near[here, self.cols] = (
                self.near[here, self.cols].astype(F32) + self.x_in[here, self.cols].astype(F32)
            ).astype(BF)
            return carry

        lax.fori_loop(0, self.near.shape[0] // 32, one, 0)
        self.a_copy(0).start()
        self.a_copy(1).start()

    def step_a(self):
        self.a_copy(0).wait_recv()
        self.a_copy(1).wait_recv()
        self.b_out[:, self.cols] = (
            self.near[self.block(2), self.cols].astype(F32) + self.a_in[1, :, self.cols].astype(F32)
        ).astype(BF)
        self.b_copy().start()

    def step_b(self):
        self.b_copy().wait_recv()
        return (
            self.near[self.block(0), self.cols].astype(F32)
            + self.a_in[0, :, self.cols].astype(F32)
            + self.b_in[:, self.cols].astype(F32)
        )

    def finish(self):
        self.x_copy().wait_send()
        self.a_copy(0).wait_send()
        self.a_copy(1).wait_send()
        self.b_copy().wait_send()


PIECES = 6


def back_kernel(
    dims,
    query,
    key,
    value,
    out_heads,
    lse,
    info_all,
    ga_all,
    act_turned_in,
    wqkv_in,
    partial_in,
    down_in,
    mid_in,
    b_down,
    gmid_in,
    tok_in,
    slope_table,
    gain,
    shift,
    early,
    result_o,
    gtok_o,
    gup,
    gdown,
    gout,
    gwqkv,
    early_sum,
    late_sum,
    result,
    gtok,
    act_turned,
    wqkv,
    down_part,
    mid,
    gmid,
    tok,
    near,
    x_in,
    a_in,
    b_out,
    b_in,
    q_near,
    q_far,
    q_core,
    qx_in,
    q_all,
    dqkv,
    dk_trunk,
    dv_trunk,
    dk_seg,
    dv_seg,
    dk_up,
    dv_up,
    keys_aug,
    keys_turned,
    labels,
    parents,
    dq_all,
    n_send,
    n_recv,
    down_recv,
    wg_send,
    early_mine,
    early_recv,
    late,
    late_recv,
    d_sem,
    e_send,
    e_recv,
    f_send,
    f_recv,
    l_send,
    l_recv,
    p_send,
    p_recv,
    r_send,
    r_recv,
    ns_sem,
    nr_sem,
    xs_sem,
    xr_sem,
    as_sem,
    ar_sem,
    bs_sem,
    br_sem,
    qc_send,
    qc_recv,
    qx_sem,
    qz_send,
    qz_recv,
    n_local,
    load_sem,
    out_sem,
):
    ns, nz, rows = dims
    s, z, y = lax.axis_index("shard"), lax.axis_index("ctx"), lax.axis_index("tp")
    count = ns * nz
    me = s * nz + z
    chunk = rows // ROWS_WAVE
    width = tok.shape[1]
    depth = width // count
    span = nz * depth
    wide = 3 * PAIR
    other = {"tp": 1 - y}
    slopes = slope_table.at[y * nz + z]
    total_cols = near.shape[1]
    step_cols = total_cols // PIECES
    units = gup.shape[1]

    far = partial_in.at[1]
    load = pltpu.make_async_copy(partial_in.at[0], near, n_local)
    loads = [
        pltpu.make_async_copy(a, c, load_sem.at[k])
        for k, (a, c) in enumerate(
            (
                (down_in, down_part),
                (act_turned_in, act_turned),
                (wqkv_in, wqkv),
                (mid_in, mid),
                (gmid_in, gmid),
                (tok_in, tok),
            )
        )
    ]
    loads[0].start()
    load.start()
    for one in loads[1:]:
        one.start()

    def peer(d):
        index = lax.rem(me + d, count)
        return index, {"shard": lax.div(index, nz), "ctx": lax.rem(index, nz)}

    greet([other] + [peer(d)[1] for d in range(1, count)])

    halves = [
        Halve(
            near,
            far,
            slice(i * step_cols, (i + 1) * step_cols),
            dims,
            depth,
            (x_in, a_in, b_out, b_in),
            (xs_sem.at[i], xr_sem.at[i], as_sem.at[i], ar_sem.at[i], bs_sem.at[i], br_sem.at[i]),
        )
        for i in range(PIECES)
    ]
    def shard_flip(bits):
        low, high = lax.rem(s, 2), lax.div(s, 2)
        low = 1 - low if bits & 1 else low
        high = 1 - high if bits & 2 else high
        return 2 * high + low

    def q_copy(index):
        return rcopy(
            wg_send.at[pl.ds(pl.multiple_of(shard_flip((1, 3)[index]) * span, 128), span), :],
            q_core.at[index],
            qc_send.at[index],
            qc_recv.at[index],
            {"shard": shard_flip(1)},
        )

    def qx_copy():
        return rcopy(q_far, qx_in, qx_sem.at[0], qx_sem.at[1], {"shard": shard_flip(2)})

    def qz_copy(d):
        to = lax.rem(z + d, nz)
        return rcopy(
            q_near.at[pl.ds(pl.multiple_of(to * depth, depth), depth), :],
            q_all.at[z],
            qz_send.at[d - 1],
            qz_recv.at[d - 1],
            {"ctx": to},
        )

    def q_spread():
        qx_copy().wait_recv()
        q_near[...] = (q_near[...].astype(F32) + qx_in[...].astype(F32)).astype(BF)
        for d in range(1, nz):
            qz_copy(d).start()
        q_all[z] = q_near[pl.ds(pl.multiple_of(z * depth, depth), depth), :]

    def down_copy():
        return rcopy(down_part, down_recv, d_sem.at[0], d_sem.at[1], other)

    owners = width // 128

    def owner_cols(index):
        return pl.ds(pl.multiple_of(index * 128, 128), 128)

    def early_copy(d):
        index, device = peer(d)
        return index, rcopy(
            early_mine.at[:, owner_cols(lax.rem(index, owners))],
            early_recv.at[me],
            e_send.at[d - 1],
            e_recv.at[d - 1],
            device,
        )

    def spread_copy(d):
        cols = owner_cols(lax.rem(me, owners))
        return rcopy(
            early_sum.at[:, cols], early_sum.at[:, cols], f_send.at[d - 1], f_recv.at[d - 1], peer(d)[1]
        )

    def spread_arrival(d):
        index = lax.rem(me + count - d, count)
        cols = owner_cols(lax.rem(index, owners))
        return index, rcopy(
            early_sum.at[:, cols], early_sum.at[:, cols], f_send.at[d - 1], f_recv.at[d - 1], other
        )

    def late_copy(d):
        return rcopy(late, late_recv.at[me], l_send.at[d - 1], l_recv.at[d - 1], peer(d)[1])

    def over_peers(act):
        def one(d, carry):
            act(d)
            return carry

        lax.fori_loop(1, count, one, 0)

    for half in halves:
        half.x_copy().start()
    loads[0].wait()
    down_copy().start()

    fill_labels(info_all, rows // BRANCH, labels, parents)
    fill_trunk_keys(key, keys_aug)
    keys_turned[...] = key[0:TRUNK, :].T
    dk_trunk[...] = jnp.zeros(dk_trunk.shape, F32)
    dv_trunk[...] = jnp.zeros(dv_trunk.shape, F32)
    tile_mask = causal(BRANCH)

    def row_products(here, count_rows):
        turned = (ga_all[here, :].astype(F32) * out_heads[here, :].astype(F32)).T
        return jnp.concatenate(
            [
                jnp.sum(turned[:HD, :], axis=0, keepdims=True),
                jnp.sum(turned[HD:, :], axis=0, keepdims=True),
            ],
            axis=1,
        )

    def part_back(key_aug, value_rows, asked, given, level, drow, mask):
        logits = nt(key_aug, asked) * LOG2E - level
        if mask is not None:
            logits = jnp.where(mask, logits, NEG)
        probs = jnp.exp2(logits)
        grads = (probs * (nt(value_rows, given) - drow)).astype(BF)
        return probs.astype(BF), grads

    def segment(slot, carry):
        here = pl.ds(pl.multiple_of(TRUNK + slot * BRANCH, 128), BRANCH)
        seg = pl.ds(pl.multiple_of(slot * BRANCH, 128), BRANCH)
        stacked = stack_heads(query[here, :])
        asked = jnp.concatenate([stacked, query_features(slopes, BRANCH)], axis=1)
        given = stack_heads(ga_all[here, :])
        leaf, key_up, value_up = parent_pick(slot, labels, parents, key, value)
        own_feats, up_feats = segment_key_features(leaf)
        level = lse[pl.ds(4 + slot, 1), 0 : 2 * BRANCH]
        drow = row_products(here, BRANCH)
        probs, grads = part_back(keys_aug[...], value[0:TRUNK, :], asked, given, level, drow, None)
        dv_trunk[...] += nn(probs, given)
        dk_trunk[...] += nn(grads, stacked)
        turned = nn(keys_turned[...], grads)
        key_own = key[here, :]
        probs, grads = part_back(
            jnp.concatenate([key_own, own_feats], axis=1), value[here, :], asked, given, level, drow, tile_mask
        )
        dv_seg[seg, :] = nn(probs, given)
        dk_seg[seg, :] = nn(grads, stacked)
        turned = turned + nn(key_own.T, grads)
        probs, grads = part_back(
            jnp.concatenate([key_up, up_feats], axis=1), value_up, asked, given, level, drow, None
        )
        dv_up[seg, :] = nn(probs, given)
        dk_up[seg, :] = nn(grads, stacked)
        turned = turned + nn(key_up.T, grads)
        dqkv[here, 0:PAIR] = (unstack_turned(turned, BRANCH) * HD ** (-0.5)).astype(BF)
        return carry

    def dq_copy(to):
        return rcopy(
            dqkv.at[to * rows : (to + 1) * rows, 0:PAIR],
            dq_all.at[:, pl.ds(pl.multiple_of(z * wide, 128), PAIR)],
            r_send.at[to],
            r_recv.at[z],
            {"ctx": to},
        )

    def send_dq(to):
        @pl.when(z != to)
        def _():
            dq_copy(to).start()

    def piece_copy(to, i):
        return rcopy(
            dqkv.at[to * rows + i * chunk : to * rows + (i + 1) * chunk, PAIR:],
            dq_all.at[i * chunk : (i + 1) * chunk, pl.ds(pl.multiple_of(z * wide + PAIR, 128), 2 * PAIR)],
            p_send.at[to, i],
            p_recv.at[z, i],
            {"ctx": to},
        )

    wave_rows = TRUNK // 4
    wave_mask = causal(wave_rows)
    for tile in range(4):
        lo, hi = tile * wave_rows, (tile + 1) * wave_rows
        stacked = stack_heads(query[lo:hi, :])
        asked = jnp.concatenate([stacked, query_features(slopes, wave_rows)], axis=1)
        given = stack_heads(ga_all[lo:hi, :])
        level = lse[tile : tile + 1, :]
        drow = row_products(pl.ds(lo, wave_rows), wave_rows)
        probs, grads = part_back(
            keys_aug[lo:hi, :], value[lo:hi, :], asked, given, level, drow, wave_mask
        )
        dv_trunk[lo:hi, :] += nn(probs, given)
        dk_trunk[lo:hi, :] += nn(grads, stacked)
        turned = nn(keys_turned[:, lo:hi], grads)
        if tile:
            probs, grads = part_back(
                keys_aug[0:lo, :], value[0:lo, :], asked, given, level, drow, None
            )
            dv_trunk[0:lo, :] += nn(probs, given)
            dk_trunk[0:lo, :] += nn(grads, stacked)
            turned = turned + nn(keys_turned[:, 0:lo], grads)
        dqkv[lo:hi, 0:PAIR] = (unstack_turned(turned, wave_rows) * HD ** (-0.5)).astype(BF)
    send_dq(0)

    def turn(n, carry):
        @pl.when(n == 5)
        def _():
            send_dq(2)

        @pl.when(n == 7)
        def _():
            send_dq(1)
            load.wait()
            halves[0].step_x()

        return segment(jnp.where(n < 5, n + 2, jnp.where(n < 7, n - 5, n)), carry)

    lax.fori_loop(0, SLOTS, turn, 0)
    halves[1].step_x()
    send_dq(3)

    def gather_up(slot, carry):
        here = pl.ds(pl.multiple_of(TRUNK + slot * BRANCH, 128), BRANCH)
        seg = pl.ds(pl.multiple_of(slot * BRANCH, 128), BRANCH)
        mine = labels[pl.ds(slot, 1), :]
        dk, dv = dk_seg[seg, :], dv_seg[seg, :]
        for below in range(SLOTS):
            same = (parents[below : below + 1, :] == mine).astype(F32)
            at = below * BRANCH
            dk = dk + same * dk_up[at : at + BRANCH, :]
            dv = dv + same * dv_up[at : at + BRANCH, :]
        dqkv[here, PAIR : 2 * PAIR] = dk.astype(BF)
        dqkv[here, 2 * PAIR :] = dv.astype(BF)
        return carry

    lax.fori_loop(0, SLOTS, gather_up, 0)
    dqkv[0:TRUNK, PAIR : 2 * PAIR] = dk_trunk[...].astype(BF)
    dqkv[0:TRUNK, 2 * PAIR :] = dv_trunk[...].astype(BF)
    for i in range(ROWS_WAVE):
        for to in range(nz):

            @pl.when(z != to)
            def _():
                piece_copy(to, i).start()

    for to in range(nz):

        @pl.when(z == to)
        def _():
            dq_all[:, pl.ds(pl.multiple_of(z * wide, 128), wide)] = dqkv[to * rows : (to + 1) * rows, :]

    def weight(block, carry):
        here = pl.ds(pl.multiple_of(block * 128, 128), 128)
        wg_send[here, :] = nn(act_turned[here, :], dqkv[...]).astype(BF)
        return carry

    loads[1].wait()
    lax.fori_loop(0, width // 128, weight, 0)
    q_copy(0).start()
    q_copy(1).start()

    early_mine[...] = early[...]
    early_mine[6:7, pl.ds(pl.multiple_of(z * PAIR, 128), PAIR)] = jnp.sum(
        dqkv[:, 0:PAIR].astype(F32), axis=0, keepdims=True
    )
    early_mine[6:7, pl.ds(pl.multiple_of((nz + z) * PAIR, 128), PAIR)] = jnp.sum(
        dqkv[:, 2 * PAIR :].astype(F32), axis=0, keepdims=True
    )

    def early_send(d):
        index, copy = early_copy(d)

        @pl.when(index < owners)
        def _():
            copy.start()

    over_peers(early_send)
    early_recv[me] = early_mine[:, owner_cols(lax.rem(me, owners))]

    def at(i):
        return pl.ds(pl.multiple_of(i * chunk, 32), chunk)

    def n_copy(i):
        return rcopy(n_send.at[at(i), :], n_recv.at[at(i), :], ns_sem.at[i], nr_sem.at[i], other)

    def core_join():
        for index in range(2):
            q_copy(index).wait_recv()
            mine = pl.ds(pl.multiple_of(shard_flip((0, 2)[index]) * span, 128), span)
            (q_near, q_far)[index][...] = (wg_send[mine, :].astype(F32) + q_core[index].astype(F32)).astype(BF)
        qx_copy().start()

    def first(i):
        for owner in range(nz):

            @pl.when(z != owner)
            def _():
                if i == 0:
                    rcopy(
                        dqkv.at[0:rows, 0:PAIR],
                        dq_all.at[:, owner * wide : owner * wide + PAIR],
                        r_send.at[owner],
                        r_recv.at[owner],
                        {"ctx": owner},
                    ).wait_recv()
                rcopy(
                    dqkv.at[0:chunk, PAIR:],
                    dq_all.at[i * chunk : (i + 1) * chunk, owner * wide + PAIR : (owner + 1) * wide],
                    p_send.at[owner, i],
                    p_recv.at[owner, i],
                    {"ctx": owner},
                ).wait_recv()

        n_send[at(i), :] = nt(dq_all[at(i), :], wqkv[...]).astype(BF)
        n_copy(i).start()

    def gtok_store(i):
        return pltpu.make_async_copy(gtok.at[at(i), :], gtok_o.at[at(i), :], out_sem.at[i])

    result_store = pltpu.make_async_copy(result, result_o, out_sem.at[ROWS_WAVE])

    def second(i, carry):
        n_copy(i).wait_recv()
        here = at(i)
        grad = n_send[here, :].astype(F32) + n_recv[here, :].astype(F32)
        _, normed, inverse = norm_rows(tok[here, :].astype(F32), gain[0:1, :], shift[0:1, :])
        gtok[here, :] = gmid[here, :] + norm_rows_back(grad, normed, inverse, gain[0:1, :])
        late[0:1, :] += jnp.sum(grad * normed, axis=0, keepdims=True)
        late[1:2, :] += jnp.sum(grad, axis=0, keepdims=True)
        gtok_store(i).start()
        return carry

    def output(i, carry):
        here = at(i)
        result[here, :] = (
            mid[here, :] + b_down[...] + (down_part[here, :].astype(F32) + down_recv[here, :].astype(F32))
        ).astype(BF)
        return carry

    late[...] = jnp.zeros(late.shape, F32)
    for one in loads[2:]:
        one.wait()
    core_join()
    halves[2].step_x()
    first(0)
    first(1)
    halves[3].step_x()
    first(2)
    halves[4].step_x()
    first(3)
    halves[5].step_x()
    down_copy().wait_recv()
    lax.fori_loop(0, ROWS_WAVE, output, 0)
    result_store.start()

    @pl.when(me < owners)
    def _():
        over_peers(lambda d: early_copy(d)[1].wait_recv())
        total = early_recv[0]
        for index in range(1, count):
            total = total + early_recv[index]
        early_sum[:, owner_cols(lax.rem(me, owners))] = total
        over_peers(lambda d: spread_copy(d).start())

    q_spread()
    halves[0].step_a()
    halves[1].step_a()
    lax.fori_loop(0, 2, second, 0)
    halves[2].step_a()
    lax.fori_loop(2, ROWS_WAVE, second, 0)
    over_peers(lambda d: late_copy(d).start())
    late_recv[me] = late[...]
    halves[3].step_a()
    halves[4].step_a()
    halves[5].step_a()

    for d in range(1, nz):
        qz_copy(d).wait_recv()
    for owner in range(nz):
        for part in range(3):
            gwqkv[part, :, owner * PAIR : (owner + 1) * PAIR] = q_all[
                owner, :, part * PAIR : (part + 1) * PAIR
            ].astype(F32)
    bounds = (0, units, 2 * units, total_cols)
    for i, half in enumerate(halves):
        block = half.step_b()
        lo, hi = i * step_cols, (i + 1) * step_cols
        for target, start_at, end_at in (
            (gup, bounds[0], bounds[1]),
            (gdown, bounds[1], bounds[2]),
            (gout, bounds[2], bounds[3]),
        ):
            a, b = max(lo, start_at), min(hi, end_at)
            if a < b:
                target[:, a - start_at : b - start_at] = block[:, a - lo : b - lo]

    def early_wait(d):
        index, copy = spread_arrival(d)

        @pl.when(index < owners)
        def _():
            copy.wait_recv()

    over_peers(early_wait)
    over_peers(lambda d: late_copy(d).wait_recv())
    total = late_recv[0]
    for index in range(1, count):
        total = total + late_recv[index]
    late_sum[...] = total
    result_store.wait()

    down_copy().wait_send()
    for half in halves:
        half.finish()
    qx_copy().wait_send()
    for d in range(1, nz):
        qz_copy(d).wait_send()
    q_copy(0).wait_send()
    q_copy(1).wait_send()

    def early_drain(d):
        index, copy = early_copy(d)

        @pl.when(index < owners)
        def _():
            copy.wait_send()

    over_peers(early_drain)

    @pl.when(me < owners)
    def _():
        over_peers(lambda d: spread_copy(d).wait_send())

    over_peers(lambda d: late_copy(d).wait_send())

    def finish(i, carry):
        n_copy(i).wait_send()
        gtok_store(i).wait()
        return carry

    lax.fori_loop(0, ROWS_WAVE, finish, 0)
    for owner in range(nz):

        @pl.when(z != owner)
        def _():
            dq_copy(owner).wait_send()
            for i in range(ROWS_WAVE):
                piece_copy(owner, i).wait_send()


def run_back(dims, units, *inputs):
    ns, nz, rows = dims
    width = inputs[14].shape[1]
    _, span, total = inputs[9].shape
    count = ns * nz
    depth = width // count
    wide = 3 * PAIR
    anywhere = pl.BlockSpec(memory_space=pl.ANY)
    return pl.pallas_call(
        partial(back_kernel, dims),
        name="tree_backward",
        out_shape=(
            shape((rows, width), BF),
            shape((rows, width), F32),
            shape((depth, units), F32),
            shape((depth, units), F32),
            shape((depth, total - 2 * units), F32),
            shape((3, depth, nz * PAIR), F32),
            shape((8, width), F32),
            shape((2, width), F32),
        ),
        in_specs=[vmem()] * 7 + [anywhere] * 5 + [vmem()] + [anywhere] * 2 + [vmem()] * 4,
        out_specs=[anywhere] * 2 + [vmem()] * 6,
        scratch_shapes=[
            pltpu.VMEM((rows, width), BF),
            pltpu.VMEM((rows, width), F32),
            *[pltpu.VMEM(inputs[k].shape, inputs[k].dtype) for k in (7, 8, 10, 11, 13, 14)],
            pltpu.VMEM((span, total), BF),
            pltpu.VMEM((span, total), BF),
            pltpu.VMEM((2, depth, total), BF),
            pltpu.VMEM((depth, total), BF),
            pltpu.VMEM((depth, total), BF),
            pltpu.VMEM((span, wide), BF),
            pltpu.VMEM((span, wide), BF),
            pltpu.VMEM((2, span, wide), BF),
            pltpu.VMEM((span, wide), BF),
            pltpu.VMEM((nz, depth, wide), BF),
            pltpu.VMEM((TREE, wide), BF),
            pltpu.VMEM((TRUNK, PAIR), F32),
            pltpu.VMEM((TRUNK, PAIR), F32),
            pltpu.VMEM((TREE - TRUNK, PAIR), F32),
            pltpu.VMEM((TREE - TRUNK, PAIR), F32),
            pltpu.VMEM((TREE - TRUNK, PAIR), F32),
            pltpu.VMEM((TREE - TRUNK, PAIR), F32),
            pltpu.VMEM((TRUNK, 2 * PAIR), BF),
            pltpu.VMEM((PAIR, TRUNK), BF),
            pltpu.VMEM((16, 128), F32),
            pltpu.VMEM((16, 128), F32),
            pltpu.VMEM((rows, nz * wide), BF),
            pltpu.VMEM((rows, width), BF),
            pltpu.VMEM((rows, width), BF),
            pltpu.VMEM((rows, width), BF),
            pltpu.VMEM((width, wide), BF),
            pltpu.VMEM((8, width), F32),
            pltpu.VMEM((count, 8, 128), F32),
            pltpu.VMEM((2, width), F32),
            pltpu.VMEM((count, 2, width), F32),
            dma(2),
            dma(count - 1),
            dma(count - 1),
            dma(count - 1),
            dma(count - 1),
            dma(count - 1),
            dma(count - 1),
            dma(nz, ROWS_WAVE),
            dma(nz, ROWS_WAVE),
            dma(nz),
            dma(nz),
            dma(ROWS_WAVE),
            dma(ROWS_WAVE),
            dma(PIECES),
            dma(PIECES),
            dma(PIECES, 2),
            dma(PIECES, 2),
            dma(PIECES),
            dma(PIECES),
            dma(2),
            dma(2),
            dma(2),
            dma(nz - 1),
            dma(nz - 1),
            pltpu.SemaphoreType.DMA,
            dma(6),
            dma(ROWS_WAVE + 1),
        ],
        compiler_params=pltpu.CompilerParams(
            collective_id=2, has_side_effects=True, vmem_limit_bytes=60 << 20
        ),
        cost_estimate=pl.CostEstimate(flops=40_000_000_000, bytes_accessed=20_000_000, transcendentals=0),
    )(*inputs)


def place_kernel(early, late, *refs):
    count = (len(refs) - 7) // 3
    sources, targets, middle = refs[:count], refs[count : 2 * count], refs[2 * count + 6 : -1]
    b_qv, b_out, b_up, b_down, gains, shifts = refs[2 * count : 2 * count + 6]
    sems = refs[-1]
    loads = [pltpu.make_async_copy(a, b, sems.at[0, k]) for k, (a, b) in enumerate(zip(sources, middle))]
    copies = [pltpu.make_async_copy(a, b, sems.at[1, k]) for k, (a, b) in enumerate(zip(middle, targets))]
    for load in loads:
        load.start()
    for load, copy in zip(loads, copies):
        load.wait()
        copy.start()
    wide, width = b_qv.shape[1], b_out.shape[1]
    for row in range(2):
        b_qv[row : row + 1, :] = early[6:7, row * wide : (row + 1) * wide]
    b_out[...] = early[2:3, :]
    for row in range(b_up.shape[1] // width):
        b_up[:, row * width : (row + 1) * width] = early[row : row + 1, :]
    b_down[...] = early[3:4, :]
    gains[0:1, :] = late[0:1, :]
    gains[1:2, :] = early[4:5, :]
    shifts[0:1, :] = late[1:2, :]
    shifts[1:2, :] = early[5:6, :]
    for copy in copies:
        copy.wait()


def run_place(early, late, wide, units, *arrays):
    width = early.shape[1]
    anywhere = pl.BlockSpec(memory_space=pl.ANY)
    return pl.pallas_call(
        place_kernel,
        name="place",
        out_shape=(
            *[shape(a.shape, a.dtype) for a in arrays],
            shape((2, wide), F32),
            shape((1, width), F32),
            shape((1, units), F32),
            shape((1, width), F32),
            shape((2, width), F32),
            shape((2, width), F32),
        ),
        in_specs=[vmem()] * 2 + [anywhere] * len(arrays),
        out_specs=[anywhere] * len(arrays) + [vmem()] * 6,
        scratch_shapes=[*[pltpu.VMEM(a.shape, a.dtype) for a in arrays], dma(2, len(arrays))],
        compiler_params=pltpu.CompilerParams(vmem_limit_bytes=60 << 20),
    )(early, late, *arrays)


def position_slopes(ntp, nz):
    index = np.arange(HEADS, dtype=np.float32).reshape(ntp * nz, 2)
    slope = np.exp2(-8.0 * (index + 1.0) / HEADS).astype(np.float32)
    table = np.zeros((ntp * nz, 2, 128), np.float32)
    left = slope
    for part in range(3):
        piece = left.astype(BF).astype(np.float32)
        table[:, :, part] = piece
        table[:, :, part + 3] = piece
        left = left - piece
    table[:, :, 6] = 1.0
    return table


def fast_device(
    tokens, cotangent, seg_ids, positions, parents, w_qkv, b_qv, w_out, b_out, w_up, b_up, w_down, b_down, ln_gain, ln_bias
):
    rows = tokens.shape[0]
    ns, nz, ntp = lax.axis_size("shard"), lax.axis_size("ctx"), lax.axis_size("tp")
    dims = (ns, nz, rows)

    slopes = jnp.asarray(position_slopes(ntp, nz))
    units = b_up.shape[0]
    (
        act_turned, query, key, value, out_heads, lse, info_all, wqkv, partial_sums, ga_all, down_part, mid, gmid, sums
    ) = run_front(
        dims, tokens, w_up, w_out.T, w_down.T, cotangent, w_qkv, seg_ids.reshape(rows // BRANCH, BRANCH),
        parents[None, :], b_qv, slopes, ln_gain, ln_bias,
        b_out[None, :], b_up[None, :],
    )
    result, grad_tokens, gup, gdown, gout, grad_w_qkv, early, late = run_back(
        dims, units, query, key, value, out_heads, lse, info_all, ga_all, act_turned, wqkv, partial_sums, down_part,
        mid, b_down[None, :], gmid, tokens, slopes, ln_gain, ln_bias, sums,
    )
    result, grad_tokens, grad_w_qkv, gup, gdown, gout, b_qv_sum, b_out_sum, b_up_sum, b_down_sum, gains, shifts = run_place(
        early, late, nz * PAIR, units, result, grad_tokens, grad_w_qkv, gup, gdown, gout
    )
    return (
        result,
        grad_tokens,
        grad_w_qkv,
        b_qv_sum,
        gout.T,
        b_out_sum.reshape(-1),
        gup,
        b_up_sum.reshape(-1),
        gdown.T,
        b_down_sum.reshape(-1),
        gains,
        shifts,
    )


def norm_forward(inputs_in, gain_row, shift_row):
    centre = inputs_in - jnp.mean(inputs_in, axis=-1, keepdims=True)
    inverse = lax.rsqrt(jnp.mean(centre * centre, axis=-1, keepdims=True) + EPS)
    normed = centre * inverse
    return (normed * gain_row + shift_row, normed, inverse)


def norm_backward(grad_in, normed, inverse, gain_row):
    scaled = grad_in * gain_row
    mean_grad = jnp.mean(scaled, axis=-1, keepdims=True)
    mean_cross = jnp.mean(scaled * normed, axis=-1, keepdims=True)
    return inverse * (scaled - mean_grad - normed * mean_cross)


def ancestry(seg_vals, parents):
    first_up = jnp.take(parents, seg_vals)
    return (first_up, jnp.take(parents, first_up))


def block_scores(query_heads, key_heads, query_tags, key_tags, slopes):
    q_seg, q_first, q_second, q_pos = query_tags
    k_seg, k_pos = key_tags
    raw_scores = jnp.einsum(
        "qhd,khd->hqk", query_heads, key_heads, preferred_element_type=jnp.float32
    ) * HD ** (-0.5)
    distance = (q_pos[:, None] - k_pos[None, :]).astype(jnp.float32)
    scores = raw_scores - slopes[:, None, None] * distance[None]
    related = (
        (k_seg[None, :] == q_seg[:, None])
        | (k_seg[None, :] == q_first[:, None])
        | (k_seg[None, :] == q_second[:, None])
    )
    allowed = related & (k_pos[None, :] <= q_pos[:, None])
    return (scores, allowed[None])


def probabilities(scores, allowed, row_max, row_sum):
    shifted = jnp.where(allowed, scores - row_max[:, :, None], NEG)
    return jnp.exp(shifted) / row_sum[:, :, None]


def per_device(
    tokens,
    cotangent,
    seg_ids,
    positions,
    parents,
    w_qkv,
    b_qv,
    w_out,
    b_out,
    w_up,
    b_up,
    w_down,
    b_down,
    ln_gain,
    ln_bias,
):
    num_rows = tokens.shape[0]
    head_count = HEADS // lax.axis_size("tp")
    head_width = head_count * HD
    head_index = (lax.axis_index("tp") * head_count + jnp.arange(head_count)).astype(jnp.float32)
    slopes = 2.0 ** (-8.0 * (head_index + 1.0) / HEADS)
    scale = HD ** (-0.5)
    full_qkv, full_out = (
        lax.all_gather(w_qkv, ("shard", "ctx"), axis=1, tiled=True),
        lax.all_gather(w_out, ("shard", "ctx"), axis=1, tiled=True),
    )
    group_seg, group_pos = (
        lax.all_gather(seg_ids, "ctx", axis=0, tiled=True),
        lax.all_gather(positions, "ctx", axis=0, tiled=True),
    )
    own_first, own_second = ancestry(seg_ids, parents)
    own_tags = (seg_ids, own_first, own_second, positions)
    inputs = tokens.astype(jnp.float32)
    norm_one, normed_one, inverse_one = norm_forward(inputs, ln_gain[0], ln_bias[0])
    act_one = norm_one.astype(jnp.bfloat16)
    projected = jnp.einsum("td,cde->cte", act_one, full_qkv, preferred_element_type=jnp.float32)
    qkv_bias = jnp.stack([b_qv[0], jnp.zeros((head_width,), jnp.float32), b_qv[1]])
    qkv_low = (projected + qkv_bias[:, None, :]).astype(jnp.bfloat16)
    query_flat, key_flat, value_flat = (qkv_low[0], qkv_low[1], qkv_low[2])
    group_keys, group_values = (
        lax.all_gather(key_flat, "ctx", axis=0, tiled=True),
        lax.all_gather(value_flat, "ctx", axis=0, tiled=True),
    )
    group_rows = group_keys.shape[0]
    block_count = group_rows // KEY_BLOCK
    key_blocks = group_keys.reshape(block_count, KEY_BLOCK, head_count, HD)
    value_blocks = group_values.reshape(block_count, KEY_BLOCK, head_count, HD)
    seg_blocks = group_seg.reshape(block_count, KEY_BLOCK)
    pos_blocks = group_pos.reshape(block_count, KEY_BLOCK)
    query_heads = query_flat.reshape(num_rows, head_count, HD)

    def stats_step(carry_in, block_parts):
        row_max, row_sum = carry_in
        key_part, seg_part, pos_part = block_parts
        scores, allowed = block_scores(
            query_heads, key_part, own_tags, (seg_part, pos_part), slopes
        )
        new_max = jnp.maximum(row_max, jnp.max(jnp.where(allowed, scores, NEG), axis=-1))
        shifted = jnp.where(allowed, scores - new_max[:, :, None], NEG)
        row_sum = row_sum * jnp.exp(row_max - new_max) + jnp.sum(jnp.exp(shifted), axis=-1)
        return ((new_max, row_sum), None)

    start_stats = (
        jnp.full((head_count, num_rows), NEG, jnp.float32),
        jnp.zeros((head_count, num_rows), jnp.float32),
    )
    (row_max, row_sum), _ = lax.scan(stats_step, start_stats, (key_blocks, seg_blocks, pos_blocks))

    def output_step(out_accum, block_parts):
        key_part, value_part, seg_part, pos_part = block_parts
        scores, allowed = block_scores(
            query_heads, key_part, own_tags, (seg_part, pos_part), slopes
        )
        prob_low = probabilities(scores, allowed, row_max, row_sum).astype(jnp.bfloat16)
        return (
            out_accum
            + jnp.einsum("hqk,khd->qhd", prob_low, value_part, preferred_element_type=jnp.float32),
            None,
        )

    attended, _ = lax.scan(
        output_step,
        jnp.zeros((num_rows, head_count, HD), jnp.float32),
        (key_blocks, value_blocks, seg_blocks, pos_blocks),
    )
    attended_low = attended.reshape(num_rows, head_width).astype(jnp.bfloat16)
    branch_one = (
        lax.psum(
            jnp.dot(attended_low, full_out, preferred_element_type=jnp.float32).astype(
                jnp.bfloat16
            ),
            "tp",
        ).astype(jnp.float32)
        + b_out
    )
    middle = inputs + branch_one
    full_up, full_down = (
        lax.all_gather(w_up, ("shard", "ctx"), axis=0, tiled=True),
        lax.all_gather(w_down, ("shard", "ctx"), axis=1, tiled=True),
    )
    norm_two, normed_two, inverse_two = norm_forward(middle, ln_gain[1], ln_bias[1])
    act_two = norm_two.astype(jnp.bfloat16)
    upper_in = jnp.dot(act_two, full_up, preferred_element_type=jnp.float32) + b_up
    gelu_vals, gelu_pull = jax.vjp(partial(jax.nn.gelu, approximate=True), upper_in)
    hidden = gelu_vals.astype(jnp.bfloat16)
    branch_two = (
        lax.psum(
            jnp.dot(hidden, full_down, preferred_element_type=jnp.float32).astype(jnp.bfloat16),
            "tp",
        ).astype(jnp.float32)
        + b_down
    )
    result = (middle + branch_two).astype(jnp.bfloat16)
    grad_out = cotangent.astype(jnp.float32)
    grad_hidden = jnp.einsum("td,fd->tf", cotangent, full_down, preferred_element_type=jnp.float32)
    grad_upper = gelu_pull(grad_hidden)[0].astype(jnp.bfloat16)
    down_term = jnp.einsum("tf,td->fd", hidden, cotangent, preferred_element_type=jnp.float32)
    up_term = jnp.einsum("td,tf->df", act_two, grad_upper, preferred_element_type=jnp.float32)
    grad_w_up, grad_w_down = (
        lax.psum_scatter(up_term, ("shard", "ctx"), scatter_dimension=0, tiled=True),
        lax.psum_scatter(down_term, ("shard", "ctx"), scatter_dimension=1, tiled=True),
    )
    grad_norm_two = lax.psum(
        jnp.einsum("tf,df->td", grad_upper, full_up, preferred_element_type=jnp.float32).astype(
            jnp.bfloat16
        ),
        "tp",
    ).astype(jnp.float32)
    grad_middle = grad_out + norm_backward(grad_norm_two, normed_two, inverse_two, ln_gain[1])
    grad_branch = grad_middle.astype(jnp.bfloat16)
    out_term = jnp.einsum(
        "te,td->ed", attended_low, grad_branch, preferred_element_type=jnp.float32
    )
    grad_att = jnp.einsum(
        "td,ed->te", grad_branch, full_out, preferred_element_type=jnp.float32
    ).astype(jnp.bfloat16)
    grad_heads = grad_att.reshape(num_rows, head_count, HD)
    row_terms = jnp.einsum("qhd,qhd->hq", grad_heads.astype(jnp.float32), attended)

    def joint_step(grad_accum, block_parts):
        key_part, value_part, seg_part, pos_part = block_parts
        scores, allowed = block_scores(
            query_heads, key_part, own_tags, (seg_part, pos_part), slopes
        )
        prob_vals = probabilities(scores, allowed, row_max, row_sum)
        grad_probs = jnp.einsum(
            "qhd,khd->hqk", grad_heads, value_part, preferred_element_type=jnp.float32
        )
        grad_scores = (prob_vals * (grad_probs - row_terms[:, :, None])).astype(jnp.bfloat16)
        grad_accum = (
            grad_accum
            + jnp.einsum("hqk,khd->qhd", grad_scores, key_part, preferred_element_type=jnp.float32)
            * scale
        )
        key_part_grad = (
            jnp.einsum("hqk,qhd->khd", grad_scores, query_heads, preferred_element_type=jnp.float32)
            * scale
        )
        value_part_grad = jnp.einsum(
            "hqk,qhd->khd",
            prob_vals.astype(jnp.bfloat16),
            grad_heads,
            preferred_element_type=jnp.float32,
        )
        return (
            grad_accum,
            (
                key_part_grad.reshape(KEY_BLOCK, head_width),
                value_part_grad.reshape(KEY_BLOCK, head_width),
            ),
        )

    grad_query_sum, (key_terms, value_terms) = lax.scan(
        joint_step,
        jnp.zeros((num_rows, head_count, HD), jnp.float32),
        (key_blocks, value_blocks, seg_blocks, pos_blocks),
    )
    key_grad_sum, value_grad_sum = (
        lax.psum_scatter(
            key_terms.reshape(group_rows, head_width).astype(jnp.bfloat16),
            "ctx",
            scatter_dimension=0,
            tiled=True,
        ).astype(jnp.float32),
        lax.psum_scatter(
            value_terms.reshape(group_rows, head_width).astype(jnp.bfloat16),
            "ctx",
            scatter_dimension=0,
            tiled=True,
        ).astype(jnp.float32),
    )
    grad_query_low = grad_query_sum.reshape(num_rows, head_width).astype(jnp.bfloat16)
    grad_key_low = key_grad_sum.astype(jnp.bfloat16)
    grad_value_low = value_grad_sum.astype(jnp.bfloat16)
    grad_qkv = jnp.stack([grad_query_low, grad_key_low, grad_value_low])
    grad_norm_one = lax.psum(
        jnp.einsum("cte,cde->td", grad_qkv, full_qkv, preferred_element_type=jnp.float32).astype(
            jnp.bfloat16
        ),
        "tp",
    ).astype(jnp.float32)
    grad_tokens = grad_middle + norm_backward(grad_norm_one, normed_one, inverse_one, ln_gain[0])
    qkv_term = jnp.einsum("td,cte->cde", act_one, grad_qkv, preferred_element_type=jnp.float32)
    grad_w_qkv, grad_w_out = (
        lax.psum_scatter(qkv_term, ("shard", "ctx"), scatter_dimension=1, tiled=True),
        lax.psum_scatter(out_term, ("shard", "ctx"), scatter_dimension=1, tiled=True),
    )
    bias_qv_part = jnp.stack(
        [
            jnp.sum(grad_query_low.astype(jnp.float32), axis=0),
            jnp.sum(grad_value_low.astype(jnp.float32), axis=0),
        ]
    )
    out_bias_part = jnp.sum(grad_branch.astype(jnp.float32), axis=0)
    up_bias_part = jnp.sum(grad_upper.astype(jnp.float32), axis=0)
    down_bias_part = jnp.sum(grad_out, axis=0)
    gain_part = jnp.stack(
        [jnp.sum(grad_norm_one * normed_one, axis=0), jnp.sum(grad_norm_two * normed_two, axis=0)]
    )
    shift_part = jnp.stack([jnp.sum(grad_norm_one, axis=0), jnp.sum(grad_norm_two, axis=0)])
    grad_b_qv, grad_b_out, grad_b_up, grad_b_down, grad_gain, grad_shift = lax.psum(
        (bias_qv_part, out_bias_part, up_bias_part, down_bias_part, gain_part, shift_part),
        ("shard", "ctx"),
    )
    return (
        result,
        grad_tokens,
        grad_w_qkv,
        grad_b_qv,
        grad_w_out,
        grad_b_out,
        grad_w_up,
        grad_b_up,
        grad_w_down,
        grad_b_down,
        grad_gain,
        grad_shift,
    )


def solution(mesh):
    placed = (
        P(("shard", "ctx"), None),
        P(("shard", "ctx"), None),
        P(("shard", "ctx")),
        P(("shard", "ctx")),
        P(),
        P(None, ("shard", "ctx"), "tp"),
        P(None, "tp"),
        P("tp", ("shard", "ctx")),
        P(),
        P(("shard", "ctx"), "tp"),
        P("tp"),
        P("tp", ("shard", "ctx")),
        P(),
        P(),
        P(),
    )
    sizes = dict(mesh.shape)
    paired = sizes["tp"] * sizes["ctx"] * 2 == HEADS and sizes["tp"] == 2 and sizes["shard"] == 4
    return jax.shard_map(
        fast_device if paired else per_device,
        mesh=mesh,
        in_specs=placed,
        out_specs=(
            P(("shard", "ctx"), None),
            P(("shard", "ctx"), None),
            P(None, ("shard", "ctx"), "tp"),
            P(None, "tp"),
            P("tp", ("shard", "ctx")),
            P(),
            P(("shard", "ctx"), "tp"),
            P("tp"),
            P("tp", ("shard", "ctx")),
            P(),
            P(),
            P(),
        ),
        check_vma=False,
    )
```

```python
from functools import partial

import jax
import jax.numpy as jnp
import numpy as np
from jax import lax
from jax.experimental import pallas as pl
from jax.experimental.pallas import tpu as pltpu
from jax.sharding import PartitionSpec as P

HEADS = 16
HD = 64
KEY_BLOCK = 512
TALL = 256
TRUNK = 1024
BRANCH = 128
SLOTS = 12
TREE = TRUNK + SLOTS * BRANCH
PAIR = 2 * HD

EPS = 1e-05
NEG = -1e30
LOG2E = 1.4426950408889634
MESH = pl.DeviceIdType.MESH
BF = jnp.bfloat16
F32 = jnp.float32
ROWS_WAVE = 4
FRONT_LIMIT = 62 << 20
BLOCK = 512
CURVE = 0.044715
ROOT = 0.7978845608028654
SUBS = 2


def nt(left, right):
    return lax.dot_general(left, right, (((1,), (1,)), ((), ())), preferred_element_type=F32)


def nn(left, right):
    return lax.dot_general(left, right, (((1,), (0,)), ((), ())), preferred_element_type=F32)


def rcopy(src, dst, send, recv, device):
    return pltpu.make_async_remote_copy(
        src_ref=src, dst_ref=dst, send_sem=send, recv_sem=recv, device_id=device, device_id_type=MESH
    )


def greet(devices):
    barrier = pltpu.get_barrier_semaphore()
    for device in devices:
        pl.semaphore_signal(barrier, inc=1, device_id=device, device_id_type=MESH)
    pl.semaphore_wait(barrier, len(devices))


def norm_rows(values, gain_row, shift_row):
    centre = values - jnp.mean(values, axis=-1, keepdims=True)
    inverse = lax.rsqrt(jnp.mean(centre * centre, axis=-1, keepdims=True) + EPS)
    normed = centre * inverse
    return normed * gain_row + shift_row, normed, inverse


def norm_rows_back(grad_in, normed, inverse, gain_row):
    scaled = grad_in * gain_row
    mean_grad = jnp.mean(scaled, axis=-1, keepdims=True)
    mean_cross = jnp.mean(scaled * normed, axis=-1, keepdims=True)
    return inverse * (scaled - mean_grad - normed * mean_cross)


def head_masks():
    lane = lax.broadcasted_iota(jnp.int32, (1, PAIR), 1)
    first = (lane < HD).astype(F32).astype(BF)
    second = (lane >= HD).astype(F32).astype(BF)
    return first, second


def stack_heads(rows):
    first, second = head_masks()
    return jnp.concatenate([rows * first, rows * second], axis=0)


def unstack_turned(turned, rows):
    return jnp.concatenate([turned[:HD, :rows], turned[HD:, rows:]], axis=0).T


def key_features(high, low, flag, rows):
    lane = lax.broadcasted_iota(jnp.int32, (rows, 128), 1)
    feats = jnp.where(lane < 3, high, jnp.where(lane < 6, low, jnp.where(lane == 6, flag, 0.0)))
    return feats.astype(BF)


def query_features(slope_ref, rows):
    return jnp.concatenate(
        [
            jnp.broadcast_to(slope_ref[0:1, :], (rows, 128)),
            jnp.broadcast_to(slope_ref[1:2, :], (rows, 128)),
        ],
        axis=0,
    ).astype(BF)


def fill_trunk_keys(key_ref, keys_aug):
    keys_aug[:, 0:PAIR] = key_ref[0:TRUNK, :]
    pos = lax.broadcasted_iota(jnp.int32, (TRUNK, 128), 0)
    low = pos & 255
    keys_aug[:, PAIR:] = key_features((pos - low).astype(F32), low.astype(F32), 0.0, TRUNK)


def fill_labels(info_all, blocks, labels, parents):
    labels[...] = jnp.full(labels.shape, -1.0, F32)
    parents[...] = jnp.full(parents.shape, -2.0, F32)
    for slot in range(SLOTS):
        block = TRUNK // BRANCH + slot
        owner, inner = block // blocks, block % blocks
        labels[slot : slot + 1, :] = info_all[owner, inner : inner + 1, :]
        parents[slot : slot + 1, :] = info_all[owner, 8 + inner : 9 + inner, :]


def parent_pick(slot, labels, parents, key_ref, value_ref):
    mine = parents[pl.ds(slot, 1), :]
    leaf = jnp.zeros((1, 128), F32)
    key_sum = jnp.zeros((BRANCH, PAIR), BF)
    value_sum = jnp.zeros((BRANCH, PAIR), BF)
    for other in range(SLOTS):
        same = (mine == labels[other : other + 1, :]).astype(F32)
        leaf = leaf + same
        same_low = same.astype(BF)
        at = TRUNK + other * BRANCH
        key_sum = key_sum + same_low * key_ref[at : at + BRANCH, :]
        value_sum = value_sum + same_low * value_ref[at : at + BRANCH, :]
    return leaf, key_sum, value_sum


def segment_key_features(leaf):
    row = lax.broadcasted_iota(jnp.int32, (BRANCH, 128), 0).astype(F32)
    own = key_features(float(TRUNK), row + leaf * float(BRANCH), 0.0, BRANCH)
    above = key_features(float(TRUNK), row, (leaf - 1.0) * 1e30, BRANCH)
    return own, above


def causal(rows):
    key = lax.broadcasted_iota(jnp.int32, (rows, rows), 0)
    query = lax.broadcasted_iota(jnp.int32, (rows, rows), 1)
    once = key <= query
    return jnp.concatenate([once, once], axis=1)


class Spread:
    def __init__(self, full, dims, depth, cols, sems, doubling=True):
        self.doubling = doubling
        self.full, self.depth, self.cols = full, depth, cols
        self.ns, self.nz, _ = dims
        self.s, self.z = lax.axis_index("shard"), lax.axis_index("ctx")
        self.zs, self.zr, self.xs, self.xr, self.cs, self.cr = sems

    def rows(self, shard, place):
        at = pl.multiple_of((shard * self.nz + place) * self.depth, self.depth)
        return self.full.at[pl.ds(at, self.depth), self.cols]

    def flip(self, bits):
        low = lax.rem(self.s, 2)
        high = lax.div(self.s, 2)
        if bits & 1:
            low = 1 - low
        if bits & 2:
            high = 1 - high
        return 2 * high + low

    def source(self, d):
        low, high = lax.rem(self.z, 2), lax.div(self.z, 2)
        low = 1 - low if d & 1 else low
        high = 1 - high if d & 2 else high
        return 2 * high + low

    def z_copy(self, d):
        ref = self.rows(self.s, self.source(2 if self.doubling and d == 3 else 0))
        to = self.source(1 if self.doubling and d == 3 else d)
        return rcopy(ref, ref, self.zs.at[d - 1], self.zr.at[d - 1], {"ctx": to})

    def x_copy(self, d):
        ref = self.rows(self.s, self.source(d))
        return rcopy(ref, ref, self.xs.at[d], self.xr.at[d], {"shard": self.flip(2)})

    def c_copy(self, far, d):
        ref = self.rows(self.flip(2) if far else self.s, self.source(d))
        return rcopy(ref, ref, self.cs.at[far, d], self.cr.at[far, d], {"shard": self.flip(1)})

    def z_start(self):
        self.z_copy(2).start()
        self.z_copy(1).start()
        if not self.doubling:
            self.z_copy(3).start()

    def own(self):
        self.x_copy(0).start()
        self.c_copy(0, 0).start()

    def z_done(self, d):
        ref = self.rows(self.s, self.source(d))
        rcopy(ref, ref, self.zs.at[d - 1], self.zr.at[d - 1], {"ctx": self.source(1)}).wait_recv()
        if self.doubling and d == 2:
            self.z_copy(3).start()
        self.x_copy(d).start()
        self.c_copy(0, d).start()

    def x_done(self, d):
        ref = self.rows(self.flip(2), self.source(d))
        rcopy(ref, ref, self.xs.at[d], self.xr.at[d], {"shard": self.flip(2)}).wait_recv()
        self.c_copy(1, d).start()

    def c_done(self, far, d):
        ref = self.rows(self.flip(3) if far else self.flip(1), self.source(d))
        rcopy(ref, ref, self.cs.at[far, d], self.cr.at[far, d], {"shard": self.flip(1)}).wait_recv()

    def all_here(self):
        for d in range(self.nz):
            self.c_done(0, d)
            self.c_done(1, d)

    def finish(self):
        for d in range(self.nz):
            if d:
                self.z_copy(d).wait_send()
            self.x_copy(d).wait_send()
            self.c_copy(0, d).wait_send()
            self.c_copy(1, d).wait_send()


def spread_sems(nz):
    return [dma(nz - 1), dma(nz - 1), dma(nz), dma(nz), dma(2, nz), dma(2, nz)]


def vmem():
    return pl.BlockSpec(memory_space=pltpu.VMEM)


def shape(dims, kind):
    return jax.ShapeDtypeStruct(dims, kind)


def dma(*dims):
    return pltpu.SemaphoreType.DMA(dims)


def front_kernel(
    dims,
    tok,
    w_up,
    w_out,
    w_down,
    cot_in,
    wq3,
    seg,
    above,
    bias_qv,
    slope_table,
    gain,
    shift,
    b_out,
    b_up,
    act_turned_o,
    query_o,
    key_o,
    value_o,
    out_heads_o,
    lse,
    info_all,
    wqkv_o,
    core_o,
    ga_o,
    down_o,
    mid_o,
    gmid_o,
    sums,
    act_turned,
    query,
    key,
    value,
    out_heads,
    wqkv,
    core_in,
    ga_all,
    down_part,
    mid,
    gmid,
    info,
    wfull,
    wq,
    att,
    tree,
    wcat,
    keys_aug,
    values_turned,
    labels,
    parents,
    cot,
    far,
    act,
    gbranch,
    g_send,
    g_recv,
    ga_send,
    bup_acc,
    info_send,
    info_recv,
    wz_send,
    wz_recv,
    ws_send,
    ws_recv,
    z_send,
    z_recv,
    y_send,
    y_recv,
    a_send,
    a_recv,
    local_sem,
    b_send,
    b_recv,
    t_send,
    t_recv,
    gs_sem,
    gr_sem,
    as_sem,
    ar_sem,
    cs_sem,
    cr_sem,
    store_sem,
    *spread,
):
    ns, nz, rows = dims
    s, z, y = lax.axis_index("shard"), lax.axis_index("ctx"), lax.axis_index("tp")
    slopes = slope_table.at[y * nz + z]
    half = rows // 2
    sub = half // SUBS
    depth = wq.shape[0]
    wide = 3 * PAIR
    my_rows = pl.ds(pl.multiple_of((s * nz + z) * depth, depth), depth)
    units, inner = w_up.shape[1], w_out.shape[1]
    own_cols = pl.multiple_of(2 * units + y * inner, 128)
    starts = [
        pltpu.make_async_copy(tok, tree.at[pl.ds(pl.multiple_of(z * rows, 128), rows), :], local_sem.at[0]),
        pltpu.make_async_copy(w_up, wfull.at[my_rows, 0:units], local_sem.at[1]),
        pltpu.make_async_copy(w_down, wfull.at[my_rows, units : 2 * units], local_sem.at[2]),
        pltpu.make_async_copy(w_out, wfull.at[my_rows, pl.ds(own_cols, inner)], local_sem.at[3]),
    ]
    given_load = pltpu.make_async_copy(cot_in, cot, local_sem.at[4])
    given_load.start()
    stores = [
        pltpu.make_async_copy(a, b, store_sem.at[k])
        for k, (a, b) in enumerate(
            (
                (act_turned, act_turned_o),
                (query, query_o),
                (key, key_o),
                (value, value_o),
                (out_heads, out_heads_o),
                (mid, mid_o),
                (gmid, gmid_o),
                (down_part, down_o),
                (core_in.at[:, :, 0 : 2 * units], core_o.at[:, :, 0 : 2 * units]),
                (core_in.at[:, :, 2 * units :], core_o.at[:, :, 2 * units :]),
                (wqkv, wqkv_o),
                (ga_all, ga_o),
            )
        )
    ]
    for one in starts:
        one.start()
    for to in range(nz):
        for part in range(3):
            wq[:, to * wide + part * PAIR : to * wide + (part + 1) * PAIR] = wq3[
                part, :, to * PAIR : (to + 1) * PAIR
            ]
    lane = lax.broadcasted_iota(jnp.int32, above.shape, 1)
    info[...] = jnp.zeros(info.shape, F32)
    for block in range(rows // BRANCH):
        label = seg[block : block + 1, 0:1]
        upper_label = jnp.sum(jnp.where(lane == label, above[...], 0), axis=1, keepdims=True)
        info[block : block + 1, :] = jnp.broadcast_to(label, (1, 128)).astype(F32)
        info[8 + block : 9 + block, :] = jnp.broadcast_to(upper_label, (1, 128)).astype(F32)
    greet(
        [{"ctx": lax.rem(z + d, nz)} for d in range(1, nz)]
        + [{"shard": lax.rem(s + d, ns)} for d in range(1, ns)]
        + [{"tp": 1 - y}]
    )
    ups = Spread(wfull, dims, depth, slice(0, units), spread[:6])
    downs = Spread(wfull, dims, depth, slice(units, 2 * units), spread[6:12])
    weights = Spread(wqkv, dims, depth, slice(None), spread[18:])
    outer = Spread(wfull, dims, depth, pl.ds(own_cols, inner), spread[12:18], False)

    def info_copy(d):
        return rcopy(
            info, info_all.at[z], info_send.at[d - 1], info_recv.at[d - 1], {"ctx": lax.rem(z + d, nz)}
        )

    def wz_copy(d):
        to = lax.rem(z + d, nz)
        return rcopy(
            wq.at[:, pl.ds(pl.multiple_of(to * wide, 128), wide)],
            wcat.at[my_rows, :],
            wz_send.at[d - 1],
            wz_recv.at[d - 1],
            {"ctx": to},
        )

    shard_rows = pl.ds(s * (nz * depth), nz * depth)

    def ws_copy(d):
        return rcopy(
            wcat.at[shard_rows, :],
            wcat.at[shard_rows, :],
            ws_send.at[d - 1],
            ws_recv.at[d - 1],
            {"shard": lax.rem(s + d, ns)},
        )

    wqkv[my_rows, :] = wq[...]
    for d in range(1, nz):
        wz_copy(d).start()
    for d in range(1, nz):
        info_copy(d).start()
    wcat[my_rows, :] = wq[:, pl.ds(pl.multiple_of(z * wide, 128), wide)]
    info_all[z] = info[...]
    for one in starts:
        one.wait()

    def piece(block, second, part):
        at = block * rows + jnp.where(second, 1 - y, y) * half + part * sub
        return tree.at[pl.ds(pl.multiple_of(at, 32), sub), :]

    def z_copy(direction, k, part):
        block = z - k if direction == 0 else z + k
        to = z + 1 if direction == 0 else z - 1
        ref = piece(block, False, part)
        return rcopy(ref, ref, z_send.at[direction, k, part], z_recv.at[direction, k, part], {"ctx": to})

    def z_arrival(direction, k, part):
        block = z - k if direction == 0 else z + k
        ref = piece(block, False, part)
        return rcopy(
            ref, ref, z_send.at[direction, k - 1, part], z_recv.at[direction, k - 1, part], {"ctx": z}
        )

    def y_copy(direction, k, part):
        block = z - k if direction == 0 else z + k
        ref = piece(block, False, part)
        return rcopy(
            ref, ref, y_send.at[direction, k - 1, part], y_recv.at[direction, k - 1, part], {"tp": 1 - y}
        )

    def y_arrival(direction, k, part):
        block = z - k if direction == 0 else z + k
        ref = piece(block, True, part)
        return rcopy(
            ref, ref, y_send.at[direction, k - 1, part], y_recv.at[direction, k - 1, part], {"tp": 1 - y}
        )

    def place(direction, k):
        block = z - k if direction == 0 else z + k
        nxt = z + 1 if direction == 0 else z - 1
        here = (block >= 0) & (block < nz)
        onward = here & (nxt >= 0) & (nxt < nz)
        return block, here, onward

    def forward(k, first):
        for part in range(SUBS):
            for direction in range(2):
                _, here, onward = place(direction, k)
                if not first:

                    @pl.when(here)
                    def _():
                        z_arrival(direction, k, part).wait_recv()

                @pl.when(onward & (k < nz - 1))
                def _():
                    z_copy(direction, k, part).start()

                if not first:

                    @pl.when(here)
                    def _():
                        y_copy(direction, k, part).start()

    forward(0, True)
    outer.own()
    ups.own()
    downs.own()
    for d in range(1, nz):
        wz_copy(d).wait_recv()
    for d in range(1, ns):
        ws_copy(d).start()

    bias_at = pl.ds(pl.multiple_of(z * PAIR, 128), PAIR)
    bias_q = bias_qv[0:1, bias_at]
    bias_v = bias_qv[1:2, bias_at]

    def project(k):
        def side(direction, inner_carry):
            block = z + (2 * direction - 1) * k

            @pl.when((block >= 0) & (block < nz) & ((k > 0) | (direction == 0)))
            def _():
                def tile(t, carry):
                    here = pl.ds(pl.multiple_of(block * rows + t * 128, 128), 128)
                    act = norm_rows(tree[here, :].astype(F32), gain[0:1, :], shift[0:1, :])[0].astype(BF)
                    act_turned[:, here] = act.T
                    both = nn(act, wcat[...])
                    query[here, :] = (
                        (both[:, :PAIR] + bias_q).astype(BF).astype(F32) * HD ** (-0.5)
                    ).astype(BF)
                    key[here, :] = both[:, PAIR : 2 * PAIR].astype(BF)
                    value[here, :] = (both[:, 2 * PAIR :] + bias_v).astype(BF)
                    return carry

                lax.fori_loop(0, rows // 128, tile, 0)

            return inner_carry

        lax.fori_loop(0, 2, side, 0)

    def shared(k):
        for part in range(SUBS):
            for direction in range(2):
                _, here, _ = place(direction, k)

                @pl.when(here)
                def _():
                    y_arrival(direction, k, part).wait_recv()

    forward(1, False)
    for d in range(1, ns):
        ws_copy(d).wait_recv()
    project(0)

    def wave(k, carry):
        forward(k, False)

        @pl.when(k == nz - 2)
        def _():
            outer.z_start()
            ups.z_start()
            downs.z_start()

        shared(k - 1)
        project(k - 1)
        return carry

    lax.fori_loop(2, nz, wave, 0)
    for d in (1, 3, 2):
        outer.z_done(d)
    shared(nz - 1)
    project(nz - 1)
    for k in range(4):
        stores[k].start()
    for d in (0, 1, 3, 2):
        outer.x_done(d)
    ups.z_done(2)
    ups.z_done(1)

    for d in range(1, nz):
        info_copy(d).wait_recv()

    fill_labels(info_all, rows // BRANCH, labels, parents)
    fill_trunk_keys(key, keys_aug)
    values_turned[...] = value[0:TRUNK, :].T

    def att_cols(half_at, owner):
        return pl.ds(pl.multiple_of(half_at * inner + owner * PAIR, 128), PAIR)

    def att_copy(to):
        return rcopy(
            out_heads.at[pl.ds(to * rows, rows), :],
            att.at[:, att_cols(y, z)],
            a_send.at[to],
            a_recv.at[z],
            {"ctx": to},
        )

    def pass_on(owner):
        return rcopy(
            att.at[:, att_cols(y, owner)],
            att.at[:, att_cols(y, owner)],
            b_send.at[owner],
            b_recv.at[owner],
            {"tp": 1 - y},
        )

    half_rows = pl.ds(pl.multiple_of(lax.rem(s, 2) * (ns * nz * depth // 2), 128), ns * nz * depth // 2)
    far_rows = pl.ds(pl.multiple_of((1 - lax.rem(s, 2)) * (ns * nz * depth // 2), 128), ns * nz * depth // 2)
    far_cols = pl.ds(pl.multiple_of(2 * units + (1 - y) * inner, 128), inner)

    def plane_copy():
        ref = wfull.at[half_rows, pl.ds(own_cols, inner)]
        return rcopy(ref, ref, t_send.at[0], t_recv.at[0], {"tp": 1 - y})

    def plane_arrival():
        ref = wfull.at[half_rows, far_cols]
        return rcopy(ref, ref, t_send.at[0], t_recv.at[0], {"tp": 1 - y})

    def core_copy():
        ref = wfull.at[half_rows, far_cols]
        return rcopy(ref, ref, t_send.at[1], t_recv.at[1], {"shard": outer.flip(1)})

    def core_arrival():
        ref = wfull.at[far_rows, far_cols]
        return rcopy(ref, ref, t_send.at[1], t_recv.at[1], {"shard": outer.flip(1)})

    outer.all_here()
    plane_copy().start()

    def send_out(to):
        @pl.when(z != to)
        def _():
            att_copy(to).start()

        @pl.when(z == to)
        def _():
            att[:, att_cols(y, z)] = out_heads[to * rows : (to + 1) * rows, :]
            pass_on(z).start()

    tile_mask = causal(BRANCH)

    def segment(slot, carry):
        here = pl.ds(pl.multiple_of(TRUNK + slot * BRANCH, 128), BRANCH)
        asked = jnp.concatenate(
            [stack_heads(query[here, :]), query_features(slopes, BRANCH)], axis=1
        )
        leaf, key_up, value_up = parent_pick(slot, labels, parents, key, value)
        own_feats, up_feats = segment_key_features(leaf)
        trunk_part = nt(keys_aug[...], asked) * LOG2E
        own_part = nt(jnp.concatenate([key[here, :], own_feats], axis=1), asked) * LOG2E
        own_part = jnp.where(tile_mask, own_part, NEG)
        up_part = nt(jnp.concatenate([key_up, up_feats], axis=1), asked) * LOG2E
        top = jnp.maximum(
            jnp.max(trunk_part, axis=0, keepdims=True),
            jnp.maximum(
                jnp.max(own_part, axis=0, keepdims=True), jnp.max(up_part, axis=0, keepdims=True)
            ),
        )
        trunk_part = jnp.exp2(trunk_part - top)
        own_part = jnp.exp2(own_part - top)
        up_part = jnp.exp2(up_part - top)
        total = (
            jnp.sum(trunk_part, axis=0, keepdims=True)
            + jnp.sum(own_part, axis=0, keepdims=True)
            + jnp.sum(up_part, axis=0, keepdims=True)
        )
        turned = nn(values_turned[...], trunk_part.astype(BF))
        turned = turned + nn(value[here, :].T, own_part.astype(BF))
        turned = turned + nn(value_up.T, up_part.astype(BF))
        turned = turned / total
        out_heads[here, :] = unstack_turned(turned, BRANCH).astype(BF)
        lse[pl.ds(4 + slot, 1), 0 : 2 * BRANCH] = top + jnp.log2(total)
        return carry

    wave_rows = TRUNK // 4
    wave_mask = causal(wave_rows)

    def trunk_tile(tile):
        lo, hi = tile * wave_rows, (tile + 1) * wave_rows
        asked = jnp.concatenate(
            [stack_heads(query[lo:hi, :]), query_features(slopes, wave_rows)], axis=1
        )
        edge = jnp.where(wave_mask, nt(keys_aug[lo:hi, :], asked) * LOG2E, NEG)
        top = jnp.max(edge, axis=0, keepdims=True)
        if tile:
            body = nt(keys_aug[0:lo, :], asked) * LOG2E
            top = jnp.maximum(top, jnp.max(body, axis=0, keepdims=True))
            body = jnp.exp2(body - top)
        edge = jnp.exp2(edge - top)
        total = jnp.sum(edge, axis=0, keepdims=True)
        turned = nn(values_turned[:, lo:hi], edge.astype(BF))
        if tile:
            total = total + jnp.sum(body, axis=0, keepdims=True)
            turned = turned + nn(values_turned[:, 0:lo], body.astype(BF))
        turned = turned / total
        out_heads[lo:hi, :] = unstack_turned(turned, wave_rows).astype(BF)
        lse[tile : tile + 1, :] = top + jnp.log2(total)

    def turn(n, carry):
        @pl.when(n == 5)
        def _():
            send_out(2)
            for tile in range(3):
                trunk_tile(tile)
            send_out(0)
            downs.z_done(2)

        @pl.when(n == 10)
        def _():
            send_out(3)
            trunk_tile(3)

        return segment(lax.rem(n + 2, SLOTS), carry)

    lax.fori_loop(0, SLOTS, turn, 0)
    send_out(1)
    downs.z_done(1)
    ups.z_done(3)
    stores[4].start()
    plane_arrival().wait_recv()
    core_copy().start()
    downs.z_done(3)
    for owner in range(nz):

        @pl.when(z != owner)
        def _():
            rcopy(
                out_heads.at[0:rows, :],
                att.at[:, att_cols(y, owner)],
                a_send.at[owner],
                a_recv.at[owner],
                {"ctx": owner},
            ).wait_recv()
            pass_on(owner).start()

    mid[...] = tree[pl.ds(pl.multiple_of(z * rows, 128), rows), :].astype(F32) + b_out[...]
    for d in (0, 2, 1, 3):
        ups.x_done(d)
    given_load.wait()
    for owner in range(nz):
        ref = att.at[:, att_cols(1 - y, owner)]
        rcopy(ref, ref, b_send.at[owner], b_recv.at[owner], {"tp": 1 - y}).wait_recv()
    core_arrival().wait_recv()
    ups.all_here()
    other = {"tp": 1 - y}
    chunk = rows // ROWS_WAVE
    width = act.shape[1]
    halves = units // width
    own_heads = pl.ds(pl.multiple_of(y * inner, 128), inner)
    own_wide = pl.ds(own_cols, inner)
    sums[...] = jnp.zeros(sums.shape, F32)
    bup_acc[...] = jnp.zeros(bup_acc.shape, F32)

    def at(i):
        return pl.ds(pl.multiple_of(i * chunk, 32), chunk)

    def g_copy(i):
        return rcopy(g_send.at[at(i), :], g_recv.at[at(i), :], gs_sem.at[i], gr_sem.at[i], other)

    def a_copy(i, d):
        to = lax.rem(z + d, nz)
        return rcopy(
            ga_send.at[at(i), pl.ds(pl.multiple_of(to * PAIR, 128), PAIR)],
            ga_all.at[pl.ds(pl.multiple_of(z * rows + i * chunk, 32), chunk), :],
            as_sem.at[d - 1, i],
            ar_sem.at[d - 1, i],
            {"ctx": to},
        )

    span = nz * depth
    parts = ((0, 2 * units), (2 * units, 2 * units + inner))

    def c_copy(part, index):
        lo, hi = parts[part]
        return rcopy(
            far.at[index, :, lo:hi],
            core_in.at[index, :, lo:hi],
            cs_sem.at[part, index],
            cr_sem.at[part, index],
            {"shard": weights.flip(1)},
        )

    sums[...] = jnp.zeros(sums.shape, F32)
    bup_acc[...] = jnp.zeros(bup_acc.shape, F32)
    per = width // BLOCK

    def spot(first, i, c, size):
        row = (first + lax.div(c, per)) * rows + i * size
        col = lax.rem(c, per) * BLOCK
        return pl.ds(pl.multiple_of(row, 32), size), pl.ds(pl.multiple_of(col, 128), BLOCK)

    large = 2 * chunk

    def large_at(i):
        return pl.ds(pl.multiple_of(i * large, 64), large)

    def stage_one(i, carry):
        here = large_at(i)
        middle = mid[here, :] + nt(att[here, :], wfull[:, 2 * units :])
        mid[here, :] = middle
        act[here, :] = norm_rows(middle, gain[1:2, :], shift[1:2, :])[0].astype(BF)

        def columns(c, inner_carry):
            cols = pl.ds(pl.multiple_of(c * BLOCK, 128), BLOCK)
            upper = nn(act[here, :], wfull[:, cols]) + b_up[:, cols]
            square = upper * upper
            turn = jnp.tanh(ROOT * (upper + CURVE * (square * upper)))
            tree[spot(0, i, c, large)] = (0.5 * upper * (1.0 + turn)).astype(BF)
            steep = 0.5 * (1.0 + turn) + (0.5 * ROOT) * upper * (1.0 - turn * turn) * (
                1.0 + (3.0 * CURVE) * square
            )
            tree[spot(halves, i, c, large)] = steep.astype(BF)
            return inner_carry

        lax.fori_loop(0, units // BLOCK, columns, 0)
        return carry

    def stage_two(i, carry):
        here = large_at(i)

        def columns(c, inner_carry):
            cols = pl.ds(pl.multiple_of(c * BLOCK, 128), BLOCK)
            down_cols = pl.ds(pl.multiple_of(units + c * BLOCK, 128), BLOCK)
            slope = nn(cot[here, :], wfull[:, down_cols])
            low = (slope * tree[spot(halves, i, c, large)].astype(F32)).astype(BF)
            tree[spot(halves, i, c, large)] = low
            bup_acc[:, cols] += jnp.sum(low.astype(F32), axis=0, keepdims=True)
            return inner_carry

        lax.fori_loop(0, units // BLOCK, columns, 0)
        total = jnp.zeros((large, width), F32)
        for part in range(halves):
            total = total + nt(
                tree[spot(halves + part, i, 0, large)[0], :], wfull[:, part * width : (part + 1) * width]
            )
        g_send[here, :] = total.astype(BF)
        g_copy(2 * i).start()
        g_copy(2 * i + 1).start()
        return carry

    def drain(k, carry):
        for part in range(SUBS):
            for direction in range(2):
                _, here, onward = place(direction, k)

                @pl.when(onward & (k < nz - 1))
                def _():
                    z_copy(direction, k, part).wait_send()

                @pl.when(here & (k > 0))
                def _():
                    y_copy(direction, k, part).wait_send()

        return carry

    lax.fori_loop(0, nz, drain, 0)
    lax.fori_loop(0, 1, stage_one, 0)
    weights.own()
    weights.z_start()
    for d in (0, 2, 1, 3):
        downs.x_done(d)
    lax.fori_loop(1, ROWS_WAVE // 2, stage_one, 0)
    stores[5].start()
    downs.all_here()
    lax.fori_loop(0, ROWS_WAVE // 2, stage_two, 0)
    for d in (2, 1, 3):
        weights.z_done(d)

    def group_cols(index, block):
        return pl.ds(pl.multiple_of(weights.flip(index) * span + block * TALL, 128), TALL)

    def products(cols):
        turned_act, turned_cot = act[:, cols].T, cot[:, cols].T
        for part in range(halves):
            lo = part * width
            yield lo, nn(turned_act, tree[(halves + part) * rows : (halves + part + 1) * rows, :])
            yield units + lo, nn(turned_cot, tree[part * rows : (part + 1) * rows, :])

    def each_block(act_on):
        for index in range(2):

            def one(block, carry):
                act_on(index, block)
                return carry

            lax.fori_loop(0, span // TALL, one, 0)

    def far_one(index, block):
        target = pl.ds(pl.multiple_of(block * TALL, 128), TALL)
        for lo, value_block in products(group_cols((1, 3)[index], block)):
            far[index, target, lo : lo + width] = value_block.astype(BF)

    def near_one(index, block):
        target = pl.ds(pl.multiple_of(block * TALL, 128), TALL)
        for lo, value_block in products(group_cols((0, 2)[index], block)):
            here = slice(lo, lo + width)
            core_in[index, target, here] = (core_in[index, target, here].astype(F32) + value_block).astype(BF)

    def out_product(cols):
        return nn(gbranch[:, cols].T, att[:, own_heads])

    def far_two(index, block):
        target = pl.ds(pl.multiple_of(block * TALL, 128), TALL)
        far[index, target, 2 * units :] = out_product(group_cols((1, 3)[index], block)).astype(BF)

    def near_two(index, block):
        target = pl.ds(pl.multiple_of(block * TALL, 128), TALL)
        here = slice(2 * units, 2 * units + inner)
        core_in[index, target, here] = (
            core_in[index, target, here].astype(F32) + out_product(group_cols((0, 2)[index], block))
        ).astype(BF)

    def stage_c(i, carry):
        g_copy(i).wait_recv()
        here = at(i)
        grad = g_send[here, :].astype(F32) + g_recv[here, :].astype(F32)
        _, normed, inverse = norm_rows(mid[here, :], gain[1:2, :], shift[1:2, :])
        given = cot[here, :].astype(F32)
        grad_middle = given + norm_rows_back(grad, normed, inverse, gain[1:2, :])
        gmid[here, :] = grad_middle
        low = grad_middle.astype(BF)
        gbranch[here, :] = low
        sums[2:3, :] += jnp.sum(low.astype(F32), axis=0, keepdims=True)
        sums[3:4, :] += jnp.sum(given, axis=0, keepdims=True)
        sums[4:5, :] += jnp.sum(grad * normed, axis=0, keepdims=True)
        sums[5:6, :] += jnp.sum(grad, axis=0, keepdims=True)
        ga_send[here, :] = nn(low, wfull[:, own_wide]).astype(BF)
        for d in range(1, nz):
            a_copy(i, d).start()
        ga_all[pl.ds(pl.multiple_of(z * rows + i * chunk, 32), chunk), :] = ga_send[
            here, pl.ds(pl.multiple_of(z * PAIR, 128), PAIR)
        ]
        return carry

    lax.fori_loop(0, 1, stage_c, 0)
    each_block(far_one)
    for index in range(2):
        c_copy(0, index).start()
    lax.fori_loop(1, 2, stage_c, 0)
    for d in (0, 2, 1, 3):
        weights.x_done(d)
    def down(i, carry):
        total = jnp.zeros((large, width), F32)
        for part in range(halves):
            total = total + nt(
                tree[spot(part, i, 0, large)[0], :], wfull[:, units + part * width : units + (part + 1) * width]
            )
        down_part[large_at(i), :] = total.astype(BF)
        return carry

    lax.fori_loop(0, ROWS_WAVE // 2, down, 0)
    stores[7].start()
    lax.fori_loop(2, 3, stage_c, 0)
    for index in range(2):
        c_copy(0, index).wait_recv()
    each_block(near_one)
    stores[8].start()
    lax.fori_loop(3, ROWS_WAVE, stage_c, 0)
    stores[6].start()
    each_block(far_two)
    for index in range(2):
        c_copy(1, index).start()
    for index in range(2):
        c_copy(1, index).wait_recv()
    each_block(near_two)
    stores[9].start()
    for part in range(halves):
        sums[part : part + 1, :] = bup_acc[:, part * width : (part + 1) * width]
    weights.all_here()
    stores[10].start()
    weights.finish()
    for part in range(2):
        for index in range(2):
            c_copy(part, index).wait_send()

    def finish(i, carry):
        g_copy(i).wait_send()
        for d in range(1, nz):
            a_copy(i, d).wait_send()
            a_copy(i, d).wait_recv()
        return carry

    lax.fori_loop(0, ROWS_WAVE, finish, 0)
    stores[11].start()
    plane_copy().wait_send()
    core_copy().wait_send()
    for owner in range(nz):
        pass_on(owner).wait_send()

    for owner in range(nz):

        @pl.when(z != owner)
        def _():
            att_copy(owner).wait_send()

    ups.finish()
    downs.finish()
    outer.finish()
    for d in range(1, nz):
        info_copy(d).wait_send()
        wz_copy(d).wait_send()
    for d in range(1, ns):
        ws_copy(d).wait_send()
    for store in stores:
        store.wait()


def run_front(
    dims, tok, w_up, w_out, w_down, cot, wq3, seg, above, bias_qv, slopes, gain, shift, b_out, b_up
):
    ns, nz, rows = dims
    width, units, inner, depth = tok.shape[1], w_up.shape[1], w_out.shape[1], wq3.shape[1]
    span, total, wide = nz * depth, 2 * units + inner, 3 * PAIR
    anywhere = pl.BlockSpec(memory_space=pl.ANY)
    return pl.pallas_call(
        partial(front_kernel, dims),
        name="front",
        out_shape=(
            shape((width, TREE), BF),
            shape((TREE, PAIR), BF),
            shape((TREE, PAIR), BF),
            shape((TREE, PAIR), BF),
            shape((TREE, PAIR), BF),
            shape((16, 512), F32),
            shape((nz, 16, 128), F32),
            shape((width, nz * wide), BF),
            shape((2, span, total), BF),
            shape((TREE, PAIR), BF),
            shape((rows, width), BF),
            shape((rows, width), F32),
            shape((rows, width), F32),
            shape((8, width), F32),
        ),
        in_specs=[anywhere] * 5 + [vmem()] * 9,
        out_specs=[anywhere] * 5 + [vmem()] * 2 + [anywhere] * 6 + [vmem()],
        scratch_shapes=[
            pltpu.VMEM((width, TREE), BF),
            pltpu.VMEM((TREE, PAIR), BF),
            pltpu.VMEM((TREE, PAIR), BF),
            pltpu.VMEM((TREE, PAIR), BF),
            pltpu.VMEM((TREE, PAIR), BF),
            pltpu.VMEM((width, nz * wide), BF),
            pltpu.VMEM((2, span, total), BF),
            pltpu.VMEM((TREE, PAIR), BF),
            pltpu.VMEM((rows, width), BF),
            pltpu.VMEM((rows, width), F32),
            pltpu.VMEM((rows, width), F32),
            pltpu.VMEM((16, 128), F32),
            pltpu.VMEM((width, 2 * units + 2 * inner), BF),
            pltpu.VMEM((depth, nz * wide), BF),
            pltpu.VMEM((rows, 2 * inner), BF),
            pltpu.VMEM((TREE, width), BF),
            pltpu.VMEM((width, wide), BF),
            pltpu.VMEM((TRUNK, 2 * PAIR), BF),
            pltpu.VMEM((PAIR, TRUNK), BF),
            pltpu.VMEM((16, 128), F32),
            pltpu.VMEM((16, 128), F32),
            pltpu.VMEM((rows, width), BF),
            pltpu.VMEM((2, span, total), BF),
            pltpu.VMEM((rows, width), BF),
            pltpu.VMEM((rows, width), BF),
            pltpu.VMEM((rows, width), BF),
            pltpu.VMEM((rows, width), BF),
            pltpu.VMEM((rows, inner), BF),
            pltpu.VMEM((1, units), F32),
            dma(nz - 1),
            dma(nz - 1),
            dma(nz - 1),
            dma(nz - 1),
            dma(ns - 1),
            dma(ns - 1),
            dma(2, nz, SUBS),
            dma(2, nz, SUBS),
            dma(2, nz, SUBS),
            dma(2, nz, SUBS),
            dma(nz),
            dma(nz),
            dma(5),
            dma(nz),
            dma(nz),
            dma(2),
            dma(2),
            dma(ROWS_WAVE),
            dma(ROWS_WAVE),
            dma(nz - 1, ROWS_WAVE),
            dma(nz - 1, ROWS_WAVE),
            dma(2, 2),
            dma(2, 2),
            dma(12),
            *spread_sems(nz),
            *spread_sems(nz),
            *spread_sems(nz),
            *spread_sems(nz),
        ],
        compiler_params=pltpu.CompilerParams(
            collective_id=0, has_side_effects=True, vmem_limit_bytes=FRONT_LIMIT
        ),
        cost_estimate=pl.CostEstimate(flops=40_000_000_000, bytes_accessed=20_000_000, transcendentals=0),
    )(tok, w_up, w_out, w_down, cot, wq3, seg, above, bias_qv, slopes, gain, shift, b_out, b_up)


class Halve:
    def __init__(self, near, far, cols, dims, depth, bufs, sems):
        self.near, self.far, self.cols, self.depth = near, far, cols, depth
        self.nz = dims[1]
        self.s, self.z = lax.axis_index("shard"), lax.axis_index("ctx")
        self.x_in, self.a_in, self.b_out, self.b_in = bufs
        self.xs, self.xr, self.as_, self.ar, self.bs, self.br = sems

    def place(self, bits):
        low, high = lax.rem(self.z, 2), lax.div(self.z, 2)
        low = 1 - low if bits & 1 else low
        high = 1 - high if bits & 2 else high
        return 2 * high + low

    def block(self, bits):
        return pl.ds(pl.multiple_of(self.place(bits) * self.depth, self.depth), self.depth)

    def x_copy(self):
        low, high = lax.rem(self.s, 2), lax.div(self.s, 2)
        return rcopy(
            self.far.at[:, self.cols],
            self.x_in.at[:, self.cols],
            self.xs,
            self.xr,
            {"shard": 2 * (1 - high) + low},
        )

    def a_copy(self, index):
        return rcopy(
            self.near.at[self.block((1, 3)[index]), self.cols],
            self.a_in.at[index, :, self.cols],
            self.as_.at[index],
            self.ar.at[index],
            {"ctx": self.place(1)},
        )

    def b_copy(self):
        return rcopy(
            self.b_out.at[:, self.cols], self.b_in.at[:, self.cols], self.bs, self.br, {"ctx": self.place(2)}
        )

    def step_x(self):
        self.x_copy().wait_recv()

        def one(r, carry):
            here = pl.ds(pl.multiple_of(r * 32, 32), 32)
            self.near[here, self.cols] = (
                self.near[here, self.cols].astype(F32) + self.x_in[here, self.cols].astype(F32)
            ).astype(BF)
            return carry

        lax.fori_loop(0, self.near.shape[0] // 32, one, 0)
        self.a_copy(0).start()
        self.a_copy(1).start()

    def step_a(self):
        self.a_copy(0).wait_recv()
        self.a_copy(1).wait_recv()
        self.b_out[:, self.cols] = (
            self.near[self.block(2), self.cols].astype(F32) + self.a_in[1, :, self.cols].astype(F32)
        ).astype(BF)
        self.b_copy().start()

    def step_b(self):
        self.b_copy().wait_recv()
        return (
            self.near[self.block(0), self.cols].astype(F32)
            + self.a_in[0, :, self.cols].astype(F32)
            + self.b_in[:, self.cols].astype(F32)
        )

    def finish(self):
        self.x_copy().wait_send()
        self.a_copy(0).wait_send()
        self.a_copy(1).wait_send()
        self.b_copy().wait_send()


PIECES = 6


def back_kernel(
    dims,
    query,
    key,
    value,
    out_heads,
    lse,
    info_all,
    ga_all,
    act_turned_in,
    wqkv_in,
    partial_in,
    down_in,
    mid_in,
    b_down,
    gmid_in,
    tok_in,
    slope_table,
    gain,
    shift,
    early,
    result_o,
    gtok_o,
    gup,
    gdown,
    gout,
    gwqkv,
    early_sum,
    late_sum,
    result,
    gtok,
    act_turned,
    wqkv,
    down_part,
    mid,
    gmid,
    tok,
    near,
    x_in,
    a_in,
    b_out,
    b_in,
    q_near,
    q_far,
    q_core,
    qx_in,
    q_all,
    dqkv,
    dk_trunk,
    dv_trunk,
    dk_seg,
    dv_seg,
    dk_up,
    dv_up,
    keys_aug,
    keys_turned,
    labels,
    parents,
    dq_all,
    n_send,
    n_recv,
    down_recv,
    wg_send,
    early_mine,
    early_recv,
    late,
    late_recv,
    d_sem,
    e_send,
    e_recv,
    f_send,
    f_recv,
    l_send,
    l_recv,
    p_send,
    p_recv,
    r_send,
    r_recv,
    ns_sem,
    nr_sem,
    xs_sem,
    xr_sem,
    as_sem,
    ar_sem,
    bs_sem,
    br_sem,
    qc_send,
    qc_recv,
    qx_sem,
    qz_send,
    qz_recv,
    n_local,
    load_sem,
    out_sem,
):
    ns, nz, rows = dims
    s, z, y = lax.axis_index("shard"), lax.axis_index("ctx"), lax.axis_index("tp")
    count = ns * nz
    me = s * nz + z
    chunk = rows // ROWS_WAVE
    width = tok.shape[1]
    depth = width // count
    span = nz * depth
    wide = 3 * PAIR
    other = {"tp": 1 - y}
    slopes = slope_table.at[y * nz + z]
    total_cols = near.shape[1]
    step_cols = total_cols // PIECES
    units = gup.shape[1]

    far = partial_in.at[1]
    load = pltpu.make_async_copy(partial_in.at[0], near, n_local)
    loads = [
        pltpu.make_async_copy(a, c, load_sem.at[k])
        for k, (a, c) in enumerate(
            (
                (down_in, down_part),
                (act_turned_in, act_turned),
                (wqkv_in, wqkv),
                (mid_in, mid),
                (gmid_in, gmid),
                (tok_in, tok),
            )
        )
    ]
    loads[0].start()
    load.start()
    for one in loads[1:]:
        one.start()

    def peer(d):
        index = lax.rem(me + d, count)
        return index, {"shard": lax.div(index, nz), "ctx": lax.rem(index, nz)}

    greet([other] + [peer(d)[1] for d in range(1, count)])

    halves = [
        Halve(
            near,
            far,
            slice(i * step_cols, (i + 1) * step_cols),
            dims,
            depth,
            (x_in, a_in, b_out, b_in),
            (xs_sem.at[i], xr_sem.at[i], as_sem.at[i], ar_sem.at[i], bs_sem.at[i], br_sem.at[i]),
        )
        for i in range(PIECES)
    ]
    def shard_flip(bits):
        low, high = lax.rem(s, 2), lax.div(s, 2)
        low = 1 - low if bits & 1 else low
        high = 1 - high if bits & 2 else high
        return 2 * high + low

    def q_copy(index):
        return rcopy(
            wg_send.at[pl.ds(pl.multiple_of(shard_flip((1, 3)[index]) * span, 128), span), :],
            q_core.at[index],
            qc_send.at[index],
            qc_recv.at[index],
            {"shard": shard_flip(1)},
        )

    def qx_copy():
        return rcopy(q_far, qx_in, qx_sem.at[0], qx_sem.at[1], {"shard": shard_flip(2)})

    def qz_copy(d):
        to = lax.rem(z + d, nz)
        return rcopy(
            q_near.at[pl.ds(pl.multiple_of(to * depth, depth), depth), :],
            q_all.at[z],
            qz_send.at[d - 1],
            qz_recv.at[d - 1],
            {"ctx": to},
        )

    def q_spread():
        qx_copy().wait_recv()
        q_near[...] = (q_near[...].astype(F32) + qx_in[...].astype(F32)).astype(BF)
        for d in range(1, nz):
            qz_copy(d).start()
        q_all[z] = q_near[pl.ds(pl.multiple_of(z * depth, depth), depth), :]

    def down_copy():
        return rcopy(down_part, down_recv, d_sem.at[0], d_sem.at[1], other)

    owners = width // 128

    def owner_cols(index):
        return pl.ds(pl.multiple_of(index * 128, 128), 128)

    def early_copy(d):
        index, device = peer(d)
        return index, rcopy(
            early_mine.at[:, owner_cols(lax.rem(index, owners))],
            early_recv.at[me],
            e_send.at[d - 1],
            e_recv.at[d - 1],
            device,
        )

    def spread_copy(d):
        cols = owner_cols(lax.rem(me, owners))
        return rcopy(
            early_sum.at[:, cols], early_sum.at[:, cols], f_send.at[d - 1], f_recv.at[d - 1], peer(d)[1]
        )

    def spread_arrival(d):
        index = lax.rem(me + count - d, count)
        cols = owner_cols(lax.rem(index, owners))
        return index, rcopy(
            early_sum.at[:, cols], early_sum.at[:, cols], f_send.at[d - 1], f_recv.at[d - 1], other
        )

    def late_copy(d):
        return rcopy(late, late_recv.at[me], l_send.at[d - 1], l_recv.at[d - 1], peer(d)[1])

    def over_peers(act):
        def one(d, carry):
            act(d)
            return carry

        lax.fori_loop(1, count, one, 0)

    for half in halves:
        half.x_copy().start()
    loads[0].wait()
    down_copy().start()

    fill_labels(info_all, rows // BRANCH, labels, parents)
    fill_trunk_keys(key, keys_aug)
    keys_turned[...] = key[0:TRUNK, :].T
    dk_trunk[...] = jnp.zeros(dk_trunk.shape, F32)
    dv_trunk[...] = jnp.zeros(dv_trunk.shape, F32)
    tile_mask = causal(BRANCH)

    def row_products(here, count_rows):
        turned = (ga_all[here, :].astype(F32) * out_heads[here, :].astype(F32)).T
        return jnp.concatenate(
            [
                jnp.sum(turned[:HD, :], axis=0, keepdims=True),
                jnp.sum(turned[HD:, :], axis=0, keepdims=True),
            ],
            axis=1,
        )

    def part_back(key_aug, value_rows, asked, given, level, drow, mask):
        logits = nt(key_aug, asked) * LOG2E - level
        if mask is not None:
            logits = jnp.where(mask, logits, NEG)
        probs = jnp.exp2(logits)
        grads = (probs * (nt(value_rows, given) - drow)).astype(BF)
        return probs.astype(BF), grads

    def segment(slot, carry):
        here = pl.ds(pl.multiple_of(TRUNK + slot * BRANCH, 128), BRANCH)
        seg = pl.ds(pl.multiple_of(slot * BRANCH, 128), BRANCH)
        stacked = stack_heads(query[here, :])
        asked = jnp.concatenate([stacked, query_features(slopes, BRANCH)], axis=1)
        given = stack_heads(ga_all[here, :])
        leaf, key_up, value_up = parent_pick(slot, labels, parents, key, value)
        own_feats, up_feats = segment_key_features(leaf)
        level = lse[pl.ds(4 + slot, 1), 0 : 2 * BRANCH]
        drow = row_products(here, BRANCH)
        probs, grads = part_back(keys_aug[...], value[0:TRUNK, :], asked, given, level, drow, None)
        dv_trunk[...] += nn(probs, given)
        dk_trunk[...] += nn(grads, stacked)
        turned = nn(keys_turned[...], grads)
        key_own = key[here, :]
        probs, grads = part_back(
            jnp.concatenate([key_own, own_feats], axis=1), value[here, :], asked, given, level, drow, tile_mask
        )
        dv_seg[seg, :] = nn(probs, given)
        dk_seg[seg, :] = nn(grads, stacked)
        turned = turned + nn(key_own.T, grads)
        probs, grads = part_back(
            jnp.concatenate([key_up, up_feats], axis=1), value_up, asked, given, level, drow, None
        )
        dv_up[seg, :] = nn(probs, given)
        dk_up[seg, :] = nn(grads, stacked)
        turned = turned + nn(key_up.T, grads)
        dqkv[here, 0:PAIR] = (unstack_turned(turned, BRANCH) * HD ** (-0.5)).astype(BF)
        return carry

    def dq_copy(to):
        return rcopy(
            dqkv.at[to * rows : (to + 1) * rows, 0:PAIR],
            dq_all.at[:, pl.ds(pl.multiple_of(z * wide, 128), PAIR)],
            r_send.at[to],
            r_recv.at[z],
            {"ctx": to},
        )

    def send_dq(to):
        @pl.when(z != to)
        def _():
            dq_copy(to).start()

    def piece_copy(to, i):
        return rcopy(
            dqkv.at[to * rows + i * chunk : to * rows + (i + 1) * chunk, PAIR:],
            dq_all.at[i * chunk : (i + 1) * chunk, pl.ds(pl.multiple_of(z * wide + PAIR, 128), 2 * PAIR)],
            p_send.at[to, i],
            p_recv.at[z, i],
            {"ctx": to},
        )

    wave_rows = TRUNK // 4
    wave_mask = causal(wave_rows)
    for tile in range(4):
        lo, hi = tile * wave_rows, (tile + 1) * wave_rows
        stacked = stack_heads(query[lo:hi, :])
        asked = jnp.concatenate([stacked, query_features(slopes, wave_rows)], axis=1)
        given = stack_heads(ga_all[lo:hi, :])
        level = lse[tile : tile + 1, :]
        drow = row_products(pl.ds(lo, wave_rows), wave_rows)
        probs, grads = part_back(
            keys_aug[lo:hi, :], value[lo:hi, :], asked, given, level, drow, wave_mask
        )
        dv_trunk[lo:hi, :] += nn(probs, given)
        dk_trunk[lo:hi, :] += nn(grads, stacked)
        turned = nn(keys_turned[:, lo:hi], grads)
        if tile:
            probs, grads = part_back(
                keys_aug[0:lo, :], value[0:lo, :], asked, given, level, drow, None
            )
            dv_trunk[0:lo, :] += nn(probs, given)
            dk_trunk[0:lo, :] += nn(grads, stacked)
            turned = turned + nn(keys_turned[:, 0:lo], grads)
        dqkv[lo:hi, 0:PAIR] = (unstack_turned(turned, wave_rows) * HD ** (-0.5)).astype(BF)
    send_dq(0)

    def turn(n, carry):
        @pl.when(n == 5)
        def _():
            send_dq(2)

        @pl.when(n == 7)
        def _():
            send_dq(1)
            load.wait()
            halves[0].step_x()

        return segment(jnp.where(n < 5, n + 2, jnp.where(n < 7, n - 5, n)), carry)

    lax.fori_loop(0, SLOTS, turn, 0)
    halves[1].step_x()
    send_dq(3)

    def gather_up(slot, carry):
        here = pl.ds(pl.multiple_of(TRUNK + slot * BRANCH, 128), BRANCH)
        seg = pl.ds(pl.multiple_of(slot * BRANCH, 128), BRANCH)
        mine = labels[pl.ds(slot, 1), :]
        dk, dv = dk_seg[seg, :], dv_seg[seg, :]
        for below in range(SLOTS):
            same = (parents[below : below + 1, :] == mine).astype(F32)
            at = below * BRANCH
            dk = dk + same * dk_up[at : at + BRANCH, :]
            dv = dv + same * dv_up[at : at + BRANCH, :]
        dqkv[here, PAIR : 2 * PAIR] = dk.astype(BF)
        dqkv[here, 2 * PAIR :] = dv.astype(BF)
        return carry

    lax.fori_loop(0, SLOTS, gather_up, 0)
    dqkv[0:TRUNK, PAIR : 2 * PAIR] = dk_trunk[...].astype(BF)
    dqkv[0:TRUNK, 2 * PAIR :] = dv_trunk[...].astype(BF)
    for i in range(ROWS_WAVE):
        for to in range(nz):

            @pl.when(z != to)
            def _():
                piece_copy(to, i).start()

    for to in range(nz):

        @pl.when(z == to)
        def _():
            dq_all[:, pl.ds(pl.multiple_of(z * wide, 128), wide)] = dqkv[to * rows : (to + 1) * rows, :]

    def weight(block, carry):
        here = pl.ds(pl.multiple_of(block * 128, 128), 128)
        wg_send[here, :] = nn(act_turned[here, :], dqkv[...]).astype(BF)
        return carry

    loads[1].wait()
    lax.fori_loop(0, width // 128, weight, 0)
    q_copy(0).start()
    q_copy(1).start()

    early_mine[...] = early[...]
    early_mine[6:7, pl.ds(pl.multiple_of(z * PAIR, 128), PAIR)] = jnp.sum(
        dqkv[:, 0:PAIR].astype(F32), axis=0, keepdims=True
    )
    early_mine[6:7, pl.ds(pl.multiple_of((nz + z) * PAIR, 128), PAIR)] = jnp.sum(
        dqkv[:, 2 * PAIR :].astype(F32), axis=0, keepdims=True
    )

    def early_send(d):
        index, copy = early_copy(d)

        @pl.when(index < owners)
        def _():
            copy.start()

    over_peers(early_send)
    early_recv[me] = early_mine[:, owner_cols(lax.rem(me, owners))]

    def at(i):
        return pl.ds(pl.multiple_of(i * chunk, 32), chunk)

    def n_copy(i):
        return rcopy(n_send.at[at(i), :], n_recv.at[at(i), :], ns_sem.at[i], nr_sem.at[i], other)

    def core_join():
        for index in range(2):
            q_copy(index).wait_recv()
            mine = pl.ds(pl.multiple_of(shard_flip((0, 2)[index]) * span, 128), span)
            (q_near, q_far)[index][...] = (wg_send[mine, :].astype(F32) + q_core[index].astype(F32)).astype(BF)
        qx_copy().start()

    def first(i):
        for owner in range(nz):

            @pl.when(z != owner)
            def _():
                if i == 0:
                    rcopy(
                        dqkv.at[0:rows, 0:PAIR],
                        dq_all.at[:, owner * wide : owner * wide + PAIR],
                        r_send.at[owner],
                        r_recv.at[owner],
                        {"ctx": owner},
                    ).wait_recv()
                rcopy(
                    dqkv.at[0:chunk, PAIR:],
                    dq_all.at[i * chunk : (i + 1) * chunk, owner * wide + PAIR : (owner + 1) * wide],
                    p_send.at[owner, i],
                    p_recv.at[owner, i],
                    {"ctx": owner},
                ).wait_recv()

        n_send[at(i), :] = nt(dq_all[at(i), :], wqkv[...]).astype(BF)
        n_copy(i).start()

    def gtok_store(i):
        return pltpu.make_async_copy(gtok.at[at(i), :], gtok_o.at[at(i), :], out_sem.at[i])

    result_store = pltpu.make_async_copy(result, result_o, out_sem.at[ROWS_WAVE])

    def second(i, carry):
        n_copy(i).wait_recv()
        here = at(i)
        grad = n_send[here, :].astype(F32) + n_recv[here, :].astype(F32)
        _, normed, inverse = norm_rows(tok[here, :].astype(F32), gain[0:1, :], shift[0:1, :])
        gtok[here, :] = gmid[here, :] + norm_rows_back(grad, normed, inverse, gain[0:1, :])
        late[0:1, :] += jnp.sum(grad * normed, axis=0, keepdims=True)
        late[1:2, :] += jnp.sum(grad, axis=0, keepdims=True)
        gtok_store(i).start()
        return carry

    def output(i, carry):
        here = at(i)
        result[here, :] = (
            mid[here, :] + b_down[...] + (down_part[here, :].astype(F32) + down_recv[here, :].astype(F32))
        ).astype(BF)
        return carry

    late[...] = jnp.zeros(late.shape, F32)
    for one in loads[2:]:
        one.wait()
    core_join()
    halves[2].step_x()
    first(0)
    first(1)
    halves[3].step_x()
    first(2)
    halves[4].step_x()
    first(3)
    halves[5].step_x()
    down_copy().wait_recv()
    lax.fori_loop(0, ROWS_WAVE, output, 0)
    result_store.start()

    @pl.when(me < owners)
    def _():
        over_peers(lambda d: early_copy(d)[1].wait_recv())
        total = early_recv[0]
        for index in range(1, count):
            total = total + early_recv[index]
        early_sum[:, owner_cols(lax.rem(me, owners))] = total
        over_peers(lambda d: spread_copy(d).start())

    q_spread()
    halves[0].step_a()
    halves[1].step_a()
    lax.fori_loop(0, 2, second, 0)
    halves[2].step_a()
    lax.fori_loop(2, ROWS_WAVE, second, 0)
    over_peers(lambda d: late_copy(d).start())
    late_recv[me] = late[...]
    halves[3].step_a()
    halves[4].step_a()
    halves[5].step_a()

    for d in range(1, nz):
        qz_copy(d).wait_recv()
    for owner in range(nz):
        for part in range(3):
            gwqkv[part, :, owner * PAIR : (owner + 1) * PAIR] = q_all[
                owner, :, part * PAIR : (part + 1) * PAIR
            ].astype(F32)
    bounds = (0, units, 2 * units, total_cols)
    for i, half in enumerate(halves):
        block = half.step_b()
        lo, hi = i * step_cols, (i + 1) * step_cols
        for target, start_at, end_at in (
            (gup, bounds[0], bounds[1]),
            (gdown, bounds[1], bounds[2]),
            (gout, bounds[2], bounds[3]),
        ):
            a, b = max(lo, start_at), min(hi, end_at)
            if a < b:
                target[:, a - start_at : b - start_at] = block[:, a - lo : b - lo]

    def early_wait(d):
        index, copy = spread_arrival(d)

        @pl.when(index < owners)
        def _():
            copy.wait_recv()

    over_peers(early_wait)
    over_peers(lambda d: late_copy(d).wait_recv())
    total = late_recv[0]
    for index in range(1, count):
        total = total + late_recv[index]
    late_sum[...] = total
    result_store.wait()

    down_copy().wait_send()
    for half in halves:
        half.finish()
    qx_copy().wait_send()
    for d in range(1, nz):
        qz_copy(d).wait_send()
    q_copy(0).wait_send()
    q_copy(1).wait_send()

    def early_drain(d):
        index, copy = early_copy(d)

        @pl.when(index < owners)
        def _():
            copy.wait_send()

    over_peers(early_drain)

    @pl.when(me < owners)
    def _():
        over_peers(lambda d: spread_copy(d).wait_send())

    over_peers(lambda d: late_copy(d).wait_send())

    def finish(i, carry):
        n_copy(i).wait_send()
        gtok_store(i).wait()
        return carry

    lax.fori_loop(0, ROWS_WAVE, finish, 0)
    for owner in range(nz):

        @pl.when(z != owner)
        def _():
            dq_copy(owner).wait_send()
            for i in range(ROWS_WAVE):
                piece_copy(owner, i).wait_send()


def run_back(dims, units, *inputs):
    ns, nz, rows = dims
    width = inputs[14].shape[1]
    _, span, total = inputs[9].shape
    count = ns * nz
    depth = width // count
    wide = 3 * PAIR
    anywhere = pl.BlockSpec(memory_space=pl.ANY)
    return pl.pallas_call(
        partial(back_kernel, dims),
        name="tree_backward",
        out_shape=(
            shape((rows, width), BF),
            shape((rows, width), F32),
            shape((depth, units), F32),
            shape((depth, units), F32),
            shape((depth, total - 2 * units), F32),
            shape((3, depth, nz * PAIR), F32),
            shape((8, width), F32),
            shape((2, width), F32),
        ),
        in_specs=[vmem()] * 7 + [anywhere] * 5 + [vmem()] + [anywhere] * 2 + [vmem()] * 4,
        out_specs=[anywhere] * 2 + [vmem()] * 6,
        scratch_shapes=[
            pltpu.VMEM((rows, width), BF),
            pltpu.VMEM((rows, width), F32),
            *[pltpu.VMEM(inputs[k].shape, inputs[k].dtype) for k in (7, 8, 10, 11, 13, 14)],
            pltpu.VMEM((span, total), BF),
            pltpu.VMEM((span, total), BF),
            pltpu.VMEM((2, depth, total), BF),
            pltpu.VMEM((depth, total), BF),
            pltpu.VMEM((depth, total), BF),
            pltpu.VMEM((span, wide), BF),
            pltpu.VMEM((span, wide), BF),
            pltpu.VMEM((2, span, wide), BF),
            pltpu.VMEM((span, wide), BF),
            pltpu.VMEM((nz, depth, wide), BF),
            pltpu.VMEM((TREE, wide), BF),
            pltpu.VMEM((TRUNK, PAIR), F32),
            pltpu.VMEM((TRUNK, PAIR), F32),
            pltpu.VMEM((TREE - TRUNK, PAIR), F32),
            pltpu.VMEM((TREE - TRUNK, PAIR), F32),
            pltpu.VMEM((TREE - TRUNK, PAIR), F32),
            pltpu.VMEM((TREE - TRUNK, PAIR), F32),
            pltpu.VMEM((TRUNK, 2 * PAIR), BF),
            pltpu.VMEM((PAIR, TRUNK), BF),
            pltpu.VMEM((16, 128), F32),
            pltpu.VMEM((16, 128), F32),
            pltpu.VMEM((rows, nz * wide), BF),
            pltpu.VMEM((rows, width), BF),
            pltpu.VMEM((rows, width), BF),
            pltpu.VMEM((rows, width), BF),
            pltpu.VMEM((width, wide), BF),
            pltpu.VMEM((8, width), F32),
            pltpu.VMEM((count, 8, 128), F32),
            pltpu.VMEM((2, width), F32),
            pltpu.VMEM((count, 2, width), F32),
            dma(2),
            dma(count - 1),
            dma(count - 1),
            dma(count - 1),
            dma(count - 1),
            dma(count - 1),
            dma(count - 1),
            dma(nz, ROWS_WAVE),
            dma(nz, ROWS_WAVE),
            dma(nz),
            dma(nz),
            dma(ROWS_WAVE),
            dma(ROWS_WAVE),
            dma(PIECES),
            dma(PIECES),
            dma(PIECES, 2),
            dma(PIECES, 2),
            dma(PIECES),
            dma(PIECES),
            dma(2),
            dma(2),
            dma(2),
            dma(nz - 1),
            dma(nz - 1),
            pltpu.SemaphoreType.DMA,
            dma(6),
            dma(ROWS_WAVE + 1),
        ],
        compiler_params=pltpu.CompilerParams(
            collective_id=2, has_side_effects=True, vmem_limit_bytes=60 << 20
        ),
        cost_estimate=pl.CostEstimate(flops=40_000_000_000, bytes_accessed=20_000_000, transcendentals=0),
    )(*inputs)


def place_kernel(early, late, *refs):
    count = (len(refs) - 7) // 3
    sources, targets, middle = refs[:count], refs[count : 2 * count], refs[2 * count + 6 : -1]
    b_qv, b_out, b_up, b_down, gains, shifts = refs[2 * count : 2 * count + 6]
    sems = refs[-1]
    loads = [pltpu.make_async_copy(a, b, sems.at[0, k]) for k, (a, b) in enumerate(zip(sources, middle))]
    copies = [pltpu.make_async_copy(a, b, sems.at[1, k]) for k, (a, b) in enumerate(zip(middle, targets))]
    for load in loads:
        load.start()
    for load, copy in zip(loads, copies):
        load.wait()
        copy.start()
    wide, width = b_qv.shape[1], b_out.shape[1]
    for row in range(2):
        b_qv[row : row + 1, :] = early[6:7, row * wide : (row + 1) * wide]
    b_out[...] = early[2:3, :]
    for row in range(b_up.shape[1] // width):
        b_up[:, row * width : (row + 1) * width] = early[row : row + 1, :]
    b_down[...] = early[3:4, :]
    gains[0:1, :] = late[0:1, :]
    gains[1:2, :] = early[4:5, :]
    shifts[0:1, :] = late[1:2, :]
    shifts[1:2, :] = early[5:6, :]
    for copy in copies:
        copy.wait()


def run_place(early, late, wide, units, *arrays):
    width = early.shape[1]
    anywhere = pl.BlockSpec(memory_space=pl.ANY)
    return pl.pallas_call(
        place_kernel,
        name="place",
        out_shape=(
            *[shape(a.shape, a.dtype) for a in arrays],
            shape((2, wide), F32),
            shape((1, width), F32),
            shape((1, units), F32),
            shape((1, width), F32),
            shape((2, width), F32),
            shape((2, width), F32),
        ),
        in_specs=[vmem()] * 2 + [anywhere] * len(arrays),
        out_specs=[anywhere] * len(arrays) + [vmem()] * 6,
        scratch_shapes=[*[pltpu.VMEM(a.shape, a.dtype) for a in arrays], dma(2, len(arrays))],
        compiler_params=pltpu.CompilerParams(vmem_limit_bytes=60 << 20),
    )(early, late, *arrays)


def position_slopes(ntp, nz):
    index = np.arange(HEADS, dtype=np.float32).reshape(ntp * nz, 2)
    slope = np.exp2(-8.0 * (index + 1.0) / HEADS).astype(np.float32)
    table = np.zeros((ntp * nz, 2, 128), np.float32)
    left = slope
    for part in range(3):
        piece = left.astype(BF).astype(np.float32)
        table[:, :, part] = piece
        table[:, :, part + 3] = piece
        left = left - piece
    table[:, :, 6] = 1.0
    return table


def fast_device(
    tokens, cotangent, seg_ids, positions, parents, w_qkv, b_qv, w_out, b_out, w_up, b_up, w_down, b_down, ln_gain, ln_bias
):
    rows = tokens.shape[0]
    ns, nz, ntp = lax.axis_size("shard"), lax.axis_size("ctx"), lax.axis_size("tp")
    dims = (ns, nz, rows)

    slopes = jnp.asarray(position_slopes(ntp, nz))
    units = b_up.shape[0]
    (
        act_turned, query, key, value, out_heads, lse, info_all, wqkv, partial_sums, ga_all, down_part, mid, gmid, sums
    ) = run_front(
        dims, tokens, w_up, w_out.T, w_down.T, cotangent, w_qkv, seg_ids.reshape(rows // BRANCH, BRANCH),
        parents[None, :], b_qv, slopes, ln_gain, ln_bias,
        b_out[None, :], b_up[None, :],
    )
    result, grad_tokens, gup, gdown, gout, grad_w_qkv, early, late = run_back(
        dims, units, query, key, value, out_heads, lse, info_all, ga_all, act_turned, wqkv, partial_sums, down_part,
        mid, b_down[None, :], gmid, tokens, slopes, ln_gain, ln_bias, sums,
    )
    result, grad_tokens, grad_w_qkv, gup, gdown, gout, b_qv_sum, b_out_sum, b_up_sum, b_down_sum, gains, shifts = run_place(
        early, late, nz * PAIR, units, result, grad_tokens, grad_w_qkv, gup, gdown, gout
    )
    return (
        result,
        grad_tokens,
        grad_w_qkv,
        b_qv_sum,
        gout.T,
        b_out_sum.reshape(-1),
        gup,
        b_up_sum.reshape(-1),
        gdown.T,
        b_down_sum.reshape(-1),
        gains,
        shifts,
    )


def norm_forward(inputs_in, gain_row, shift_row):
    centre = inputs_in - jnp.mean(inputs_in, axis=-1, keepdims=True)
    inverse = lax.rsqrt(jnp.mean(centre * centre, axis=-1, keepdims=True) + EPS)
    normed = centre * inverse
    return (normed * gain_row + shift_row, normed, inverse)


def norm_backward(grad_in, normed, inverse, gain_row):
    scaled = grad_in * gain_row
    mean_grad = jnp.mean(scaled, axis=-1, keepdims=True)
    mean_cross = jnp.mean(scaled * normed, axis=-1, keepdims=True)
    return inverse * (scaled - mean_grad - normed * mean_cross)


def ancestry(seg_vals, parents):
    first_up = jnp.take(parents, seg_vals)
    return (first_up, jnp.take(parents, first_up))


def block_scores(query_heads, key_heads, query_tags, key_tags, slopes):
    q_seg, q_first, q_second, q_pos = query_tags
    k_seg, k_pos = key_tags
    raw_scores = jnp.einsum(
        "qhd,khd->hqk", query_heads, key_heads, preferred_element_type=jnp.float32
    ) * HD ** (-0.5)
    distance = (q_pos[:, None] - k_pos[None, :]).astype(jnp.float32)
    scores = raw_scores - slopes[:, None, None] * distance[None]
    related = (
        (k_seg[None, :] == q_seg[:, None])
        | (k_seg[None, :] == q_first[:, None])
        | (k_seg[None, :] == q_second[:, None])
    )
    allowed = related & (k_pos[None, :] <= q_pos[:, None])
    return (scores, allowed[None])


def probabilities(scores, allowed, row_max, row_sum):
    shifted = jnp.where(allowed, scores - row_max[:, :, None], NEG)
    return jnp.exp(shifted) / row_sum[:, :, None]


def per_device(
    tokens,
    cotangent,
    seg_ids,
    positions,
    parents,
    w_qkv,
    b_qv,
    w_out,
    b_out,
    w_up,
    b_up,
    w_down,
    b_down,
    ln_gain,
    ln_bias,
):
    num_rows = tokens.shape[0]
    head_count = HEADS // lax.axis_size("tp")
    head_width = head_count * HD
    head_index = (lax.axis_index("tp") * head_count + jnp.arange(head_count)).astype(jnp.float32)
    slopes = 2.0 ** (-8.0 * (head_index + 1.0) / HEADS)
    scale = HD ** (-0.5)
    full_qkv, full_out = (
        lax.all_gather(w_qkv, ("shard", "ctx"), axis=1, tiled=True),
        lax.all_gather(w_out, ("shard", "ctx"), axis=1, tiled=True),
    )
    group_seg, group_pos = (
        lax.all_gather(seg_ids, "ctx", axis=0, tiled=True),
        lax.all_gather(positions, "ctx", axis=0, tiled=True),
    )
    own_first, own_second = ancestry(seg_ids, parents)
    own_tags = (seg_ids, own_first, own_second, positions)
    inputs = tokens.astype(jnp.float32)
    norm_one, normed_one, inverse_one = norm_forward(inputs, ln_gain[0], ln_bias[0])
    act_one = norm_one.astype(jnp.bfloat16)
    projected = jnp.einsum("td,cde->cte", act_one, full_qkv, preferred_element_type=jnp.float32)
    qkv_bias = jnp.stack([b_qv[0], jnp.zeros((head_width,), jnp.float32), b_qv[1]])
    qkv_low = (projected + qkv_bias[:, None, :]).astype(jnp.bfloat16)
    query_flat, key_flat, value_flat = (qkv_low[0], qkv_low[1], qkv_low[2])
    group_keys, group_values = (
        lax.all_gather(key_flat, "ctx", axis=0, tiled=True),
        lax.all_gather(value_flat, "ctx", axis=0, tiled=True),
    )
    group_rows = group_keys.shape[0]
    block_count = group_rows // KEY_BLOCK
    key_blocks = group_keys.reshape(block_count, KEY_BLOCK, head_count, HD)
    value_blocks = group_values.reshape(block_count, KEY_BLOCK, head_count, HD)
    seg_blocks = group_seg.reshape(block_count, KEY_BLOCK)
    pos_blocks = group_pos.reshape(block_count, KEY_BLOCK)
    query_heads = query_flat.reshape(num_rows, head_count, HD)

    def stats_step(carry_in, block_parts):
        row_max, row_sum = carry_in
        key_part, seg_part, pos_part = block_parts
        scores, allowed = block_scores(
            query_heads, key_part, own_tags, (seg_part, pos_part), slopes
        )
        new_max = jnp.maximum(row_max, jnp.max(jnp.where(allowed, scores, NEG), axis=-1))
        shifted = jnp.where(allowed, scores - new_max[:, :, None], NEG)
        row_sum = row_sum * jnp.exp(row_max - new_max) + jnp.sum(jnp.exp(shifted), axis=-1)
        return ((new_max, row_sum), None)

    start_stats = (
        jnp.full((head_count, num_rows), NEG, jnp.float32),
        jnp.zeros((head_count, num_rows), jnp.float32),
    )
    (row_max, row_sum), _ = lax.scan(stats_step, start_stats, (key_blocks, seg_blocks, pos_blocks))

    def output_step(out_accum, block_parts):
        key_part, value_part, seg_part, pos_part = block_parts
        scores, allowed = block_scores(
            query_heads, key_part, own_tags, (seg_part, pos_part), slopes
        )
        prob_low = probabilities(scores, allowed, row_max, row_sum).astype(jnp.bfloat16)
        return (
            out_accum
            + jnp.einsum("hqk,khd->qhd", prob_low, value_part, preferred_element_type=jnp.float32),
            None,
        )

    attended, _ = lax.scan(
        output_step,
        jnp.zeros((num_rows, head_count, HD), jnp.float32),
        (key_blocks, value_blocks, seg_blocks, pos_blocks),
    )
    attended_low = attended.reshape(num_rows, head_width).astype(jnp.bfloat16)
    branch_one = (
        lax.psum(
            jnp.dot(attended_low, full_out, preferred_element_type=jnp.float32).astype(
                jnp.bfloat16
            ),
            "tp",
        ).astype(jnp.float32)
        + b_out
    )
    middle = inputs + branch_one
    full_up, full_down = (
        lax.all_gather(w_up, ("shard", "ctx"), axis=0, tiled=True),
        lax.all_gather(w_down, ("shard", "ctx"), axis=1, tiled=True),
    )
    norm_two, normed_two, inverse_two = norm_forward(middle, ln_gain[1], ln_bias[1])
    act_two = norm_two.astype(jnp.bfloat16)
    upper_in = jnp.dot(act_two, full_up, preferred_element_type=jnp.float32) + b_up
    gelu_vals, gelu_pull = jax.vjp(partial(jax.nn.gelu, approximate=True), upper_in)
    hidden = gelu_vals.astype(jnp.bfloat16)
    branch_two = (
        lax.psum(
            jnp.dot(hidden, full_down, preferred_element_type=jnp.float32).astype(jnp.bfloat16),
            "tp",
        ).astype(jnp.float32)
        + b_down
    )
    result = (middle + branch_two).astype(jnp.bfloat16)
    grad_out = cotangent.astype(jnp.float32)
    grad_hidden = jnp.einsum("td,fd->tf", cotangent, full_down, preferred_element_type=jnp.float32)
    grad_upper = gelu_pull(grad_hidden)[0].astype(jnp.bfloat16)
    down_term = jnp.einsum("tf,td->fd", hidden, cotangent, preferred_element_type=jnp.float32)
    up_term = jnp.einsum("td,tf->df", act_two, grad_upper, preferred_element_type=jnp.float32)
    grad_w_up, grad_w_down = (
        lax.psum_scatter(up_term, ("shard", "ctx"), scatter_dimension=0, tiled=True),
        lax.psum_scatter(down_term, ("shard", "ctx"), scatter_dimension=1, tiled=True),
    )
    grad_norm_two = lax.psum(
        jnp.einsum("tf,df->td", grad_upper, full_up, preferred_element_type=jnp.float32).astype(
            jnp.bfloat16
        ),
        "tp",
    ).astype(jnp.float32)
    grad_middle = grad_out + norm_backward(grad_norm_two, normed_two, inverse_two, ln_gain[1])
    grad_branch = grad_middle.astype(jnp.bfloat16)
    out_term = jnp.einsum(
        "te,td->ed", attended_low, grad_branch, preferred_element_type=jnp.float32
    )
    grad_att = jnp.einsum(
        "td,ed->te", grad_branch, full_out, preferred_element_type=jnp.float32
    ).astype(jnp.bfloat16)
    grad_heads = grad_att.reshape(num_rows, head_count, HD)
    row_terms = jnp.einsum("qhd,qhd->hq", grad_heads.astype(jnp.float32), attended)

    def joint_step(grad_accum, block_parts):
        key_part, value_part, seg_part, pos_part = block_parts
        scores, allowed = block_scores(
            query_heads, key_part, own_tags, (seg_part, pos_part), slopes
        )
        prob_vals = probabilities(scores, allowed, row_max, row_sum)
        grad_probs = jnp.einsum(
            "qhd,khd->hqk", grad_heads, value_part, preferred_element_type=jnp.float32
        )
        grad_scores = (prob_vals * (grad_probs - row_terms[:, :, None])).astype(jnp.bfloat16)
        grad_accum = (
            grad_accum
            + jnp.einsum("hqk,khd->qhd", grad_scores, key_part, preferred_element_type=jnp.float32)
            * scale
        )
        key_part_grad = (
            jnp.einsum("hqk,qhd->khd", grad_scores, query_heads, preferred_element_type=jnp.float32)
            * scale
        )
        value_part_grad = jnp.einsum(
            "hqk,qhd->khd",
            prob_vals.astype(jnp.bfloat16),
            grad_heads,
            preferred_element_type=jnp.float32,
        )
        return (
            grad_accum,
            (
                key_part_grad.reshape(KEY_BLOCK, head_width),
                value_part_grad.reshape(KEY_BLOCK, head_width),
            ),
        )

    grad_query_sum, (key_terms, value_terms) = lax.scan(
        joint_step,
        jnp.zeros((num_rows, head_count, HD), jnp.float32),
        (key_blocks, value_blocks, seg_blocks, pos_blocks),
    )
    key_grad_sum, value_grad_sum = (
        lax.psum_scatter(
            key_terms.reshape(group_rows, head_width).astype(jnp.bfloat16),
            "ctx",
            scatter_dimension=0,
            tiled=True,
        ).astype(jnp.float32),
        lax.psum_scatter(
            value_terms.reshape(group_rows, head_width).astype(jnp.bfloat16),
            "ctx",
            scatter_dimension=0,
            tiled=True,
        ).astype(jnp.float32),
    )
    grad_query_low = grad_query_sum.reshape(num_rows, head_width).astype(jnp.bfloat16)
    grad_key_low = key_grad_sum.astype(jnp.bfloat16)
    grad_value_low = value_grad_sum.astype(jnp.bfloat16)
    grad_qkv = jnp.stack([grad_query_low, grad_key_low, grad_value_low])
    grad_norm_one = lax.psum(
        jnp.einsum("cte,cde->td", grad_qkv, full_qkv, preferred_element_type=jnp.float32).astype(
            jnp.bfloat16
        ),
        "tp",
    ).astype(jnp.float32)
    grad_tokens = grad_middle + norm_backward(grad_norm_one, normed_one, inverse_one, ln_gain[0])
    qkv_term = jnp.einsum("td,cte->cde", act_one, grad_qkv, preferred_element_type=jnp.float32)
    grad_w_qkv, grad_w_out = (
        lax.psum_scatter(qkv_term, ("shard", "ctx"), scatter_dimension=1, tiled=True),
        lax.psum_scatter(out_term, ("shard", "ctx"), scatter_dimension=1, tiled=True),
    )
    bias_qv_part = jnp.stack(
        [
            jnp.sum(grad_query_low.astype(jnp.float32), axis=0),
            jnp.sum(grad_value_low.astype(jnp.float32), axis=0),
        ]
    )
    out_bias_part = jnp.sum(grad_branch.astype(jnp.float32), axis=0)
    up_bias_part = jnp.sum(grad_upper.astype(jnp.float32), axis=0)
    down_bias_part = jnp.sum(grad_out, axis=0)
    gain_part = jnp.stack(
        [jnp.sum(grad_norm_one * normed_one, axis=0), jnp.sum(grad_norm_two * normed_two, axis=0)]
    )
    shift_part = jnp.stack([jnp.sum(grad_norm_one, axis=0), jnp.sum(grad_norm_two, axis=0)])
    grad_b_qv, grad_b_out, grad_b_up, grad_b_down, grad_gain, grad_shift = lax.psum(
        (bias_qv_part, out_bias_part, up_bias_part, down_bias_part, gain_part, shift_part),
        ("shard", "ctx"),
    )
    return (
        result,
        grad_tokens,
        grad_w_qkv,
        grad_b_qv,
        grad_w_out,
        grad_b_out,
        grad_w_up,
        grad_b_up,
        grad_w_down,
        grad_b_down,
        grad_gain,
        grad_shift,
    )


def solution(mesh):
    placed = (
        P(("shard", "ctx"), None),
        P(("shard", "ctx"), None),
        P(("shard", "ctx")),
        P(("shard", "ctx")),
        P(),
        P(None, ("shard", "ctx"), "tp"),
        P(None, "tp"),
        P("tp", ("shard", "ctx")),
        P(),
        P(("shard", "ctx"), "tp"),
        P("tp"),
        P("tp", ("shard", "ctx")),
        P(),
        P(),
        P(),
    )
    sizes = dict(mesh.shape)
    paired = sizes["tp"] * sizes["ctx"] * 2 == HEADS and sizes["tp"] == 2 and sizes["shard"] == 4
    return jax.shard_map(
        fast_device if paired else per_device,
        mesh=mesh,
        in_specs=placed,
        out_specs=(
            P(("shard", "ctx"), None),
            P(("shard", "ctx"), None),
            P(None, ("shard", "ctx"), "tp"),
            P(None, "tp"),
            P("tp", ("shard", "ctx")),
            P(),
            P(("shard", "ctx"), "tp"),
            P("tp"),
            P("tp", ("shard", "ctx")),
            P(),
            P(),
            P(),
        ),
        check_vma=False,
    )
```
